32 devices in a mesh: sec: 8 (over y, x, core), tile: 4 (over z).
Axes of the slice: x: 2, y: 2, z: 4, core: 2. Of those that a mesh axis runs over, the one named last changes fastest.
Arguments:
- section_image: bfloat16 [8, 2048, 1024], P('sec', 'tile')
- offsets: int32 [8, 4, 2], P('sec', 'tile'), may hold values from -16 to 16, as said below
- peak_shift: int32 [8, 16, 8, 2], P('sec', 'tile'), may hold values from -8 to 8
- accepted: int32 [8, 16, 8], P('sec', 'tile'), may hold values 0 or 1
Outputs:
- coarse_map: float32 [8, 512, 256], P('sec', 'tile')
- flow_map: float32 [8, 2048, 1024], P('sec', 'tile')
The draws below stay inside these ranges and needn't reach their ends.
Inputs may be any that keep to these rules, and one draw needn't show every extreme that they name: `offsets`: in every section some strip has row offset 16 and another strip row offset -16.
All inputs are finite; a program needn't handle non-finite values. No bound on the sum of `accepted` on one device may be relied on, other than what follows from the above.
Results may differ from the reference program's by a relative error of at most 0.0065.
Values may be sent and summed in bfloat16 or wider, within the bound.
A program may use at most 192 MiB of HBM per device.

```python
import math
import jax
import jax.numpy as jnp
from jax import lax

P_SIZE = 128
DS = 4
COARSE = 16
PEAK = 8
TH = 512
W = 1024
SECTIONS = 8
TILES = 4
H4 = 128
W4 = 256
NPR = 4
NPC = 8
RIM = 72


def draw_section_image(key, part):
    key_one, key_two, key_three = jax.random.split(key, 3)
    shape_all = (SECTIONS, TILES * TH, W)
    noise = jax.random.normal(key_one, shape_all, jnp.float32)
    row_scale = jnp.exp(jax.random.uniform(key_two, (SECTIONS, TILES * TH, 1), jnp.float32, 0.0, math.log(10.0)))
    col_scale = jnp.exp(jax.random.uniform(key_three, (SECTIONS, 1, W), jnp.float32, 0.0, math.log(10.0)))
    return (noise * row_scale * col_scale * 0.1).astype(jnp.bfloat16)


def draw_offsets(key, part):
    key_one, key_two = jax.random.split(jax.random.fold_in(key, 7), 2)
    draws_int = jax.random.randint(key_one, (SECTIONS, TILES, 2), -COARSE, COARSE + 1, dtype=jnp.int32)
    chosen = jax.random.randint(key_two, (SECTIONS, 1), 0, TILES, dtype=jnp.int32)
    counter = jnp.arange(TILES, dtype=jnp.int32)[None, :]
    row_shift = jnp.where(counter == chosen, COARSE, draws_int[:, :, 0])
    row_shift = jnp.where(counter == (chosen + 1) % TILES, -COARSE, row_shift)
    return jnp.stack([row_shift, draws_int[:, :, 1]], axis=2).astype(jnp.int32)


def set_ends(array, own_key, smallest, high):
    longest = array.shape.index(max(array.shape))
    spots = []
    for shift in (0, 1):
        where = [jax.random.randint(jax.random.fold_in(own_key, axis), (), 0, length) for axis, length in enumerate(array.shape)]
        where[longest] = (where[longest] + shift) % array.shape[longest]
        spots.append(tuple(where))
    return array.at[spots[0]].set(smallest).at[spots[1]].set(high)


def setup_inputs(seed: int = 0) -> dict:
    key_of = jax.random.split(jax.random.key(seed), 5)
    section_image = draw_section_image(jax.random.fold_in(key_of[4], 71), 0)
    offsets = draw_offsets(jax.random.fold_in(key_of[4], 71), 0)
    peak_shift = set_ends(jax.random.randint(key_of[2], (SECTIONS, TILES * NPR, NPC, 2), -PEAK, PEAK + 1), jax.random.fold_in(key_of[2], 1), -PEAK, PEAK).astype(jnp.int32)
    accepted = set_ends((jax.random.randint(key_of[3], (SECTIONS, TILES * NPR, NPC), 0, 4) < 3).astype(jnp.int32), jax.random.fold_in(key_of[3], 1), 0, 1)
    return {"section_image": section_image, "offsets": offsets, "peak_shift": peak_shift, "accepted": accepted}


epsilon = 1e-05

def shrink(field):
    return field.astype(jnp.float32).reshape(field.shape[0] // DS, DS, field.shape[1] // DS, DS).mean(axis=(1, 3)).astype(jnp.bfloat16)

def standardize(field):
    centre = lax.optimization_barrier(jnp.mean(field, axis=(1, 2), keepdims=True))
    centred = field - centre
    spread = lax.optimization_barrier(jnp.mean(centred * centred, axis=(1, 2), keepdims=True))
    return centred / jnp.sqrt(spread + epsilon)

def spectral_corr(left_side, right_side):
    left_spec = jnp.fft.fft2(left_side, axes=(1, 2))
    right_spec = jnp.fft.fft2(right_side, axes=(1, 2))
    return jnp.real(jnp.fft.ifft2(jnp.conj(left_spec) * right_spec, axes=(1, 2))).astype(jnp.float32)

def reference(section_image, offsets, peak_shift, accepted):
    previous_all = jnp.concatenate([jnp.zeros_like(section_image[:1]), section_image[:-1]], axis=0)

    def one_section(items):
        current, previous, tile_offs, peaks_here, keep_here = items
        small_now = shrink(current)
        small_prev = shrink(previous)
        padded_small = jnp.pad(small_prev, COARSE)
        own_small = small_now.reshape(TILES, H4, W4)
        tile_ids = jnp.arange(TILES, dtype=jnp.int32)

        def grab_small(tile_id, offset_pair):
            row_at = (tile_id * H4 + offset_pair[0] + COARSE).astype(jnp.int32)
            col_at = (offset_pair[1] + COARSE).astype(jnp.int32)
            return lax.dynamic_slice(padded_small, (row_at, col_at), (H4, W4))
        windows = jax.vmap(grab_small)(tile_ids, tile_offs)
        coarse = spectral_corr(standardize(own_small.astype(jnp.float32)), standardize(windows.astype(jnp.float32)))
        coarse_part = (coarse / math.sqrt(H4 * W4)).reshape(TILES * H4, W4)
        padded_full = jnp.pad(previous, RIM)
        own_patches = current.reshape(TILES * NPR, P_SIZE, NPC, P_SIZE).transpose(0, 2, 1, 3)
        row_offs = jnp.repeat(tile_offs[:, 0], NPR).astype(jnp.int32)
        col_offs = jnp.repeat(tile_offs[:, 1], NPR).astype(jnp.int32)
        row_base = (RIM + jnp.arange(TILES * NPR, dtype=jnp.int32)[:, None] * P_SIZE + DS * row_offs[:, None] + peaks_here[:, :, 0]).astype(jnp.int32)
        col_base = (RIM + jnp.arange(NPC, dtype=jnp.int32)[None, :] * P_SIZE + DS * col_offs[:, None] + peaks_here[:, :, 1]).astype(jnp.int32)

        def one_row(row_items):
            own_row, row_starts, col_starts, keep = row_items

            def grab(row_at, col_at):
                return lax.dynamic_slice(padded_full, (row_at, col_at), (P_SIZE, P_SIZE))
            windows_row = jax.vmap(grab)(row_starts, col_starts)
            result = spectral_corr(standardize(own_row.astype(jnp.float32)), standardize(windows_row.astype(jnp.float32)))
            return result / float(P_SIZE) * keep.astype(jnp.float32)[:, None, None]
        flows = lax.map(one_row, (own_patches, row_base, col_base, keep_here))
        flow_part = flows.transpose(0, 2, 1, 3).reshape(TILES * TH, W)
        return (coarse_part, flow_part)
    coarse_map, flow_map = lax.map(one_section, (section_image, previous_all, offsets, peak_shift, accepted))
    return (coarse_map, flow_map)
```

```python
import functools
import math

import jax
import jax.numpy as jnp
import ml_dtypes
import numpy as np
from jax import lax
from jax.experimental import pallas as pl
from jax.experimental.pallas import tpu as pltpu
from jax.sharding import PartitionSpec as P

P_SIZE = 128
HALF = P_SIZE // 2
DS = 4
COARSE = 16
HALO = 80
LANES = 128
PAIR = 2 * P_SIZE
SUB = 8
POOLED = P_SIZE // DS
EPSILON = 1e-05
MESH = pl.DeviceIdType.MESH


def quantized(table):
    return table.astype(np.float32).astype(ml_dtypes.bfloat16)


def table_scale(n):
    cosines = np.cos(2.0 * np.pi * np.arange(n) / n)
    best = None
    for factor in np.linspace(1.0, 2.0, 4001):
        table = quantized(cosines * factor).astype(np.float64)
        gain = (table @ cosines) / (cosines @ cosines)
        error = np.mean((table / gain - cosines) ** 2)
        if best is None or error < best[0]:
            best = (error, factor, gain)
    return best[1], best[2]


def waves(n):
    k = np.arange(n)
    angles = (k[:, None] * k[None, :] % n) * (2.0 * np.pi / n)
    return np.cos(angles), np.sin(angles)


def row_tables():
    n = P_SIZE
    factor, gain = table_scale(n)
    cosines, sines = waves(n)
    alternating = np.where(np.arange(n) % 2 == 0, 1.0, -1.0)
    forward = np.concatenate([cosines[:HALF], sines[:HALF]])
    forward[HALF] = alternating
    weight = np.where(np.arange(HALF) == 0, 1.0, 2.0)[:, None]
    inverse = np.concatenate([cosines[:HALF] * weight, -sines[:HALF] * weight])
    inverse[HALF] = alternating
    pool = (np.arange(POOLED)[:, None] == np.arange(n)[None, :] // DS).astype(np.float64)
    forward = np.concatenate([forward * (factor / n), pool])
    return quantized(forward), quantized(inverse.T * (factor / n)), gain


def col_table(n):
    factor, gain = table_scale(n)
    cosines, sines = waves(n)
    table = np.block([[cosines, sines], [-sines, cosines]]) * (factor / n)
    return quantized(table), gain


def mm(a, b):
    return jnp.dot(a, b, preferred_element_type=jnp.float32)


def sublanes():
    return lax.broadcasted_iota(jnp.int32, (SUB, LANES), 0)


def to_lhs(rows):
    return jnp.concatenate([rows[:HALF], rows[HALF:]], axis=1).astype(jnp.bfloat16)


def energy(block):
    width = block.shape[1] // 2
    total = block[:, :width] * block[:, :width] + block[:, width:] * block[:, width:]
    head = jnp.where(lax.broadcasted_iota(jnp.int32, (SUB, width), 0) == 0, 0.0, total[:SUB])
    for at in range(SUB, HALF, SUB):
        head = head + total[at : at + SUB]
    return jnp.sum(head, axis=0, keepdims=True)


def spectrum(blocks, table):
    count = len(blocks)
    width = blocks[0].shape[1]
    sub = lax.broadcasted_iota(jnp.int32, (SUB, width), 0)
    first = jnp.zeros((SUB, width), jnp.float32)
    middle = jnp.zeros((SUB, width), jnp.float32)
    for p, rows in enumerate(blocks):
        first = jnp.where(sub == p, rows[0:1], first)
        middle = jnp.where(sub == p, rows[HALF : HALF + 1], middle)
    first = first - jnp.sum(first, axis=1, keepdims=True) * (1.0 / width)
    ends = jnp.concatenate([first, middle], axis=0)
    ends = jnp.concatenate([ends, jnp.zeros_like(ends)], axis=1).astype(jnp.bfloat16)
    freq = mm(jnp.concatenate([to_lhs(rows) for rows in blocks] + [ends], axis=0), table)
    power = jnp.zeros((SUB, width), jnp.float32)
    for p in range(count):
        power = jnp.where(sub == p, energy(freq[p * HALF : (p + 1) * HALF]), power)
    tail = freq[count * HALF :] * freq[count * HALF :]
    tail = tail[:SUB] + tail[SUB:]
    power = 2.0 * power + tail[:, :width] + tail[:, width:]
    return freq, jnp.sum(power, axis=1, keepdims=True)


def scaled(freq, count, factors):
    parts = [freq[p * HALF : (p + 1) * HALF] * factors[p : p + 1] for p in range(count)]
    for at in (0, SUB):
        parts.append(freq[count * HALF + at : count * HALF + at + SUB] * factors)
    return parts


def correlate(own, other, count, table):
    width = own.shape[1] // 2
    a_re, a_im = own[:, :width], own[:, width:]
    b_re, b_im = other[:, :width], other[:, width:]
    product = jnp.concatenate([a_re * b_re + a_im * b_im, a_im * b_re - a_re * b_im], axis=1)
    rows = mm(product.astype(jnp.bfloat16), table)
    sub = lax.broadcasted_iota(jnp.int32, (SUB, width), 0)
    at = count * HALF
    blocks = []
    for p in range(count):
        block = rows[p * HALF : (p + 1) * HALF]
        first = rows[at + p : at + p + 1, :width]
        middle = rows[at + SUB + p : at + SUB + p + 1, :width]
        parts = [
            jnp.where(sub == 0, first, block[:SUB, :width]),
            block[SUB:, :width],
            jnp.where(sub == 0, middle, block[:SUB, width:]),
            block[SUB:, width:],
        ]
        blocks.append(jnp.concatenate(parts, axis=0).astype(jnp.bfloat16))
    return blocks


def window_at(ref, row_at, col_at, height):
    block = lax.div(col_at, LANES)
    shift = lax.rem(col_at, LANES)
    left = ref[block, pl.ds(row_at, height), :]
    right = ref[block + 1, pl.ds(row_at, height), :]
    lane = lax.broadcasted_iota(jnp.int32, (height, LANES), 1)
    return pltpu.roll(jnp.where(lane >= shift, left, right), lax.rem(LANES - shift, LANES), 1)


def match_unit(unit, bands, gains, offsets, peaks, keep, ext, own, row_tab, col_tab, inv_tab, write):
    row_gain, col_gain = gains
    off_row = HALO + DS * offsets[0, 0, 0]
    off_col = LANES + DS * offsets[0, 0, 1]
    blocks = []
    for i in range(bands):
        pair = []
        for h in range(2):
            column = 2 * unit + h
            row_at = off_row + i * P_SIZE + peaks[0, i, 0, column]
            col_at = off_col + column * P_SIZE + peaks[0, i, 1, column]
            pair.append(window_at(ext, row_at, col_at, P_SIZE).astype(jnp.bfloat16))
        rows = mm(row_tab[:P_SIZE, :], jnp.concatenate(pair, axis=1))
        blocks += [rows[:, :P_SIZE], rows[:, P_SIZE:]]
    freq, power = spectrum(blocks, col_tab[...])
    gain = row_gain * col_gain
    scale = (P_SIZE * P_SIZE / gain) ** 2 / P_SIZE
    factors = scale / jnp.sqrt(power * (1.0 / gain**2) + EPSILON)
    rows = correlate(own, freq, 2 * bands, col_tab[...])
    for i in range(bands):
        maps = mm(inv_tab[...], jnp.concatenate(rows[2 * i : 2 * i + 2], axis=1))
        for h in range(2):
            p = 2 * i + h
            factor = factors[p : p + 1] * keep[0, i, 2 * unit + h].astype(jnp.float32)
            write(i, h, maps[:, h * P_SIZE : (h + 1) * P_SIZE] * factor)


def split(x):
    hi = x.astype(jnp.bfloat16)
    return hi, (x - hi.astype(jnp.float32)).astype(jnp.bfloat16)


def pooled(hi, lo, pool):
    span = pool.shape[0]
    parts = []
    for at in range(0, hi.shape[1], span):
        sums = mm(hi[:, at : at + span], pool) + mm(lo[:, at : at + span], pool)
        parts.append((sums * (1.0 / (DS * DS))).astype(jnp.bfloat16))
    return parts


def exchange_kernel(
    bands,
    units,
    gains,
    offsets,
    peaks,
    keep,
    img,
    row_hbm,
    col_hbm,
    inv_hbm,
    wide_hbm,
    pool_hbm,
    maps,
    ext,
    last_spec,
    small_spec,
    sum_hi,
    sum_lo,
    own,
    land,
    spec,
    own_hi,
    own_lo,
    row_tab,
    col_tab,
    inv_tab,
    wide_tab,
    pool,
    send_sems,
    recv_sems,
    side_send,
    side_recv,
    local_sems,
):
    s = lax.axis_index("sec")
    t = lax.axis_index("tile")
    ns = lax.axis_size("sec")
    nt = lax.axis_size("tile")
    rows, width = own.shape
    columns = width // LANES
    centre = rows - 2 * HALO
    reach = rows + 2 * HALO
    row_gain, col_gain, wide_gain = gains

    sends = s < ns - 1
    receives = s > 0
    has_up = t > 0
    has_down = t < nt - 1
    s_next = jnp.minimum(s + 1, ns - 1)
    s_prev = jnp.maximum(s - 1, 0)
    t_next = jnp.minimum(t + 1, nt - 1)
    t_prev = jnp.maximum(t - 1, 0)

    barrier = pltpu.get_barrier_semaphore()
    for cond, peer in (
        (sends, (s_next, t)),
        (receives, (s_prev, t)),
        (has_up, (s, t_prev)),
        (has_down, (s, t_next)),
    ):

        @pl.when(cond)
        def _(peer=peer):
            pl.semaphore_signal(barrier, inc=1, device_id=peer, device_id_type=MESH)

    loads = [
        pltpu.make_async_copy(source, target, local_sems.at[n])
        for n, (source, target) in enumerate(
            (
                (img, own),
                (row_hbm, row_tab),
                (col_hbm, col_tab),
                (inv_hbm, inv_tab),
                (wide_hbm, wide_tab),
                (pool_hbm, pool),
            )
        )
    ]
    for load in loads:
        load.start()
    peers = sum(jnp.where(cond, 1, 0) for cond in (sends, receives, has_up, has_down))
    pl.semaphore_wait(barrier, peers)

    def edge_copy(n):
        start = n * (rows - HALO)
        return pltpu.make_async_remote_copy(
            src_ref=img.at[pl.ds(start, HALO)],
            dst_ref=land.at[pl.ds(HALO + start, HALO)],
            send_sem=send_sems.at[n],
            recv_sem=recv_sems.at[n],
            device_id=(s_next, t),
            device_id_type=MESH,
        )

    def column_copy(c):
        at = pl.multiple_of(c * LANES, LANES)
        return pltpu.make_async_remote_copy(
            src_ref=img.at[pl.ds(HALO, centre), pl.ds(at, LANES)],
            dst_ref=land.at[pl.ds(2 * HALO, centre), pl.ds(at, LANES)],
            send_sem=send_sems.at[2 + c],
            recv_sem=recv_sems.at[2 + c],
            device_id=(s_next, t),
            device_id_type=MESH,
        )

    def side_copy(n):
        source, target, peer = ((HALO, HALO + rows, t_prev), (rows, 0, t_next))[n]
        return pltpu.make_async_remote_copy(
            src_ref=land.at[pl.ds(source, HALO)],
            dst_ref=land.at[pl.ds(target, HALO)],
            send_sem=side_send.at[n],
            recv_sem=side_recv.at[n],
            device_id=(s, peer),
            device_id_type=MESH,
        )

    @pl.when(sends)
    def _():
        edge_copy(0).start()
        edge_copy(1).start()
        for c in range(columns):
            column_copy(c).start()

    @pl.when(jnp.logical_not(receives))
    def _():
        land[...] = jnp.zeros_like(land)

    @pl.when(receives & jnp.logical_not(has_up))
    def _():
        land[:HALO, :] = jnp.zeros((HALO, width), jnp.bfloat16)

    @pl.when(receives & jnp.logical_not(has_down))
    def _():
        land[HALO + rows :, :] = jnp.zeros((HALO, width), jnp.bfloat16)

    ext[0] = jnp.zeros((reach, LANES), jnp.float32)
    ext[columns + 1] = jnp.zeros((reach, LANES), jnp.float32)
    for load in loads:
        load.wait()

    def own_unit(u, carry):
        at = pl.multiple_of(u * PAIR, PAIR)
        blocks = []
        for i in range(bands):
            both = mm(row_tab[...], own[i * P_SIZE : (i + 1) * P_SIZE, pl.ds(at, PAIR)])
            blocks += [both[:P_SIZE, :P_SIZE], both[:P_SIZE, P_SIZE:]]
            hi, lo = split(both[P_SIZE:])
            own_hi[i * POOLED : (i + 1) * POOLED, pl.ds(at, PAIR)] = hi
            own_lo[i * POOLED : (i + 1) * POOLED, pl.ds(at, PAIR)] = lo
        freq, power = spectrum(blocks, col_tab[...])
        gain = row_gain * col_gain
        factors = (1.0 / gain) / jnp.sqrt(power * (1.0 / gain**2) + EPSILON)
        parts = scaled(freq, 2 * bands, factors)
        base = 0
        for part in parts:
            spec[u, base : base + part.shape[0], :] = part
            base += part.shape[0]
        return carry

    lax.fori_loop(0, units, own_unit, 0)

    @pl.when(receives)
    def _():
        edge_copy(0).wait_recv()

        @pl.when(has_up)
        def _():
            side_copy(0).start()

        edge_copy(1).wait_recv()

        @pl.when(has_down)
        def _():
            side_copy(1).start()

    last_spec[...] = spec[units - 1]
    small = jnp.concatenate(pooled(own_hi[...], own_lo[...], pool[...]), axis=1)
    freq, power = spectrum([mm(row_tab[:P_SIZE, :], small)], wide_tab[...])
    gain = row_gain * wide_gain
    factors = (1.0 / gain) / jnp.sqrt(power * (1.0 / gain**2) + EPSILON)
    base = 0
    for part in scaled(freq, 1, factors):
        small_spec[base : base + part.shape[0], :] = part
        base += part.shape[0]

    @pl.when(receives)
    def _():
        @pl.when(has_up)
        def _():
            side_copy(1).wait_recv()

        @pl.when(has_down)
        def _():
            side_copy(0).wait_recv()

    def arrive(c):
        @pl.when(receives)
        def _():
            column_copy(c).wait_recv()

        at = pl.multiple_of(c * LANES, LANES)
        ext[c + 1] = land[:, pl.ds(at, LANES)].astype(jnp.float32)
        count = sum_hi.shape[0]
        sums = ext[c + 1, pl.ds(HALO - DS * COARSE, count, stride=DS), :]
        for k in range(1, DS):
            sums = sums + ext[c + 1, pl.ds(HALO - DS * COARSE + k, count, stride=DS), :]
        hi, lo = split(sums)
        sum_hi[:, pl.ds(at, LANES)] = hi
        sum_lo[:, pl.ds(at, LANES)] = lo

    arrive(0)

    def unit_step(u, carry):
        arrive(2 * u + 1)
        arrive(2 * u + 2)

        def write(i, h, value):
            at = pl.multiple_of(u * PAIR + h * P_SIZE, P_SIZE)
            maps[i * P_SIZE : (i + 1) * P_SIZE, pl.ds(at, P_SIZE)] = value

        match_unit(
            u, bands, (row_gain, col_gain), offsets, peaks, keep, ext, spec[u], row_tab, col_tab, inv_tab, write
        )
        return carry

    lax.fori_loop(0, units - 1, unit_step, 0)
    arrive(columns - 1)

    @pl.when(receives & has_up)
    def _():
        side_copy(0).wait_send()

    @pl.when(receives & has_down)
    def _():
        side_copy(1).wait_send()

    @pl.when(sends)
    def _():
        edge_copy(0).wait_send()
        edge_copy(1).wait_send()
        for c in range(columns):
            column_copy(c).wait_send()


def finish_kernel(
    bands,
    units,
    gains,
    offsets,
    peaks,
    keep,
    maps,
    ext,
    last_spec,
    small_spec,
    sum_hi,
    sum_lo,
    row_tab,
    col_tab,
    inv_tab,
    wide_tab,
    pool,
    coarse_out,
    flow_out,
    last_maps,
    coarse,
    small,
    sems,
):
    row_gain, col_gain, wide_gain = gains
    done = maps.shape[1]
    copies = []
    for i in range(bands):
        band = pl.ds(i * P_SIZE, P_SIZE)
        copies.append(pltpu.make_async_copy(maps.at[band], flow_out.at[0, band, pl.ds(0, done)], sems.at[i]))
        copies[-1].start()

    def write(i, h, value):
        last_maps[i * P_SIZE : (i + 1) * P_SIZE, h * P_SIZE : (h + 1) * P_SIZE] = value

    match_unit(
        units - 1, bands, (row_gain, col_gain), offsets, peaks, keep, ext, last_spec[...], row_tab, col_tab, inv_tab, write
    )
    copies.append(pltpu.make_async_copy(last_maps, flow_out.at[0, :, pl.ds(done, PAIR)], sems.at[bands]))
    copies[-1].start()

    all_rows = small.shape[1]
    parts = pooled(sum_hi[...], sum_lo[...], pool[...])
    count = len(parts)
    small[0] = jnp.zeros((all_rows, LANES), jnp.float32)
    small[count + 1] = jnp.zeros((all_rows, LANES), jnp.float32)
    for n, part in enumerate(parts):
        small[n + 1] = part.astype(jnp.float32)
    height = all_rows - 2 * COARSE
    window = [
        window_at(
            small, COARSE + offsets[0, 0, 0], LANES * (n + 1) + offsets[0, 0, 1], height
        ).astype(jnp.bfloat16)
        for n in range(count)
    ]
    freq, power = spectrum([mm(row_tab[:P_SIZE, :], jnp.concatenate(window, axis=1))], wide_tab[...])
    gain = row_gain * wide_gain
    size = height * count * LANES
    scale = (size / gain) ** 2 / math.sqrt(size)
    factors = scale / jnp.sqrt(power * (1.0 / gain**2) + EPSILON)
    rows = correlate(small_spec[...], freq, 1, wide_tab[...])[0]
    coarse[...] = mm(inv_tab[...], rows) * factors[0:1]
    copies.append(pltpu.make_async_copy(coarse, coarse_out.at[0], sems.at[bands + 1]))
    copies[-1].start()
    for copy in copies:
        copy.wait()


def shards(section_image, offsets, peak_shift, accepted):
    own = section_image[0]
    rows, width = own.shape
    bands = rows // P_SIZE
    units = width // PAIR
    columns = width // LANES
    reach = rows + 2 * HALO
    small_width = width // DS
    forward_row, inverse_row, row_gain = row_tables()
    col, col_gain = col_table(P_SIZE)
    wide, wide_gain = col_table(small_width)
    gains = (float(row_gain), float(col_gain), float(wide_gain))
    span = DS * LANES
    pool = quantized(np.arange(span)[:, None] // DS == np.arange(LANES)[None, :])
    tables = [jnp.asarray(x) for x in (forward_row, col, inverse_row, wide, pool)]
    scalars = (offsets, jnp.swapaxes(peak_shift, 2, 3), accepted)
    high = 2 * bands * HALF + 2 * SUB
    small_high = HALF + 2 * SUB
    small_rows = rows // DS + 2 * COARSE
    hbm = pl.BlockSpec(memory_space=pltpu.HBM)
    vmem = pl.BlockSpec(memory_space=pltpu.VMEM)
    smem = pl.BlockSpec(memory_space=pltpu.SMEM)
    limit = 30 * 2**20
    between = pl.pallas_call(
        functools.partial(exchange_kernel, bands, units, gains),
        name="exchange",
        out_shape=(
            jax.ShapeDtypeStruct((rows, width - PAIR), jnp.float32),
            jax.ShapeDtypeStruct((columns + 2, reach, LANES), jnp.float32),
            jax.ShapeDtypeStruct((high, PAIR), jnp.float32),
            jax.ShapeDtypeStruct((small_high, 2 * small_width), jnp.float32),
            jax.ShapeDtypeStruct((small_rows, width), jnp.bfloat16),
            jax.ShapeDtypeStruct((small_rows, width), jnp.bfloat16),
        ),
        in_specs=[smem] * 3 + [hbm] * 6,
        out_specs=(vmem,) * 6,
        scratch_shapes=[
            pltpu.VMEM((rows, width), jnp.bfloat16),
            pltpu.VMEM((reach, width), jnp.bfloat16),
            pltpu.VMEM((units, high, PAIR), jnp.float32),
            pltpu.VMEM((rows // DS, width), jnp.bfloat16),
            pltpu.VMEM((rows // DS, width), jnp.bfloat16),
        ]
        + [pltpu.VMEM(x.shape, jnp.bfloat16) for x in tables]
        + [
            pltpu.SemaphoreType.DMA((columns + 2,)),
            pltpu.SemaphoreType.DMA((columns + 2,)),
            pltpu.SemaphoreType.DMA((2,)),
            pltpu.SemaphoreType.DMA((2,)),
            pltpu.SemaphoreType.DMA((len(tables) + 1,)),
        ],
        compiler_params=pltpu.CompilerParams(
            collective_id=0, has_side_effects=True, vmem_limit_bytes=limit
        ),
    )(*scalars, own, *tables)
    return pl.pallas_call(
        functools.partial(finish_kernel, bands, units, gains),
        name="finish",
        out_shape=(
            jax.ShapeDtypeStruct((1, rows // DS, small_width), jnp.float32),
            jax.ShapeDtypeStruct((1, rows, width), jnp.float32),
        ),
        in_specs=[smem] * 3 + [vmem] * 11,
        out_specs=(hbm, hbm),
        scratch_shapes=[
            pltpu.VMEM((rows, PAIR), jnp.float32),
            pltpu.VMEM((rows // DS, small_width), jnp.float32),
            pltpu.VMEM((small_width // LANES + 2, small_rows, LANES), jnp.float32),
            pltpu.SemaphoreType.DMA((bands + 2,)),
        ],
        compiler_params=pltpu.CompilerParams(vmem_limit_bytes=limit),
    )(*scalars, *between, *tables)


def solution(mesh):
    return jax.shard_map(
        shards,
        mesh=mesh,
        in_specs=(
            P("sec", "tile", None),
            P("sec", "tile", None),
            P("sec", "tile", None, None),
            P("sec", "tile", None),
        ),
        out_specs=(P("sec", "tile", None), P("sec", "tile", None)),
        check_vma=False,
    )
```

```python
import functools
import math

import jax
import jax.numpy as jnp
import ml_dtypes
import numpy as np
from jax import lax
from jax.experimental import pallas as pl
from jax.experimental.pallas import tpu as pltpu
from jax.sharding import PartitionSpec as P

P_SIZE = 128
HALF = P_SIZE // 2
DS = 4
COARSE = 16
HALO = 80
LANES = 128
PAIR = 2 * P_SIZE
SUB = 8
POOLED = P_SIZE // DS
EPSILON = 1e-05
MESH = pl.DeviceIdType.MESH


def quantized(table):
    return table.astype(np.float32).astype(ml_dtypes.bfloat16)


def table_scale(n):
    cosines = np.cos(2.0 * np.pi * np.arange(n) / n)
    best = None
    for factor in np.linspace(1.0, 2.0, 4001):
        table = quantized(cosines * factor).astype(np.float64)
        gain = (table @ cosines) / (cosines @ cosines)
        error = np.mean((table / gain - cosines) ** 2)
        if best is None or error < best[0]:
            best = (error, factor, gain)
    return best[1], best[2]


def waves(n):
    k = np.arange(n)
    angles = (k[:, None] * k[None, :] % n) * (2.0 * np.pi / n)
    return np.cos(angles), np.sin(angles)


def row_tables():
    n = P_SIZE
    factor, gain = table_scale(n)
    cosines, sines = waves(n)
    alternating = np.where(np.arange(n) % 2 == 0, 1.0, -1.0)
    forward = np.concatenate([cosines[:HALF], sines[:HALF]])
    forward[HALF] = alternating
    weight = np.where(np.arange(HALF) == 0, 1.0, 2.0)[:, None]
    inverse = np.concatenate([cosines[:HALF] * weight, -sines[:HALF] * weight])
    inverse[HALF] = alternating
    pool = (np.arange(POOLED)[:, None] == np.arange(n)[None, :] // DS).astype(np.float64)
    forward = np.concatenate([forward * (factor / n), pool])
    return quantized(forward), quantized(inverse.T * (factor / n)), gain


def col_table(n):
    factor, gain = table_scale(n)
    cosines, sines = waves(n)
    table = np.block([[cosines, sines], [-sines, cosines]]) * (factor / n)
    return quantized(table), gain


def mm(a, b):
    return jnp.dot(a, b, preferred_element_type=jnp.float32)


def sublanes():
    return lax.broadcasted_iota(jnp.int32, (SUB, LANES), 0)


def to_lhs(rows):
    return jnp.concatenate([rows[:HALF], rows[HALF:]], axis=1).astype(jnp.bfloat16)


def energy(block):
    width = block.shape[1] // 2
    total = block[:, :width] * block[:, :width] + block[:, width:] * block[:, width:]
    head = jnp.where(lax.broadcasted_iota(jnp.int32, (SUB, width), 0) == 0, 0.0, total[:SUB])
    for at in range(SUB, HALF, SUB):
        head = head + total[at : at + SUB]
    return jnp.sum(head, axis=0, keepdims=True)


def spectrum(blocks, table):
    count = len(blocks)
    width = blocks[0].shape[1]
    sub = lax.broadcasted_iota(jnp.int32, (SUB, width), 0)
    first = jnp.zeros((SUB, width), jnp.float32)
    middle = jnp.zeros((SUB, width), jnp.float32)
    for p, rows in enumerate(blocks):
        first = jnp.where(sub == p, rows[0:1], first)
        middle = jnp.where(sub == p, rows[HALF : HALF + 1], middle)
    first = first - jnp.sum(first, axis=1, keepdims=True) * (1.0 / width)
    ends = jnp.concatenate([first, middle], axis=0)
    ends = jnp.concatenate([ends, jnp.zeros_like(ends)], axis=1).astype(jnp.bfloat16)
    freq = mm(jnp.concatenate([to_lhs(rows) for rows in blocks] + [ends], axis=0), table)
    power = jnp.zeros((SUB, width), jnp.float32)
    for p in range(count):
        power = jnp.where(sub == p, energy(freq[p * HALF : (p + 1) * HALF]), power)
    tail = freq[count * HALF :] * freq[count * HALF :]
    tail = tail[:SUB] + tail[SUB:]
    power = 2.0 * power + tail[:, :width] + tail[:, width:]
    return freq, jnp.sum(power, axis=1, keepdims=True)


def scaled(freq, count, factors):
    parts = [freq[p * HALF : (p + 1) * HALF] * factors[p : p + 1] for p in range(count)]
    for at in (0, SUB):
        parts.append(freq[count * HALF + at : count * HALF + at + SUB] * factors)
    return parts


def correlate(own, other, count, table):
    width = own.shape[1] // 2
    a_re, a_im = own[:, :width], own[:, width:]
    b_re, b_im = other[:, :width], other[:, width:]
    product = jnp.concatenate([a_re * b_re + a_im * b_im, a_im * b_re - a_re * b_im], axis=1)
    rows = mm(product.astype(jnp.bfloat16), table)
    sub = lax.broadcasted_iota(jnp.int32, (SUB, width), 0)
    at = count * HALF
    blocks = []
    for p in range(count):
        block = rows[p * HALF : (p + 1) * HALF]
        first = rows[at + p : at + p + 1, :width]
        middle = rows[at + SUB + p : at + SUB + p + 1, :width]
        parts = [
            jnp.where(sub == 0, first, block[:SUB, :width]),
            block[SUB:, :width],
            jnp.where(sub == 0, middle, block[:SUB, width:]),
            block[SUB:, width:],
        ]
        blocks.append(jnp.concatenate(parts, axis=0).astype(jnp.bfloat16))
    return blocks


def window_at(ref, row_at, col_at, height):
    block = lax.div(col_at, LANES)
    shift = lax.rem(col_at, LANES)
    left = ref[block, pl.ds(row_at, height), :]
    right = ref[block + 1, pl.ds(row_at, height), :]
    lane = lax.broadcasted_iota(jnp.int32, (height, LANES), 1)
    return pltpu.roll(jnp.where(lane >= shift, left, right), lax.rem(LANES - shift, LANES), 1)


def unit_windows(unit, bands, offsets, peaks, ext):
    off_row = HALO + DS * offsets[0, 0, 0]
    off_col = LANES + DS * offsets[0, 0, 1]
    windows = []
    for i in range(bands):
        pair = []
        for h in range(2):
            column = 2 * unit + h
            row_at = off_row + i * P_SIZE + peaks[0, i, 0, column]
            col_at = off_col + column * P_SIZE + peaks[0, i, 1, column]
            pair.append(window_at(ext, row_at, col_at, P_SIZE).astype(jnp.bfloat16))
        windows.append(jnp.concatenate(pair, axis=1))
    return windows


def unit_keep(unit, bands, keep):
    sub = sublanes()
    flags = jnp.zeros((SUB, LANES), jnp.float32)
    for i in range(bands):
        for h in range(2):
            flag = keep[0, i, 2 * unit + h].astype(jnp.float32)
            flags = jnp.where(sub == 2 * i + h, flag, flags)
    return flags


def match_unit(bands, gains, windows, flags, own, row_tab, col_tab, inv_tab, write):
    blocks = []
    for window in windows:
        rows = mm(row_tab[:P_SIZE, :], window)
        blocks += [rows[:, :P_SIZE], rows[:, P_SIZE:]]
    freq, power = spectrum(blocks, col_tab[...])
    gain = gains[0] * gains[1]
    scale = (P_SIZE * P_SIZE / gain) ** 2 / P_SIZE
    factors = flags * (scale / jnp.sqrt(power * (1.0 / gain**2) + EPSILON))
    rows = correlate(own, freq, 2 * bands, col_tab[...])
    for i in range(bands):
        maps = mm(inv_tab[...], jnp.concatenate(rows[2 * i : 2 * i + 2], axis=1))
        for h in range(2):
            p = 2 * i + h
            write(i, h, maps[:, h * P_SIZE : (h + 1) * P_SIZE] * factors[p : p + 1])


def split(x):
    hi = x.astype(jnp.bfloat16)
    return hi, (x - hi.astype(jnp.float32)).astype(jnp.bfloat16)


def pooled(hi, lo, pool):
    span = pool.shape[0]
    parts = []
    for at in range(0, hi.shape[1], span):
        sums = mm(hi[:, at : at + span], pool) + mm(lo[:, at : at + span], pool)
        parts.append((sums * (1.0 / (DS * DS))).astype(jnp.bfloat16))
    return parts


def exchange_kernel(
    bands,
    units,
    gains,
    offsets_hbm,
    peaks_hbm,
    keep_hbm,
    img,
    row_hbm,
    col_hbm,
    inv_hbm,
    wide_hbm,
    pool_hbm,
    maps,
    coarse,
    windows,
    last_spec,
    flags,
    row_tab,
    col_tab,
    inv_tab,
    own,
    land,
    ext,
    spec,
    small_own,
    small_land,
    small,
    small_spec,
    own_hi,
    own_lo,
    sum_hi,
    sum_lo,
    wide_tab,
    pool,
    offsets,
    peaks,
    keep,
    send_sems,
    recv_sems,
    side_send,
    side_recv,
    local_sems,
):
    s = lax.axis_index("sec")
    t = lax.axis_index("tile")
    ns = lax.axis_size("sec")
    nt = lax.axis_size("tile")
    rows, width = own.shape
    columns = width // LANES
    centre = rows - 2 * HALO
    reach = rows + 2 * HALO
    row_gain, col_gain, wide_gain = gains
    early = columns // 2 + 1

    sends = s < ns - 1
    receives = s > 0
    has_up = t > 0
    has_down = t < nt - 1
    s_next = jnp.minimum(s + 1, ns - 1)
    s_prev = jnp.maximum(s - 1, 0)
    t_next = jnp.minimum(t + 1, nt - 1)
    t_prev = jnp.maximum(t - 1, 0)

    barrier = pltpu.get_barrier_semaphore()
    for cond, peer in (
        (receives, (s_prev, t)),
        (sends, (s_next, t)),
        (has_up, (s, t_prev)),
        (has_down, (s, t_next)),
    ):

        @pl.when(cond)
        def _(peer=peer):
            pl.semaphore_signal(barrier, inc=1, device_id=peer, device_id_type=MESH)

    loads = [
        pltpu.make_async_copy(source, target, local_sems.at[n])
        for n, (source, target) in enumerate(
            (
                (img, own),
                (row_hbm, row_tab),
                (col_hbm, col_tab),
                (inv_hbm, inv_tab),
                (wide_hbm, wide_tab),
                (pool_hbm, pool),
                (offsets_hbm, offsets),
                (peaks_hbm, peaks),
                (keep_hbm, keep),
            )
        )
    ]
    for load in loads:
        load.start()
    peers = sum(jnp.where(cond, 1, 0) for cond in (sends, receives, has_up, has_down))
    pl.semaphore_wait(barrier, peers)

    def edge_copy(n):
        start = n * (rows - HALO)
        return pltpu.make_async_remote_copy(
            src_ref=img.at[pl.ds(start, HALO)],
            dst_ref=land.at[pl.ds(HALO + start, HALO)],
            send_sem=send_sems.at[n],
            recv_sem=recv_sems.at[n],
            device_id=(s_next, t),
            device_id_type=MESH,
        )

    def column_copy(c):
        at = pl.multiple_of(c * LANES, LANES)
        return pltpu.make_async_remote_copy(
            src_ref=img.at[pl.ds(HALO, centre), pl.ds(at, LANES)],
            dst_ref=land.at[pl.ds(2 * HALO, centre), pl.ds(at, LANES)],
            send_sem=send_sems.at[3 + c],
            recv_sem=recv_sems.at[3 + c],
            device_id=(s_next, t),
            device_id_type=MESH,
        )

    def small_copy():
        return pltpu.make_async_remote_copy(
            src_ref=small_own.at[pl.ds(COARSE, small_land.shape[0]), pl.ds(LANES, LANES)],
            dst_ref=small_land,
            send_sem=send_sems.at[2],
            recv_sem=recv_sems.at[2],
            device_id=(s_next, t),
            device_id_type=MESH,
        )

    def side_copy(n):
        source, target, peer = ((HALO, HALO + rows, t_prev), (rows, 0, t_next))[n]
        return pltpu.make_async_remote_copy(
            src_ref=land.at[pl.ds(source, HALO)],
            dst_ref=land.at[pl.ds(target, HALO)],
            send_sem=side_send.at[n],
            recv_sem=side_recv.at[n],
            device_id=(s, peer),
            device_id_type=MESH,
        )

    @pl.when(sends)
    def _():
        edge_copy(0).start()
        edge_copy(1).start()
        for c in range(early):
            column_copy(c).start()

    @pl.when(jnp.logical_not(receives))
    def _():
        land[...] = jnp.zeros_like(land)
        small_land[...] = jnp.zeros_like(small_land)

    @pl.when(receives & jnp.logical_not(has_up))
    def _():
        land[:HALO, :] = jnp.zeros((HALO, width), jnp.bfloat16)

    @pl.when(receives & jnp.logical_not(has_down))
    def _():
        land[HALO + rows :, :] = jnp.zeros((HALO, width), jnp.bfloat16)

    ext[0] = jnp.zeros((reach, LANES), jnp.float32)
    ext[columns + 1] = jnp.zeros((reach, LANES), jnp.float32)
    small[0] = jnp.zeros(small.shape[1:], jnp.float32)
    small[3] = jnp.zeros(small.shape[1:], jnp.float32)
    for load in loads:
        load.wait()

    def own_unit(u, carry):
        at = pl.multiple_of(u * PAIR, PAIR)
        blocks = []
        for i in range(bands):
            both = mm(row_tab[...], own[i * P_SIZE : (i + 1) * P_SIZE, pl.ds(at, PAIR)])
            blocks += [both[:P_SIZE, :P_SIZE], both[:P_SIZE, P_SIZE:]]
            hi, lo = split(both[P_SIZE:])
            own_hi[i * POOLED : (i + 1) * POOLED, pl.ds(at, PAIR)] = hi
            own_lo[i * POOLED : (i + 1) * POOLED, pl.ds(at, PAIR)] = lo
        freq, power = spectrum(blocks, col_tab[...])
        gain = row_gain * col_gain
        factors = (1.0 / gain) / jnp.sqrt(power * (1.0 / gain**2) + EPSILON)
        base = 0
        for part in scaled(freq, 2 * bands, factors):
            spec[u, base : base + part.shape[0], :] = part
            base += part.shape[0]
        return carry

    lax.fori_loop(0, units, own_unit, 0)
    for n, part in enumerate(pooled(own_hi[...], own_lo[...], pool[...])):
        small_own[:, n * LANES : (n + 1) * LANES] = part

    @pl.when(sends)
    def _():
        small_copy().start()
        for c in range(early, columns):
            column_copy(c).start()

    @pl.when(receives)
    def _():
        edge_copy(0).wait_recv()

        @pl.when(has_up)
        def _():
            side_copy(0).start()

        edge_copy(1).wait_recv()

        @pl.when(has_down)
        def _():
            side_copy(1).start()

    last_spec[...] = spec[units - 1]
    flags[...] = unit_keep(units - 1, bands, keep)
    freq, power = spectrum([mm(row_tab[:P_SIZE, :], small_own[...])], wide_tab[...])
    gain = row_gain * wide_gain
    factors = (1.0 / gain) / jnp.sqrt(power * (1.0 / gain**2) + EPSILON)
    base = 0
    for part in scaled(freq, 1, factors):
        small_spec[base : base + part.shape[0], :] = part
        base += part.shape[0]

    @pl.when(receives)
    def _():
        @pl.when(has_up)
        def _():
            side_copy(1).wait_recv()

        @pl.when(has_down)
        def _():
            side_copy(0).wait_recv()

    for at in (0, HALO + rows - HALO):
        for c in range(columns):
            ext[c + 1, at : at + 2 * HALO, :] = land[
                at : at + 2 * HALO, c * LANES : (c + 1) * LANES
            ].astype(jnp.float32)

    def row_sums(c, at, count):
        sums = ext[c + 1, pl.ds(at, count, stride=DS), :]
        for k in range(1, DS):
            sums = sums + ext[c + 1, pl.ds(at + k, count, stride=DS), :]
        return split(sums)

    def arrive(c):
        @pl.when(receives)
        def _():
            column_copy(c).wait_recv()

        at = pl.multiple_of(c * LANES, LANES)
        ext[c + 1, 2 * HALO : 2 * HALO + centre, :] = land[
            2 * HALO : 2 * HALO + centre, pl.ds(at, LANES)
        ].astype(jnp.float32)

    def coarse_map():
        half = columns // 2
        first = HALO - DS * COARSE
        count = small.shape[1]
        for c in range(half):
            hi, lo = row_sums(c, first, count)
            sum_hi[:, c * LANES : (c + 1) * LANES] = hi
            sum_lo[:, c * LANES : (c + 1) * LANES] = lo
        small[1] = pooled(sum_hi[...], sum_lo[...], pool[...])[0].astype(jnp.float32)
        side = 2 * COARSE
        for c in range(half):
            for n, at in enumerate((first, first + DS * (count - side))):
                hi, lo = row_sums(half + c, at, side)
                sum_hi[n * side : (n + 1) * side, c * LANES : (c + 1) * LANES] = hi
                sum_lo[n * side : (n + 1) * side, c * LANES : (c + 1) * LANES] = lo

        @pl.when(receives)
        def _():
            small_copy().wait_recv()

        ends = pooled(sum_hi[: 2 * side], sum_lo[: 2 * side], pool[...])[0].astype(jnp.float32)
        small[2, :side] = ends[:side]
        small[2, side : count - side] = small_land[...].astype(jnp.float32)
        small[2, count - side :] = ends[side:]
        height = count - 2 * COARSE
        window = [
            window_at(
                small, COARSE + offsets[0, 0, 0], LANES * (n + 1) + offsets[0, 0, 1], height
            ).astype(jnp.bfloat16)
            for n in range(2)
        ]
        freq, power = spectrum(
            [mm(row_tab[:P_SIZE, :], jnp.concatenate(window, axis=1))], wide_tab[...]
        )
        gain = row_gain * wide_gain
        size = height * 2 * LANES
        scale = (size / gain) ** 2 / math.sqrt(size)
        factors = scale / jnp.sqrt(power * (1.0 / gain**2) + EPSILON)
        found = correlate(small_spec[...], freq, 1, wide_tab[...])[0]
        coarse[...] = mm(inv_tab[...], found) * factors[0:1]

    arrive(0)

    def unit_step(u, carry):
        arrive(2 * u + 1)

        @pl.when(u == columns // 4 - 1)
        def _():
            coarse_map()

        arrive(2 * u + 2)

        def write(i, h, value):
            at = pl.multiple_of(u * PAIR + h * P_SIZE, P_SIZE)
            maps[i * P_SIZE : (i + 1) * P_SIZE, pl.ds(at, P_SIZE)] = value

        match_unit(
            bands,
            (row_gain, col_gain),
            unit_windows(u, bands, offsets, peaks, ext),
            unit_keep(u, bands, keep),
            spec[u],
            row_tab,
            col_tab,
            inv_tab,
            write,
        )
        return carry

    lax.fori_loop(0, units - 1, unit_step, 0)
    arrive(columns - 1)
    for i, window in enumerate(unit_windows(units - 1, bands, offsets, peaks, ext)):
        windows[i] = window

    @pl.when(receives & has_up)
    def _():
        side_copy(0).wait_send()

    @pl.when(receives & has_down)
    def _():
        side_copy(1).wait_send()

    @pl.when(sends)
    def _():
        edge_copy(0).wait_send()
        edge_copy(1).wait_send()
        small_copy().wait_send()
        for c in range(columns):
            column_copy(c).wait_send()


def finish_kernel(
    bands,
    gains,
    maps,
    coarse,
    windows,
    last_spec,
    flags,
    row_tab,
    col_tab,
    inv_tab,
    coarse_out,
    flow_out,
    last_maps,
    sems,
):
    done = maps.shape[1]
    copies = [pltpu.make_async_copy(coarse, coarse_out.at[0], sems.at[2 * bands])]
    for i in range(bands):
        band = pl.ds(i * P_SIZE, P_SIZE)
        copies.append(pltpu.make_async_copy(maps.at[band], flow_out.at[0, band, pl.ds(0, done)], sems.at[i]))
    for copy in copies:
        copy.start()

    def write(i, h, value):
        last_maps[i * P_SIZE : (i + 1) * P_SIZE, h * P_SIZE : (h + 1) * P_SIZE] = value

    match_unit(
        bands,
        gains[:2],
        [windows[i] for i in range(bands)],
        flags[...],
        last_spec[...],
        row_tab,
        col_tab,
        inv_tab,
        write,
    )
    for i in range(bands):
        band = pl.ds(i * P_SIZE, P_SIZE)
        copies.append(
            pltpu.make_async_copy(last_maps.at[band], flow_out.at[0, band, pl.ds(done, PAIR)], sems.at[bands + i])
        )
        copies[-1].start()
    for copy in copies:
        copy.wait()


def shards(section_image, offsets, peak_shift, accepted):
    own = section_image[0]
    rows, width = own.shape
    bands = rows // P_SIZE
    units = width // PAIR
    columns = width // LANES
    reach = rows + 2 * HALO
    small_width = width // DS
    forward_row, inverse_row, row_gain = row_tables()
    col, col_gain = col_table(P_SIZE)
    wide, wide_gain = col_table(small_width)
    gains = (float(row_gain), float(col_gain), float(wide_gain))
    span = DS * LANES
    pool = quantized(np.arange(span)[:, None] // DS == np.arange(LANES)[None, :])
    tables = [jnp.asarray(x) for x in (forward_row, col, inverse_row, wide, pool)]
    scalars = (offsets, jnp.swapaxes(peak_shift, 2, 3), accepted)
    high = 2 * bands * HALF + 2 * SUB
    small_high = HALF + 2 * SUB
    small_rows = rows // DS + 2 * COARSE
    hbm = pl.BlockSpec(memory_space=pltpu.HBM)
    vmem = pl.BlockSpec(memory_space=pltpu.VMEM)
    limit = 30 * 2**20
    operands = [pltpu.with_memory_space_constraint(x, pltpu.HBM) for x in (*scalars, own, *tables)]
    between = pl.pallas_call(
        functools.partial(exchange_kernel, bands, units, gains),
        name="exchange",
        out_shape=(
            jax.ShapeDtypeStruct((rows, width - PAIR), jnp.float32),
            jax.ShapeDtypeStruct((rows // DS, small_width), jnp.float32),
            jax.ShapeDtypeStruct((bands, P_SIZE, PAIR), jnp.bfloat16),
            jax.ShapeDtypeStruct((high, PAIR), jnp.float32),
            jax.ShapeDtypeStruct((SUB, LANES), jnp.float32),
        )
        + tuple(jax.ShapeDtypeStruct(x.shape, x.dtype) for x in tables[:3]),
        in_specs=[hbm] * 9,
        out_specs=(vmem,) * 8,
        scratch_shapes=[
            pltpu.VMEM((rows, width), jnp.bfloat16),
            pltpu.VMEM((reach, width), jnp.bfloat16),
            pltpu.VMEM((columns + 2, reach, LANES), jnp.float32),
            pltpu.VMEM((units, high, PAIR), jnp.float32),
            pltpu.VMEM((rows // DS, small_width), jnp.bfloat16),
            pltpu.VMEM((rows // DS - 2 * COARSE, LANES), jnp.bfloat16),
            pltpu.VMEM((small_width // LANES + 2, small_rows, LANES), jnp.float32),
            pltpu.VMEM((small_high, 2 * small_width), jnp.float32),
            pltpu.VMEM((rows // DS, width), jnp.bfloat16),
            pltpu.VMEM((rows // DS, width), jnp.bfloat16),
            pltpu.VMEM((small_rows, span), jnp.bfloat16),
            pltpu.VMEM((small_rows, span), jnp.bfloat16),
            pltpu.VMEM(wide.shape, jnp.bfloat16),
            pltpu.VMEM(pool.shape, jnp.bfloat16),
        ]
        + [pltpu.SMEM(x.shape, jnp.int32) for x in scalars]
        + [
            pltpu.SemaphoreType.DMA((columns + 3,)),
            pltpu.SemaphoreType.DMA((columns + 3,)),
            pltpu.SemaphoreType.DMA((2,)),
            pltpu.SemaphoreType.DMA((2,)),
            pltpu.SemaphoreType.DMA((len(operands),)),
        ],
        compiler_params=pltpu.CompilerParams(
            collective_id=0, has_side_effects=True, vmem_limit_bytes=limit
        ),
    )(*operands)
    return pl.pallas_call(
        functools.partial(finish_kernel, bands, gains),
        name="finish",
        out_shape=(
            jax.ShapeDtypeStruct((1, rows // DS, small_width), jnp.float32),
            jax.ShapeDtypeStruct((1, rows, width), jnp.float32),
        ),
        in_specs=[vmem] * 8,
        out_specs=(hbm, hbm),
        scratch_shapes=[
            pltpu.VMEM((rows, PAIR), jnp.float32),
            pltpu.SemaphoreType.DMA((2 * bands + 1,)),
        ],
        compiler_params=pltpu.CompilerParams(vmem_limit_bytes=limit),
    )(*between)


def solution(mesh):
    return jax.shard_map(
        shards,
        mesh=mesh,
        in_specs=(
            P("sec", "tile", None),
            P("sec", "tile", None),
            P("sec", "tile", None, None),
            P("sec", "tile", None),
        ),
        out_specs=(P("sec", "tile", None), P("sec", "tile", None)),
        check_vma=False,
    )
```

```python
import functools
import math

import jax
import jax.numpy as jnp
import ml_dtypes
import numpy as np
from jax import lax
from jax.experimental import pallas as pl
from jax.experimental.pallas import tpu as pltpu
from jax.sharding import PartitionSpec as P

P_SIZE = 128
HALF = P_SIZE // 2
DS = 4
COARSE = 16
HALO = 80
LANES = 128
PAIR = 2 * P_SIZE
SUB = 8
GROUP = 4
POOLED = P_SIZE // DS
EPSILON = 1e-05
MESH = pl.DeviceIdType.MESH


def quantized(table):
    return table.astype(np.float32).astype(ml_dtypes.bfloat16)


def table_scale(n):
    cosines = np.cos(2.0 * np.pi * np.arange(n) / n)
    best = None
    for factor in np.linspace(1.0, 2.0, 4001):
        table = quantized(cosines * factor).astype(np.float64)
        gain = (table @ cosines) / (cosines @ cosines)
        error = np.mean((table / gain - cosines) ** 2)
        if best is None or error < best[0]:
            best = (error, factor, gain)
    return best[1], best[2]


def waves(n):
    k = np.arange(n)
    angles = (k[:, None] * k[None, :] % n) * (2.0 * np.pi / n)
    return np.cos(angles), np.sin(angles)


def row_tables():
    n = P_SIZE
    factor, gain = table_scale(n)
    cosines, sines = waves(n)
    alternating = np.where(np.arange(n) % 2 == 0, 1.0, -1.0)
    forward = np.concatenate([cosines[:HALF], sines[:HALF]])
    forward[HALF] = alternating
    weight = np.where(np.arange(HALF) == 0, 1.0, 2.0)[:, None]
    inverse = np.concatenate([cosines[:HALF] * weight, -sines[:HALF] * weight])
    inverse[HALF] = alternating
    pool = (np.arange(POOLED)[:, None] == np.arange(n)[None, :] // DS).astype(np.float64)
    forward = np.concatenate([forward * (factor / n), pool])
    return quantized(forward), quantized(inverse.T * (factor / n)), gain


def col_table(n):
    factor, gain = table_scale(n)
    cosines, sines = waves(n)
    table = np.block([[cosines, sines], [-sines, cosines]]) * (factor / n)
    return quantized(table), gain


def mm(a, b):
    return jnp.dot(a, b, preferred_element_type=jnp.float32)


def sublanes():
    return lax.broadcasted_iota(jnp.int32, (SUB, LANES), 0)


def to_lhs(rows):
    return jnp.concatenate([rows[:HALF], rows[HALF:]], axis=1).astype(jnp.bfloat16)


def energy(block):
    width = block.shape[1] // 2
    total = block[:, :width] * block[:, :width] + block[:, width:] * block[:, width:]
    head = jnp.where(lax.broadcasted_iota(jnp.int32, (SUB, width), 0) == 0, 0.0, total[:SUB])
    for at in range(SUB, HALF, SUB):
        head = head + total[at : at + SUB]
    return jnp.sum(head, axis=0, keepdims=True)


def spectrum(blocks, table):
    count = len(blocks)
    width = blocks[0].shape[1]
    sub = lax.broadcasted_iota(jnp.int32, (SUB, width), 0)
    ends = jnp.zeros((SUB, width), jnp.float32)
    for p, rows in enumerate(blocks):
        ends = jnp.where(sub == p, rows[0:1], ends)
        ends = jnp.where(sub == GROUP + p, rows[HALF : HALF + 1], ends)
    mean = jnp.sum(ends, axis=1, keepdims=True) * (1.0 / width)
    ends = ends - jnp.where(sub < GROUP, mean, 0.0)
    ends = jnp.concatenate([ends, jnp.zeros_like(ends)], axis=0)
    ends = jnp.concatenate([ends, jnp.zeros_like(ends)], axis=1).astype(jnp.bfloat16)
    freq = mm(jnp.concatenate([to_lhs(rows) for rows in blocks] + [ends], axis=0), table)
    power = jnp.zeros((SUB, width), jnp.float32)
    for p in range(count):
        row = energy(freq[p * HALF : (p + 1) * HALF])
        power = jnp.where((sub == p) | (sub == GROUP + p), row, power)
    tail = freq[count * HALF : count * HALF + SUB]
    tail = tail * tail
    tail = tail[:, :width] + tail[:, width:]
    power = 2.0 * power + tail + pltpu.roll(tail, GROUP, 0)
    return freq, jnp.sum(power, axis=1, keepdims=True)


def store_scaled(ref, freq, count, factors):
    at = count * HALF
    for p in range(count):
        block = slice(p * HALF, (p + 1) * HALF)
        ref[block, :] = freq[block] * factors[p : p + 1]
    ref[at : at + SUB, :] = freq[at : at + SUB] * factors
    ref[at + SUB :, :] = jnp.zeros((SUB, freq.shape[1]), jnp.float32)


def correlate(own, other, count, table):
    width = own.shape[1] // 2
    a_re, a_im = own[:, :width], own[:, width:]
    b_re, b_im = other[:, :width], other[:, width:]
    product = jnp.concatenate([a_re * b_re + a_im * b_im, a_im * b_re - a_re * b_im], axis=1)
    rows = mm(product.astype(jnp.bfloat16), table)
    sub = lax.broadcasted_iota(jnp.int32, (SUB, width), 0)
    at = count * HALF
    blocks = []
    for p in range(count):
        block = rows[p * HALF : (p + 1) * HALF]
        first = rows[at + p : at + p + 1, :width]
        middle = rows[at + GROUP + p : at + GROUP + p + 1, :width]
        parts = [
            jnp.where(sub == 0, first, block[:SUB, :width]),
            block[SUB:, :width],
            jnp.where(sub == 0, middle, block[:SUB, width:]),
            block[SUB:, width:],
        ]
        blocks.append(jnp.concatenate(parts, axis=0).astype(jnp.bfloat16))
    return blocks


def groups_of(bands):
    return [(g, bands - 1 - g) for g in range(bands // 2)]


def window_at(ref, place, height):
    row_at, col_at = place
    block = lax.shift_right_logical(col_at, 7)
    shift = col_at & (LANES - 1)
    left = ref[block, pl.ds(row_at, height), :]
    right = ref[block + 1, pl.ds(row_at, height), :]
    lane = lax.broadcasted_iota(jnp.int32, (height, LANES), 1)
    return pltpu.roll(jnp.where(lane >= shift, left, right), (LANES - shift) & (LANES - 1), 1)


def unit_places(unit, bands, offsets, peaks):
    off_row = HALO + DS * offsets[0, 0, 0]
    off_col = LANES + DS * offsets[0, 0, 1]
    places = {}
    for i in range(bands):
        for h in range(2):
            column = 2 * unit + h
            row_at = off_row + i * P_SIZE + peaks[0, i, 0, column]
            col_at = off_col + column * P_SIZE + peaks[0, i, 1, column]
            places[i, h] = row_at, col_at
    return places


def band_window(ext, places, i):
    pair = [window_at(ext, places[i, h], P_SIZE).astype(jnp.bfloat16) for h in range(2)]
    return jnp.concatenate(pair, axis=1)


def group_flags(unit, group, keep):
    sub = sublanes()
    flags = jnp.zeros((SUB, LANES), jnp.float32)
    for n, i in enumerate(group):
        for h in range(2):
            flag = keep[0, i, 2 * unit + h].astype(jnp.float32)
            flags = jnp.where(sub == 2 * n + h, flag, flags)
    return flags


def halves(rows):
    return [rows[:, :P_SIZE], rows[:, P_SIZE:]]


def match_unit(bands, gains, windows, flags, owns, row_tab, col_tab, inv_tab, write):
    gain = gains[0] * gains[1]
    scale = (P_SIZE * P_SIZE / gain) ** 2 / P_SIZE
    groups = groups_of(bands)
    spectra = []
    for group in groups:
        blocks = sum((halves(mm(row_tab[:P_SIZE, :], windows[i])) for i in group), [])
        spectra.append(spectrum(blocks, col_tab[...]))
    found = [correlate(own, freq, GROUP, col_tab[...]) for own, (freq, _) in zip(owns, spectra)]
    for group, rows, flag, (_, power) in zip(groups, found, flags, spectra):
        factors = flag * (scale / jnp.sqrt(power * (1.0 / gain**2) + EPSILON))
        for n, i in enumerate(group):
            maps = mm(inv_tab[...], jnp.concatenate(rows[2 * n : 2 * n + 2], axis=1))
            for h, value in enumerate(halves(maps)):
                p = 2 * n + h
                write(i, h, value * factors[p : p + 1])


def split(x):
    hi = x.astype(jnp.bfloat16)
    return hi, (x - hi.astype(jnp.float32)).astype(jnp.bfloat16)


def pooled(hi, lo, pool):
    span = pool.shape[0]
    parts = []
    for at in range(0, hi.shape[1], span):
        sums = mm(hi[:, at : at + span], pool) + mm(lo[:, at : at + span], pool)
        parts.append((sums * (1.0 / (DS * DS))).astype(jnp.bfloat16))
    return parts


def exchange_kernel(
    bands,
    units,
    gains,
    offsets_hbm,
    peaks_hbm,
    keep_hbm,
    img,
    row_hbm,
    col_hbm,
    inv_hbm,
    wide_hbm,
    pool_hbm,
    maps,
    coarse,
    windows,
    last_spec,
    flags,
    row_tab,
    col_tab,
    inv_tab,
    own,
    land,
    ext,
    spec,
    small_own,
    small_land,
    small,
    small_spec,
    own_hi,
    own_lo,
    sum_hi,
    sum_lo,
    wide_tab,
    pool,
    offsets,
    peaks,
    keep,
    relayed,
    send_sems,
    recv_sems,
    side_send,
    side_recv,
    relay_sems,
    local_sems,
):
    s = lax.axis_index("sec")
    t = lax.axis_index("tile")
    ns = lax.axis_size("sec")
    nt = lax.axis_size("tile")
    rows, width = own.shape
    columns = width // LANES
    centre = rows - 2 * HALO
    reach = rows + 2 * HALO
    row_gain, col_gain, wide_gain = gains
    groups = groups_of(bands)
    early = columns // 2 + 1
    detour = columns // 2
    last = columns - 1
    top = P_SIZE + HALO
    bottom = rows - top
    spans = ((HALO, top - HALO), (bottom, rows - HALO - bottom), (top, bottom - top))

    sends = s < ns - 1
    receives = s > 0
    has_up = t > 0
    has_down = t < nt - 1
    s_next = jnp.minimum(s + 1, ns - 1)
    s_prev = jnp.maximum(s - 1, 0)
    t_next = jnp.minimum(t + 1, nt - 1)
    t_prev = jnp.maximum(t - 1, 0)
    eighth = lax.rem(s, 8)
    starts_relay = (eighth == 3) & (s + 4 < ns)
    relays = eighth == 7
    ends_relay = (eighth == 4) & (s + 3 < ns)
    relay_from = jnp.maximum(s - 4, 0)
    relay_by = jnp.minimum(s + 4, ns - 1)
    relay_to = jnp.maximum(s - 3, 0)
    relayed_by = jnp.minimum(s + 3, ns - 1)

    barrier = pltpu.get_barrier_semaphore()
    for cond, peer in (
        (receives, (s_prev, t)),
        (ends_relay, (relayed_by, t)),
        (relays, (relay_from, t)),
        (has_up, (s, t_prev)),
        (has_down, (s, t_next)),
    ):

        @pl.when(cond)
        def _(peer=peer):
            pl.semaphore_signal(barrier, inc=1, device_id=peer, device_id_type=MESH)

    loads = [
        pltpu.make_async_copy(source, target, local_sems.at[n])
        for n, (source, target) in enumerate(
            (
                (img, own),
                (row_hbm, row_tab),
                (col_hbm, col_tab),
                (inv_hbm, inv_tab),
                (wide_hbm, wide_tab),
                (pool_hbm, pool),
                (offsets_hbm, offsets),
                (peaks_hbm, peaks),
                (keep_hbm, keep),
            )
        )
    ]
    for load in loads:
        load.start()
    loads[0].wait()
    peers = sum(jnp.where(cond, 1, 0) for cond in (sends, starts_relay, relays, has_up, has_down))
    pl.semaphore_wait(barrier, peers)

    def edge_copy(n):
        start = n * (rows - HALO)
        return pltpu.make_async_remote_copy(
            src_ref=own.at[pl.ds(start, HALO)],
            dst_ref=land.at[pl.ds(HALO + start, HALO)],
            send_sem=send_sems.at[n],
            recv_sem=recv_sems.at[n],
            device_id=(s_next, t),
            device_id_type=MESH,
        )

    def column_copy(c, n=None):
        at = pl.multiple_of(c * LANES, LANES)
        start, size = (HALO, centre) if n is None else spans[n]
        sem = 3 + c if n is None else 3 + last + n
        return pltpu.make_async_remote_copy(
            src_ref=own.at[pl.ds(start, size), pl.ds(at, LANES)],
            dst_ref=land.at[pl.ds(HALO + start, size), pl.ds(at, LANES)],
            send_sem=send_sems.at[sem],
            recv_sem=recv_sems.at[sem],
            device_id=(s_next, t),
            device_id_type=MESH,
        )

    def relay_in():
        return pltpu.make_async_remote_copy(
            src_ref=own.at[pl.ds(HALO, centre), pl.ds(detour * LANES, LANES)],
            dst_ref=relayed,
            send_sem=relay_sems.at[0],
            recv_sem=relay_sems.at[1],
            device_id=(relay_by, t),
            device_id_type=MESH,
        )

    def relay_out():
        return pltpu.make_async_remote_copy(
            src_ref=relayed,
            dst_ref=land.at[pl.ds(2 * HALO, centre), pl.ds(detour * LANES, LANES)],
            send_sem=relay_sems.at[2],
            recv_sem=recv_sems.at[3 + detour],
            device_id=(relay_to, t),
            device_id_type=MESH,
        )

    def small_copy():
        return pltpu.make_async_remote_copy(
            src_ref=small_own.at[pl.ds(COARSE, small_land.shape[0]), pl.ds(LANES, LANES)],
            dst_ref=small_land,
            send_sem=send_sems.at[2],
            recv_sem=recv_sems.at[2],
            device_id=(s_next, t),
            device_id_type=MESH,
        )

    def side_copy(n):
        source, target, peer = ((HALO, HALO + rows, t_prev), (rows, 0, t_next))[n]
        return pltpu.make_async_remote_copy(
            src_ref=land.at[pl.ds(source, HALO)],
            dst_ref=land.at[pl.ds(target, HALO)],
            send_sem=side_send.at[n],
            recv_sem=side_recv.at[n],
            device_id=(s, peer),
            device_id_type=MESH,
        )

    @pl.when(sends)
    def _():
        edge_copy(0).start()
        edge_copy(1).start()
        for c in range(early):
            if c != detour:
                column_copy(c).start()

    @pl.when(starts_relay)
    def _():
        relay_in().start()

    @pl.when(sends & jnp.logical_not(starts_relay))
    def _():
        column_copy(detour).start()

    @pl.when(jnp.logical_not(receives))
    def _():
        land[...] = jnp.zeros_like(land)
        small_land[...] = jnp.zeros_like(small_land)

    @pl.when(receives & jnp.logical_not(has_up))
    def _():
        land[:HALO, :] = jnp.zeros((HALO, width), jnp.bfloat16)

    @pl.when(receives & jnp.logical_not(has_down))
    def _():
        land[HALO + rows :, :] = jnp.zeros((HALO, width), jnp.bfloat16)

    ext[0] = jnp.zeros((reach, LANES), jnp.float32)
    ext[columns + 1] = jnp.zeros((reach, LANES), jnp.float32)
    small[0] = jnp.zeros(small.shape[1:], jnp.float32)
    small[3] = jnp.zeros(small.shape[1:], jnp.float32)
    for load in loads[1:]:
        load.wait()

    def own_unit(u, carry):
        at = pl.multiple_of(u * PAIR, PAIR)
        gain = row_gain * col_gain
        spectra = []
        for group in groups:
            blocks = []
            for i in group:
                both = mm(row_tab[...], own[i * P_SIZE : (i + 1) * P_SIZE, pl.ds(at, PAIR)])
                blocks += halves(both[:P_SIZE])
                hi, lo = split(both[P_SIZE:])
                own_hi[i * POOLED : (i + 1) * POOLED, pl.ds(at, PAIR)] = hi
                own_lo[i * POOLED : (i + 1) * POOLED, pl.ds(at, PAIR)] = lo
            spectra.append(spectrum(blocks, col_tab[...]))
        for g, (freq, power) in enumerate(spectra):
            factors = (1.0 / gain) / jnp.sqrt(power * (1.0 / gain**2) + EPSILON)
            store_scaled(spec.at[u, g], freq, GROUP, factors)
        return carry

    lax.fori_loop(0, units, own_unit, 0)
    for n, part in enumerate(pooled(own_hi[...], own_lo[...], pool[...])):
        small_own[:, n * LANES : (n + 1) * LANES] = part

    @pl.when(sends)
    def _():
        small_copy().start()
        for c in range(early, last):
            column_copy(c).start()
        for n in range(len(spans)):
            column_copy(last, n).start()

    @pl.when(relays)
    def _():
        relay_in().wait_recv()
        relay_out().start()

    @pl.when(receives)
    def _():
        edge_copy(0).wait_recv()

        @pl.when(has_up)
        def _():
            side_copy(0).start()

        edge_copy(1).wait_recv()

        @pl.when(has_down)
        def _():
            side_copy(1).start()

    last_spec[...] = spec[units - 1]
    for g, group in enumerate(groups):
        flags[g] = group_flags(units - 1, group, keep)
    freq, power = spectrum([mm(row_tab[:P_SIZE, :], small_own[...])], wide_tab[...])
    gain = row_gain * wide_gain
    factors = (1.0 / gain) / jnp.sqrt(power * (1.0 / gain**2) + EPSILON)
    store_scaled(small_spec, freq, 1, factors)

    @pl.when(receives)
    def _():
        @pl.when(has_up)
        def _():
            side_copy(1).wait_recv()

        @pl.when(has_down)
        def _():
            side_copy(0).wait_recv()

    for at in (0, HALO + rows - HALO):
        for c in range(columns):
            ext[c + 1, at : at + 2 * HALO, :] = land[
                at : at + 2 * HALO, c * LANES : (c + 1) * LANES
            ].astype(jnp.float32)

    def row_sums(c, at, count):
        sums = ext[c + 1, pl.ds(at, count, stride=DS), :]
        for k in range(1, DS):
            sums = sums + ext[c + 1, pl.ds(at + k, count, stride=DS), :]
        return split(sums)

    def arrive(c, n=None):
        @pl.when(receives)
        def _():
            column_copy(c, n).wait_recv()

        at = pl.multiple_of(c * LANES, LANES)
        start, size = (HALO, centre) if n is None else spans[n]
        block = land[HALO + start : HALO + start + size, pl.ds(at, LANES)]
        ext[c + 1, HALO + start : HALO + start + size, :] = block.astype(jnp.float32)

    def coarse_map():
        half = columns // 2
        first = HALO - DS * COARSE
        count = small.shape[1]
        for c in range(half):
            hi, lo = row_sums(c, first, count)
            sum_hi[:, c * LANES : (c + 1) * LANES] = hi
            sum_lo[:, c * LANES : (c + 1) * LANES] = lo
        small[1] = pooled(sum_hi[...], sum_lo[...], pool[...])[0].astype(jnp.float32)
        side = 2 * COARSE
        for c in range(half):
            for n, at in enumerate((first, first + DS * (count - side))):
                hi, lo = row_sums(half + c, at, side)
                sum_hi[n * side : (n + 1) * side, c * LANES : (c + 1) * LANES] = hi
                sum_lo[n * side : (n + 1) * side, c * LANES : (c + 1) * LANES] = lo

        @pl.when(receives)
        def _():
            small_copy().wait_recv()

        ends = pooled(sum_hi[: 2 * side], sum_lo[: 2 * side], pool[...])[0].astype(jnp.float32)
        small[2, :side] = ends[:side]
        small[2, side : count - side] = small_land[...].astype(jnp.float32)
        small[2, count - side :] = ends[side:]
        height = count - 2 * COARSE
        row_at, col_at = COARSE + offsets[0, 0, 0], LANES + offsets[0, 0, 1]
        window = [
            window_at(small, (row_at, col_at + n * LANES), height).astype(jnp.bfloat16)
            for n in range(2)
        ]
        freq, power = spectrum(
            [mm(row_tab[:P_SIZE, :], jnp.concatenate(window, axis=1))], wide_tab[...]
        )
        gain = row_gain * wide_gain
        size = height * 2 * LANES
        scale = (size / gain) ** 2 / math.sqrt(size)
        factors = scale / jnp.sqrt(power * (1.0 / gain**2) + EPSILON)
        found = correlate(small_spec[...], freq, 1, wide_tab[...])[0]
        coarse[...] = mm(inv_tab[...], found) * factors[0:1]

    arrive(0)

    def unit_step(u, carry):
        arrive(2 * u + 1)

        @pl.when(u == columns // 4 - 1)
        def _():
            coarse_map()

        arrive(2 * u + 2)

        def write(i, h, value):
            at = pl.multiple_of(u * PAIR + h * P_SIZE, P_SIZE)
            maps[i * P_SIZE : (i + 1) * P_SIZE, pl.ds(at, P_SIZE)] = value

        places = unit_places(u, bands, offsets, peaks)
        match_unit(
            bands,
            (row_gain, col_gain),
            [band_window(ext, places, i) for i in range(bands)],
            [group_flags(u, group, keep)[:, :1] for group in groups],
            [spec[u, g] for g in range(len(groups))],
            row_tab,
            col_tab,
            inv_tab,
            write,
        )
        return carry

    lax.fori_loop(0, units - 1, unit_step, 0)

    @pl.when(receives & has_up)
    def _():
        side_copy(0).wait_send()

    @pl.when(receives & has_down)
    def _():
        side_copy(1).wait_send()

    @pl.when(relays)
    def _():
        relay_out().wait_send()

    @pl.when(starts_relay)
    def _():
        relay_in().wait_send()

    @pl.when(sends & jnp.logical_not(starts_relay))
    def _():
        column_copy(detour).wait_send()

    @pl.when(sends)
    def _():
        edge_copy(0).wait_send()
        edge_copy(1).wait_send()
        small_copy().wait_send()
        for c in range(last):
            if c != detour:
                column_copy(c).wait_send()
        for n in range(len(spans)):
            column_copy(last, n).wait_send()

    places = unit_places(units - 1, bands, offsets, peaks)
    arrive(last, 0)
    arrive(last, 1)
    for i in groups[0]:
        windows[i] = band_window(ext, places, i)
    arrive(last, 2)
    for group in groups[1:]:
        for i in group:
            windows[i] = band_window(ext, places, i)


def finish_kernel(
    bands,
    gains,
    maps,
    coarse,
    windows,
    last_spec,
    flags,
    row_tab,
    col_tab,
    inv_tab,
    coarse_out,
    flow_out,
    last_maps,
    sems,
):
    done = maps.shape[1]
    copies = [pltpu.make_async_copy(coarse, coarse_out.at[0], sems.at[2 * bands])]
    for i in range(bands):
        band = pl.ds(i * P_SIZE, P_SIZE)
        copies.append(pltpu.make_async_copy(maps.at[band], flow_out.at[0, band, pl.ds(0, done)], sems.at[i]))
    for copy in copies:
        copy.start()

    def write(i, h, value):
        last_maps[i * P_SIZE : (i + 1) * P_SIZE, h * P_SIZE : (h + 1) * P_SIZE] = value

    match_unit(
        bands,
        gains[:2],
        [windows[i] for i in range(bands)],
        [flags[g, :, :1] for g in range(flags.shape[0])],
        [last_spec[g] for g in range(flags.shape[0])],
        row_tab,
        col_tab,
        inv_tab,
        write,
    )
    for i in range(bands):
        band = pl.ds(i * P_SIZE, P_SIZE)
        copies.append(
            pltpu.make_async_copy(last_maps.at[band], flow_out.at[0, band, pl.ds(done, PAIR)], sems.at[bands + i])
        )
        copies[-1].start()
    for copy in copies:
        copy.wait()


def shards(section_image, offsets, peak_shift, accepted):
    own = section_image[0]
    rows, width = own.shape
    bands = rows // P_SIZE
    units = width // PAIR
    columns = width // LANES
    reach = rows + 2 * HALO
    small_width = width // DS
    forward_row, inverse_row, row_gain = row_tables()
    col, col_gain = col_table(P_SIZE)
    wide, wide_gain = col_table(small_width)
    gains = (float(row_gain), float(col_gain), float(wide_gain))
    span = DS * LANES
    pool = quantized(np.arange(span)[:, None] // DS == np.arange(LANES)[None, :])
    tables = [jnp.asarray(x) for x in (forward_row, col, inverse_row, wide, pool)]
    scalars = (offsets, jnp.swapaxes(peak_shift, 2, 3), accepted)
    teams = len(groups_of(bands))
    high = GROUP * HALF + 2 * SUB
    small_high = HALF + 2 * SUB
    small_rows = rows // DS + 2 * COARSE
    hbm = pl.BlockSpec(memory_space=pltpu.HBM)
    vmem = pl.BlockSpec(memory_space=pltpu.VMEM)
    limit = 30 * 2**20
    operands = [pltpu.with_memory_space_constraint(x, pltpu.HBM) for x in (*scalars, own, *tables)]
    between = pl.pallas_call(
        functools.partial(exchange_kernel, bands, units, gains),
        name="exchange",
        out_shape=(
            jax.ShapeDtypeStruct((rows, width - PAIR), jnp.float32),
            jax.ShapeDtypeStruct((rows // DS, small_width), jnp.float32),
            jax.ShapeDtypeStruct((bands, P_SIZE, PAIR), jnp.bfloat16),
            jax.ShapeDtypeStruct((teams, high, PAIR), jnp.float32),
            jax.ShapeDtypeStruct((teams, SUB, LANES), jnp.float32),
        )
        + tuple(jax.ShapeDtypeStruct(x.shape, x.dtype) for x in tables[:3]),
        in_specs=[hbm] * 9,
        out_specs=(vmem,) * 8,
        scratch_shapes=[
            pltpu.VMEM((rows, width), jnp.bfloat16),
            pltpu.VMEM((reach, width), jnp.bfloat16),
            pltpu.VMEM((columns + 2, reach, LANES), jnp.float32),
            pltpu.VMEM((units, teams, high, PAIR), jnp.float32),
            pltpu.VMEM((rows // DS, small_width), jnp.bfloat16),
            pltpu.VMEM((rows // DS - 2 * COARSE, LANES), jnp.bfloat16),
            pltpu.VMEM((small_width // LANES + 2, small_rows, LANES), jnp.float32),
            pltpu.VMEM((small_high, 2 * small_width), jnp.float32),
            pltpu.VMEM((rows // DS, width), jnp.bfloat16),
            pltpu.VMEM((rows // DS, width), jnp.bfloat16),
            pltpu.VMEM((small_rows, span), jnp.bfloat16),
            pltpu.VMEM((small_rows, span), jnp.bfloat16),
            pltpu.VMEM(wide.shape, jnp.bfloat16),
            pltpu.VMEM(pool.shape, jnp.bfloat16),
        ]
        + [pltpu.SMEM(x.shape, jnp.int32) for x in scalars]
        + [
            pltpu.VMEM((rows - 2 * HALO, LANES), jnp.bfloat16),
            pltpu.SemaphoreType.DMA((columns + 5,)),
            pltpu.SemaphoreType.DMA((columns + 5,)),
            pltpu.SemaphoreType.DMA((2,)),
            pltpu.SemaphoreType.DMA((2,)),
            pltpu.SemaphoreType.DMA((3,)),
            pltpu.SemaphoreType.DMA((len(operands),)),
        ],
        compiler_params=pltpu.CompilerParams(
            collective_id=0, has_side_effects=True, vmem_limit_bytes=limit
        ),
    )(*operands)
    return pl.pallas_call(
        functools.partial(finish_kernel, bands, gains),
        name="finish",
        out_shape=(
            jax.ShapeDtypeStruct((1, rows // DS, small_width), jnp.float32),
            jax.ShapeDtypeStruct((1, rows, width), jnp.float32),
        ),
        in_specs=[vmem] * 8,
        out_specs=(hbm, hbm),
        scratch_shapes=[
            pltpu.VMEM((rows, PAIR), jnp.float32),
            pltpu.SemaphoreType.DMA((2 * bands + 1,)),
        ],
        compiler_params=pltpu.CompilerParams(vmem_limit_bytes=limit),
    )(*between)


def solution(mesh):
    return jax.shard_map(
        shards,
        mesh=mesh,
        in_specs=(
            P("sec", "tile", None),
            P("sec", "tile", None),
            P("sec", "tile", None, None),
            P("sec", "tile", None),
        ),
        out_specs=(P("sec", "tile", None), P("sec", "tile", None)),
        check_vma=False,
    )
```

```python
import functools
import math

import jax
import jax.numpy as jnp
import ml_dtypes
import numpy as np
from jax import lax
from jax.experimental import pallas as pl
from jax.experimental.pallas import tpu as pltpu
from jax.sharding import PartitionSpec as P

P_SIZE = 128
HALF = P_SIZE // 2
DS = 4
COARSE = 16
HALO = 80
LANES = 128
PAIR = 2 * P_SIZE
SUB = 8
GROUP = 4
POOLED = P_SIZE // DS
EPSILON = 1e-05
MESH = pl.DeviceIdType.MESH


def quantized(table):
    return table.astype(np.float32).astype(ml_dtypes.bfloat16)


def table_scale(n):
    cosines = np.cos(2.0 * np.pi * np.arange(n) / n)
    best = None
    for factor in np.linspace(1.0, 2.0, 4001):
        table = quantized(cosines * factor).astype(np.float64)
        gain = (table @ cosines) / (cosines @ cosines)
        error = np.mean((table / gain - cosines) ** 2)
        if best is None or error < best[0]:
            best = (error, factor, gain)
    return best[1], best[2]


def waves(n):
    k = np.arange(n)
    angles = (k[:, None] * k[None, :] % n) * (2.0 * np.pi / n)
    return np.cos(angles), np.sin(angles)


def row_tables():
    n = P_SIZE
    factor, gain = table_scale(n)
    cosines, sines = waves(n)
    alternating = np.where(np.arange(n) % 2 == 0, 1.0, -1.0)
    forward = np.concatenate([cosines[:HALF], sines[:HALF]])
    forward[HALF] = alternating
    weight = np.where(np.arange(HALF) == 0, 1.0, 2.0)[:, None]
    inverse = np.concatenate([cosines[:HALF] * weight, -sines[:HALF] * weight])
    inverse[HALF] = alternating
    pool = (np.arange(POOLED)[:, None] == np.arange(n)[None, :] // DS).astype(np.float64)
    forward = np.concatenate([forward * (factor / n), pool])
    return quantized(forward), quantized(inverse.T * (factor / n)), gain


def col_table(n):
    factor, gain = table_scale(n)
    cosines, sines = waves(n)
    table = np.block([[cosines, sines], [-sines, cosines]]) * (factor / n)
    return quantized(table), gain


def mm(a, b):
    return jnp.dot(a, b, preferred_element_type=jnp.float32)


def to_lhs(rows):
    return jnp.concatenate([rows[:HALF], rows[HALF:]], axis=1).astype(jnp.bfloat16)


def energy(block):
    width = block.shape[1] // 2
    total = block[:, :width] * block[:, :width] + block[:, width:] * block[:, width:]
    head = jnp.where(lax.broadcasted_iota(jnp.int32, (SUB, width), 0) == 0, 0.0, total[:SUB])
    for at in range(SUB, HALF, SUB):
        head = head + total[at : at + SUB]
    return jnp.sum(head, axis=0, keepdims=True)


def spectrum(blocks, table):
    count = len(blocks)
    width = blocks[0].shape[1]
    sub = lax.broadcasted_iota(jnp.int32, (SUB, width), 0)
    ends = jnp.zeros((SUB, width), jnp.float32)
    for p, rows in enumerate(blocks):
        ends = jnp.where(sub == p, rows[0:1], ends)
        ends = jnp.where(sub == GROUP + p, rows[HALF : HALF + 1], ends)
    mean = jnp.sum(ends, axis=1, keepdims=True) * (1.0 / width)
    ends = ends - jnp.where(sub < GROUP, mean, 0.0)
    ends = jnp.concatenate([ends, jnp.zeros_like(ends)], axis=0)
    ends = jnp.concatenate([ends, jnp.zeros_like(ends)], axis=1).astype(jnp.bfloat16)
    freq = mm(jnp.concatenate([to_lhs(rows) for rows in blocks] + [ends], axis=0), table)
    power = jnp.zeros((SUB, width), jnp.float32)
    for p in range(count):
        row = energy(freq[p * HALF : (p + 1) * HALF])
        power = jnp.where((sub == p) | (sub == GROUP + p), row, power)
    tail = freq[count * HALF : count * HALF + SUB]
    tail = tail * tail
    tail = tail[:, :width] + tail[:, width:]
    power = 2.0 * power + tail + pltpu.roll(tail, GROUP, 0)
    return freq, jnp.sum(power, axis=1, keepdims=True)


def store_scaled(ref, freq, count, factors):
    at = count * HALF
    for p in range(count):
        block = slice(p * HALF, (p + 1) * HALF)
        ref[block, :] = freq[block] * factors[p : p + 1]
    ref[at : at + SUB, :] = freq[at : at + SUB] * factors
    ref[at + SUB :, :] = jnp.zeros((SUB, freq.shape[1]), jnp.float32)


def correlate(own, other, count, table):
    width = own.shape[1] // 2
    a_re, a_im = own[:, :width], own[:, width:]
    b_re, b_im = other[:, :width], other[:, width:]
    product = jnp.concatenate([a_re * b_re + a_im * b_im, a_im * b_re - a_re * b_im], axis=1)
    rows = mm(product.astype(jnp.bfloat16), table)
    sub = lax.broadcasted_iota(jnp.int32, (SUB, width), 0)
    at = count * HALF
    blocks = []
    for p in range(count):
        block = rows[p * HALF : (p + 1) * HALF]
        first = rows[at + p : at + p + 1, :width]
        middle = rows[at + GROUP + p : at + GROUP + p + 1, :width]
        parts = [
            jnp.where(sub == 0, first, block[:SUB, :width]),
            block[SUB:, :width],
            jnp.where(sub == 0, middle, block[:SUB, width:]),
            block[SUB:, width:],
        ]
        blocks.append(jnp.concatenate(parts, axis=0).astype(jnp.bfloat16))
    return blocks


def last_groups(bands, columns):
    pairs = [(g, bands - 1 - g) for g in range(bands // 2)]
    return [[(i, c) for i in pair for c in (columns - 2, columns - 1)] for pair in pairs]


def window_at(ref, place, height):
    row_at, col_at = place
    block = lax.shift_right_logical(col_at, 7)
    shift = col_at & (LANES - 1)
    left = ref[block, pl.ds(row_at, height), :]
    right = ref[block + 1, pl.ds(row_at, height), :]
    lane = lax.broadcasted_iota(jnp.int32, (height, LANES), 1)
    return pltpu.roll(jnp.where(lane >= shift, left, right), (LANES - shift) & (LANES - 1), 1)


def group_places(group, offsets, peaks):
    off_row = HALO + DS * offsets[0, 0, 0]
    off_col = LANES + DS * offsets[0, 0, 1]
    return [
        (
            off_row + i * P_SIZE + peaks[0, i, 0, column],
            off_col + column * P_SIZE + peaks[0, i, 1, column],
        )
        for i, column in group
    ]


def group_windows(ext, places):
    cut = [window_at(ext, place, P_SIZE).astype(jnp.bfloat16) for place in places]
    return [jnp.concatenate(cut[n : n + 2], axis=1) for n in range(0, len(cut), 2)]


def group_flags(group, keep):
    sub = lax.broadcasted_iota(jnp.int32, (SUB, 1), 0)
    flags = jnp.zeros((SUB, 1), jnp.float32)
    for p, (i, column) in enumerate(group):
        flags = jnp.where(sub == p, keep[0, i, column].astype(jnp.float32), flags)
    return flags


def halves(rows):
    return [rows[:, :P_SIZE], rows[:, P_SIZE:]]


def window_spectrum(windows, flags, gain, row_tab, col_tab):
    blocks = sum((halves(mm(row_tab[:P_SIZE, :], window)) for window in windows), [])
    freq, power = spectrum(blocks, col_tab[...])
    scale = (P_SIZE * P_SIZE / gain) ** 2 / P_SIZE
    return freq, flags * (scale / jnp.sqrt(power * (1.0 / gain**2) + EPSILON))


def write_maps(own, freq, factors, col_tab, inv_tab, write):
    rows = correlate(own, freq, GROUP, col_tab[...])
    for n in range(0, GROUP, 2):
        maps = mm(inv_tab[...], jnp.concatenate(rows[n : n + 2], axis=1))
        for h, value in enumerate(halves(maps)):
            write(n + h, value * factors[n + h : n + h + 1])


def split(x):
    hi = x.astype(jnp.bfloat16)
    return hi, (x - hi.astype(jnp.float32)).astype(jnp.bfloat16)


def pooled(hi, lo, pool):
    span = pool.shape[0]
    parts = []
    for at in range(0, hi.shape[1], span):
        sums = mm(hi[:, at : at + span], pool) + mm(lo[:, at : at + span], pool)
        parts.append((sums * (1.0 / (DS * DS))).astype(jnp.bfloat16))
    return parts


def exchange_kernel(
    bands,
    units,
    gains,
    offsets_hbm,
    peaks_hbm,
    keep_hbm,
    img,
    row_hbm,
    col_hbm,
    inv_hbm,
    wide_hbm,
    pool_hbm,
    maps,
    coarse,
    windows,
    last_spec,
    first_freq,
    factors_out,
    row_tab,
    col_tab,
    inv_tab,
    own,
    land,
    ext,
    spec,
    small_own,
    small_land,
    small,
    small_spec,
    own_hi,
    own_lo,
    sum_hi,
    sum_lo,
    wide_tab,
    pool,
    offsets,
    peaks,
    keep,
    relayed,
    send_sems,
    recv_sems,
    side_send,
    side_recv,
    relay_sems,
    local_sems,
):
    s = lax.axis_index("sec")
    t = lax.axis_index("tile")
    ns = lax.axis_size("sec")
    nt = lax.axis_size("tile")
    rows, width = own.shape
    columns = width // LANES
    centre = rows - 2 * HALO
    reach = rows + 2 * HALO
    row_gain, col_gain, wide_gain = gains
    flow_gain = row_gain * col_gain
    groups = last_groups(bands, columns)
    early = columns // 2 + 1
    detour = columns // 2
    last = columns - 1
    top = P_SIZE + HALO
    bottom = rows - top
    spans = ((HALO, top - HALO), (bottom, rows - HALO - bottom), (top, bottom - top))

    sends = s < ns - 1
    receives = s > 0
    has_up = t > 0
    has_down = t < nt - 1
    s_next = jnp.minimum(s + 1, ns - 1)
    s_prev = jnp.maximum(s - 1, 0)
    t_next = jnp.minimum(t + 1, nt - 1)
    t_prev = jnp.maximum(t - 1, 0)
    eighth = lax.rem(s, 8)
    starts_relay = (eighth == 3) & (s + 4 < ns)
    relays = eighth == 7
    ends_relay = (eighth == 4) & (s + 3 < ns)
    relay_from = jnp.maximum(s - 4, 0)
    relay_by = jnp.minimum(s + 4, ns - 1)
    relay_to = jnp.maximum(s - 3, 0)
    relayed_by = jnp.minimum(s + 3, ns - 1)

    barrier = pltpu.get_barrier_semaphore()
    for cond, peer in (
        (receives, (s_prev, t)),
        (ends_relay, (relayed_by, t)),
        (relays, (relay_from, t)),
        (has_up, (s, t_prev)),
        (has_down, (s, t_next)),
    ):

        @pl.when(cond)
        def _(peer=peer):
            pl.semaphore_signal(barrier, inc=1, device_id=peer, device_id_type=MESH)

    loads = [
        pltpu.make_async_copy(source, target, local_sems.at[n])
        for n, (source, target) in enumerate(
            (
                (img, own),
                (row_hbm, row_tab),
                (col_hbm, col_tab),
                (inv_hbm, inv_tab),
                (wide_hbm, wide_tab),
                (pool_hbm, pool),
                (offsets_hbm, offsets),
                (peaks_hbm, peaks),
                (keep_hbm, keep),
            )
        )
    ]
    for load in loads:
        load.start()
    loads[0].wait()
    peers = sum(jnp.where(cond, 1, 0) for cond in (sends, starts_relay, relays, has_up, has_down))
    pl.semaphore_wait(barrier, peers)

    def edge_copy(n):
        start = n * (rows - HALO)
        return pltpu.make_async_remote_copy(
            src_ref=own.at[pl.ds(start, HALO)],
            dst_ref=land.at[pl.ds(HALO + start, HALO)],
            send_sem=send_sems.at[n],
            recv_sem=recv_sems.at[n],
            device_id=(s_next, t),
            device_id_type=MESH,
        )

    def column_copy(c, n=None):
        at = pl.multiple_of(c * LANES, LANES)
        start, size = (HALO, centre) if n is None else spans[n]
        sem = 3 + c if n is None else 3 + last + n
        return pltpu.make_async_remote_copy(
            src_ref=own.at[pl.ds(start, size), pl.ds(at, LANES)],
            dst_ref=land.at[pl.ds(HALO + start, size), pl.ds(at, LANES)],
            send_sem=send_sems.at[sem],
            recv_sem=recv_sems.at[sem],
            device_id=(s_next, t),
            device_id_type=MESH,
        )

    def relay_in():
        return pltpu.make_async_remote_copy(
            src_ref=own.at[pl.ds(HALO, centre), pl.ds(detour * LANES, LANES)],
            dst_ref=relayed,
            send_sem=relay_sems.at[0],
            recv_sem=relay_sems.at[1],
            device_id=(relay_by, t),
            device_id_type=MESH,
        )

    def relay_out():
        return pltpu.make_async_remote_copy(
            src_ref=relayed,
            dst_ref=land.at[pl.ds(2 * HALO, centre), pl.ds(detour * LANES, LANES)],
            send_sem=relay_sems.at[2],
            recv_sem=recv_sems.at[3 + detour],
            device_id=(relay_to, t),
            device_id_type=MESH,
        )

    def small_copy():
        return pltpu.make_async_remote_copy(
            src_ref=small_own.at[pl.ds(COARSE, small_land.shape[0]), pl.ds(LANES, LANES)],
            dst_ref=small_land,
            send_sem=send_sems.at[2],
            recv_sem=recv_sems.at[2],
            device_id=(s_next, t),
            device_id_type=MESH,
        )

    def side_copy(n):
        source, target, peer = ((HALO, HALO + rows, t_prev), (rows, 0, t_next))[n]
        return pltpu.make_async_remote_copy(
            src_ref=land.at[pl.ds(source, HALO)],
            dst_ref=land.at[pl.ds(target, HALO)],
            send_sem=side_send.at[n],
            recv_sem=side_recv.at[n],
            device_id=(s, peer),
            device_id_type=MESH,
        )

    @pl.when(sends)
    def _():
        edge_copy(0).start()
        edge_copy(1).start()
        for c in range(early):
            if c != detour:
                column_copy(c).start()

    @pl.when(starts_relay)
    def _():
        relay_in().start()

    @pl.when(sends & jnp.logical_not(starts_relay))
    def _():
        column_copy(detour).start()

    @pl.when(jnp.logical_not(receives))
    def _():
        land[...] = jnp.zeros_like(land)
        small_land[...] = jnp.zeros_like(small_land)

    @pl.when(receives & jnp.logical_not(has_up))
    def _():
        land[:HALO, :] = jnp.zeros((HALO, width), jnp.bfloat16)

    @pl.when(receives & jnp.logical_not(has_down))
    def _():
        land[HALO + rows :, :] = jnp.zeros((HALO, width), jnp.bfloat16)

    ext[0] = jnp.zeros((reach, LANES), jnp.float32)
    ext[columns + 1] = jnp.zeros((reach, LANES), jnp.float32)
    small[0] = jnp.zeros(small.shape[1:], jnp.float32)
    small[3] = jnp.zeros(small.shape[1:], jnp.float32)
    for load in loads[1:]:
        load.wait()

    def own_unit(u, carry):
        at = pl.multiple_of(u * PAIR, PAIR)
        blocks = [[], []]
        for i in range(bands):
            both = mm(row_tab[...], own[i * P_SIZE : (i + 1) * P_SIZE, pl.ds(at, PAIR)])
            for h, block in enumerate(halves(both[:P_SIZE])):
                blocks[h].append(block)
            hi, lo = split(both[P_SIZE:])
            own_hi[i * POOLED : (i + 1) * POOLED, pl.ds(at, PAIR)] = hi
            own_lo[i * POOLED : (i + 1) * POOLED, pl.ds(at, PAIR)] = lo
        for h in range(2):
            freq, power = spectrum(blocks[h], col_tab[...])
            factors = (1.0 / flow_gain) / jnp.sqrt(power * (1.0 / flow_gain**2) + EPSILON)
            store_scaled(spec.at[2 * u + h], freq, GROUP, factors)
        return carry

    lax.fori_loop(0, units, own_unit, 0)
    for n, part in enumerate(pooled(own_hi[...], own_lo[...], pool[...])):
        small_own[:, n * LANES : (n + 1) * LANES] = part

    @pl.when(sends)
    def _():
        small_copy().start()
        for c in range(early, last):
            column_copy(c).start()
        for n in range(len(spans)):
            column_copy(last, n).start()

    @pl.when(relays)
    def _():
        relay_in().wait_recv()
        relay_out().start()

    @pl.when(receives)
    def _():
        edge_copy(0).wait_recv()

        @pl.when(has_up)
        def _():
            side_copy(0).start()

        edge_copy(1).wait_recv()

        @pl.when(has_down)
        def _():
            side_copy(1).start()

    row = lax.broadcasted_iota(jnp.int32, (SUB, PAIR), 0)
    tail = GROUP * HALF
    for g, group in enumerate(groups):
        ends = jnp.zeros((SUB, PAIR), jnp.float32)
        for p, (i, c) in enumerate(group):
            last_spec[g, p * HALF : (p + 1) * HALF, :] = spec[c, i * HALF : (i + 1) * HALF, :]
            known = spec[c, tail : tail + SUB, :]
            ends = jnp.where(row == p, known[i : i + 1], ends)
            ends = jnp.where(row == GROUP + p, known[GROUP + i : GROUP + i + 1], ends)
        last_spec[g, tail : tail + SUB, :] = ends
        last_spec[g, tail + SUB :, :] = jnp.zeros((SUB, PAIR), jnp.float32)
        factors_out[g] = jnp.broadcast_to(group_flags(group, keep), (SUB, LANES))
    freq, power = spectrum([mm(row_tab[:P_SIZE, :], small_own[...])], wide_tab[...])
    gain = row_gain * wide_gain
    factors = (1.0 / gain) / jnp.sqrt(power * (1.0 / gain**2) + EPSILON)
    store_scaled(small_spec, freq, 1, factors)

    @pl.when(receives)
    def _():
        @pl.when(has_up)
        def _():
            side_copy(1).wait_recv()

        @pl.when(has_down)
        def _():
            side_copy(0).wait_recv()

    for at in (0, HALO + rows - HALO):
        for c in range(columns):
            ext[c + 1, at : at + 2 * HALO, :] = land[
                at : at + 2 * HALO, c * LANES : (c + 1) * LANES
            ].astype(jnp.float32)

    def row_sums(c, at, count):
        sums = ext[c + 1, pl.ds(at, count, stride=DS), :]
        for k in range(1, DS):
            sums = sums + ext[c + 1, pl.ds(at + k, count, stride=DS), :]
        return split(sums)

    def arrive(c, n=None):
        @pl.when(receives)
        def _():
            column_copy(c, n).wait_recv()

        at = pl.multiple_of(c * LANES, LANES)
        start, size = (HALO, centre) if n is None else spans[n]
        block = land[HALO + start : HALO + start + size, pl.ds(at, LANES)]
        ext[c + 1, HALO + start : HALO + start + size, :] = block.astype(jnp.float32)

    def coarse_map():
        half = columns // 2
        first = HALO - DS * COARSE
        count = small.shape[1]
        for c in range(half):
            hi, lo = row_sums(c, first, count)
            sum_hi[:, c * LANES : (c + 1) * LANES] = hi
            sum_lo[:, c * LANES : (c + 1) * LANES] = lo
        small[1] = pooled(sum_hi[...], sum_lo[...], pool[...])[0].astype(jnp.float32)
        side = 2 * COARSE
        for c in range(half):
            for n, at in enumerate((first, first + DS * (count - side))):
                hi, lo = row_sums(half + c, at, side)
                sum_hi[n * side : (n + 1) * side, c * LANES : (c + 1) * LANES] = hi
                sum_lo[n * side : (n + 1) * side, c * LANES : (c + 1) * LANES] = lo

        @pl.when(receives)
        def _():
            small_copy().wait_recv()

        ends = pooled(sum_hi[: 2 * side], sum_lo[: 2 * side], pool[...])[0].astype(jnp.float32)
        small[2, :side] = ends[:side]
        small[2, side : count - side] = small_land[...].astype(jnp.float32)
        small[2, count - side :] = ends[side:]
        height = count - 2 * COARSE
        row_at, col_at = COARSE + offsets[0, 0, 0], LANES + offsets[0, 0, 1]
        window = [
            window_at(small, (row_at, col_at + n * LANES), height).astype(jnp.bfloat16)
            for n in range(2)
        ]
        freq, power = spectrum(
            [mm(row_tab[:P_SIZE, :], jnp.concatenate(window, axis=1))], wide_tab[...]
        )
        gain = row_gain * wide_gain
        size = height * 2 * LANES
        scale = (size / gain) ** 2 / math.sqrt(size)
        factors = scale / jnp.sqrt(power * (1.0 / gain**2) + EPSILON)
        found = correlate(small_spec[...], freq, 1, wide_tab[...])[0]
        coarse[...] = mm(inv_tab[...], found) * factors[0:1]

    arrive(0)

    def column_step(c, carry):
        arrive(c + 1)

        @pl.when(c == columns // 2 - 2)
        def _():
            coarse_map()

        def write(p, value):
            at = pl.multiple_of(c * P_SIZE, P_SIZE)
            maps[p * P_SIZE : (p + 1) * P_SIZE, pl.ds(at, P_SIZE)] = value

        group = [(i, c) for i in range(bands)]
        freq, factors = window_spectrum(
            group_windows(ext, group_places(group, offsets, peaks)),
            group_flags(group, keep),
            flow_gain,
            row_tab,
            col_tab,
        )
        write_maps(spec[c], freq, factors, col_tab, inv_tab, write)
        return carry

    lax.fori_loop(0, columns - 2, column_step, 0)

    @pl.when(receives & has_up)
    def _():
        side_copy(0).wait_send()

    @pl.when(receives & has_down)
    def _():
        side_copy(1).wait_send()

    @pl.when(relays)
    def _():
        relay_out().wait_send()

    @pl.when(starts_relay)
    def _():
        relay_in().wait_send()

    @pl.when(sends & jnp.logical_not(starts_relay))
    def _():
        column_copy(detour).wait_send()

    @pl.when(sends)
    def _():
        edge_copy(0).wait_send()
        edge_copy(1).wait_send()
        small_copy().wait_send()
        for c in range(last):
            if c != detour:
                column_copy(c).wait_send()
        for n in range(len(spans)):
            column_copy(last, n).wait_send()

    places = [group_places(group, offsets, peaks) for group in groups]
    arrive(last, 0)
    arrive(last, 1)
    freq, factors = window_spectrum(
        group_windows(ext, places[0]), factors_out[0, :, :1], flow_gain, row_tab, col_tab
    )
    first_freq[...] = freq
    factors_out[0] = jnp.broadcast_to(factors, (SUB, LANES))
    arrive(last, 2)
    for n, window in enumerate(group_windows(ext, places[1])):
        windows[n] = window


def finish_kernel(
    bands,
    columns,
    gain,
    maps,
    coarse,
    windows,
    last_spec,
    first_freq,
    factors_in,
    row_tab,
    col_tab,
    inv_tab,
    coarse_out,
    flow_out,
    last_maps,
    sems,
):
    done = maps.shape[1]
    copies = [pltpu.make_async_copy(coarse, coarse_out.at[0], sems.at[2 * bands])]
    for i in range(bands):
        band = pl.ds(i * P_SIZE, P_SIZE)
        copies.append(pltpu.make_async_copy(maps.at[band], flow_out.at[0, band, pl.ds(0, done)], sems.at[i]))
    for copy in copies:
        copy.start()

    groups = last_groups(bands, columns)
    last = (
        [windows[n] for n in range(windows.shape[0])],
        factors_in[1, :, :1],
    )
    freq, factors = window_spectrum(*last, gain, row_tab, col_tab)
    for group, own, of, by in (
        (groups[0], last_spec[0], first_freq[...], factors_in[0, :, :1]),
        (groups[1], last_spec[1], freq, factors),
    ):

        def write(p, value, group=group):
            i, c = group[p]
            at = (c - columns + 2) * P_SIZE
            last_maps[i * P_SIZE : (i + 1) * P_SIZE, at : at + P_SIZE] = value

        write_maps(own, of, by, col_tab, inv_tab, write)
    for i in range(bands):
        band = pl.ds(i * P_SIZE, P_SIZE)
        copies.append(
            pltpu.make_async_copy(last_maps.at[band], flow_out.at[0, band, pl.ds(done, PAIR)], sems.at[bands + i])
        )
        copies[-1].start()
    for copy in copies:
        copy.wait()


def shards(section_image, offsets, peak_shift, accepted):
    own = section_image[0]
    rows, width = own.shape
    bands = rows // P_SIZE
    units = width // PAIR
    columns = width // LANES
    reach = rows + 2 * HALO
    small_width = width // DS
    forward_row, inverse_row, row_gain = row_tables()
    col, col_gain = col_table(P_SIZE)
    wide, wide_gain = col_table(small_width)
    gains = (float(row_gain), float(col_gain), float(wide_gain))
    span = DS * LANES
    pool = quantized(np.arange(span)[:, None] // DS == np.arange(LANES)[None, :])
    tables = [jnp.asarray(x) for x in (forward_row, col, inverse_row, wide, pool)]
    scalars = (offsets, jnp.swapaxes(peak_shift, 2, 3), accepted)
    teams = bands // 2
    high = GROUP * HALF + 2 * SUB
    small_high = HALF + 2 * SUB
    small_rows = rows // DS + 2 * COARSE
    hbm = pl.BlockSpec(memory_space=pltpu.HBM)
    vmem = pl.BlockSpec(memory_space=pltpu.VMEM)
    limit = 30 * 2**20
    operands = [pltpu.with_memory_space_constraint(x, pltpu.HBM) for x in (*scalars, own, *tables)]
    between = pl.pallas_call(
        functools.partial(exchange_kernel, bands, units, gains),
        name="exchange",
        out_shape=(
            jax.ShapeDtypeStruct((rows, width - PAIR), jnp.float32),
            jax.ShapeDtypeStruct((rows // DS, small_width), jnp.float32),
            jax.ShapeDtypeStruct((bands // 2, P_SIZE, PAIR), jnp.bfloat16),
            jax.ShapeDtypeStruct((teams, high, PAIR), jnp.float32),
            jax.ShapeDtypeStruct((high, PAIR), jnp.float32),
            jax.ShapeDtypeStruct((teams, SUB, LANES), jnp.float32),
        )
        + tuple(jax.ShapeDtypeStruct(x.shape, x.dtype) for x in tables[:3]),
        in_specs=[hbm] * 9,
        out_specs=(vmem,) * 9,
        scratch_shapes=[
            pltpu.VMEM((rows, width), jnp.bfloat16),
            pltpu.VMEM((reach, width), jnp.bfloat16),
            pltpu.VMEM((columns + 2, reach, LANES), jnp.float32),
            pltpu.VMEM((columns, high, PAIR), jnp.float32),
            pltpu.VMEM((rows // DS, small_width), jnp.bfloat16),
            pltpu.VMEM((rows // DS - 2 * COARSE, LANES), jnp.bfloat16),
            pltpu.VMEM((small_width // LANES + 2, small_rows, LANES), jnp.float32),
            pltpu.VMEM((small_high, 2 * small_width), jnp.float32),
            pltpu.VMEM((rows // DS, width), jnp.bfloat16),
            pltpu.VMEM((rows // DS, width), jnp.bfloat16),
            pltpu.VMEM((small_rows, span), jnp.bfloat16),
            pltpu.VMEM((small_rows, span), jnp.bfloat16),
            pltpu.VMEM(wide.shape, jnp.bfloat16),
            pltpu.VMEM(pool.shape, jnp.bfloat16),
        ]
        + [pltpu.SMEM(x.shape, jnp.int32) for x in scalars]
        + [
            pltpu.VMEM((rows - 2 * HALO, LANES), jnp.bfloat16),
            pltpu.SemaphoreType.DMA((columns + 5,)),
            pltpu.SemaphoreType.DMA((columns + 5,)),
            pltpu.SemaphoreType.DMA((2,)),
            pltpu.SemaphoreType.DMA((2,)),
            pltpu.SemaphoreType.DMA((3,)),
            pltpu.SemaphoreType.DMA((len(operands),)),
        ],
        compiler_params=pltpu.CompilerParams(
            collective_id=0, has_side_effects=True, vmem_limit_bytes=limit
        ),
    )(*operands)
    return pl.pallas_call(
        functools.partial(finish_kernel, bands, columns, gains[0] * gains[1]),
        name="finish",
        out_shape=(
            jax.ShapeDtypeStruct((1, rows // DS, small_width), jnp.float32),
            jax.ShapeDtypeStruct((1, rows, width), jnp.float32),
        ),
        in_specs=[vmem] * 9,
        out_specs=(hbm, hbm),
        scratch_shapes=[
            pltpu.VMEM((rows, PAIR), jnp.float32),
            pltpu.SemaphoreType.DMA((2 * bands + 1,)),
        ],
        compiler_params=pltpu.CompilerParams(vmem_limit_bytes=limit),
    )(*between)


def solution(mesh):
    return jax.shard_map(
        shards,
        mesh=mesh,
        in_specs=(
            P("sec", "tile", None),
            P("sec", "tile", None),
            P("sec", "tile", None, None),
            P("sec", "tile", None),
        ),
        out_specs=(P("sec", "tile", None), P("sec", "tile", None)),
        check_vma=False,
    )
```

```python
import functools
import math

import jax
import jax.numpy as jnp
import ml_dtypes
import numpy as np
from jax import lax
from jax.experimental import pallas as pl
from jax.experimental.pallas import tpu as pltpu
from jax.sharding import PartitionSpec as P

P_SIZE = 128
HALF = P_SIZE // 2
DS = 4
COARSE = 16
HALO = 80
LANES = 128
PAIR = 2 * P_SIZE
SUB = 8
GROUP = 4
POOLED = P_SIZE // DS
EPSILON = 1e-05
MESH = pl.DeviceIdType.MESH


def quantized(table):
    return table.astype(np.float32).astype(ml_dtypes.bfloat16)


def table_scale(n):
    cosines = np.cos(2.0 * np.pi * np.arange(n) / n)
    best = None
    for factor in np.linspace(1.0, 2.0, 4001):
        table = quantized(cosines * factor).astype(np.float64)
        gain = (table @ cosines) / (cosines @ cosines)
        error = np.mean((table / gain - cosines) ** 2)
        if best is None or error < best[0]:
            best = (error, factor, gain)
    return best[1], best[2]


def waves(n):
    k = np.arange(n)
    angles = (k[:, None] * k[None, :] % n) * (2.0 * np.pi / n)
    return np.cos(angles), np.sin(angles)


def row_tables():
    n = P_SIZE
    factor, gain = table_scale(n)
    cosines, sines = waves(n)
    alternating = np.where(np.arange(n) % 2 == 0, 1.0, -1.0)
    forward = np.concatenate([cosines[:HALF], sines[:HALF]])
    forward[HALF] = alternating
    weight = np.where(np.arange(HALF) == 0, 1.0, 2.0)[:, None]
    inverse = np.concatenate([cosines[:HALF] * weight, -sines[:HALF] * weight])
    inverse[HALF] = alternating
    pool = (np.arange(POOLED)[:, None] == np.arange(n)[None, :] // DS).astype(np.float64)
    forward = np.concatenate([forward * (factor / n), pool])
    return quantized(forward), quantized(inverse.T * (factor / n)), gain


def col_table(n):
    factor, gain = table_scale(n)
    cosines, sines = waves(n)
    table = np.block([[cosines, sines], [-sines, cosines]]) * (factor / n)
    return quantized(table), gain


def mm(a, b):
    return jnp.dot(a, b, preferred_element_type=jnp.float32)


def to_lhs(rows):
    return jnp.concatenate([rows[:HALF], rows[HALF:]], axis=1).astype(jnp.bfloat16)


def energy(block):
    width = block.shape[1] // 2
    total = block[:, :width] * block[:, :width] + block[:, width:] * block[:, width:]
    head = jnp.where(lax.broadcasted_iota(jnp.int32, (SUB, width), 0) == 0, 0.0, total[:SUB])
    for at in range(SUB, HALF, SUB):
        head = head + total[at : at + SUB]
    return jnp.sum(head, axis=0, keepdims=True)


def spectrum(blocks, table):
    count = len(blocks)
    width = blocks[0].shape[1]
    sub = lax.broadcasted_iota(jnp.int32, (SUB, width), 0)
    ends = jnp.zeros((SUB, width), jnp.float32)
    for p, rows in enumerate(blocks):
        ends = jnp.where(sub == p, rows[0:1], ends)
        ends = jnp.where(sub == GROUP + p, rows[HALF : HALF + 1], ends)
    mean = jnp.sum(ends, axis=1, keepdims=True) * (1.0 / width)
    ends = ends - jnp.where(sub < GROUP, mean, 0.0)
    ends = jnp.concatenate([ends, jnp.zeros_like(ends)], axis=0)
    ends = jnp.concatenate([ends, jnp.zeros_like(ends)], axis=1).astype(jnp.bfloat16)
    freq = mm(jnp.concatenate([to_lhs(rows) for rows in blocks] + [ends], axis=0), table)
    power = jnp.zeros((SUB, width), jnp.float32)
    for p in range(count):
        row = energy(freq[p * HALF : (p + 1) * HALF])
        power = jnp.where((sub == p) | (sub == GROUP + p), row, power)
    tail = freq[count * HALF : count * HALF + SUB]
    tail = tail * tail
    tail = tail[:, :width] + tail[:, width:]
    power = 2.0 * power + tail + pltpu.roll(tail, GROUP, 0)
    return freq, jnp.sum(power, axis=1, keepdims=True)


def store_scaled(ref, freq, count, factors):
    at = count * HALF
    for p in range(count):
        block = slice(p * HALF, (p + 1) * HALF)
        ref[block, :] = freq[block] * factors[p : p + 1]
    ref[at : at + SUB, :] = freq[at : at + SUB] * factors
    ref[at + SUB :, :] = jnp.zeros((SUB, freq.shape[1]), jnp.float32)


def correlate(own, other, count, table):
    width = own.shape[1] // 2
    a_re, a_im = own[:, :width], own[:, width:]
    b_re, b_im = other[:, :width], other[:, width:]
    product = jnp.concatenate([a_re * b_re + a_im * b_im, a_im * b_re - a_re * b_im], axis=1)
    rows = mm(product.astype(jnp.bfloat16), table)
    sub = lax.broadcasted_iota(jnp.int32, (SUB, width), 0)
    at = count * HALF
    blocks = []
    for p in range(count):
        block = rows[p * HALF : (p + 1) * HALF]
        first = rows[at + p : at + p + 1, :width]
        middle = rows[at + GROUP + p : at + GROUP + p + 1, :width]
        parts = [
            jnp.where(sub == 0, first, block[:SUB, :width]),
            block[SUB:, :width],
            jnp.where(sub == 0, middle, block[:SUB, width:]),
            block[SUB:, width:],
        ]
        blocks.append(jnp.concatenate(parts, axis=0).astype(jnp.bfloat16))
    return blocks


def window_at(ref, place, height):
    row_at, col_at = place
    block = lax.shift_right_logical(col_at, 7)
    shift = col_at & (LANES - 1)
    left = ref[block, pl.ds(row_at, height), :]
    right = ref[block + 1, pl.ds(row_at, height), :]
    lane = lax.broadcasted_iota(jnp.int32, (height, LANES), 1)
    return pltpu.roll(jnp.where(lane >= shift, left, right), (LANES - shift) & (LANES - 1), 1)


def group_places(group, offsets, peaks):
    off_row = HALO + DS * offsets[0, 0, 0]
    off_col = LANES + DS * offsets[0, 0, 1]
    return [
        (
            off_row + i * P_SIZE + peaks[0, i, 0, column],
            off_col + column * P_SIZE + peaks[0, i, 1, column],
        )
        for i, column in group
    ]


def group_windows(ext, places):
    cut = [window_at(ext, place, P_SIZE).astype(jnp.bfloat16) for place in places]
    return [jnp.concatenate(cut[n : n + 2], axis=1) for n in range(0, len(cut), 2)]


def group_flags(group, keep):
    sub = lax.broadcasted_iota(jnp.int32, (SUB, 1), 0)
    flags = jnp.zeros((SUB, 1), jnp.float32)
    for p, (i, column) in enumerate(group):
        flags = jnp.where(sub == p, keep[0, i, column].astype(jnp.float32), flags)
    return flags


def halves(rows):
    return [rows[:, :P_SIZE], rows[:, P_SIZE:]]


def window_spectrum(windows, flags, gain, row_tab, col_tab):
    blocks = sum((halves(mm(row_tab[:P_SIZE, :], window)) for window in windows), [])
    freq, power = spectrum(blocks, col_tab[...])
    scale = (P_SIZE * P_SIZE / gain) ** 2 / P_SIZE
    return freq, flags * (scale / jnp.sqrt(power * (1.0 / gain**2) + EPSILON))


def write_maps(own, freq, factors, col_tab, inv_tab, write):
    rows = correlate(own, freq, GROUP, col_tab[...])
    for n in range(0, GROUP, 2):
        maps = mm(inv_tab[...], jnp.concatenate(rows[n : n + 2], axis=1))
        for h, value in enumerate(halves(maps)):
            write(n + h, value * factors[n + h : n + h + 1])


def split(x):
    hi = x.astype(jnp.bfloat16)
    return hi, (x - hi.astype(jnp.float32)).astype(jnp.bfloat16)


def pooled(hi, lo, pool):
    span = pool.shape[0]
    parts = []
    for at in range(0, hi.shape[1], span):
        sums = mm(hi[:, at : at + span], pool) + mm(lo[:, at : at + span], pool)
        parts.append((sums * (1.0 / (DS * DS))).astype(jnp.bfloat16))
    return parts


def exchange_kernel(
    bands,
    units,
    gains,
    offsets_hbm,
    peaks_hbm,
    keep_hbm,
    img,
    row_hbm,
    col_hbm,
    inv_hbm,
    wide_hbm,
    pool_hbm,
    maps,
    coarse,
    own,
    land,
    ext,
    spec,
    small_own,
    small_land,
    small,
    small_spec,
    own_hi,
    own_lo,
    sum_hi,
    sum_lo,
    end_hi,
    end_lo,
    row_tab,
    col_tab,
    inv_tab,
    wide_tab,
    pool,
    offsets,
    peaks,
    keep,
    relayed,
    send_sems,
    recv_sems,
    side_send,
    side_recv,
    relay_sems,
    local_sems,
):
    s = lax.axis_index("sec")
    t = lax.axis_index("tile")
    ns = lax.axis_size("sec")
    nt = lax.axis_size("tile")
    rows, width = own.shape
    columns = width // LANES
    centre = rows - 2 * HALO
    reach = rows + 2 * HALO
    row_gain, col_gain, wide_gain = gains
    flow_gain = row_gain * col_gain
    half = columns // 2
    early = half + 1
    detour = half
    last = columns - 1

    sends = s < ns - 1
    receives = s > 0
    has_up = t > 0
    has_down = t < nt - 1
    s_next = jnp.minimum(s + 1, ns - 1)
    s_prev = jnp.maximum(s - 1, 0)
    t_next = jnp.minimum(t + 1, nt - 1)
    t_prev = jnp.maximum(t - 1, 0)
    eighth = lax.rem(s, 8)
    starts_relay = (eighth == 3) & (s + 4 < ns)
    relays = eighth == 7
    ends_relay = (eighth == 4) & (s + 3 < ns)
    relay_from = jnp.maximum(s - 4, 0)
    relay_by = jnp.minimum(s + 4, ns - 1)
    relay_to = jnp.maximum(s - 3, 0)
    relayed_by = jnp.minimum(s + 3, ns - 1)

    barrier = pltpu.get_barrier_semaphore()
    for cond, peer in (
        (receives, (s_prev, t)),
        (ends_relay, (relayed_by, t)),
        (relays, (relay_from, t)),
        (has_up, (s, t_prev)),
        (has_down, (s, t_next)),
    ):

        @pl.when(cond)
        def _(peer=peer):
            pl.semaphore_signal(barrier, inc=1, device_id=peer, device_id_type=MESH)

    loads = [
        pltpu.make_async_copy(source, target, local_sems.at[n])
        for n, (source, target) in enumerate(
            (
                (img, own),
                (row_hbm, row_tab),
                (col_hbm, col_tab),
                (inv_hbm, inv_tab),
                (wide_hbm, wide_tab),
                (pool_hbm, pool),
                (offsets_hbm, offsets),
                (peaks_hbm, peaks),
                (keep_hbm, keep),
            )
        )
    ]
    for load in loads:
        load.start()
    loads[0].wait()
    peers = sum(jnp.where(cond, 1, 0) for cond in (sends, starts_relay, relays, has_up, has_down))
    pl.semaphore_wait(barrier, peers)

    def edge_copy(n):
        start = n * (rows - HALO)
        return pltpu.make_async_remote_copy(
            src_ref=own.at[pl.ds(start, HALO)],
            dst_ref=land.at[pl.ds(HALO + start, HALO)],
            send_sem=send_sems.at[n],
            recv_sem=recv_sems.at[n],
            device_id=(s_next, t),
            device_id_type=MESH,
        )

    def column_copy(c):
        at = pl.multiple_of(c * LANES, LANES)
        return pltpu.make_async_remote_copy(
            src_ref=own.at[pl.ds(HALO, centre), pl.ds(at, LANES)],
            dst_ref=land.at[pl.ds(2 * HALO, centre), pl.ds(at, LANES)],
            send_sem=send_sems.at[3 + c],
            recv_sem=recv_sems.at[3 + c],
            device_id=(s_next, t),
            device_id_type=MESH,
        )

    def relay_in():
        return pltpu.make_async_remote_copy(
            src_ref=own.at[pl.ds(HALO, centre), pl.ds(detour * LANES, LANES)],
            dst_ref=relayed,
            send_sem=send_sems.at[3 + detour],
            recv_sem=relay_sems.at[0],
            device_id=(relay_by, t),
            device_id_type=MESH,
        )

    def relay_out():
        return pltpu.make_async_remote_copy(
            src_ref=relayed,
            dst_ref=land.at[pl.ds(2 * HALO, centre), pl.ds(detour * LANES, LANES)],
            send_sem=relay_sems.at[1],
            recv_sem=recv_sems.at[3 + detour],
            device_id=(relay_to, t),
            device_id_type=MESH,
        )

    def small_copy():
        return pltpu.make_async_remote_copy(
            src_ref=small_own.at[pl.ds(COARSE, small_land.shape[0]), pl.ds(LANES, LANES)],
            dst_ref=small_land,
            send_sem=send_sems.at[2],
            recv_sem=recv_sems.at[2],
            device_id=(s_next, t),
            device_id_type=MESH,
        )

    def side_copy(n):
        source, target, peer = ((HALO, HALO + rows, t_prev), (rows, 0, t_next))[n]
        return pltpu.make_async_remote_copy(
            src_ref=land.at[pl.ds(source, HALO)],
            dst_ref=land.at[pl.ds(target, HALO)],
            send_sem=side_send.at[n],
            recv_sem=side_recv.at[n],
            device_id=(s, peer),
            device_id_type=MESH,
        )

    @pl.when(sends)
    def _():
        edge_copy(0).start()
        edge_copy(1).start()
        for c in range(early):
            if c != detour:
                column_copy(c).start()

    @pl.when(starts_relay)
    def _():
        relay_in().start()

    @pl.when(sends & jnp.logical_not(starts_relay))
    def _():
        column_copy(detour).start()

    @pl.when(jnp.logical_not(receives))
    def _():
        land[...] = jnp.zeros_like(land)
        small_land[...] = jnp.zeros_like(small_land)

    @pl.when(receives & jnp.logical_not(has_up))
    def _():
        land[:HALO, :] = jnp.zeros((HALO, width), jnp.bfloat16)

    @pl.when(receives & jnp.logical_not(has_down))
    def _():
        land[HALO + rows :, :] = jnp.zeros((HALO, width), jnp.bfloat16)

    ext[0] = jnp.zeros((reach, LANES), jnp.float32)
    ext[columns + 1] = jnp.zeros((reach, LANES), jnp.float32)
    small[0] = jnp.zeros(small.shape[1:], jnp.float32)
    small[3] = jnp.zeros(small.shape[1:], jnp.float32)
    for load in loads[1:]:
        load.wait()

    def own_unit(u, carry):
        at = pl.multiple_of(u * PAIR, PAIR)
        blocks = [[], []]
        for i in range(bands):
            both = mm(row_tab[...], own[i * P_SIZE : (i + 1) * P_SIZE, pl.ds(at, PAIR)])
            for h, block in enumerate(halves(both[:P_SIZE])):
                blocks[h].append(block)
            hi, lo = split(both[P_SIZE:])
            own_hi[i * POOLED : (i + 1) * POOLED, pl.ds(at, PAIR)] = hi
            own_lo[i * POOLED : (i + 1) * POOLED, pl.ds(at, PAIR)] = lo
        for h in range(2):
            freq, power = spectrum(blocks[h], col_tab[...])
            factors = (1.0 / flow_gain) / jnp.sqrt(power * (1.0 / flow_gain**2) + EPSILON)
            store_scaled(spec.at[2 * u + h], freq, GROUP, factors)
        return carry

    lax.fori_loop(0, units, own_unit, 0)
    for n, part in enumerate(pooled(own_hi[...], own_lo[...], pool[...])):
        small_own[:, n * LANES : (n + 1) * LANES] = part

    @pl.when(sends)
    def _():
        small_copy().start()
        for c in range(early, columns):
            column_copy(c).start()

    @pl.when(relays)
    def _():
        relay_in().wait_recv()
        relay_out().start()

    @pl.when(receives)
    def _():
        edge_copy(0).wait_recv()

        @pl.when(has_up)
        def _():
            side_copy(0).start()

        edge_copy(1).wait_recv()

        @pl.when(has_down)
        def _():
            side_copy(1).start()

    freq, power = spectrum([mm(row_tab[:P_SIZE, :], small_own[...])], wide_tab[...])
    gain = row_gain * wide_gain
    factors = (1.0 / gain) / jnp.sqrt(power * (1.0 / gain**2) + EPSILON)
    store_scaled(small_spec, freq, 1, factors)

    @pl.when(receives)
    def _():
        @pl.when(has_up)
        def _():
            side_copy(1).wait_recv()

        @pl.when(has_down)
        def _():
            side_copy(0).wait_recv()

    first = HALO - DS * COARSE
    count = small.shape[1]
    side = 2 * COARSE

    def row_sums(c, at, size):
        sums = ext[c + 1, pl.ds(at, size, stride=DS), :]
        for k in range(1, DS):
            sums = sums + ext[c + 1, pl.ds(at + k, size, stride=DS), :]
        return split(sums)

    def edge_step(c, carry):
        at = pl.multiple_of(c * LANES, LANES)
        for n, row in enumerate((0, rows)):
            block = land[row : row + 2 * HALO, pl.ds(at, LANES)]
            ext[c + 1, row : row + 2 * HALO, :] = block.astype(jnp.float32)
            hi, lo = row_sums(c, first + n * DS * (count - side), side)
            end_hi[n * side : (n + 1) * side, pl.ds(at, LANES)] = hi
            end_lo[n * side : (n + 1) * side, pl.ds(at, LANES)] = lo
        return carry

    lax.fori_loop(0, columns, edge_step, 0)

    def arrive(c):
        @pl.when(receives)
        def _():
            column_copy(c).wait_recv()

        at = pl.multiple_of(c * LANES, LANES)
        block = land[2 * HALO : 2 * HALO + centre, pl.ds(at, LANES)]
        ext[c + 1, 2 * HALO : 2 * HALO + centre, :] = block.astype(jnp.float32)

    def early_step(c, carry):
        arrive(c)
        at = pl.multiple_of(c * LANES, LANES)
        hi, lo = row_sums(c, first, count)
        sum_hi[:, pl.ds(at, LANES)] = hi
        sum_lo[:, pl.ds(at, LANES)] = lo
        return carry

    lax.fori_loop(0, half, early_step, 0)

    @pl.when(receives)
    def _():
        small_copy().wait_recv()

    def coarse_map():
        span = half * LANES
        small[1] = pooled(sum_hi[...], sum_lo[...], pool[...])[0].astype(jnp.float32)
        ends = pooled(end_hi[:, span:], end_lo[:, span:], pool[...])[0].astype(jnp.float32)
        small[2, :side] = ends[:side]
        small[2, side : count - side] = small_land[...].astype(jnp.float32)
        small[2, count - side :] = ends[side:]
        height = count - 2 * COARSE
        row_at, col_at = COARSE + offsets[0, 0, 0], LANES + offsets[0, 0, 1]
        window = [
            window_at(small, (row_at, col_at + n * LANES), height).astype(jnp.bfloat16)
            for n in range(2)
        ]
        freq, power = spectrum(
            [mm(row_tab[:P_SIZE, :], jnp.concatenate(window, axis=1))], wide_tab[...]
        )
        gain = row_gain * wide_gain
        size = height * 2 * LANES
        scale = (size / gain) ** 2 / math.sqrt(size)
        factors = scale / jnp.sqrt(power * (1.0 / gain**2) + EPSILON)
        found = correlate(small_spec[...], freq, 1, wide_tab[...])[0]
        coarse[...] = mm(inv_tab[...], found) * factors[0:1]

    coarse_map()

    def column_step(c, carry):
        @pl.when((c >= half - 1) & (c < last))
        def _():
            arrive(c + 1)

        @pl.when(sends)
        def _():
            column_copy(c).wait_send()

        def write(p, value):
            at = pl.multiple_of(c * P_SIZE, P_SIZE)
            maps[p * P_SIZE : (p + 1) * P_SIZE, pl.ds(at, P_SIZE)] = value

        group = [(i, c) for i in range(bands)]
        freq, factors = window_spectrum(
            group_windows(ext, group_places(group, offsets, peaks)),
            group_flags(group, keep),
            flow_gain,
            row_tab,
            col_tab,
        )
        write_maps(spec[c], freq, factors, col_tab, inv_tab, write)
        return carry

    @pl.when(sends)
    def _():
        edge_copy(0).wait_send()
        edge_copy(1).wait_send()
        small_copy().wait_send()

    @pl.when(receives & has_up)
    def _():
        side_copy(0).wait_send()

    @pl.when(receives & has_down)
    def _():
        side_copy(1).wait_send()

    @pl.when(relays)
    def _():
        relay_out().wait_send()

    lax.fori_loop(0, columns, column_step, 0)


def finish_kernel(maps, coarse, coarse_out, flow_out, sems):
    count = sems.shape[0] - 1
    size = maps.shape[0] // count
    copies = [pltpu.make_async_copy(coarse, coarse_out.at[0], sems.at[count])]
    for n in range(count):
        band = pl.ds(n * size, size)
        copies.append(pltpu.make_async_copy(maps.at[band], flow_out.at[0, band], sems.at[n]))
    for copy in copies:
        copy.start()
    for copy in copies:
        copy.wait()


def shards(section_image, offsets, peak_shift, accepted):
    own = section_image[0]
    rows, width = own.shape
    bands = rows // P_SIZE
    units = width // PAIR
    columns = width // LANES
    reach = rows + 2 * HALO
    small_width = width // DS
    forward_row, inverse_row, row_gain = row_tables()
    col, col_gain = col_table(P_SIZE)
    wide, wide_gain = col_table(small_width)
    gains = (float(row_gain), float(col_gain), float(wide_gain))
    span = DS * LANES
    pool = quantized(np.arange(span)[:, None] // DS == np.arange(LANES)[None, :])
    tables = [jnp.asarray(x) for x in (forward_row, col, inverse_row, wide, pool)]
    scalars = (offsets, jnp.swapaxes(peak_shift, 2, 3), accepted)
    high = GROUP * HALF + 2 * SUB
    small_high = HALF + 2 * SUB
    small_rows = rows // DS + 2 * COARSE
    hbm = pl.BlockSpec(memory_space=pltpu.HBM)
    vmem = pl.BlockSpec(memory_space=pltpu.VMEM)
    limit = 30 * 2**20
    operands = [pltpu.with_memory_space_constraint(x, pltpu.HBM) for x in (*scalars, own, *tables)]
    maps, coarse = pl.pallas_call(
        functools.partial(exchange_kernel, bands, units, gains),
        name="exchange",
        out_shape=(
            jax.ShapeDtypeStruct((rows, width), jnp.float32),
            jax.ShapeDtypeStruct((rows // DS, small_width), jnp.float32),
        ),
        in_specs=[hbm] * 9,
        out_specs=(vmem,) * 2,
        scratch_shapes=[
            pltpu.VMEM((rows, width), jnp.bfloat16),
            pltpu.VMEM((reach, width), jnp.bfloat16),
            pltpu.VMEM((columns + 2, reach, LANES), jnp.float32),
            pltpu.VMEM((columns, high, PAIR), jnp.float32),
            pltpu.VMEM((rows // DS, small_width), jnp.bfloat16),
            pltpu.VMEM((rows // DS - 2 * COARSE, LANES), jnp.bfloat16),
            pltpu.VMEM((small_width // LANES + 2, small_rows, LANES), jnp.float32),
            pltpu.VMEM((small_high, 2 * small_width), jnp.float32),
            pltpu.VMEM((rows // DS, width), jnp.bfloat16),
            pltpu.VMEM((rows // DS, width), jnp.bfloat16),
            pltpu.VMEM((small_rows, span), jnp.bfloat16),
            pltpu.VMEM((small_rows, span), jnp.bfloat16),
            pltpu.VMEM((4 * COARSE, width), jnp.bfloat16),
            pltpu.VMEM((4 * COARSE, width), jnp.bfloat16),
        ]
        + [pltpu.VMEM(x.shape, jnp.bfloat16) for x in tables]
        + [pltpu.SMEM(x.shape, jnp.int32) for x in scalars]
        + [
            pltpu.VMEM((rows - 2 * HALO, LANES), jnp.bfloat16),
            pltpu.SemaphoreType.DMA((columns + 3,)),
            pltpu.SemaphoreType.DMA((columns + 3,)),
            pltpu.SemaphoreType.DMA((2,)),
            pltpu.SemaphoreType.DMA((2,)),
            pltpu.SemaphoreType.DMA((2,)),
            pltpu.SemaphoreType.DMA((len(operands),)),
        ],
        compiler_params=pltpu.CompilerParams(
            collective_id=0, has_side_effects=True, vmem_limit_bytes=limit
        ),
    )(*operands)
    return pl.pallas_call(
        finish_kernel,
        name="finish",
        out_shape=(
            jax.ShapeDtypeStruct((1, rows // DS, small_width), jnp.float32),
            jax.ShapeDtypeStruct((1, rows, width), jnp.float32),
        ),
        in_specs=[vmem] * 2,
        out_specs=(hbm, hbm),
        scratch_shapes=[pltpu.SemaphoreType.DMA((bands + 1,))],
        compiler_params=pltpu.CompilerParams(vmem_limit_bytes=limit),
    )(maps, coarse)


def solution(mesh):
    return jax.shard_map(
        shards,
        mesh=mesh,
        in_specs=(
            P("sec", "tile", None),
            P("sec", "tile", None),
            P("sec", "tile", None, None),
            P("sec", "tile", None),
        ),
        out_specs=(P("sec", "tile", None), P("sec", "tile", None)),
        check_vma=False,
    )
```

```python
import functools
import math

import jax
import jax.numpy as jnp
import ml_dtypes
import numpy as np
from jax import lax
from jax.experimental import pallas as pl
from jax.experimental.pallas import tpu as pltpu
from jax.sharding import PartitionSpec as P

P_SIZE = 128
HALF = P_SIZE // 2
DS = 4
COARSE = 16
HALO = 80
LANES = 128
PAIR = 2 * P_SIZE
SUB = 8
GROUP = 4
POOLED = P_SIZE // DS
EPSILON = 1e-05
MESH = pl.DeviceIdType.MESH


def quantized(table):
    return table.astype(np.float32).astype(ml_dtypes.bfloat16)


def table_scale(n):
    cosines = np.cos(2.0 * np.pi * np.arange(n) / n)
    best = None
    for factor in np.linspace(1.0, 2.0, 4001):
        table = quantized(cosines * factor).astype(np.float64)
        gain = (table @ cosines) / (cosines @ cosines)
        error = np.mean((table / gain - cosines) ** 2)
        if best is None or error < best[0]:
            best = (error, factor, gain)
    return best[1], best[2]


def waves(n):
    k = np.arange(n)
    angles = (k[:, None] * k[None, :] % n) * (2.0 * np.pi / n)
    return np.cos(angles), np.sin(angles)


def row_tables():
    n = P_SIZE
    factor, gain = table_scale(n)
    cosines, sines = waves(n)
    alternating = np.where(np.arange(n) % 2 == 0, 1.0, -1.0)
    forward = np.concatenate([cosines[:HALF], sines[:HALF]])
    forward[HALF] = alternating
    weight = np.where(np.arange(HALF) == 0, 1.0, 2.0)[:, None]
    inverse = np.concatenate([cosines[:HALF] * weight, -sines[:HALF] * weight])
    inverse[HALF] = alternating
    pool = (np.arange(POOLED)[:, None] == np.arange(n)[None, :] // DS).astype(np.float64)
    forward = np.concatenate([forward * (factor / n), pool])
    return quantized(forward), quantized(inverse.T * (factor / n)), gain


def col_table(n):
    factor, gain = table_scale(n)
    cosines, sines = waves(n)
    table = np.block([[cosines, sines], [-sines, cosines]]) * (factor / n)
    return quantized(table), gain


def mm(a, b):
    return jnp.dot(a, b, preferred_element_type=jnp.float32)


def to_lhs(rows):
    return jnp.concatenate([rows[:HALF], rows[HALF:]], axis=1).astype(jnp.bfloat16)


def energy(block):
    width = block.shape[1] // 2
    total = block[:, :width] * block[:, :width] + block[:, width:] * block[:, width:]
    head = jnp.where(lax.broadcasted_iota(jnp.int32, (SUB, width), 0) == 0, 0.0, total[:SUB])
    for at in range(SUB, HALF, SUB):
        head = head + total[at : at + SUB]
    return jnp.sum(head, axis=0, keepdims=True)


def spectrum(blocks, table):
    count = len(blocks)
    width = blocks[0].shape[1]
    sub = lax.broadcasted_iota(jnp.int32, (SUB, width), 0)
    ends = jnp.zeros((SUB, width), jnp.float32)
    for p, rows in enumerate(blocks):
        ends = jnp.where(sub == p, rows[0:1], ends)
        ends = jnp.where(sub == GROUP + p, rows[HALF : HALF + 1], ends)
    mean = jnp.sum(ends, axis=1, keepdims=True) * (1.0 / width)
    ends = ends - jnp.where(sub < GROUP, mean, 0.0)
    ends = jnp.concatenate([ends, jnp.zeros_like(ends)], axis=0)
    ends = jnp.concatenate([ends, jnp.zeros_like(ends)], axis=1).astype(jnp.bfloat16)
    freq = mm(jnp.concatenate([to_lhs(rows) for rows in blocks] + [ends], axis=0), table)
    power = jnp.zeros((SUB, width), jnp.float32)
    for p in range(count):
        row = energy(freq[p * HALF : (p + 1) * HALF])
        power = jnp.where((sub == p) | (sub == GROUP + p), row, power)
    tail = freq[count * HALF : count * HALF + SUB]
    tail = tail * tail
    tail = tail[:, :width] + tail[:, width:]
    power = 2.0 * power + tail + pltpu.roll(tail, GROUP, 0)
    return freq, jnp.sum(power, axis=1, keepdims=True)


def store_scaled(ref, freq, count, factors):
    at = count * HALF
    for p in range(count):
        block = slice(p * HALF, (p + 1) * HALF)
        ref[block, :] = freq[block] * factors[p : p + 1]
    ref[at : at + SUB, :] = freq[at : at + SUB] * factors
    ref[at + SUB :, :] = jnp.zeros((SUB, freq.shape[1]), jnp.float32)


def correlate(own, other, count, table):
    width = own.shape[1] // 2
    a_re, a_im = own[:, :width], own[:, width:]
    b_re, b_im = other[:, :width], other[:, width:]
    product = jnp.concatenate([a_re * b_re + a_im * b_im, a_im * b_re - a_re * b_im], axis=1)
    rows = mm(product.astype(jnp.bfloat16), table)
    sub = lax.broadcasted_iota(jnp.int32, (SUB, width), 0)
    at = count * HALF
    blocks = []
    for p in range(count):
        block = rows[p * HALF : (p + 1) * HALF]
        first = rows[at + p : at + p + 1, :width]
        middle = rows[at + GROUP + p : at + GROUP + p + 1, :width]
        parts = [
            jnp.where(sub == 0, first, block[:SUB, :width]),
            block[SUB:, :width],
            jnp.where(sub == 0, middle, block[:SUB, width:]),
            block[SUB:, width:],
        ]
        blocks.append(jnp.concatenate(parts, axis=0).astype(jnp.bfloat16))
    return blocks


def window_at(ref, place, height):
    row_at, col_at = place
    block = lax.shift_right_logical(col_at, 7)
    shift = col_at & (LANES - 1)
    left = ref[block, pl.ds(row_at, height), :]
    right = ref[block + 1, pl.ds(row_at, height), :]
    lane = lax.broadcasted_iota(jnp.int32, (height, LANES), 1)
    return pltpu.roll(jnp.where(lane >= shift, left, right), (LANES - shift) & (LANES - 1), 1)


def group_places(group, offsets, peaks):
    off_row = HALO + DS * offsets[0, 0, 0]
    off_col = LANES + DS * offsets[0, 0, 1]
    return [
        (
            off_row + i * P_SIZE + peaks[0, i, 0, column],
            off_col + column * P_SIZE + peaks[0, i, 1, column],
        )
        for i, column in group
    ]


def group_windows(ext, places):
    cut = [window_at(ext, place, P_SIZE).astype(jnp.bfloat16) for place in places]
    return [jnp.concatenate(cut[n : n + 2], axis=1) for n in range(0, len(cut), 2)]


def group_flags(group, keep):
    sub = lax.broadcasted_iota(jnp.int32, (SUB, 1), 0)
    flags = jnp.zeros((SUB, 1), jnp.float32)
    for p, (i, column) in enumerate(group):
        flags = jnp.where(sub == p, keep[0, i, column].astype(jnp.float32), flags)
    return flags


def halves(rows):
    return [rows[:, :P_SIZE], rows[:, P_SIZE:]]


def window_spectrum(windows, flags, gain, row_tab, col_tab):
    blocks = sum((halves(mm(row_tab[:P_SIZE, :], window)) for window in windows), [])
    freq, power = spectrum(blocks, col_tab[...])
    scale = (P_SIZE * P_SIZE / gain) ** 2 / P_SIZE
    return freq, flags * (scale / jnp.sqrt(power * (1.0 / gain**2) + EPSILON))


def write_maps(own, freq, factors, col_tab, inv_tab, write):
    rows = correlate(own, freq, GROUP, col_tab[...])
    for n in range(0, GROUP, 2):
        maps = mm(inv_tab[...], jnp.concatenate(rows[n : n + 2], axis=1))
        for h, value in enumerate(halves(maps)):
            write(n + h, value * factors[n + h : n + h + 1])


def split(x):
    hi = x.astype(jnp.bfloat16)
    return hi, (x - hi.astype(jnp.float32)).astype(jnp.bfloat16)


def pooled(hi, lo, pool):
    span = pool.shape[0]
    parts = []
    for at in range(0, hi.shape[1], span):
        sums = mm(hi[:, at : at + span], pool) + mm(lo[:, at : at + span], pool)
        parts.append((sums * (1.0 / (DS * DS))).astype(jnp.bfloat16))
    return parts


def exchange_kernel(
    bands,
    units,
    gains,
    offsets_hbm,
    peaks_hbm,
    keep_hbm,
    img,
    row_hbm,
    col_hbm,
    inv_hbm,
    wide_hbm,
    pool_hbm,
    maps,
    coarse,
    windows,
    last_spec,
    last_flags,
    row_tab,
    col_tab,
    inv_tab,
    own,
    land,
    ext,
    spec,
    small_own,
    small_land,
    small,
    small_spec,
    own_hi,
    own_lo,
    sum_hi,
    sum_lo,
    end_hi,
    end_lo,
    wide_tab,
    pool,
    offsets,
    peaks,
    keep,
    relayed,
    send_sems,
    recv_sems,
    side_send,
    side_recv,
    relay_sems,
    local_sems,
):
    s = lax.axis_index("sec")
    t = lax.axis_index("tile")
    ns = lax.axis_size("sec")
    nt = lax.axis_size("tile")
    rows, width = own.shape
    columns = width // LANES
    centre = rows - 2 * HALO
    reach = rows + 2 * HALO
    row_gain, col_gain, wide_gain = gains
    flow_gain = row_gain * col_gain
    half = columns // 2
    early = half + 1
    detours = (half, half + 1)
    last = columns - 1
    top = P_SIZE + HALO
    bottom = rows - top
    spans = ((HALO, top - HALO), (bottom, rows - HALO - bottom), (top, bottom - top))

    sends = s < ns - 1
    receives = s > 0
    has_up = t > 0
    has_down = t < nt - 1
    s_next = jnp.minimum(s + 1, ns - 1)
    s_prev = jnp.maximum(s - 1, 0)
    t_next = jnp.minimum(t + 1, nt - 1)
    t_prev = jnp.maximum(t - 1, 0)
    eighth = lax.rem(s, 8)
    starts_relay = (eighth == 3) & (s + 4 < ns)
    relays = eighth == 7
    ends_relay = (eighth == 4) & (s + 3 < ns)
    relay_from = jnp.maximum(s - 4, 0)
    relay_by = jnp.minimum(s + 4, ns - 1)
    relay_to = jnp.maximum(s - 3, 0)
    relayed_by = jnp.minimum(s + 3, ns - 1)

    barrier = pltpu.get_barrier_semaphore()
    for cond, peer in (
        (receives, (s_prev, t)),
        (ends_relay, (relayed_by, t)),
        (relays, (relay_from, t)),
        (has_up, (s, t_prev)),
        (has_down, (s, t_next)),
    ):

        @pl.when(cond)
        def _(peer=peer):
            pl.semaphore_signal(barrier, inc=1, device_id=peer, device_id_type=MESH)

    loads = [
        pltpu.make_async_copy(source, target, local_sems.at[n])
        for n, (source, target) in enumerate(
            (
                (img, own),
                (row_hbm, row_tab),
                (col_hbm, col_tab),
                (inv_hbm, inv_tab),
                (wide_hbm, wide_tab),
                (pool_hbm, pool),
                (offsets_hbm, offsets),
                (peaks_hbm, peaks),
                (keep_hbm, keep),
            )
        )
    ]
    for load in loads:
        load.start()
    loads[0].wait()
    peers = sum(jnp.where(cond, 1, 0) for cond in (sends, starts_relay, relays, has_up, has_down))
    pl.semaphore_wait(barrier, peers)

    def edge_copy(n):
        start = n * (rows - HALO)
        return pltpu.make_async_remote_copy(
            src_ref=own.at[pl.ds(start, HALO)],
            dst_ref=land.at[pl.ds(HALO + start, HALO)],
            send_sem=send_sems.at[n],
            recv_sem=recv_sems.at[n],
            device_id=(s_next, t),
            device_id_type=MESH,
        )

    def column_copy(c, n=None):
        at = pl.multiple_of(c * LANES, LANES)
        start, size = (HALO, centre) if n is None else spans[n]
        sem = 3 + c if n is None else 3 + last + n
        return pltpu.make_async_remote_copy(
            src_ref=own.at[pl.ds(start, size), pl.ds(at, LANES)],
            dst_ref=land.at[pl.ds(HALO + start, size), pl.ds(at, LANES)],
            send_sem=send_sems.at[sem],
            recv_sem=recv_sems.at[sem],
            device_id=(s_next, t),
            device_id_type=MESH,
        )

    def relay_in(n):
        return pltpu.make_async_remote_copy(
            src_ref=own.at[pl.ds(HALO, centre), pl.ds(detours[n] * LANES, LANES)],
            dst_ref=relayed.at[n],
            send_sem=send_sems.at[3 + detours[n]],
            recv_sem=relay_sems.at[n],
            device_id=(relay_by, t),
            device_id_type=MESH,
        )

    def relay_out(n):
        return pltpu.make_async_remote_copy(
            src_ref=relayed.at[n],
            dst_ref=land.at[pl.ds(2 * HALO, centre), pl.ds(detours[n] * LANES, LANES)],
            send_sem=relay_sems.at[2 + n],
            recv_sem=recv_sems.at[3 + detours[n]],
            device_id=(relay_to, t),
            device_id_type=MESH,
        )

    def small_copy():
        return pltpu.make_async_remote_copy(
            src_ref=small_own.at[pl.ds(COARSE, small_land.shape[0]), pl.ds(LANES, LANES)],
            dst_ref=small_land,
            send_sem=send_sems.at[2],
            recv_sem=recv_sems.at[2],
            device_id=(s_next, t),
            device_id_type=MESH,
        )

    def side_copy(n):
        source, target, peer = ((HALO, HALO + rows, t_prev), (rows, 0, t_next))[n]
        return pltpu.make_async_remote_copy(
            src_ref=land.at[pl.ds(source, HALO)],
            dst_ref=land.at[pl.ds(target, HALO)],
            send_sem=side_send.at[n],
            recv_sem=side_recv.at[n],
            device_id=(s, peer),
            device_id_type=MESH,
        )

    @pl.when(sends)
    def _():
        edge_copy(0).start()
        edge_copy(1).start()
        for c in range(early):
            if c not in detours:
                column_copy(c).start()

    @pl.when(starts_relay)
    def _():
        for n in range(len(detours)):
            relay_in(n).start()

    @pl.when(sends & jnp.logical_not(starts_relay))
    def _():
        for c in range(early):
            if c in detours:
                column_copy(c).start()

    @pl.when(jnp.logical_not(receives))
    def _():
        land[...] = jnp.zeros_like(land)
        small_land[...] = jnp.zeros_like(small_land)

    @pl.when(receives & jnp.logical_not(has_up))
    def _():
        land[:HALO, :] = jnp.zeros((HALO, width), jnp.bfloat16)

    @pl.when(receives & jnp.logical_not(has_down))
    def _():
        land[HALO + rows :, :] = jnp.zeros((HALO, width), jnp.bfloat16)

    ext[0] = jnp.zeros((reach, LANES), jnp.float32)
    ext[columns + 1] = jnp.zeros((reach, LANES), jnp.float32)
    small[0] = jnp.zeros(small.shape[1:], jnp.float32)
    small[3] = jnp.zeros(small.shape[1:], jnp.float32)
    for load in loads[1:]:
        load.wait()

    def own_unit(u, carry):
        at = pl.multiple_of(u * PAIR, PAIR)
        blocks = [[], []]
        for i in range(bands):
            both = mm(row_tab[...], own[i * P_SIZE : (i + 1) * P_SIZE, pl.ds(at, PAIR)])
            for h, block in enumerate(halves(both[:P_SIZE])):
                blocks[h].append(block)
            hi, lo = split(both[P_SIZE:])
            own_hi[i * POOLED : (i + 1) * POOLED, pl.ds(at, PAIR)] = hi
            own_lo[i * POOLED : (i + 1) * POOLED, pl.ds(at, PAIR)] = lo
        for h in range(2):
            freq, power = spectrum(blocks[h], col_tab[...])
            factors = (1.0 / flow_gain) / jnp.sqrt(power * (1.0 / flow_gain**2) + EPSILON)
            store_scaled(spec.at[2 * u + h], freq, GROUP, factors)
        return carry

    lax.fori_loop(0, units, own_unit, 0)
    for n, part in enumerate(pooled(own_hi[...], own_lo[...], pool[...])):
        small_own[:, n * LANES : (n + 1) * LANES] = part

    @pl.when(sends)
    def _():
        small_copy().start()

    @pl.when(sends & jnp.logical_not(starts_relay))
    def _():
        for c in range(early, last):
            if c in detours:
                column_copy(c).start()

    @pl.when(sends)
    def _():
        for c in range(early, last):
            if c not in detours:
                column_copy(c).start()
        for n in range(len(spans)):
            column_copy(last, n).start()

    @pl.when(relays)
    def _():
        for n in range(len(detours)):
            relay_in(n).wait_recv()
            relay_out(n).start()

    @pl.when(receives)
    def _():
        edge_copy(0).wait_recv()

        @pl.when(has_up)
        def _():
            side_copy(0).start()

        edge_copy(1).wait_recv()

        @pl.when(has_down)
        def _():
            side_copy(1).start()

    last_group = [[(i, c) for i in range(bands)] for c in range(columns - 2, columns)]
    for h, group in enumerate(last_group):
        last_spec[h] = spec[columns - 2 + h]
        last_flags[h] = jnp.broadcast_to(group_flags(group, keep), (SUB, LANES))
    freq, power = spectrum([mm(row_tab[:P_SIZE, :], small_own[...])], wide_tab[...])
    gain = row_gain * wide_gain
    factors = (1.0 / gain) / jnp.sqrt(power * (1.0 / gain**2) + EPSILON)
    store_scaled(small_spec, freq, 1, factors)

    @pl.when(receives)
    def _():
        @pl.when(has_up)
        def _():
            side_copy(1).wait_recv()

        @pl.when(has_down)
        def _():
            side_copy(0).wait_recv()

    first = HALO - DS * COARSE
    count = small.shape[1]
    side = 2 * COARSE

    def row_sums(c, at, size):
        sums = ext[c + 1, pl.ds(at, size, stride=DS), :]
        for k in range(1, DS):
            sums = sums + ext[c + 1, pl.ds(at + k, size, stride=DS), :]
        return split(sums)

    def edge_step(c, carry):
        at = pl.multiple_of(c * LANES, LANES)
        for n, row in enumerate((0, rows)):
            block = land[row : row + 2 * HALO, pl.ds(at, LANES)]
            ext[c + 1, row : row + 2 * HALO, :] = block.astype(jnp.float32)
            hi, lo = row_sums(c, first + n * DS * (count - side), side)
            end_hi[n * side : (n + 1) * side, pl.ds(at, LANES)] = hi
            end_lo[n * side : (n + 1) * side, pl.ds(at, LANES)] = lo
        return carry

    lax.fori_loop(0, columns, edge_step, 0)

    def arrive(c, n=None):
        @pl.when(receives)
        def _():
            column_copy(c, n).wait_recv()

        at = pl.multiple_of(c * LANES, LANES)
        start, size = (HALO, centre) if n is None else spans[n]
        block = land[HALO + start : HALO + start + size, pl.ds(at, LANES)]
        ext[c + 1, HALO + start : HALO + start + size, :] = block.astype(jnp.float32)

    def coarse_map():
        @pl.when(receives)
        def _():
            small_copy().wait_recv()

        def sum_step(c, carry):
            at = pl.multiple_of(c * LANES, LANES)
            hi, lo = row_sums(c, first, count)
            sum_hi[:, pl.ds(at, LANES)] = hi
            sum_lo[:, pl.ds(at, LANES)] = lo
            return carry

        lax.fori_loop(0, half, sum_step, 0)
        span = half * LANES
        small[1] = pooled(sum_hi[...], sum_lo[...], pool[...])[0].astype(jnp.float32)
        ends = pooled(end_hi[:, span:], end_lo[:, span:], pool[...])[0].astype(jnp.float32)
        small[2, :side] = ends[:side]
        small[2, side : count - side] = small_land[...].astype(jnp.float32)
        small[2, count - side :] = ends[side:]
        height = count - 2 * COARSE
        row_at, col_at = COARSE + offsets[0, 0, 0], LANES + offsets[0, 0, 1]
        window = [
            window_at(small, (row_at, col_at + n * LANES), height).astype(jnp.bfloat16)
            for n in range(2)
        ]
        freq, power = spectrum(
            [mm(row_tab[:P_SIZE, :], jnp.concatenate(window, axis=1))], wide_tab[...]
        )
        gain = row_gain * wide_gain
        size = height * 2 * LANES
        scale = (size / gain) ** 2 / math.sqrt(size)
        factors = scale / jnp.sqrt(power * (1.0 / gain**2) + EPSILON)
        found = correlate(small_spec[...], freq, 1, wide_tab[...])[0]
        coarse[...] = mm(inv_tab[...], found) * factors[0:1]

    def match_step(k, carry):
        arrive(2 * k)

        @pl.when(k < half - 1)
        def _():
            arrive(2 * k + 1)

        @pl.when(k == half // 2)
        def _():
            coarse_map()

        cols = (jnp.maximum(2 * k - 1, 0), jnp.minimum(2 * k, columns - 3))
        found = []
        for c in cols:
            group = [(i, c) for i in range(bands)]
            found.append(
                window_spectrum(
                    group_windows(ext, group_places(group, offsets, peaks)),
                    group_flags(group, keep),
                    flow_gain,
                    row_tab,
                    col_tab,
                )
            )
        for c, (freq, factors) in zip(cols, found):

            def write(p, value, c=c):
                at = pl.multiple_of(c * P_SIZE, P_SIZE)
                maps[p * P_SIZE : (p + 1) * P_SIZE, pl.ds(at, P_SIZE)] = value

            write_maps(spec[c], freq, factors, col_tab, inv_tab, write)
        return carry

    lax.fori_loop(0, half, match_step, 0)

    @pl.when(receives & has_up)
    def _():
        side_copy(0).wait_send()

    @pl.when(receives & has_down)
    def _():
        side_copy(1).wait_send()

    @pl.when(relays)
    def _():
        for n in range(len(detours)):
            relay_out(n).wait_send()

    @pl.when(sends)
    def _():
        edge_copy(0).wait_send()
        edge_copy(1).wait_send()
        small_copy().wait_send()
        for c in range(last):
            column_copy(c).wait_send()
        for n in range(len(spans)):
            column_copy(last, n).wait_send()

    def cut(bands_here):
        for i in bands_here:
            lanes = slice(i % 2 * P_SIZE, (i % 2 + 1) * P_SIZE)
            for h, group in enumerate(last_group):
                window = window_at(ext, places[h][i], P_SIZE).astype(jnp.bfloat16)
                windows[h, i // 2, :, lanes] = window

    places = [group_places(group, offsets, peaks) for group in last_group]
    arrive(last, 0)
    arrive(last, 1)
    cut((0, bands - 1))
    arrive(last, 2)
    cut(range(1, bands - 1))


def finish_kernel(
    gain,
    maps,
    coarse,
    windows,
    last_spec,
    last_flags,
    row_tab,
    col_tab,
    inv_tab,
    coarse_out,
    flow_out,
    last_maps,
    sems,
):
    rows, done = maps.shape
    pair = windows.shape[0]
    count = sems.shape[0] - pair - 1
    size = rows // count
    copies = [pltpu.make_async_copy(coarse, coarse_out.at[0], sems.at[count])]
    for n in range(count):
        band = pl.ds(n * size, size)
        copies.append(pltpu.make_async_copy(maps.at[band], flow_out.at[0, band, pl.ds(0, done)], sems.at[n]))
    for copy in copies:
        copy.start()
    found = [
        window_spectrum(
            [windows[h, n] for n in range(windows.shape[1])],
            last_flags[h, :, :1],
            gain,
            row_tab,
            col_tab,
        )
        for h in range(pair)
    ]
    for h, (freq, factors) in enumerate(found):

        def write(p, value, h=h):
            last_maps[h, p * P_SIZE : (p + 1) * P_SIZE, :] = value

        write_maps(last_spec[h], freq, factors, col_tab, inv_tab, write)
        column = flow_out.at[0, :, pl.ds(done + h * P_SIZE, P_SIZE)]
        copies.append(pltpu.make_async_copy(last_maps.at[h], column, sems.at[count + 1 + h]))
        copies[-1].start()
    for copy in copies:
        copy.wait()


def shards(section_image, offsets, peak_shift, accepted):
    own = section_image[0]
    rows, width = own.shape
    bands = rows // P_SIZE
    units = width // PAIR
    columns = width // LANES
    reach = rows + 2 * HALO
    small_width = width // DS
    forward_row, inverse_row, row_gain = row_tables()
    col, col_gain = col_table(P_SIZE)
    wide, wide_gain = col_table(small_width)
    gains = (float(row_gain), float(col_gain), float(wide_gain))
    span = DS * LANES
    pool = quantized(np.arange(span)[:, None] // DS == np.arange(LANES)[None, :])
    tables = [jnp.asarray(x) for x in (forward_row, col, inverse_row, wide, pool)]
    scalars = (offsets, jnp.swapaxes(peak_shift, 2, 3), accepted)
    high = GROUP * HALF + 2 * SUB
    small_high = HALF + 2 * SUB
    small_rows = rows // DS + 2 * COARSE
    hbm = pl.BlockSpec(memory_space=pltpu.HBM)
    vmem = pl.BlockSpec(memory_space=pltpu.VMEM)
    limit = 30 * 2**20
    operands = [pltpu.with_memory_space_constraint(x, pltpu.HBM) for x in (*scalars, own, *tables)]
    between = pl.pallas_call(
        functools.partial(exchange_kernel, bands, units, gains),
        name="exchange",
        out_shape=(
            jax.ShapeDtypeStruct((rows, width - PAIR), jnp.float32),
            jax.ShapeDtypeStruct((rows // DS, small_width), jnp.float32),
            jax.ShapeDtypeStruct((2, bands // 2, P_SIZE, PAIR), jnp.bfloat16),
            jax.ShapeDtypeStruct((2, high, PAIR), jnp.float32),
            jax.ShapeDtypeStruct((2, SUB, LANES), jnp.float32),
        )
        + tuple(jax.ShapeDtypeStruct(x.shape, x.dtype) for x in tables[:3]),
        in_specs=[hbm] * 9,
        out_specs=(vmem,) * 8,
        scratch_shapes=[
            pltpu.VMEM((rows, width), jnp.bfloat16),
            pltpu.VMEM((reach, width), jnp.bfloat16),
            pltpu.VMEM((columns + 2, reach, LANES), jnp.float32),
            pltpu.VMEM((columns, high, PAIR), jnp.float32),
            pltpu.VMEM((rows // DS, small_width), jnp.bfloat16),
            pltpu.VMEM((rows // DS - 2 * COARSE, LANES), jnp.bfloat16),
            pltpu.VMEM((small_width // LANES + 2, small_rows, LANES), jnp.float32),
            pltpu.VMEM((small_high, 2 * small_width), jnp.float32),
            pltpu.VMEM((rows // DS, width), jnp.bfloat16),
            pltpu.VMEM((rows // DS, width), jnp.bfloat16),
            pltpu.VMEM((small_rows, span), jnp.bfloat16),
            pltpu.VMEM((small_rows, span), jnp.bfloat16),
            pltpu.VMEM((4 * COARSE, width), jnp.bfloat16),
            pltpu.VMEM((4 * COARSE, width), jnp.bfloat16),
        ]
        + [pltpu.VMEM(x.shape, jnp.bfloat16) for x in tables[3:]]
        + [pltpu.SMEM(x.shape, jnp.int32) for x in scalars]
        + [
            pltpu.VMEM((2, rows - 2 * HALO, LANES), jnp.bfloat16),
            pltpu.SemaphoreType.DMA((columns + 5,)),
            pltpu.SemaphoreType.DMA((columns + 5,)),
            pltpu.SemaphoreType.DMA((2,)),
            pltpu.SemaphoreType.DMA((2,)),
            pltpu.SemaphoreType.DMA((4,)),
            pltpu.SemaphoreType.DMA((len(operands),)),
        ],
        compiler_params=pltpu.CompilerParams(
            collective_id=0, has_side_effects=True, vmem_limit_bytes=limit
        ),
    )(*operands)
    return pl.pallas_call(
        functools.partial(finish_kernel, gains[0] * gains[1]),
        name="finish",
        out_shape=(
            jax.ShapeDtypeStruct((1, rows // DS, small_width), jnp.float32),
            jax.ShapeDtypeStruct((1, rows, width), jnp.float32),
        ),
        in_specs=[vmem] * 8,
        out_specs=(hbm, hbm),
        scratch_shapes=[
            pltpu.VMEM((2, rows, P_SIZE), jnp.float32),
            pltpu.SemaphoreType.DMA((bands + 3,)),
        ],
        compiler_params=pltpu.CompilerParams(vmem_limit_bytes=limit),
    )(*between)


def solution(mesh):
    return jax.shard_map(
        shards,
        mesh=mesh,
        in_specs=(
            P("sec", "tile", None),
            P("sec", "tile", None),
            P("sec", "tile", None, None),
            P("sec", "tile", None),
        ),
        out_specs=(P("sec", "tile", None), P("sec", "tile", None)),
        check_vma=False,
    )
```

```python
import functools
import math

import jax
import jax.numpy as jnp
import ml_dtypes
import numpy as np
from jax import lax
from jax.experimental import pallas as pl
from jax.experimental.pallas import tpu as pltpu
from jax.sharding import PartitionSpec as P

P_SIZE = 128
HALF = P_SIZE // 2
DS = 4
COARSE = 16
HALO = 80
LANES = 128
PAIR = 2 * P_SIZE
SUB = 8
GROUP = 4
POOLED = P_SIZE // DS
EPSILON = 1e-05
MESH = pl.DeviceIdType.MESH


def quantized(table):
    return table.astype(np.float32).astype(ml_dtypes.bfloat16)


def table_scale(n):
    cosines = np.cos(2.0 * np.pi * np.arange(n) / n)
    best = None
    for factor in np.linspace(1.0, 2.0, 4001):
        table = quantized(cosines * factor).astype(np.float64)
        gain = (table @ cosines) / (cosines @ cosines)
        error = np.mean((table / gain - cosines) ** 2)
        if best is None or error < best[0]:
            best = (error, factor, gain)
    return best[1], best[2]


def waves(n):
    k = np.arange(n)
    angles = (k[:, None] * k[None, :] % n) * (2.0 * np.pi / n)
    return np.cos(angles), np.sin(angles)


def row_tables():
    n = P_SIZE
    factor, gain = table_scale(n)
    cosines, sines = waves(n)
    alternating = np.where(np.arange(n) % 2 == 0, 1.0, -1.0)
    forward = np.concatenate([cosines[:HALF], sines[:HALF]])
    forward[HALF] = alternating
    weight = np.where(np.arange(HALF) == 0, 1.0, 2.0)[:, None]
    inverse = np.concatenate([cosines[:HALF] * weight, -sines[:HALF] * weight])
    inverse[HALF] = alternating
    pool = (np.arange(POOLED)[:, None] == np.arange(n)[None, :] // DS).astype(np.float64)
    forward = np.concatenate([forward * (factor / n), pool])
    return quantized(forward), quantized(inverse.T * (factor / n)), gain


def col_table(n):
    factor, gain = table_scale(n)
    cosines, sines = waves(n)
    table = np.block([[cosines, sines], [-sines, cosines]]) * (factor / n)
    return quantized(table), gain


def mm(a, b):
    return jnp.dot(a, b, preferred_element_type=jnp.float32)


def to_lhs(rows):
    return jnp.concatenate([rows[:HALF], rows[HALF:]], axis=1).astype(jnp.bfloat16)


def energy(block):
    width = block.shape[1] // 2
    total = block[:, :width] * block[:, :width] + block[:, width:] * block[:, width:]
    head = jnp.where(lax.broadcasted_iota(jnp.int32, (SUB, width), 0) == 0, 0.0, total[:SUB])
    for at in range(SUB, HALF, SUB):
        head = head + total[at : at + SUB]
    return jnp.sum(head, axis=0, keepdims=True)


def spectrum(blocks, table):
    count = len(blocks)
    width = blocks[0].shape[1]
    sub = lax.broadcasted_iota(jnp.int32, (SUB, width), 0)
    ends = jnp.zeros((SUB, width), jnp.float32)
    for p, rows in enumerate(blocks):
        ends = jnp.where(sub == p, rows[0:1], ends)
        ends = jnp.where(sub == GROUP + p, rows[HALF : HALF + 1], ends)
    mean = jnp.sum(ends, axis=1, keepdims=True) * (1.0 / width)
    ends = ends - jnp.where(sub < GROUP, mean, 0.0)
    ends = jnp.concatenate([ends, jnp.zeros_like(ends)], axis=0)
    ends = jnp.concatenate([ends, jnp.zeros_like(ends)], axis=1).astype(jnp.bfloat16)
    freq = mm(jnp.concatenate([to_lhs(rows) for rows in blocks] + [ends], axis=0), table)
    power = jnp.zeros((SUB, width), jnp.float32)
    for p in range(count):
        row = energy(freq[p * HALF : (p + 1) * HALF])
        power = jnp.where((sub == p) | (sub == GROUP + p), row, power)
    tail = freq[count * HALF : count * HALF + SUB]
    tail = tail * tail
    tail = tail[:, :width] + tail[:, width:]
    power = 2.0 * power + tail + pltpu.roll(tail, GROUP, 0)
    return freq, jnp.sum(power, axis=1, keepdims=True)


def store_scaled(ref, freq, count, factors):
    at = count * HALF
    for p in range(count):
        block = slice(p * HALF, (p + 1) * HALF)
        ref[block, :] = freq[block] * factors[p : p + 1]
    ref[at : at + SUB, :] = freq[at : at + SUB] * factors
    ref[at + SUB :, :] = jnp.zeros((SUB, freq.shape[1]), jnp.float32)


def correlate(own, other, count, table):
    width = own.shape[1] // 2
    a_re, a_im = own[:, :width], own[:, width:]
    b_re, b_im = other[:, :width], other[:, width:]
    product = jnp.concatenate([a_re * b_re + a_im * b_im, a_im * b_re - a_re * b_im], axis=1)
    rows = mm(product.astype(jnp.bfloat16), table)
    sub = lax.broadcasted_iota(jnp.int32, (SUB, width), 0)
    at = count * HALF
    blocks = []
    for p in range(count):
        block = rows[p * HALF : (p + 1) * HALF]
        first = rows[at + p : at + p + 1, :width]
        middle = rows[at + GROUP + p : at + GROUP + p + 1, :width]
        parts = [
            jnp.where(sub == 0, first, block[:SUB, :width]),
            block[SUB:, :width],
            jnp.where(sub == 0, middle, block[:SUB, width:]),
            block[SUB:, width:],
        ]
        blocks.append(jnp.concatenate(parts, axis=0).astype(jnp.bfloat16))
    return blocks


def window_at(ref, place, height):
    row_at, col_at = place
    block = lax.shift_right_logical(col_at, 7)
    shift = col_at & (LANES - 1)
    left = ref[block, pl.ds(row_at, height), :]
    right = ref[block + 1, pl.ds(row_at, height), :]
    lane = lax.broadcasted_iota(jnp.int32, (height, LANES), 1)
    return pltpu.roll(jnp.where(lane >= shift, left, right), (LANES - shift) & (LANES - 1), 1)


def group_places(group, offsets, peaks):
    off_row = HALO + DS * offsets[0, 0, 0]
    off_col = LANES + DS * offsets[0, 0, 1]
    return [
        (
            off_row + i * P_SIZE + peaks[0, i, 0, column],
            off_col + column * P_SIZE + peaks[0, i, 1, column],
        )
        for i, column in group
    ]


def group_windows(ext, places):
    cut = [window_at(ext, place, P_SIZE).astype(jnp.bfloat16) for place in places]
    return [jnp.concatenate(cut[n : n + 2], axis=1) for n in range(0, len(cut), 2)]


def group_flags(group, keep):
    sub = lax.broadcasted_iota(jnp.int32, (SUB, 1), 0)
    flags = jnp.zeros((SUB, 1), jnp.float32)
    for p, (i, column) in enumerate(group):
        flags = jnp.where(sub == p, keep[0, i, column].astype(jnp.float32), flags)
    return flags


def halves(rows):
    return [rows[:, :P_SIZE], rows[:, P_SIZE:]]


def window_spectrum(windows, flags, gain, row_tab, col_tab):
    blocks = sum((halves(mm(row_tab[:P_SIZE, :], window)) for window in windows), [])
    freq, power = spectrum(blocks, col_tab[...])
    scale = (P_SIZE * P_SIZE / gain) ** 2 / P_SIZE
    return freq, flags * (scale / jnp.sqrt(power * (1.0 / gain**2) + EPSILON))


def write_maps(own, freq, factors, col_tab, inv_tab, write):
    rows = correlate(own, freq, GROUP, col_tab[...])
    for n in range(0, GROUP, 2):
        maps = mm(inv_tab[...], jnp.concatenate(rows[n : n + 2], axis=1))
        for h, value in enumerate(halves(maps)):
            write(n + h, value * factors[n + h : n + h + 1])


def split(x):
    hi = x.astype(jnp.bfloat16)
    return hi, (x - hi.astype(jnp.float32)).astype(jnp.bfloat16)


def pooled(hi, lo, pool):
    span = pool.shape[0]
    parts = []
    for at in range(0, hi.shape[1], span):
        sums = mm(hi[:, at : at + span], pool) + mm(lo[:, at : at + span], pool)
        parts.append((sums * (1.0 / (DS * DS))).astype(jnp.bfloat16))
    return parts


def exchange_kernel(
    bands,
    units,
    gains,
    offsets_hbm,
    peaks_hbm,
    keep_hbm,
    img,
    row_hbm,
    col_hbm,
    inv_hbm,
    wide_hbm,
    pool_hbm,
    maps,
    coarse,
    windows,
    last_spec,
    last_flags,
    row_tab,
    col_tab,
    inv_tab,
    own,
    land,
    ext,
    spec,
    small_own,
    small_land,
    small,
    small_spec,
    own_hi,
    own_lo,
    sum_hi,
    sum_lo,
    end_hi,
    end_lo,
    wide_tab,
    pool,
    offsets,
    peaks,
    keep,
    relayed,
    send_sems,
    recv_sems,
    side_send,
    side_recv,
    relay_sems,
    local_sems,
):
    s = lax.axis_index("sec")
    t = lax.axis_index("tile")
    ns = lax.axis_size("sec")
    nt = lax.axis_size("tile")
    rows, width = own.shape
    columns = width // LANES
    centre = rows - 2 * HALO
    reach = rows + 2 * HALO
    row_gain, col_gain, wide_gain = gains
    flow_gain = row_gain * col_gain
    half = columns // 2
    early = half + 1
    detours = (half, half + 1)
    last = columns - 1
    top = P_SIZE + HALO
    bottom = rows - top
    spans = ((HALO, top - HALO), (bottom, rows - HALO - bottom), (top, bottom - top))

    sends = s < ns - 1
    receives = s > 0
    has_up = t > 0
    has_down = t < nt - 1
    s_next = jnp.minimum(s + 1, ns - 1)
    s_prev = jnp.maximum(s - 1, 0)
    t_next = jnp.minimum(t + 1, nt - 1)
    t_prev = jnp.maximum(t - 1, 0)
    eighth = lax.rem(s, 8)
    starts_relay = (eighth == 3) & (s + 4 < ns)
    relays = eighth == 7
    ends_relay = (eighth == 4) & (s + 3 < ns)
    relay_from = jnp.maximum(s - 4, 0)
    relay_by = jnp.minimum(s + 4, ns - 1)
    relay_to = jnp.maximum(s - 3, 0)
    relayed_by = jnp.minimum(s + 3, ns - 1)

    barrier = pltpu.get_barrier_semaphore()
    for cond, peer in (
        (receives, (s_prev, t)),
        (ends_relay, (relayed_by, t)),
        (relays, (relay_from, t)),
        (has_up, (s, t_prev)),
        (has_down, (s, t_next)),
    ):

        @pl.when(cond)
        def _(peer=peer):
            pl.semaphore_signal(barrier, inc=1, device_id=peer, device_id_type=MESH)

    loads = [
        pltpu.make_async_copy(source, target, local_sems.at[n])
        for n, (source, target) in enumerate(
            (
                (img, own),
                (row_hbm, row_tab),
                (col_hbm, col_tab),
                (inv_hbm, inv_tab),
                (wide_hbm, wide_tab),
                (pool_hbm, pool),
                (offsets_hbm, offsets),
                (peaks_hbm, peaks),
                (keep_hbm, keep),
            )
        )
    ]
    for load in loads:
        load.start()
    loads[0].wait()
    peers = sum(jnp.where(cond, 1, 0) for cond in (sends, starts_relay, relays, has_up, has_down))
    pl.semaphore_wait(barrier, peers)

    def edge_copy(n):
        start = n * (rows - HALO)
        return pltpu.make_async_remote_copy(
            src_ref=own.at[pl.ds(start, HALO)],
            dst_ref=land.at[pl.ds(HALO + start, HALO)],
            send_sem=send_sems.at[n],
            recv_sem=recv_sems.at[n],
            device_id=(s_next, t),
            device_id_type=MESH,
        )

    def column_copy(c, n=None):
        at = pl.multiple_of(c * LANES, LANES)
        start, size = (HALO, centre) if n is None else spans[n]
        sem = 3 + c if n is None else 3 + last + n
        return pltpu.make_async_remote_copy(
            src_ref=own.at[pl.ds(start, size), pl.ds(at, LANES)],
            dst_ref=land.at[pl.ds(HALO + start, size), pl.ds(at, LANES)],
            send_sem=send_sems.at[sem],
            recv_sem=recv_sems.at[sem],
            device_id=(s_next, t),
            device_id_type=MESH,
        )

    def relay_in(n):
        return pltpu.make_async_remote_copy(
            src_ref=own.at[pl.ds(HALO, centre), pl.ds(detours[n] * LANES, LANES)],
            dst_ref=relayed.at[n],
            send_sem=send_sems.at[3 + detours[n]],
            recv_sem=relay_sems.at[n],
            device_id=(relay_by, t),
            device_id_type=MESH,
        )

    def relay_out(n):
        return pltpu.make_async_remote_copy(
            src_ref=relayed.at[n],
            dst_ref=land.at[pl.ds(2 * HALO, centre), pl.ds(detours[n] * LANES, LANES)],
            send_sem=relay_sems.at[2 + n],
            recv_sem=recv_sems.at[3 + detours[n]],
            device_id=(relay_to, t),
            device_id_type=MESH,
        )

    def small_copy():
        return pltpu.make_async_remote_copy(
            src_ref=small_own.at[pl.ds(COARSE, small_land.shape[0]), pl.ds(LANES, LANES)],
            dst_ref=small_land,
            send_sem=send_sems.at[2],
            recv_sem=recv_sems.at[2],
            device_id=(s_next, t),
            device_id_type=MESH,
        )

    def side_copy(n):
        source, target, peer = ((HALO, HALO + rows, t_prev), (rows, 0, t_next))[n]
        return pltpu.make_async_remote_copy(
            src_ref=land.at[pl.ds(source, HALO)],
            dst_ref=land.at[pl.ds(target, HALO)],
            send_sem=side_send.at[n],
            recv_sem=side_recv.at[n],
            device_id=(s, peer),
            device_id_type=MESH,
        )

    @pl.when(sends)
    def _():
        edge_copy(0).start()
        edge_copy(1).start()
        for c in range(early):
            if c not in detours:
                column_copy(c).start()

    @pl.when(starts_relay)
    def _():
        for n in range(len(detours)):
            relay_in(n).start()

    @pl.when(sends & jnp.logical_not(starts_relay))
    def _():
        for c in range(early):
            if c in detours:
                column_copy(c).start()

    @pl.when(jnp.logical_not(receives))
    def _():
        land[...] = jnp.zeros_like(land)
        small_land[...] = jnp.zeros_like(small_land)

    @pl.when(receives & jnp.logical_not(has_up))
    def _():
        land[:HALO, :] = jnp.zeros((HALO, width), jnp.bfloat16)

    @pl.when(receives & jnp.logical_not(has_down))
    def _():
        land[HALO + rows :, :] = jnp.zeros((HALO, width), jnp.bfloat16)

    ext[0] = jnp.zeros((reach, LANES), jnp.float32)
    ext[columns + 1] = jnp.zeros((reach, LANES), jnp.float32)
    small[0] = jnp.zeros(small.shape[1:], jnp.float32)
    small[3] = jnp.zeros(small.shape[1:], jnp.float32)
    for load in loads[1:]:
        load.wait()

    def own_unit(u, carry):
        at = pl.multiple_of(u * PAIR, PAIR)
        blocks = [[], []]
        for i in range(bands):
            both = mm(row_tab[...], own[i * P_SIZE : (i + 1) * P_SIZE, pl.ds(at, PAIR)])
            for h, block in enumerate(halves(both[:P_SIZE])):
                blocks[h].append(block)
            hi, lo = split(both[P_SIZE:])
            own_hi[i * POOLED : (i + 1) * POOLED, pl.ds(at, PAIR)] = hi
            own_lo[i * POOLED : (i + 1) * POOLED, pl.ds(at, PAIR)] = lo
        for h in range(2):
            freq, power = spectrum(blocks[h], col_tab[...])
            factors = (1.0 / flow_gain) / jnp.sqrt(power * (1.0 / flow_gain**2) + EPSILON)
            store_scaled(spec.at[2 * u + h], freq, GROUP, factors)
        return carry

    lax.fori_loop(0, units, own_unit, 0)
    for n, part in enumerate(pooled(own_hi[...], own_lo[...], pool[...])):
        small_own[:, n * LANES : (n + 1) * LANES] = part

    @pl.when(sends)
    def _():
        small_copy().start()

    @pl.when(sends & jnp.logical_not(starts_relay))
    def _():
        for c in range(early, last):
            if c in detours:
                column_copy(c).start()

    @pl.when(sends)
    def _():
        for c in range(early, last):
            if c not in detours:
                column_copy(c).start()
        for n in range(len(spans)):
            column_copy(last, n).start()

    @pl.when(relays)
    def _():
        for n in range(len(detours)):
            relay_in(n).wait_recv()
            relay_out(n).start()

    @pl.when(receives)
    def _():
        edge_copy(0).wait_recv()

        @pl.when(has_up)
        def _():
            side_copy(0).start()

        edge_copy(1).wait_recv()

        @pl.when(has_down)
        def _():
            side_copy(1).start()

    last_group = [[(i, c) for i in range(bands)] for c in range(columns - 2, columns)]
    for h, group in enumerate(last_group):
        last_spec[h] = spec[columns - 2 + h]
        last_flags[h] = jnp.broadcast_to(group_flags(group, keep), (SUB, LANES))
    freq, power = spectrum([mm(row_tab[:P_SIZE, :], small_own[...])], wide_tab[...])
    gain = row_gain * wide_gain
    factors = (1.0 / gain) / jnp.sqrt(power * (1.0 / gain**2) + EPSILON)
    store_scaled(small_spec, freq, 1, factors)

    @pl.when(receives)
    def _():
        @pl.when(has_up)
        def _():
            side_copy(1).wait_recv()

        @pl.when(has_down)
        def _():
            side_copy(0).wait_recv()

    first = HALO - DS * COARSE
    count = small.shape[1]
    side = 2 * COARSE

    def row_sums(c, at, size):
        sums = ext[c + 1, pl.ds(at, size, stride=DS), :]
        for k in range(1, DS):
            sums = sums + ext[c + 1, pl.ds(at + k, size, stride=DS), :]
        return split(sums)

    def edge_step(c, carry):
        at = pl.multiple_of(c * LANES, LANES)
        for n, row in enumerate((0, rows)):
            block = land[row : row + 2 * HALO, pl.ds(at, LANES)]
            ext[c + 1, row : row + 2 * HALO, :] = block.astype(jnp.float32)
            hi, lo = row_sums(c, first + n * DS * (count - side), side)
            end_hi[n * side : (n + 1) * side, pl.ds(at, LANES)] = hi
            end_lo[n * side : (n + 1) * side, pl.ds(at, LANES)] = lo
        return carry

    lax.fori_loop(0, columns, edge_step, 0)

    def arrive(c, n=None):
        @pl.when(receives)
        def _():
            column_copy(c, n).wait_recv()

        at = pl.multiple_of(c * LANES, LANES)
        start, size = (HALO, centre) if n is None else spans[n]
        block = land[HALO + start : HALO + start + size, pl.ds(at, LANES)]
        ext[c + 1, HALO + start : HALO + start + size, :] = block.astype(jnp.float32)

    def coarse_map():
        @pl.when(receives)
        def _():
            small_copy().wait_recv()

        def sum_step(c, carry):
            at = pl.multiple_of(c * LANES, LANES)
            hi, lo = row_sums(c, first, count)
            sum_hi[:, pl.ds(at, LANES)] = hi
            sum_lo[:, pl.ds(at, LANES)] = lo
            return carry

        lax.fori_loop(0, half, sum_step, 0)
        span = half * LANES
        small[1] = pooled(sum_hi[...], sum_lo[...], pool[...])[0].astype(jnp.float32)
        ends = pooled(end_hi[:, span:], end_lo[:, span:], pool[...])[0].astype(jnp.float32)
        small[2, :side] = ends[:side]
        small[2, side : count - side] = small_land[...].astype(jnp.float32)
        small[2, count - side :] = ends[side:]
        height = count - 2 * COARSE
        row_at, col_at = COARSE + offsets[0, 0, 0], LANES + offsets[0, 0, 1]
        window = [
            window_at(small, (row_at, col_at + n * LANES), height).astype(jnp.bfloat16)
            for n in range(2)
        ]
        freq, power = spectrum(
            [mm(row_tab[:P_SIZE, :], jnp.concatenate(window, axis=1))], wide_tab[...]
        )
        gain = row_gain * wide_gain
        size = height * 2 * LANES
        scale = (size / gain) ** 2 / math.sqrt(size)
        factors = scale / jnp.sqrt(power * (1.0 / gain**2) + EPSILON)
        found = correlate(small_spec[...], freq, 1, wide_tab[...])[0]
        coarse[...] = mm(inv_tab[...], found) * factors[0:1]

    def match_step(k, carry):
        arrive(2 * k)

        @pl.when(k < half - 1)
        def _():
            arrive(2 * k + 1)

        @pl.when(k == half // 2 - 1)
        def _():
            coarse_map()

        cols = (jnp.maximum(2 * k - 1, 0), jnp.minimum(2 * k, columns - 3))
        found = []
        for c in cols:
            group = [(i, c) for i in range(bands)]
            found.append(
                window_spectrum(
                    group_windows(ext, group_places(group, offsets, peaks)),
                    group_flags(group, keep),
                    flow_gain,
                    row_tab,
                    col_tab,
                )
            )
        for c, (freq, factors) in zip(cols, found):

            def write(p, value, c=c):
                at = pl.multiple_of(c * P_SIZE, P_SIZE)
                maps[p * P_SIZE : (p + 1) * P_SIZE, pl.ds(at, P_SIZE)] = value

            write_maps(spec[c], freq, factors, col_tab, inv_tab, write)
        return carry

    lax.fori_loop(0, half, match_step, 0)

    @pl.when(receives & has_up)
    def _():
        side_copy(0).wait_send()

    @pl.when(receives & has_down)
    def _():
        side_copy(1).wait_send()

    @pl.when(relays)
    def _():
        for n in range(len(detours)):
            relay_out(n).wait_send()

    @pl.when(sends)
    def _():
        edge_copy(0).wait_send()
        edge_copy(1).wait_send()
        small_copy().wait_send()
        for c in range(last):
            column_copy(c).wait_send()
        for n in range(len(spans)):
            column_copy(last, n).wait_send()

    def cut(bands_here):
        for i in bands_here:
            lanes = slice(i % 2 * P_SIZE, (i % 2 + 1) * P_SIZE)
            for h, group in enumerate(last_group):
                window = window_at(ext, places[h][i], P_SIZE).astype(jnp.bfloat16)
                windows[h, i // 2, :, lanes] = window

    places = [group_places(group, offsets, peaks) for group in last_group]
    arrive(last, 0)
    arrive(last, 1)
    cut((0, bands - 1))
    arrive(last, 2)
    cut(range(1, bands - 1))


def finish_kernel(
    gain,
    maps,
    coarse,
    windows,
    last_spec,
    last_flags,
    row_tab,
    col_tab,
    inv_tab,
    coarse_out,
    flow_out,
    last_maps,
    sems,
):
    rows, done = maps.shape
    pair = windows.shape[0]
    count = sems.shape[0] - pair - 1
    size = rows // count
    copies = [pltpu.make_async_copy(coarse, coarse_out.at[0], sems.at[count])]
    for n in range(count):
        band = pl.ds(n * size, size)
        copies.append(pltpu.make_async_copy(maps.at[band], flow_out.at[0, band, pl.ds(0, done)], sems.at[n]))
    for copy in copies:
        copy.start()
    found = [
        window_spectrum(
            [windows[h, n] for n in range(windows.shape[1])],
            last_flags[h, :, :1],
            gain,
            row_tab,
            col_tab,
        )
        for h in range(pair)
    ]
    for h, (freq, factors) in enumerate(found):

        def write(p, value, h=h):
            last_maps[h, p * P_SIZE : (p + 1) * P_SIZE, :] = value

        write_maps(last_spec[h], freq, factors, col_tab, inv_tab, write)
        column = flow_out.at[0, :, pl.ds(done + h * P_SIZE, P_SIZE)]
        copies.append(pltpu.make_async_copy(last_maps.at[h], column, sems.at[count + 1 + h]))
        copies[-1].start()
    for copy in copies:
        copy.wait()


def shards(section_image, offsets, peak_shift, accepted):
    own = section_image[0]
    rows, width = own.shape
    bands = rows // P_SIZE
    units = width // PAIR
    columns = width // LANES
    reach = rows + 2 * HALO
    small_width = width // DS
    forward_row, inverse_row, row_gain = row_tables()
    col, col_gain = col_table(P_SIZE)
    wide, wide_gain = col_table(small_width)
    gains = (float(row_gain), float(col_gain), float(wide_gain))
    span = DS * LANES
    pool = quantized(np.arange(span)[:, None] // DS == np.arange(LANES)[None, :])
    tables = [jnp.asarray(x) for x in (forward_row, col, inverse_row, wide, pool)]
    scalars = (offsets, jnp.swapaxes(peak_shift, 2, 3), accepted)
    high = GROUP * HALF + 2 * SUB
    small_high = HALF + 2 * SUB
    small_rows = rows // DS + 2 * COARSE
    hbm = pl.BlockSpec(memory_space=pltpu.HBM)
    vmem = pl.BlockSpec(memory_space=pltpu.VMEM)
    limit = 30 * 2**20
    operands = [pltpu.with_memory_space_constraint(x, pltpu.HBM) for x in (*scalars, own, *tables)]
    between = pl.pallas_call(
        functools.partial(exchange_kernel, bands, units, gains),
        name="exchange",
        out_shape=(
            jax.ShapeDtypeStruct((rows, width - PAIR), jnp.float32),
            jax.ShapeDtypeStruct((rows // DS, small_width), jnp.float32),
            jax.ShapeDtypeStruct((2, bands // 2, P_SIZE, PAIR), jnp.bfloat16),
            jax.ShapeDtypeStruct((2, high, PAIR), jnp.float32),
            jax.ShapeDtypeStruct((2, SUB, LANES), jnp.float32),
        )
        + tuple(jax.ShapeDtypeStruct(x.shape, x.dtype) for x in tables[:3]),
        in_specs=[hbm] * 9,
        out_specs=(vmem,) * 8,
        scratch_shapes=[
            pltpu.VMEM((rows, width), jnp.bfloat16),
            pltpu.VMEM((reach, width), jnp.bfloat16),
            pltpu.VMEM((columns + 2, reach, LANES), jnp.float32),
            pltpu.VMEM((columns, high, PAIR), jnp.float32),
            pltpu.VMEM((rows // DS, small_width), jnp.bfloat16),
            pltpu.VMEM((rows // DS - 2 * COARSE, LANES), jnp.bfloat16),
            pltpu.VMEM((small_width // LANES + 2, small_rows, LANES), jnp.float32),
            pltpu.VMEM((small_high, 2 * small_width), jnp.float32),
            pltpu.VMEM((rows // DS, width), jnp.bfloat16),
            pltpu.VMEM((rows // DS, width), jnp.bfloat16),
            pltpu.VMEM((small_rows, span), jnp.bfloat16),
            pltpu.VMEM((small_rows, span), jnp.bfloat16),
            pltpu.VMEM((4 * COARSE, width), jnp.bfloat16),
            pltpu.VMEM((4 * COARSE, width), jnp.bfloat16),
        ]
        + [pltpu.VMEM(x.shape, jnp.bfloat16) for x in tables[3:]]
        + [pltpu.SMEM(x.shape, jnp.int32) for x in scalars]
        + [
            pltpu.VMEM((2, rows - 2 * HALO, LANES), jnp.bfloat16),
            pltpu.SemaphoreType.DMA((columns + 5,)),
            pltpu.SemaphoreType.DMA((columns + 5,)),
            pltpu.SemaphoreType.DMA((2,)),
            pltpu.SemaphoreType.DMA((2,)),
            pltpu.SemaphoreType.DMA((4,)),
            pltpu.SemaphoreType.DMA((len(operands),)),
        ],
        compiler_params=pltpu.CompilerParams(
            collective_id=0, has_side_effects=True, vmem_limit_bytes=limit
        ),
    )(*operands)
    return pl.pallas_call(
        functools.partial(finish_kernel, gains[0] * gains[1]),
        name="finish",
        out_shape=(
            jax.ShapeDtypeStruct((1, rows // DS, small_width), jnp.float32),
            jax.ShapeDtypeStruct((1, rows, width), jnp.float32),
        ),
        in_specs=[vmem] * 8,
        out_specs=(hbm, hbm),
        scratch_shapes=[
            pltpu.VMEM((2, rows, P_SIZE), jnp.float32),
            pltpu.SemaphoreType.DMA((bands + 3,)),
        ],
        compiler_params=pltpu.CompilerParams(vmem_limit_bytes=limit),
    )(*between)


def solution(mesh):
    return jax.shard_map(
        shards,
        mesh=mesh,
        in_specs=(
            P("sec", "tile", None),
            P("sec", "tile", None),
            P("sec", "tile", None, None),
            P("sec", "tile", None),
        ),
        out_specs=(P("sec", "tile", None), P("sec", "tile", None)),
        check_vma=False,
    )
```

```python
import functools
import math

import jax
import jax.numpy as jnp
import ml_dtypes
import numpy as np
from jax import lax
from jax.experimental import pallas as pl
from jax.experimental.pallas import tpu as pltpu
from jax.sharding import PartitionSpec as P

P_SIZE = 128
HALF = P_SIZE // 2
DS = 4
COARSE = 16
HALO = 80
LANES = 128
PAIR = 2 * P_SIZE
SUB = 8
POOLED = P_SIZE // DS
EPSILON = 1e-05
MESH = pl.DeviceIdType.MESH


def quantized(table):
    return table.astype(np.float32).astype(ml_dtypes.bfloat16)


def table_scale(n):
    cosines = np.cos(2.0 * np.pi * np.arange(n) / n)
    best = None
    for factor in np.linspace(1.0, 2.0, 4001):
        table = quantized(cosines * factor).astype(np.float64)
        gain = (table @ cosines) / (cosines @ cosines)
        error = np.mean((table / gain - cosines) ** 2)
        if best is None or error < best[0]:
            best = (error, factor, gain)
    return best[1], best[2]


def waves(n):
    k = np.arange(n)
    angles = (k[:, None] * k[None, :] % n) * (2.0 * np.pi / n)
    return np.cos(angles), np.sin(angles)


def row_tables():
    n = P_SIZE
    factor, gain = table_scale(n)
    cosines, sines = waves(n)
    alternating = np.where(np.arange(n) % 2 == 0, 1.0, -1.0)
    forward = np.concatenate([cosines[:HALF], sines[:HALF]])
    forward[HALF] = alternating
    weight = np.where(np.arange(HALF) == 0, 1.0, 2.0)[:, None]
    inverse = np.concatenate([cosines[:HALF] * weight, -sines[:HALF] * weight])
    inverse[HALF] = alternating
    pool = (np.arange(POOLED)[:, None] == np.arange(n)[None, :] // DS).astype(np.float64)
    forward = np.concatenate([forward * (factor / n), pool])
    return quantized(forward), quantized(inverse.T * (factor / n)), gain


def col_table(n):
    factor, gain = table_scale(n)
    cosines, sines = waves(n)
    table = np.block([[cosines, sines], [-sines, cosines]]) * (factor / n)
    return quantized(table), gain


def mm(a, b):
    return jnp.dot(a, b, preferred_element_type=jnp.float32)


def sublanes():
    return lax.broadcasted_iota(jnp.int32, (SUB, LANES), 0)


def to_lhs(rows):
    return jnp.concatenate([rows[:HALF], rows[HALF:]], axis=1).astype(jnp.bfloat16)


def energy(block):
    width = block.shape[1] // 2
    total = block[:, :width] * block[:, :width] + block[:, width:] * block[:, width:]
    head = jnp.where(lax.broadcasted_iota(jnp.int32, (SUB, width), 0) == 0, 0.0, total[:SUB])
    for at in range(SUB, HALF, SUB):
        head = head + total[at : at + SUB]
    return jnp.sum(head, axis=0, keepdims=True)


def spectrum(blocks, table):
    count = len(blocks)
    width = blocks[0].shape[1]
    sub = lax.broadcasted_iota(jnp.int32, (SUB, width), 0)
    first = jnp.zeros((SUB, width), jnp.float32)
    middle = jnp.zeros((SUB, width), jnp.float32)
    for p, rows in enumerate(blocks):
        first = jnp.where(sub == p, rows[0:1], first)
        middle = jnp.where(sub == p, rows[HALF : HALF + 1], middle)
    first = first - jnp.sum(first, axis=1, keepdims=True) * (1.0 / width)
    ends = jnp.concatenate([first, middle], axis=0)
    ends = jnp.concatenate([ends, jnp.zeros_like(ends)], axis=1).astype(jnp.bfloat16)
    freq = mm(jnp.concatenate([to_lhs(rows) for rows in blocks] + [ends], axis=0), table)
    power = jnp.zeros((SUB, width), jnp.float32)
    for p in range(count):
        power = jnp.where(sub == p, energy(freq[p * HALF : (p + 1) * HALF]), power)
    tail = freq[count * HALF :] * freq[count * HALF :]
    tail = tail[:SUB] + tail[SUB:]
    power = 2.0 * power + tail[:, :width] + tail[:, width:]
    return freq, jnp.sum(power, axis=1, keepdims=True)


def scaled(freq, count, factors):
    parts = [freq[p * HALF : (p + 1) * HALF] * factors[p : p + 1] for p in range(count)]
    for at in (0, SUB):
        parts.append(freq[count * HALF + at : count * HALF + at + SUB] * factors)
    return parts


def correlate(own, other, count, table):
    width = own.shape[1] // 2
    a_re, a_im = own[:, :width], own[:, width:]
    b_re, b_im = other[:, :width], other[:, width:]
    product = jnp.concatenate([a_re * b_re + a_im * b_im, a_im * b_re - a_re * b_im], axis=1)
    rows = mm(product.astype(jnp.bfloat16), table)
    sub = lax.broadcasted_iota(jnp.int32, (SUB, width), 0)
    at = count * HALF
    blocks = []
    for p in range(count):
        block = rows[p * HALF : (p + 1) * HALF]
        first = rows[at + p : at + p + 1, :width]
        middle = rows[at + SUB + p : at + SUB + p + 1, :width]
        parts = [
            jnp.where(sub == 0, first, block[:SUB, :width]),
            block[SUB:, :width],
            jnp.where(sub == 0, middle, block[:SUB, width:]),
            block[SUB:, width:],
        ]
        blocks.append(jnp.concatenate(parts, axis=0).astype(jnp.bfloat16))
    return blocks


def window_at(ref, row_at, col_at, height):
    block = lax.div(col_at, LANES)
    shift = lax.rem(col_at, LANES)
    left = ref[block, pl.ds(row_at, height), :]
    right = ref[block + 1, pl.ds(row_at, height), :]
    lane = lax.broadcasted_iota(jnp.int32, (height, LANES), 1)
    return pltpu.roll(jnp.where(lane >= shift, left, right), lax.rem(LANES - shift, LANES), 1)


def unit_windows(unit, bands, offsets, peaks, ext):
    off_row = HALO + DS * offsets[0, 0, 0]
    off_col = LANES + DS * offsets[0, 0, 1]
    windows = []
    for i in range(bands):
        pair = []
        for h in range(2):
            column = 2 * unit + h
            row_at = off_row + i * P_SIZE + peaks[0, i, 0, column]
            col_at = off_col + column * P_SIZE + peaks[0, i, 1, column]
            pair.append(window_at(ext, row_at, col_at, P_SIZE).astype(jnp.bfloat16))
        windows.append(jnp.concatenate(pair, axis=1))
    return windows


def unit_keep(unit, bands, keep):
    sub = sublanes()
    flags = jnp.zeros((SUB, LANES), jnp.float32)
    for i in range(bands):
        for h in range(2):
            flag = keep[0, i, 2 * unit + h].astype(jnp.float32)
            flags = jnp.where(sub == 2 * i + h, flag, flags)
    return flags


def match_unit(bands, gains, windows, flags, own, row_tab, col_tab, inv_tab, write):
    blocks = []
    for window in windows:
        rows = mm(row_tab[:P_SIZE, :], window)
        blocks += [rows[:, :P_SIZE], rows[:, P_SIZE:]]
    freq, power = spectrum(blocks, col_tab[...])
    gain = gains[0] * gains[1]
    scale = (P_SIZE * P_SIZE / gain) ** 2 / P_SIZE
    factors = flags * (scale / jnp.sqrt(power * (1.0 / gain**2) + EPSILON))
    rows = correlate(own, freq, 2 * bands, col_tab[...])
    for i in range(bands):
        maps = mm(inv_tab[...], jnp.concatenate(rows[2 * i : 2 * i + 2], axis=1))
        for h in range(2):
            p = 2 * i + h
            write(i, h, maps[:, h * P_SIZE : (h + 1) * P_SIZE] * factors[p : p + 1])


def split(x):
    hi = x.astype(jnp.bfloat16)
    return hi, (x - hi.astype(jnp.float32)).astype(jnp.bfloat16)


def pooled(hi, lo, pool):
    span = pool.shape[0]
    parts = []
    for at in range(0, hi.shape[1], span):
        sums = mm(hi[:, at : at + span], pool) + mm(lo[:, at : at + span], pool)
        parts.append((sums * (1.0 / (DS * DS))).astype(jnp.bfloat16))
    return parts


def exchange_kernel(
    bands,
    units,
    gains,
    offsets_hbm,
    peaks_hbm,
    keep_hbm,
    img,
    row_hbm,
    col_hbm,
    inv_hbm,
    wide_hbm,
    pool_hbm,
    maps,
    coarse,
    windows,
    last_spec,
    flags,
    row_tab,
    col_tab,
    inv_tab,
    own,
    land,
    ext,
    spec,
    small_own,
    small_land,
    small,
    small_spec,
    own_hi,
    own_lo,
    sum_hi,
    sum_lo,
    wide_tab,
    pool,
    offsets,
    peaks,
    keep,
    relayed,
    send_sems,
    recv_sems,
    side_send,
    side_recv,
    relay_sems,
    local_sems,
):
    s = lax.axis_index("sec")
    t = lax.axis_index("tile")
    ns = lax.axis_size("sec")
    nt = lax.axis_size("tile")
    rows, width = own.shape
    columns = width // LANES
    centre = rows - 2 * HALO
    reach = rows + 2 * HALO
    row_gain, col_gain, wide_gain = gains
    early = columns // 2 + 1
    detours = (columns // 2, columns // 2 + 1)

    sends = s < ns - 1
    receives = s > 0
    has_up = t > 0
    has_down = t < nt - 1
    s_next = jnp.minimum(s + 1, ns - 1)
    s_prev = jnp.maximum(s - 1, 0)
    t_next = jnp.minimum(t + 1, nt - 1)
    t_prev = jnp.maximum(t - 1, 0)

    eighth = lax.rem(s, 8)
    starts_relay = (eighth == 3) & (s + 4 < ns)
    relays = eighth == 7
    ends_relay = (eighth == 4) & (s + 3 < ns)
    relay_from = jnp.maximum(s - 4, 0)
    relay_by = jnp.minimum(s + 4, ns - 1)
    relay_to = jnp.maximum(s - 3, 0)
    relayed_by = jnp.minimum(s + 3, ns - 1)

    barrier = pltpu.get_barrier_semaphore()
    for cond, peer in (
        (receives, (s_prev, t)),
        (ends_relay, (relayed_by, t)),
        (relays, (relay_from, t)),
        (has_up, (s, t_prev)),
        (has_down, (s, t_next)),
    ):

        @pl.when(cond)
        def _(peer=peer):
            pl.semaphore_signal(barrier, inc=1, device_id=peer, device_id_type=MESH)

    loads = [
        pltpu.make_async_copy(source, target, local_sems.at[n])
        for n, (source, target) in enumerate(
            (
                (img, own),
                (row_hbm, row_tab),
                (col_hbm, col_tab),
                (inv_hbm, inv_tab),
                (wide_hbm, wide_tab),
                (pool_hbm, pool),
                (offsets_hbm, offsets),
                (peaks_hbm, peaks),
                (keep_hbm, keep),
            )
        )
    ]
    for load in loads:
        load.start()
    peers = sum(jnp.where(cond, 1, 0) for cond in (sends, starts_relay, relays, has_up, has_down))
    pl.semaphore_wait(barrier, peers)

    def edge_copy(n):
        start = n * (rows - HALO)
        return pltpu.make_async_remote_copy(
            src_ref=img.at[pl.ds(start, HALO)],
            dst_ref=land.at[pl.ds(HALO + start, HALO)],
            send_sem=send_sems.at[n],
            recv_sem=recv_sems.at[n],
            device_id=(s_next, t),
            device_id_type=MESH,
        )

    def column_copy(c):
        at = pl.multiple_of(c * LANES, LANES)
        return pltpu.make_async_remote_copy(
            src_ref=img.at[pl.ds(HALO, centre), pl.ds(at, LANES)],
            dst_ref=land.at[pl.ds(2 * HALO, centre), pl.ds(at, LANES)],
            send_sem=send_sems.at[3 + c],
            recv_sem=recv_sems.at[3 + c],
            device_id=(s_next, t),
            device_id_type=MESH,
        )

    def relay_in(n):
        return pltpu.make_async_remote_copy(
            src_ref=img.at[pl.ds(HALO, centre), pl.ds(detours[n] * LANES, LANES)],
            dst_ref=relayed.at[n],
            send_sem=send_sems.at[3 + detours[n]],
            recv_sem=relay_sems.at[n],
            device_id=(relay_by, t),
            device_id_type=MESH,
        )

    def relay_out(n):
        return pltpu.make_async_remote_copy(
            src_ref=relayed.at[n],
            dst_ref=land.at[pl.ds(2 * HALO, centre), pl.ds(detours[n] * LANES, LANES)],
            send_sem=relay_sems.at[2 + n],
            recv_sem=recv_sems.at[3 + detours[n]],
            device_id=(relay_to, t),
            device_id_type=MESH,
        )

    def small_copy():
        return pltpu.make_async_remote_copy(
            src_ref=small_own.at[pl.ds(COARSE, small_land.shape[0]), pl.ds(LANES, LANES)],
            dst_ref=small_land,
            send_sem=send_sems.at[2],
            recv_sem=recv_sems.at[2],
            device_id=(s_next, t),
            device_id_type=MESH,
        )

    def side_copy(n):
        source, target, peer = ((HALO, HALO + rows, t_prev), (rows, 0, t_next))[n]
        return pltpu.make_async_remote_copy(
            src_ref=land.at[pl.ds(source, HALO)],
            dst_ref=land.at[pl.ds(target, HALO)],
            send_sem=side_send.at[n],
            recv_sem=side_recv.at[n],
            device_id=(s, peer),
            device_id_type=MESH,
        )

    @pl.when(sends)
    def _():
        edge_copy(0).start()
        edge_copy(1).start()
        for c in range(early):
            if c not in detours:
                column_copy(c).start()

    @pl.when(starts_relay)
    def _():
        for n in range(len(detours)):
            relay_in(n).start()

    @pl.when(sends & jnp.logical_not(starts_relay))
    def _():
        for c in range(early):
            if c in detours:
                column_copy(c).start()

    @pl.when(jnp.logical_not(receives))
    def _():
        land[...] = jnp.zeros_like(land)
        small_land[...] = jnp.zeros_like(small_land)

    @pl.when(receives & jnp.logical_not(has_up))
    def _():
        land[:HALO, :] = jnp.zeros((HALO, width), jnp.bfloat16)

    @pl.when(receives & jnp.logical_not(has_down))
    def _():
        land[HALO + rows :, :] = jnp.zeros((HALO, width), jnp.bfloat16)

    ext[0] = jnp.zeros((reach, LANES), jnp.float32)
    ext[columns + 1] = jnp.zeros((reach, LANES), jnp.float32)
    small[0] = jnp.zeros(small.shape[1:], jnp.float32)
    small[3] = jnp.zeros(small.shape[1:], jnp.float32)
    for load in loads:
        load.wait()

    def own_unit(u, carry):
        at = pl.multiple_of(u * PAIR, PAIR)
        blocks = []
        for i in range(bands):
            both = mm(row_tab[...], own[i * P_SIZE : (i + 1) * P_SIZE, pl.ds(at, PAIR)])
            blocks += [both[:P_SIZE, :P_SIZE], both[:P_SIZE, P_SIZE:]]
            hi, lo = split(both[P_SIZE:])
            own_hi[i * POOLED : (i + 1) * POOLED, pl.ds(at, PAIR)] = hi
            own_lo[i * POOLED : (i + 1) * POOLED, pl.ds(at, PAIR)] = lo
        freq, power = spectrum(blocks, col_tab[...])
        gain = row_gain * col_gain
        factors = (1.0 / gain) / jnp.sqrt(power * (1.0 / gain**2) + EPSILON)
        base = 0
        for part in scaled(freq, 2 * bands, factors):
            spec[u, base : base + part.shape[0], :] = part
            base += part.shape[0]
        return carry

    lax.fori_loop(0, units, own_unit, 0)
    for n, part in enumerate(pooled(own_hi[...], own_lo[...], pool[...])):
        small_own[:, n * LANES : (n + 1) * LANES] = part

    @pl.when(sends)
    def _():
        small_copy().start()

    @pl.when(sends & jnp.logical_not(starts_relay))
    def _():
        for c in range(early, columns):
            if c in detours:
                column_copy(c).start()

    @pl.when(sends)
    def _():
        for c in range(early, columns):
            if c not in detours:
                column_copy(c).start()

    @pl.when(receives)
    def _():
        edge_copy(0).wait_recv()

        @pl.when(has_up)
        def _():
            side_copy(0).start()

        edge_copy(1).wait_recv()

        @pl.when(has_down)
        def _():
            side_copy(1).start()

    last_spec[...] = spec[units - 1]
    flags[...] = unit_keep(units - 1, bands, keep)
    freq, power = spectrum([mm(row_tab[:P_SIZE, :], small_own[...])], wide_tab[...])
    gain = row_gain * wide_gain
    factors = (1.0 / gain) / jnp.sqrt(power * (1.0 / gain**2) + EPSILON)
    base = 0
    for part in scaled(freq, 1, factors):
        small_spec[base : base + part.shape[0], :] = part
        base += part.shape[0]

    @pl.when(receives)
    def _():
        @pl.when(has_up)
        def _():
            side_copy(1).wait_recv()

        @pl.when(has_down)
        def _():
            side_copy(0).wait_recv()

    for at in (0, HALO + rows - HALO):
        for c in range(columns):
            ext[c + 1, at : at + 2 * HALO, :] = land[
                at : at + 2 * HALO, c * LANES : (c + 1) * LANES
            ].astype(jnp.float32)

    def row_sums(c, at, count):
        sums = ext[c + 1, pl.ds(at, count, stride=DS), :]
        for k in range(1, DS):
            sums = sums + ext[c + 1, pl.ds(at + k, count, stride=DS), :]
        return split(sums)

    def arrive(c):
        @pl.when(receives)
        def _():
            column_copy(c).wait_recv()

        at = pl.multiple_of(c * LANES, LANES)
        ext[c + 1, 2 * HALO : 2 * HALO + centre, :] = land[
            2 * HALO : 2 * HALO + centre, pl.ds(at, LANES)
        ].astype(jnp.float32)

    def coarse_map():
        half = columns // 2
        first = HALO - DS * COARSE
        count = small.shape[1]
        for c in range(half):
            hi, lo = row_sums(c, first, count)
            sum_hi[:, c * LANES : (c + 1) * LANES] = hi
            sum_lo[:, c * LANES : (c + 1) * LANES] = lo
        small[1] = pooled(sum_hi[...], sum_lo[...], pool[...])[0].astype(jnp.float32)
        side = 2 * COARSE
        for c in range(half):
            for n, at in enumerate((first, first + DS * (count - side))):
                hi, lo = row_sums(half + c, at, side)
                sum_hi[n * side : (n + 1) * side, c * LANES : (c + 1) * LANES] = hi
                sum_lo[n * side : (n + 1) * side, c * LANES : (c + 1) * LANES] = lo

        @pl.when(receives)
        def _():
            small_copy().wait_recv()

        ends = pooled(sum_hi[: 2 * side], sum_lo[: 2 * side], pool[...])[0].astype(jnp.float32)
        small[2, :side] = ends[:side]
        small[2, side : count - side] = small_land[...].astype(jnp.float32)
        small[2, count - side :] = ends[side:]
        height = count - 2 * COARSE
        window = [
            window_at(
                small, COARSE + offsets[0, 0, 0], LANES * (n + 1) + offsets[0, 0, 1], height
            ).astype(jnp.bfloat16)
            for n in range(2)
        ]
        freq, power = spectrum(
            [mm(row_tab[:P_SIZE, :], jnp.concatenate(window, axis=1))], wide_tab[...]
        )
        gain = row_gain * wide_gain
        size = height * 2 * LANES
        scale = (size / gain) ** 2 / math.sqrt(size)
        factors = scale / jnp.sqrt(power * (1.0 / gain**2) + EPSILON)
        found = correlate(small_spec[...], freq, 1, wide_tab[...])[0]
        coarse[...] = mm(inv_tab[...], found) * factors[0:1]

    arrive(0)

    def unit_step(u, carry):
        arrive(2 * u + 1)

        @pl.when(u == columns // 4 - 1)
        def _():
            coarse_map()

        arrive(2 * u + 2)

        def write(i, h, value):
            at = pl.multiple_of(u * PAIR + h * P_SIZE, P_SIZE)
            maps[i * P_SIZE : (i + 1) * P_SIZE, pl.ds(at, P_SIZE)] = value

        match_unit(
            bands,
            (row_gain, col_gain),
            unit_windows(u, bands, offsets, peaks, ext),
            unit_keep(u, bands, keep),
            spec[u],
            row_tab,
            col_tab,
            inv_tab,
            write,
        )

        @pl.when(relays & (u == 0))
        def _():
            for n in range(len(detours)):
                relay_in(n).wait_recv()
                relay_out(n).start()

        return carry

    lax.fori_loop(0, units - 1, unit_step, 0)
    @pl.when(receives & has_up)
    def _():
        side_copy(0).wait_send()

    @pl.when(receives & has_down)
    def _():
        side_copy(1).wait_send()

    @pl.when(sends)
    def _():
        edge_copy(0).wait_send()
        edge_copy(1).wait_send()
        small_copy().wait_send()
        for c in range(columns):
            column_copy(c).wait_send()

    @pl.when(relays)
    def _():
        for n in range(len(detours)):
            relay_out(n).wait_send()

    arrive(columns - 1)
    for i, window in enumerate(unit_windows(units - 1, bands, offsets, peaks, ext)):
        windows[i] = window


def finish_kernel(
    bands,
    gains,
    maps,
    coarse,
    windows,
    last_spec,
    flags,
    row_tab,
    col_tab,
    inv_tab,
    coarse_out,
    flow_out,
    last_maps,
    sems,
):
    done = maps.shape[1]
    copies = [pltpu.make_async_copy(coarse, coarse_out.at[0], sems.at[2 * bands])]
    for i in range(bands):
        band = pl.ds(i * P_SIZE, P_SIZE)
        copies.append(pltpu.make_async_copy(maps.at[band], flow_out.at[0, band, pl.ds(0, done)], sems.at[i]))
    for copy in copies:
        copy.start()

    def write(i, h, value):
        last_maps[i * P_SIZE : (i + 1) * P_SIZE, h * P_SIZE : (h + 1) * P_SIZE] = value

    match_unit(
        bands,
        gains[:2],
        [windows[i] for i in range(bands)],
        flags[...],
        last_spec[...],
        row_tab,
        col_tab,
        inv_tab,
        write,
    )
    for i in range(bands):
        band = pl.ds(i * P_SIZE, P_SIZE)
        copies.append(
            pltpu.make_async_copy(last_maps.at[band], flow_out.at[0, band, pl.ds(done, PAIR)], sems.at[bands + i])
        )
        copies[-1].start()
    for copy in copies:
        copy.wait()


def shards(section_image, offsets, peak_shift, accepted):
    own = section_image[0]
    rows, width = own.shape
    bands = rows // P_SIZE
    units = width // PAIR
    columns = width // LANES
    reach = rows + 2 * HALO
    small_width = width // DS
    forward_row, inverse_row, row_gain = row_tables()
    col, col_gain = col_table(P_SIZE)
    wide, wide_gain = col_table(small_width)
    gains = (float(row_gain), float(col_gain), float(wide_gain))
    span = DS * LANES
    pool = quantized(np.arange(span)[:, None] // DS == np.arange(LANES)[None, :])
    tables = [jnp.asarray(x) for x in (forward_row, col, inverse_row, wide, pool)]
    scalars = (offsets, jnp.swapaxes(peak_shift, 2, 3), accepted)
    high = 2 * bands * HALF + 2 * SUB
    small_high = HALF + 2 * SUB
    small_rows = rows // DS + 2 * COARSE
    hbm = pl.BlockSpec(memory_space=pltpu.HBM)
    vmem = pl.BlockSpec(memory_space=pltpu.VMEM)
    limit = 30 * 2**20
    operands = [pltpu.with_memory_space_constraint(x, pltpu.HBM) for x in (*scalars, own, *tables)]
    between = pl.pallas_call(
        functools.partial(exchange_kernel, bands, units, gains),
        name="exchange",
        out_shape=(
            jax.ShapeDtypeStruct((rows, width - PAIR), jnp.float32),
            jax.ShapeDtypeStruct((rows // DS, small_width), jnp.float32),
            jax.ShapeDtypeStruct((bands, P_SIZE, PAIR), jnp.bfloat16),
            jax.ShapeDtypeStruct((high, PAIR), jnp.float32),
            jax.ShapeDtypeStruct((SUB, LANES), jnp.float32),
        )
        + tuple(jax.ShapeDtypeStruct(x.shape, x.dtype) for x in tables[:3]),
        in_specs=[hbm] * 9,
        out_specs=(vmem,) * 8,
        scratch_shapes=[
            pltpu.VMEM((rows, width), jnp.bfloat16),
            pltpu.VMEM((reach, width), jnp.bfloat16),
            pltpu.VMEM((columns + 2, reach, LANES), jnp.float32),
            pltpu.VMEM((units, high, PAIR), jnp.float32),
            pltpu.VMEM((rows // DS, small_width), jnp.bfloat16),
            pltpu.VMEM((rows // DS - 2 * COARSE, LANES), jnp.bfloat16),
            pltpu.VMEM((small_width // LANES + 2, small_rows, LANES), jnp.float32),
            pltpu.VMEM((small_high, 2 * small_width), jnp.float32),
            pltpu.VMEM((rows // DS, width), jnp.bfloat16),
            pltpu.VMEM((rows // DS, width), jnp.bfloat16),
            pltpu.VMEM((small_rows, span), jnp.bfloat16),
            pltpu.VMEM((small_rows, span), jnp.bfloat16),
            pltpu.VMEM(wide.shape, jnp.bfloat16),
            pltpu.VMEM(pool.shape, jnp.bfloat16),
        ]
        + [pltpu.SMEM(x.shape, jnp.int32) for x in scalars]
        + [
            pltpu.VMEM((2, rows - 2 * HALO, LANES), jnp.bfloat16),
            pltpu.SemaphoreType.DMA((columns + 3,)),
            pltpu.SemaphoreType.DMA((columns + 3,)),
            pltpu.SemaphoreType.DMA((2,)),
            pltpu.SemaphoreType.DMA((2,)),
            pltpu.SemaphoreType.DMA((4,)),
            pltpu.SemaphoreType.DMA((len(operands),)),
        ],
        compiler_params=pltpu.CompilerParams(
            collective_id=0, has_side_effects=True, vmem_limit_bytes=limit
        ),
    )(*operands)
    return pl.pallas_call(
        functools.partial(finish_kernel, bands, gains),
        name="finish",
        out_shape=(
            jax.ShapeDtypeStruct((1, rows // DS, small_width), jnp.float32),
            jax.ShapeDtypeStruct((1, rows, width), jnp.float32),
        ),
        in_specs=[vmem] * 8,
        out_specs=(hbm, hbm),
        scratch_shapes=[
            pltpu.VMEM((rows, PAIR), jnp.float32),
            pltpu.SemaphoreType.DMA((2 * bands + 1,)),
        ],
        compiler_params=pltpu.CompilerParams(vmem_limit_bytes=limit),
    )(*between)


def solution(mesh):
    return jax.shard_map(
        shards,
        mesh=mesh,
        in_specs=(
            P("sec", "tile", None),
            P("sec", "tile", None),
            P("sec", "tile", None, None),
            P("sec", "tile", None),
        ),
        out_specs=(P("sec", "tile", None), P("sec", "tile", None)),
        check_vma=False,
    )
```

```python
import functools
import math

import jax
import jax.numpy as jnp
import ml_dtypes
import numpy as np
from jax import lax
from jax.experimental import pallas as pl
from jax.experimental.pallas import tpu as pltpu
from jax.sharding import PartitionSpec as P

P_SIZE = 128
HALF = P_SIZE // 2
DS = 4
COARSE = 16
HALO = 80
LANES = 128
PAIR = 2 * P_SIZE
SUB = 8
POOLED = P_SIZE // DS
EPSILON = 1e-05
MESH = pl.DeviceIdType.MESH


def quantized(table):
    return table.astype(np.float32).astype(ml_dtypes.bfloat16)


def table_scale(n):
    cosines = np.cos(2.0 * np.pi * np.arange(n) / n)
    best = None
    for factor in np.linspace(1.0, 2.0, 4001):
        table = quantized(cosines * factor).astype(np.float64)
        gain = (table @ cosines) / (cosines @ cosines)
        error = np.mean((table / gain - cosines) ** 2)
        if best is None or error < best[0]:
            best = (error, factor, gain)
    return best[1], best[2]


def waves(n):
    k = np.arange(n)
    angles = (k[:, None] * k[None, :] % n) * (2.0 * np.pi / n)
    return np.cos(angles), np.sin(angles)


def row_tables():
    n = P_SIZE
    factor, gain = table_scale(n)
    cosines, sines = waves(n)
    alternating = np.where(np.arange(n) % 2 == 0, 1.0, -1.0)
    forward = np.concatenate([cosines[:HALF], sines[:HALF]])
    forward[HALF] = alternating
    weight = np.where(np.arange(HALF) == 0, 1.0, 2.0)[:, None]
    inverse = np.concatenate([cosines[:HALF] * weight, -sines[:HALF] * weight])
    inverse[HALF] = alternating
    pool = (np.arange(POOLED)[:, None] == np.arange(n)[None, :] // DS).astype(np.float64)
    forward = np.concatenate([forward * (factor / n), pool])
    return quantized(forward), quantized(inverse.T * (factor / n)), gain


def col_table(n):
    factor, gain = table_scale(n)
    cosines, sines = waves(n)
    table = np.block([[cosines, sines], [-sines, cosines]]) * (factor / n)
    return quantized(table), gain


def mm(a, b):
    return jnp.dot(a, b, preferred_element_type=jnp.float32)


def sublanes():
    return lax.broadcasted_iota(jnp.int32, (SUB, LANES), 0)


def to_lhs(rows):
    return jnp.concatenate([rows[:HALF], rows[HALF:]], axis=1).astype(jnp.bfloat16)


def energy(block):
    width = block.shape[1] // 2
    total = block[:, :width] * block[:, :width] + block[:, width:] * block[:, width:]
    head = jnp.where(lax.broadcasted_iota(jnp.int32, (SUB, width), 0) == 0, 0.0, total[:SUB])
    for at in range(SUB, HALF, SUB):
        head = head + total[at : at + SUB]
    return jnp.sum(head, axis=0, keepdims=True)


def spectrum(blocks, table):
    count = len(blocks)
    width = blocks[0].shape[1]
    sub = lax.broadcasted_iota(jnp.int32, (SUB, width), 0)
    first = jnp.zeros((SUB, width), jnp.float32)
    middle = jnp.zeros((SUB, width), jnp.float32)
    for p, rows in enumerate(blocks):
        first = jnp.where(sub == p, rows[0:1], first)
        middle = jnp.where(sub == p, rows[HALF : HALF + 1], middle)
    first = first - jnp.sum(first, axis=1, keepdims=True) * (1.0 / width)
    ends = jnp.concatenate([first, middle], axis=0)
    ends = jnp.concatenate([ends, jnp.zeros_like(ends)], axis=1).astype(jnp.bfloat16)
    freq = mm(jnp.concatenate([to_lhs(rows) for rows in blocks] + [ends], axis=0), table)
    power = jnp.zeros((SUB, width), jnp.float32)
    for p in range(count):
        power = jnp.where(sub == p, energy(freq[p * HALF : (p + 1) * HALF]), power)
    tail = freq[count * HALF :] * freq[count * HALF :]
    tail = tail[:SUB] + tail[SUB:]
    power = 2.0 * power + tail[:, :width] + tail[:, width:]
    return freq, jnp.sum(power, axis=1, keepdims=True)


def scaled(freq, count, factors):
    parts = [freq[p * HALF : (p + 1) * HALF] * factors[p : p + 1] for p in range(count)]
    for at in (0, SUB):
        parts.append(freq[count * HALF + at : count * HALF + at + SUB] * factors)
    return parts


def correlate(own, other, count, table):
    width = own.shape[1] // 2
    a_re, a_im = own[:, :width], own[:, width:]
    b_re, b_im = other[:, :width], other[:, width:]
    product = jnp.concatenate([a_re * b_re + a_im * b_im, a_im * b_re - a_re * b_im], axis=1)
    rows = mm(product.astype(jnp.bfloat16), table)
    sub = lax.broadcasted_iota(jnp.int32, (SUB, width), 0)
    at = count * HALF
    blocks = []
    for p in range(count):
        block = rows[p * HALF : (p + 1) * HALF]
        first = rows[at + p : at + p + 1, :width]
        middle = rows[at + SUB + p : at + SUB + p + 1, :width]
        parts = [
            jnp.where(sub == 0, first, block[:SUB, :width]),
            block[SUB:, :width],
            jnp.where(sub == 0, middle, block[:SUB, width:]),
            block[SUB:, width:],
        ]
        blocks.append(jnp.concatenate(parts, axis=0).astype(jnp.bfloat16))
    return blocks


def window_at(ref, row_at, col_at, height):
    block = lax.div(col_at, LANES)
    shift = lax.rem(col_at, LANES)
    left = ref[block, pl.ds(row_at, height), :]
    right = ref[block + 1, pl.ds(row_at, height), :]
    lane = lax.broadcasted_iota(jnp.int32, (height, LANES), 1)
    return pltpu.roll(jnp.where(lane >= shift, left, right), lax.rem(LANES - shift, LANES), 1)


def unit_windows(unit, bands, offsets, peaks, ext):
    off_row = HALO + DS * offsets[0, 0, 0]
    off_col = LANES + DS * offsets[0, 0, 1]
    windows = []
    for i in range(bands):
        pair = []
        for h in range(2):
            column = 2 * unit + h
            row_at = off_row + i * P_SIZE + peaks[0, i, 0, column]
            col_at = off_col + column * P_SIZE + peaks[0, i, 1, column]
            pair.append(window_at(ext, row_at, col_at, P_SIZE).astype(jnp.bfloat16))
        windows.append(jnp.concatenate(pair, axis=1))
    return windows


def unit_keep(unit, bands, keep):
    sub = sublanes()
    flags = jnp.zeros((SUB, LANES), jnp.float32)
    for i in range(bands):
        for h in range(2):
            flag = keep[0, i, 2 * unit + h].astype(jnp.float32)
            flags = jnp.where(sub == 2 * i + h, flag, flags)
    return flags


def match_unit(bands, gains, windows, flags, own, row_tab, col_tab, inv_tab, write):
    blocks = []
    for window in windows:
        rows = mm(row_tab[:P_SIZE, :], window)
        blocks += [rows[:, :P_SIZE], rows[:, P_SIZE:]]
    freq, power = spectrum(blocks, col_tab[...])
    gain = gains[0] * gains[1]
    scale = (P_SIZE * P_SIZE / gain) ** 2 / P_SIZE
    factors = flags * (scale / jnp.sqrt(power * (1.0 / gain**2) + EPSILON))
    rows = correlate(own, freq, 2 * bands, col_tab[...])
    for i in range(bands):
        maps = mm(inv_tab[...], jnp.concatenate(rows[2 * i : 2 * i + 2], axis=1))
        for h in range(2):
            p = 2 * i + h
            write(i, h, maps[:, h * P_SIZE : (h + 1) * P_SIZE] * factors[p : p + 1])


def split(x):
    hi = x.astype(jnp.bfloat16)
    return hi, (x - hi.astype(jnp.float32)).astype(jnp.bfloat16)


def pooled(hi, lo, pool):
    span = pool.shape[0]
    parts = []
    for at in range(0, hi.shape[1], span):
        sums = mm(hi[:, at : at + span], pool) + mm(lo[:, at : at + span], pool)
        parts.append((sums * (1.0 / (DS * DS))).astype(jnp.bfloat16))
    return parts


def chunk_list(columns):
    single = [(c, 1) for c in range(3, columns - 3)]
    return [(0, 1), (1, 2)] + single + [(columns - 3, 2), (columns - 1, 1)]


def exchange_kernel(
    bands,
    units,
    gains,
    offsets_hbm,
    peaks_hbm,
    keep_hbm,
    img,
    row_hbm,
    col_hbm,
    inv_hbm,
    wide_hbm,
    pool_hbm,
    maps,
    coarse,
    windows,
    last_spec,
    flags,
    row_tab,
    col_tab,
    inv_tab,
    own,
    land,
    ext,
    spec,
    small_own,
    small_land,
    small,
    small_spec,
    own_hi,
    own_lo,
    sum_hi,
    sum_lo,
    wide_tab,
    pool,
    offsets,
    peaks,
    keep,
    relayed,
    send_sems,
    recv_sems,
    side_send,
    side_recv,
    relay_sems,
    local_sems,
):
    s = lax.axis_index("sec")
    t = lax.axis_index("tile")
    ns = lax.axis_size("sec")
    nt = lax.axis_size("tile")
    rows, width = own.shape
    columns = width // LANES
    centre = rows - 2 * HALO
    reach = rows + 2 * HALO
    row_gain, col_gain, wide_gain = gains
    chunks = chunk_list(columns)
    early = 4
    detour = 1

    sends = s < ns - 1
    receives = s > 0
    has_up = t > 0
    has_down = t < nt - 1
    s_next = jnp.minimum(s + 1, ns - 1)
    s_prev = jnp.maximum(s - 1, 0)
    t_next = jnp.minimum(t + 1, nt - 1)
    t_prev = jnp.maximum(t - 1, 0)

    eighth = lax.rem(s, 8)
    starts_relay = (eighth == 3) & (s + 4 < ns)
    relays = eighth == 7
    ends_relay = (eighth == 4) & (s + 3 < ns)
    relay_from = jnp.maximum(s - 4, 0)
    relay_by = jnp.minimum(s + 4, ns - 1)
    relay_to = jnp.maximum(s - 3, 0)
    relayed_by = jnp.minimum(s + 3, ns - 1)

    barrier = pltpu.get_barrier_semaphore()
    for cond, peer in (
        (receives, (s_prev, t)),
        (ends_relay, (relayed_by, t)),
        (relays, (relay_from, t)),
        (has_up, (s, t_prev)),
        (has_down, (s, t_next)),
    ):

        @pl.when(cond)
        def _(peer=peer):
            pl.semaphore_signal(barrier, inc=1, device_id=peer, device_id_type=MESH)

    loads = [
        pltpu.make_async_copy(source, target, local_sems.at[n])
        for n, (source, target) in enumerate(
            (
                (img, own),
                (row_hbm, row_tab),
                (col_hbm, col_tab),
                (inv_hbm, inv_tab),
                (wide_hbm, wide_tab),
                (pool_hbm, pool),
                (offsets_hbm, offsets),
                (peaks_hbm, peaks),
                (keep_hbm, keep),
            )
        )
    ]
    for load in loads:
        load.start()
    peers = sum(jnp.where(cond, 1, 0) for cond in (sends, starts_relay, relays, has_up, has_down))
    pl.semaphore_wait(barrier, peers)

    def edge_copy(n):
        start = n * (rows - HALO)
        return pltpu.make_async_remote_copy(
            src_ref=img.at[pl.ds(start, HALO)],
            dst_ref=land.at[pl.ds(HALO + start, HALO)],
            send_sem=send_sems.at[n],
            recv_sem=recv_sems.at[n],
            device_id=(s_next, t),
            device_id_type=MESH,
        )

    def chunk_copy(n):
        lanes = pl.ds(chunks[n][0] * LANES, chunks[n][1] * LANES)
        return pltpu.make_async_remote_copy(
            src_ref=img.at[pl.ds(HALO, centre), lanes],
            dst_ref=land.at[pl.ds(2 * HALO, centre), lanes],
            send_sem=send_sems.at[3 + n],
            recv_sem=recv_sems.at[3 + n],
            device_id=(s_next, t),
            device_id_type=MESH,
        )

    def relay_in():
        lanes = pl.ds(chunks[detour][0] * LANES, chunks[detour][1] * LANES)
        return pltpu.make_async_remote_copy(
            src_ref=img.at[pl.ds(HALO, centre), lanes],
            dst_ref=relayed,
            send_sem=send_sems.at[3 + detour],
            recv_sem=relay_sems.at[0],
            device_id=(relay_by, t),
            device_id_type=MESH,
        )

    def relay_out():
        lanes = pl.ds(chunks[detour][0] * LANES, chunks[detour][1] * LANES)
        return pltpu.make_async_remote_copy(
            src_ref=relayed,
            dst_ref=land.at[pl.ds(2 * HALO, centre), lanes],
            send_sem=relay_sems.at[1],
            recv_sem=recv_sems.at[3 + detour],
            device_id=(relay_to, t),
            device_id_type=MESH,
        )

    def small_copy():
        return pltpu.make_async_remote_copy(
            src_ref=small_own.at[pl.ds(COARSE, small_land.shape[0]), pl.ds(LANES, LANES)],
            dst_ref=small_land,
            send_sem=send_sems.at[2],
            recv_sem=recv_sems.at[2],
            device_id=(s_next, t),
            device_id_type=MESH,
        )

    def side_copy(n):
        source, target, peer = ((HALO, HALO + rows, t_prev), (rows, 0, t_next))[n]
        return pltpu.make_async_remote_copy(
            src_ref=land.at[pl.ds(source, HALO)],
            dst_ref=land.at[pl.ds(target, HALO)],
            send_sem=side_send.at[n],
            recv_sem=side_recv.at[n],
            device_id=(s, peer),
            device_id_type=MESH,
        )

    @pl.when(sends)
    def _():
        edge_copy(0).start()
        edge_copy(1).start()
        chunk_copy(0).start()

    @pl.when(starts_relay)
    def _():
        relay_in().start()

    @pl.when(sends & jnp.logical_not(starts_relay))
    def _():
        chunk_copy(detour).start()

    @pl.when(sends)
    def _():
        for n in range(detour + 1, early):
            chunk_copy(n).start()

    @pl.when(jnp.logical_not(receives))
    def _():
        land[...] = jnp.zeros_like(land)
        small_land[...] = jnp.zeros_like(small_land)

    @pl.when(receives & jnp.logical_not(has_up))
    def _():
        land[:HALO, :] = jnp.zeros((HALO, width), jnp.bfloat16)

    @pl.when(receives & jnp.logical_not(has_down))
    def _():
        land[HALO + rows :, :] = jnp.zeros((HALO, width), jnp.bfloat16)

    ext[0] = jnp.zeros((reach, LANES), jnp.float32)
    ext[columns + 1] = jnp.zeros((reach, LANES), jnp.float32)
    small[0] = jnp.zeros(small.shape[1:], jnp.float32)
    small[3] = jnp.zeros(small.shape[1:], jnp.float32)
    for load in loads:
        load.wait()

    def own_unit(u, carry):
        at = pl.multiple_of(u * PAIR, PAIR)
        blocks = []
        for i in range(bands):
            both = mm(row_tab[...], own[i * P_SIZE : (i + 1) * P_SIZE, pl.ds(at, PAIR)])
            blocks += [both[:P_SIZE, :P_SIZE], both[:P_SIZE, P_SIZE:]]
            hi, lo = split(both[P_SIZE:])
            own_hi[i * POOLED : (i + 1) * POOLED, pl.ds(at, PAIR)] = hi
            own_lo[i * POOLED : (i + 1) * POOLED, pl.ds(at, PAIR)] = lo
        freq, power = spectrum(blocks, col_tab[...])
        gain = row_gain * col_gain
        factors = (1.0 / gain) / jnp.sqrt(power * (1.0 / gain**2) + EPSILON)
        base = 0
        for part in scaled(freq, 2 * bands, factors):
            spec[u, base : base + part.shape[0], :] = part
            base += part.shape[0]
        return carry

    lax.fori_loop(0, units, own_unit, 0)
    for n, part in enumerate(pooled(own_hi[...], own_lo[...], pool[...])):
        small_own[:, n * LANES : (n + 1) * LANES] = part

    @pl.when(sends)
    def _():
        small_copy().start()
        for n in range(early, len(chunks)):
            chunk_copy(n).start()

    @pl.when(receives)
    def _():
        edge_copy(0).wait_recv()

        @pl.when(has_up)
        def _():
            side_copy(0).start()

        edge_copy(1).wait_recv()

        @pl.when(has_down)
        def _():
            side_copy(1).start()

    last_spec[...] = spec[units - 1]
    flags[...] = unit_keep(units - 1, bands, keep)
    freq, power = spectrum([mm(row_tab[:P_SIZE, :], small_own[...])], wide_tab[...])
    gain = row_gain * wide_gain
    factors = (1.0 / gain) / jnp.sqrt(power * (1.0 / gain**2) + EPSILON)
    base = 0
    for part in scaled(freq, 1, factors):
        small_spec[base : base + part.shape[0], :] = part
        base += part.shape[0]

    @pl.when(receives)
    def _():
        @pl.when(has_up)
        def _():
            side_copy(1).wait_recv()

        @pl.when(has_down)
        def _():
            side_copy(0).wait_recv()

    for at in (0, HALO + rows - HALO):
        for c in range(columns):
            ext[c + 1, at : at + 2 * HALO, :] = land[
                at : at + 2 * HALO, c * LANES : (c + 1) * LANES
            ].astype(jnp.float32)

    def row_sums(c, at, count):
        sums = ext[c + 1, pl.ds(at, count, stride=DS), :]
        for k in range(1, DS):
            sums = sums + ext[c + 1, pl.ds(at + k, count, stride=DS), :]
        return split(sums)

    def arrive(n):
        @pl.when(receives)
        def _():
            chunk_copy(n).wait_recv()

        for c in range(chunks[n][0], sum(chunks[n])):
            block = land[2 * HALO : 2 * HALO + centre, c * LANES : (c + 1) * LANES]
            ext[c + 1, 2 * HALO : 2 * HALO + centre, :] = block.astype(jnp.float32)

    def coarse_map():
        half = columns // 2
        first = HALO - DS * COARSE
        count = small.shape[1]
        for c in range(half):
            hi, lo = row_sums(c, first, count)
            sum_hi[:, c * LANES : (c + 1) * LANES] = hi
            sum_lo[:, c * LANES : (c + 1) * LANES] = lo
        small[1] = pooled(sum_hi[...], sum_lo[...], pool[...])[0].astype(jnp.float32)
        side = 2 * COARSE
        for c in range(half):
            for n, at in enumerate((first, first + DS * (count - side))):
                hi, lo = row_sums(half + c, at, side)
                sum_hi[n * side : (n + 1) * side, c * LANES : (c + 1) * LANES] = hi
                sum_lo[n * side : (n + 1) * side, c * LANES : (c + 1) * LANES] = lo

        @pl.when(receives)
        def _():
            small_copy().wait_recv()

        ends = pooled(sum_hi[: 2 * side], sum_lo[: 2 * side], pool[...])[0].astype(jnp.float32)
        small[2, :side] = ends[:side]
        small[2, side : count - side] = small_land[...].astype(jnp.float32)
        small[2, count - side :] = ends[side:]
        height = count - 2 * COARSE
        window = [
            window_at(
                small, COARSE + offsets[0, 0, 0], LANES * (n + 1) + offsets[0, 0, 1], height
            ).astype(jnp.bfloat16)
            for n in range(2)
        ]
        freq, power = spectrum(
            [mm(row_tab[:P_SIZE, :], jnp.concatenate(window, axis=1))], wide_tab[...]
        )
        gain = row_gain * wide_gain
        size = height * 2 * LANES
        scale = (size / gain) ** 2 / math.sqrt(size)
        factors = scale / jnp.sqrt(power * (1.0 / gain**2) + EPSILON)
        found = correlate(small_spec[...], freq, 1, wide_tab[...])[0]
        coarse[...] = mm(inv_tab[...], found) * factors[0:1]

    arrive(0)
    arrive(1)

    def unit_step(u, carry):
        @pl.when(u == 1)
        def _():
            arrive(2)
            coarse_map()

        for n in range(3, len(chunks) - 1):

            @pl.when(2 * u + 2 == sum(chunks[n]) - 1)
            def _(n=n):
                arrive(n)

        def write(i, h, value):
            at = pl.multiple_of(u * PAIR + h * P_SIZE, P_SIZE)
            maps[i * P_SIZE : (i + 1) * P_SIZE, pl.ds(at, P_SIZE)] = value

        match_unit(
            bands,
            (row_gain, col_gain),
            unit_windows(u, bands, offsets, peaks, ext),
            unit_keep(u, bands, keep),
            spec[u],
            row_tab,
            col_tab,
            inv_tab,
            write,
        )

        @pl.when(relays & (u == 0))
        def _():
            relay_in().wait_recv()
            relay_out().start()

        return carry

    lax.fori_loop(0, units - 1, unit_step, 0)
    @pl.when(receives & has_up)
    def _():
        side_copy(0).wait_send()

    @pl.when(receives & has_down)
    def _():
        side_copy(1).wait_send()

    @pl.when(sends)
    def _():
        edge_copy(0).wait_send()
        edge_copy(1).wait_send()
        small_copy().wait_send()
        for n in range(len(chunks)):
            chunk_copy(n).wait_send()

    @pl.when(relays)
    def _():
        relay_out().wait_send()

    arrive(len(chunks) - 1)
    for i, window in enumerate(unit_windows(units - 1, bands, offsets, peaks, ext)):
        windows[i] = window


def finish_kernel(
    bands,
    gains,
    maps,
    coarse,
    windows,
    last_spec,
    flags,
    row_tab,
    col_tab,
    inv_tab,
    coarse_out,
    flow_out,
    last_maps,
    sems,
):
    done = maps.shape[1]
    copies = [pltpu.make_async_copy(coarse, coarse_out.at[0], sems.at[2 * bands])]
    for i in range(bands):
        band = pl.ds(i * P_SIZE, P_SIZE)
        copies.append(pltpu.make_async_copy(maps.at[band], flow_out.at[0, band, pl.ds(0, done)], sems.at[i]))
    for copy in copies:
        copy.start()

    def write(i, h, value):
        last_maps[i * P_SIZE : (i + 1) * P_SIZE, h * P_SIZE : (h + 1) * P_SIZE] = value

    match_unit(
        bands,
        gains[:2],
        [windows[i] for i in range(bands)],
        flags[...],
        last_spec[...],
        row_tab,
        col_tab,
        inv_tab,
        write,
    )
    for i in range(bands):
        band = pl.ds(i * P_SIZE, P_SIZE)
        copies.append(
            pltpu.make_async_copy(last_maps.at[band], flow_out.at[0, band, pl.ds(done, PAIR)], sems.at[bands + i])
        )
        copies[-1].start()
    for copy in copies:
        copy.wait()


def shards(section_image, offsets, peak_shift, accepted):
    own = section_image[0]
    rows, width = own.shape
    bands = rows // P_SIZE
    units = width // PAIR
    columns = width // LANES
    reach = rows + 2 * HALO
    small_width = width // DS
    forward_row, inverse_row, row_gain = row_tables()
    col, col_gain = col_table(P_SIZE)
    wide, wide_gain = col_table(small_width)
    gains = (float(row_gain), float(col_gain), float(wide_gain))
    span = DS * LANES
    pool = quantized(np.arange(span)[:, None] // DS == np.arange(LANES)[None, :])
    tables = [jnp.asarray(x) for x in (forward_row, col, inverse_row, wide, pool)]
    scalars = (offsets, jnp.swapaxes(peak_shift, 2, 3), accepted)
    high = 2 * bands * HALF + 2 * SUB
    small_high = HALF + 2 * SUB
    small_rows = rows // DS + 2 * COARSE
    hbm = pl.BlockSpec(memory_space=pltpu.HBM)
    vmem = pl.BlockSpec(memory_space=pltpu.VMEM)
    limit = 30 * 2**20
    operands = [pltpu.with_memory_space_constraint(x, pltpu.HBM) for x in (*scalars, own, *tables)]
    between = pl.pallas_call(
        functools.partial(exchange_kernel, bands, units, gains),
        name="exchange",
        out_shape=(
            jax.ShapeDtypeStruct((rows, width - PAIR), jnp.float32),
            jax.ShapeDtypeStruct((rows // DS, small_width), jnp.float32),
            jax.ShapeDtypeStruct((bands, P_SIZE, PAIR), jnp.bfloat16),
            jax.ShapeDtypeStruct((high, PAIR), jnp.float32),
            jax.ShapeDtypeStruct((SUB, LANES), jnp.float32),
        )
        + tuple(jax.ShapeDtypeStruct(x.shape, x.dtype) for x in tables[:3]),
        in_specs=[hbm] * 9,
        out_specs=(vmem,) * 8,
        scratch_shapes=[
            pltpu.VMEM((rows, width), jnp.bfloat16),
            pltpu.VMEM((reach, width), jnp.bfloat16),
            pltpu.VMEM((columns + 2, reach, LANES), jnp.float32),
            pltpu.VMEM((units, high, PAIR), jnp.float32),
            pltpu.VMEM((rows // DS, small_width), jnp.bfloat16),
            pltpu.VMEM((rows // DS - 2 * COARSE, LANES), jnp.bfloat16),
            pltpu.VMEM((small_width // LANES + 2, small_rows, LANES), jnp.float32),
            pltpu.VMEM((small_high, 2 * small_width), jnp.float32),
            pltpu.VMEM((rows // DS, width), jnp.bfloat16),
            pltpu.VMEM((rows // DS, width), jnp.bfloat16),
            pltpu.VMEM((small_rows, span), jnp.bfloat16),
            pltpu.VMEM((small_rows, span), jnp.bfloat16),
            pltpu.VMEM(wide.shape, jnp.bfloat16),
            pltpu.VMEM(pool.shape, jnp.bfloat16),
        ]
        + [pltpu.SMEM(x.shape, jnp.int32) for x in scalars]
        + [
            pltpu.VMEM((rows - 2 * HALO, chunk_list(columns)[1][1] * LANES), jnp.bfloat16),
            pltpu.SemaphoreType.DMA((len(chunk_list(columns)) + 3,)),
            pltpu.SemaphoreType.DMA((len(chunk_list(columns)) + 3,)),
            pltpu.SemaphoreType.DMA((2,)),
            pltpu.SemaphoreType.DMA((2,)),
            pltpu.SemaphoreType.DMA((2,)),
            pltpu.SemaphoreType.DMA((len(operands),)),
        ],
        compiler_params=pltpu.CompilerParams(
            collective_id=0, has_side_effects=True, vmem_limit_bytes=limit
        ),
    )(*operands)
    return pl.pallas_call(
        functools.partial(finish_kernel, bands, gains),
        name="finish",
        out_shape=(
            jax.ShapeDtypeStruct((1, rows // DS, small_width), jnp.float32),
            jax.ShapeDtypeStruct((1, rows, width), jnp.float32),
        ),
        in_specs=[vmem] * 8,
        out_specs=(hbm, hbm),
        scratch_shapes=[
            pltpu.VMEM((rows, PAIR), jnp.float32),
            pltpu.SemaphoreType.DMA((2 * bands + 1,)),
        ],
        compiler_params=pltpu.CompilerParams(vmem_limit_bytes=limit),
    )(*between)


def solution(mesh):
    return jax.shard_map(
        shards,
        mesh=mesh,
        in_specs=(
            P("sec", "tile", None),
            P("sec", "tile", None),
            P("sec", "tile", None, None),
            P("sec", "tile", None),
        ),
        out_specs=(P("sec", "tile", None), P("sec", "tile", None)),
        check_vma=False,
    )
```

```python
import functools
import math

import jax
import jax.numpy as jnp
import ml_dtypes
import numpy as np
from jax import lax
from jax.experimental import pallas as pl
from jax.experimental.pallas import tpu as pltpu
from jax.sharding import PartitionSpec as P

P_SIZE = 128
HALF = P_SIZE // 2
DS = 4
COARSE = 16
HALO = 80
LANES = 128
PAIR = 2 * P_SIZE
SUB = 8
POOLED = P_SIZE // DS
EPSILON = 1e-05
MESH = pl.DeviceIdType.MESH


def quantized(table):
    return table.astype(np.float32).astype(ml_dtypes.bfloat16)


def table_scale(n):
    cosines = np.cos(2.0 * np.pi * np.arange(n) / n)
    best = None
    for factor in np.linspace(1.0, 2.0, 4001):
        table = quantized(cosines * factor).astype(np.float64)
        gain = (table @ cosines) / (cosines @ cosines)
        error = np.mean((table / gain - cosines) ** 2)
        if best is None or error < best[0]:
            best = (error, factor, gain)
    return best[1], best[2]


def waves(n):
    k = np.arange(n)
    angles = (k[:, None] * k[None, :] % n) * (2.0 * np.pi / n)
    return np.cos(angles), np.sin(angles)


def row_tables():
    n = P_SIZE
    factor, gain = table_scale(n)
    cosines, sines = waves(n)
    alternating = np.where(np.arange(n) % 2 == 0, 1.0, -1.0)
    forward = np.concatenate([cosines[:HALF], sines[:HALF]])
    forward[HALF] = alternating
    weight = np.where(np.arange(HALF) == 0, 1.0, 2.0)[:, None]
    inverse = np.concatenate([cosines[:HALF] * weight, -sines[:HALF] * weight])
    inverse[HALF] = alternating
    pool = (np.arange(POOLED)[:, None] == np.arange(n)[None, :] // DS).astype(np.float64)
    forward = np.concatenate([forward * (factor / n), pool])
    return quantized(forward), quantized(inverse.T * (factor / n)), gain


def col_table(n):
    factor, gain = table_scale(n)
    cosines, sines = waves(n)
    table = np.block([[cosines, sines], [-sines, cosines]]) * (factor / n)
    return quantized(table), gain


def mm(a, b):
    return jnp.dot(a, b, preferred_element_type=jnp.float32)


def sublanes():
    return lax.broadcasted_iota(jnp.int32, (SUB, LANES), 0)


def to_lhs(rows):
    return jnp.concatenate([rows[:HALF], rows[HALF:]], axis=1).astype(jnp.bfloat16)


def energy(block):
    width = block.shape[1] // 2
    total = block[:, :width] * block[:, :width] + block[:, width:] * block[:, width:]
    head = jnp.where(lax.broadcasted_iota(jnp.int32, (SUB, width), 0) == 0, 0.0, total[:SUB])
    for at in range(SUB, HALF, SUB):
        head = head + total[at : at + SUB]
    return jnp.sum(head, axis=0, keepdims=True)


def spectrum(blocks, table):
    count = len(blocks)
    width = blocks[0].shape[1]
    sub = lax.broadcasted_iota(jnp.int32, (SUB, width), 0)
    first = jnp.zeros((SUB, width), jnp.float32)
    middle = jnp.zeros((SUB, width), jnp.float32)
    for p, rows in enumerate(blocks):
        first = jnp.where(sub == p, rows[0:1], first)
        middle = jnp.where(sub == p, rows[HALF : HALF + 1], middle)
    first = first - jnp.sum(first, axis=1, keepdims=True) * (1.0 / width)
    ends = jnp.concatenate([first, middle], axis=0)
    ends = jnp.concatenate([ends, jnp.zeros_like(ends)], axis=1).astype(jnp.bfloat16)
    freq = mm(jnp.concatenate([to_lhs(rows) for rows in blocks] + [ends], axis=0), table)
    power = jnp.zeros((SUB, width), jnp.float32)
    for p in range(count):
        power = jnp.where(sub == p, energy(freq[p * HALF : (p + 1) * HALF]), power)
    tail = freq[count * HALF :] * freq[count * HALF :]
    tail = tail[:SUB] + tail[SUB:]
    power = 2.0 * power + tail[:, :width] + tail[:, width:]
    return freq, jnp.sum(power, axis=1, keepdims=True)


def scaled(freq, count, factors):
    parts = [freq[p * HALF : (p + 1) * HALF] * factors[p : p + 1] for p in range(count)]
    for at in (0, SUB):
        parts.append(freq[count * HALF + at : count * HALF + at + SUB] * factors)
    return parts


def correlate(own, other, count, table):
    width = own.shape[1] // 2
    a_re, a_im = own[:, :width], own[:, width:]
    b_re, b_im = other[:, :width], other[:, width:]
    product = jnp.concatenate([a_re * b_re + a_im * b_im, a_im * b_re - a_re * b_im], axis=1)
    rows = mm(product.astype(jnp.bfloat16), table)
    sub = lax.broadcasted_iota(jnp.int32, (SUB, width), 0)
    at = count * HALF
    blocks = []
    for p in range(count):
        block = rows[p * HALF : (p + 1) * HALF]
        first = rows[at + p : at + p + 1, :width]
        middle = rows[at + SUB + p : at + SUB + p + 1, :width]
        parts = [
            jnp.where(sub == 0, first, block[:SUB, :width]),
            block[SUB:, :width],
            jnp.where(sub == 0, middle, block[:SUB, width:]),
            block[SUB:, width:],
        ]
        blocks.append(jnp.concatenate(parts, axis=0).astype(jnp.bfloat16))
    return blocks


def window_at(ref, row_at, col_at, height):
    block = lax.div(col_at, LANES)
    shift = lax.rem(col_at, LANES)
    left = ref[block, pl.ds(row_at, height), :]
    right = ref[block + 1, pl.ds(row_at, height), :]
    lane = lax.broadcasted_iota(jnp.int32, (height, LANES), 1)
    return pltpu.roll(jnp.where(lane >= shift, left, right), lax.rem(LANES - shift, LANES), 1)


def unit_windows(unit, bands, offsets, peaks, ext):
    off_row = HALO + DS * offsets[0, 0, 0]
    off_col = LANES + DS * offsets[0, 0, 1]
    windows = []
    for i in range(bands):
        pair = []
        for h in range(2):
            column = 2 * unit + h
            row_at = off_row + i * P_SIZE + peaks[0, i, 0, column]
            col_at = off_col + column * P_SIZE + peaks[0, i, 1, column]
            pair.append(window_at(ext, row_at, col_at, P_SIZE).astype(jnp.bfloat16))
        windows.append(jnp.concatenate(pair, axis=1))
    return windows


def unit_keep(unit, bands, keep):
    sub = sublanes()
    flags = jnp.zeros((SUB, LANES), jnp.float32)
    for i in range(bands):
        for h in range(2):
            flag = keep[0, i, 2 * unit + h].astype(jnp.float32)
            flags = jnp.where(sub == 2 * i + h, flag, flags)
    return flags


def match_unit(bands, gains, windows, flags, own, row_tab, col_tab, inv_tab, write):
    blocks = []
    for window in windows:
        rows = mm(row_tab[:P_SIZE, :], window)
        blocks += [rows[:, :P_SIZE], rows[:, P_SIZE:]]
    freq, power = spectrum(blocks, col_tab[...])
    gain = gains[0] * gains[1]
    scale = (P_SIZE * P_SIZE / gain) ** 2 / P_SIZE
    factors = flags * (scale / jnp.sqrt(power * (1.0 / gain**2) + EPSILON))
    rows = correlate(own, freq, 2 * bands, col_tab[...])
    for i in range(bands):
        maps = mm(inv_tab[...], jnp.concatenate(rows[2 * i : 2 * i + 2], axis=1))
        for h in range(2):
            p = 2 * i + h
            write(i, h, maps[:, h * P_SIZE : (h + 1) * P_SIZE] * factors[p : p + 1])


def split(x):
    hi = x.astype(jnp.bfloat16)
    return hi, (x - hi.astype(jnp.float32)).astype(jnp.bfloat16)


def pooled(hi, lo, pool):
    span = pool.shape[0]
    parts = []
    for at in range(0, hi.shape[1], span):
        sums = mm(hi[:, at : at + span], pool) + mm(lo[:, at : at + span], pool)
        parts.append((sums * (1.0 / (DS * DS))).astype(jnp.bfloat16))
    return parts


def chunk_list(columns):
    single = [(c, 1) for c in range(3, columns - 3)]
    return [(0, 1), (1, 2)] + single + [(columns - 3, 2), (columns - 1, 1)]


def exchange_kernel(
    bands,
    units,
    gains,
    offsets_hbm,
    peaks_hbm,
    keep_hbm,
    img,
    row_hbm,
    col_hbm,
    inv_hbm,
    wide_hbm,
    pool_hbm,
    maps,
    coarse,
    windows,
    last_spec,
    flags,
    row_tab,
    col_tab,
    inv_tab,
    own,
    land,
    ext,
    spec,
    small_own,
    small_land,
    small,
    small_spec,
    own_hi,
    own_lo,
    sum_hi,
    sum_lo,
    wide_tab,
    pool,
    offsets,
    peaks,
    keep,
    relayed,
    send_sems,
    recv_sems,
    side_send,
    side_recv,
    relay_sems,
    local_sems,
):
    s = lax.axis_index("sec")
    t = lax.axis_index("tile")
    ns = lax.axis_size("sec")
    nt = lax.axis_size("tile")
    rows, width = own.shape
    columns = width // LANES
    centre = rows - 2 * HALO
    reach = rows + 2 * HALO
    row_gain, col_gain, wide_gain = gains
    chunks = chunk_list(columns)
    early = 4
    detour = 1

    sends = s < ns - 1
    receives = s > 0
    has_up = t > 0
    has_down = t < nt - 1
    s_next = jnp.minimum(s + 1, ns - 1)
    s_prev = jnp.maximum(s - 1, 0)
    t_next = jnp.minimum(t + 1, nt - 1)
    t_prev = jnp.maximum(t - 1, 0)

    eighth = lax.rem(s, 8)
    starts_relay = (eighth == 3) & (s + 4 < ns)
    relays = eighth == 7
    ends_relay = (eighth == 4) & (s + 3 < ns)
    relay_from = jnp.maximum(s - 4, 0)
    relay_by = jnp.minimum(s + 4, ns - 1)
    relay_to = jnp.maximum(s - 3, 0)
    relayed_by = jnp.minimum(s + 3, ns - 1)

    barrier = pltpu.get_barrier_semaphore()
    for cond, peer in (
        (receives, (s_prev, t)),
        (ends_relay, (relayed_by, t)),
        (relays, (relay_from, t)),
        (has_up, (s, t_prev)),
        (has_down, (s, t_next)),
    ):

        @pl.when(cond)
        def _(peer=peer):
            pl.semaphore_signal(barrier, inc=1, device_id=peer, device_id_type=MESH)

    loads = [
        pltpu.make_async_copy(source, target, local_sems.at[n])
        for n, (source, target) in enumerate(
            (
                (img, own),
                (row_hbm, row_tab),
                (col_hbm, col_tab),
                (inv_hbm, inv_tab),
                (wide_hbm, wide_tab),
                (pool_hbm, pool),
                (offsets_hbm, offsets),
                (peaks_hbm, peaks),
                (keep_hbm, keep),
            )
        )
    ]
    for load in loads:
        load.start()
    peers = sum(jnp.where(cond, 1, 0) for cond in (sends, starts_relay, relays, has_up, has_down))
    pl.semaphore_wait(barrier, peers)

    def edge_copy(n):
        start = n * (rows - HALO)
        return pltpu.make_async_remote_copy(
            src_ref=img.at[pl.ds(start, HALO)],
            dst_ref=land.at[pl.ds(HALO + start, HALO)],
            send_sem=send_sems.at[n],
            recv_sem=recv_sems.at[n],
            device_id=(s_next, t),
            device_id_type=MESH,
        )

    def chunk_copy(n):
        lanes = pl.ds(chunks[n][0] * LANES, chunks[n][1] * LANES)
        return pltpu.make_async_remote_copy(
            src_ref=img.at[pl.ds(HALO, centre), lanes],
            dst_ref=land.at[pl.ds(2 * HALO, centre), lanes],
            send_sem=send_sems.at[3 + n],
            recv_sem=recv_sems.at[3 + n],
            device_id=(s_next, t),
            device_id_type=MESH,
        )

    def relay_in():
        lanes = pl.ds(chunks[detour][0] * LANES, chunks[detour][1] * LANES)
        return pltpu.make_async_remote_copy(
            src_ref=img.at[pl.ds(HALO, centre), lanes],
            dst_ref=relayed,
            send_sem=send_sems.at[3 + detour],
            recv_sem=relay_sems.at[0],
            device_id=(relay_by, t),
            device_id_type=MESH,
        )

    def relay_out():
        lanes = pl.ds(chunks[detour][0] * LANES, chunks[detour][1] * LANES)
        return pltpu.make_async_remote_copy(
            src_ref=relayed,
            dst_ref=land.at[pl.ds(2 * HALO, centre), lanes],
            send_sem=relay_sems.at[1],
            recv_sem=recv_sems.at[3 + detour],
            device_id=(relay_to, t),
            device_id_type=MESH,
        )

    def small_copy():
        return pltpu.make_async_remote_copy(
            src_ref=small_own.at[pl.ds(COARSE, small_land.shape[0]), pl.ds(LANES, LANES)],
            dst_ref=small_land,
            send_sem=send_sems.at[2],
            recv_sem=recv_sems.at[2],
            device_id=(s_next, t),
            device_id_type=MESH,
        )

    def side_copy(n):
        source, target, peer = ((HALO, HALO + rows, t_prev), (rows, 0, t_next))[n]
        return pltpu.make_async_remote_copy(
            src_ref=land.at[pl.ds(source, HALO)],
            dst_ref=land.at[pl.ds(target, HALO)],
            send_sem=side_send.at[n],
            recv_sem=side_recv.at[n],
            device_id=(s, peer),
            device_id_type=MESH,
        )

    @pl.when(starts_relay)
    def _():
        relay_in().start()

    @pl.when(sends)
    def _():
        edge_copy(0).start()
        edge_copy(1).start()
        chunk_copy(0).start()

    @pl.when(sends & jnp.logical_not(starts_relay))
    def _():
        chunk_copy(detour).start()

    @pl.when(sends)
    def _():
        for n in range(detour + 1, early):
            chunk_copy(n).start()

    @pl.when(jnp.logical_not(receives))
    def _():
        land[...] = jnp.zeros_like(land)
        small_land[...] = jnp.zeros_like(small_land)

    @pl.when(receives & jnp.logical_not(has_up))
    def _():
        land[:HALO, :] = jnp.zeros((HALO, width), jnp.bfloat16)

    @pl.when(receives & jnp.logical_not(has_down))
    def _():
        land[HALO + rows :, :] = jnp.zeros((HALO, width), jnp.bfloat16)

    ext[0] = jnp.zeros((reach, LANES), jnp.float32)
    ext[columns + 1] = jnp.zeros((reach, LANES), jnp.float32)
    small[0] = jnp.zeros(small.shape[1:], jnp.float32)
    small[3] = jnp.zeros(small.shape[1:], jnp.float32)
    for load in loads:
        load.wait()

    def own_unit(u, carry):
        at = pl.multiple_of(u * PAIR, PAIR)
        blocks = []
        for i in range(bands):
            both = mm(row_tab[...], own[i * P_SIZE : (i + 1) * P_SIZE, pl.ds(at, PAIR)])
            blocks += [both[:P_SIZE, :P_SIZE], both[:P_SIZE, P_SIZE:]]
            hi, lo = split(both[P_SIZE:])
            own_hi[i * POOLED : (i + 1) * POOLED, pl.ds(at, PAIR)] = hi
            own_lo[i * POOLED : (i + 1) * POOLED, pl.ds(at, PAIR)] = lo
        freq, power = spectrum(blocks, col_tab[...])
        gain = row_gain * col_gain
        factors = (1.0 / gain) / jnp.sqrt(power * (1.0 / gain**2) + EPSILON)
        base = 0
        for part in scaled(freq, 2 * bands, factors):
            spec[u, base : base + part.shape[0], :] = part
            base += part.shape[0]
        return carry

    lax.fori_loop(0, units, own_unit, 0)

    @pl.when(relays)
    def _():
        relay_in().wait_recv()
        relay_out().start()

    for n, part in enumerate(pooled(own_hi[...], own_lo[...], pool[...])):
        small_own[:, n * LANES : (n + 1) * LANES] = part

    @pl.when(sends)
    def _():
        small_copy().start()
        for n in range(early, len(chunks)):
            chunk_copy(n).start()

    @pl.when(receives)
    def _():
        edge_copy(0).wait_recv()

        @pl.when(has_up)
        def _():
            side_copy(0).start()

        edge_copy(1).wait_recv()

        @pl.when(has_down)
        def _():
            side_copy(1).start()

    last_spec[...] = spec[units - 1]
    flags[...] = unit_keep(units - 1, bands, keep)
    freq, power = spectrum([mm(row_tab[:P_SIZE, :], small_own[...])], wide_tab[...])
    gain = row_gain * wide_gain
    factors = (1.0 / gain) / jnp.sqrt(power * (1.0 / gain**2) + EPSILON)
    base = 0
    for part in scaled(freq, 1, factors):
        small_spec[base : base + part.shape[0], :] = part
        base += part.shape[0]

    @pl.when(receives)
    def _():
        @pl.when(has_up)
        def _():
            side_copy(1).wait_recv()

        @pl.when(has_down)
        def _():
            side_copy(0).wait_recv()

    for at in (0, HALO + rows - HALO):
        for c in range(columns):
            ext[c + 1, at : at + 2 * HALO, :] = land[
                at : at + 2 * HALO, c * LANES : (c + 1) * LANES
            ].astype(jnp.float32)

    def row_sums(c, at, count):
        sums = ext[c + 1, pl.ds(at, count, stride=DS), :]
        for k in range(1, DS):
            sums = sums + ext[c + 1, pl.ds(at + k, count, stride=DS), :]
        return split(sums)

    def arrive(n):
        @pl.when(receives)
        def _():
            chunk_copy(n).wait_recv()

        for c in range(chunks[n][0], sum(chunks[n])):
            block = land[2 * HALO : 2 * HALO + centre, c * LANES : (c + 1) * LANES]
            ext[c + 1, 2 * HALO : 2 * HALO + centre, :] = block.astype(jnp.float32)

    def coarse_map():
        half = columns // 2
        first = HALO - DS * COARSE
        count = small.shape[1]
        for c in range(half):
            hi, lo = row_sums(c, first, count)
            sum_hi[:, c * LANES : (c + 1) * LANES] = hi
            sum_lo[:, c * LANES : (c + 1) * LANES] = lo
        small[1] = pooled(sum_hi[...], sum_lo[...], pool[...])[0].astype(jnp.float32)
        side = 2 * COARSE
        for c in range(half):
            for n, at in enumerate((first, first + DS * (count - side))):
                hi, lo = row_sums(half + c, at, side)
                sum_hi[n * side : (n + 1) * side, c * LANES : (c + 1) * LANES] = hi
                sum_lo[n * side : (n + 1) * side, c * LANES : (c + 1) * LANES] = lo

        @pl.when(receives)
        def _():
            small_copy().wait_recv()

        ends = pooled(sum_hi[: 2 * side], sum_lo[: 2 * side], pool[...])[0].astype(jnp.float32)
        small[2, :side] = ends[:side]
        small[2, side : count - side] = small_land[...].astype(jnp.float32)
        small[2, count - side :] = ends[side:]
        height = count - 2 * COARSE
        window = [
            window_at(
                small, COARSE + offsets[0, 0, 0], LANES * (n + 1) + offsets[0, 0, 1], height
            ).astype(jnp.bfloat16)
            for n in range(2)
        ]
        freq, power = spectrum(
            [mm(row_tab[:P_SIZE, :], jnp.concatenate(window, axis=1))], wide_tab[...]
        )
        gain = row_gain * wide_gain
        size = height * 2 * LANES
        scale = (size / gain) ** 2 / math.sqrt(size)
        factors = scale / jnp.sqrt(power * (1.0 / gain**2) + EPSILON)
        found = correlate(small_spec[...], freq, 1, wide_tab[...])[0]
        coarse[...] = mm(inv_tab[...], found) * factors[0:1]

    arrive(0)
    arrive(1)

    def unit_step(u, carry):
        @pl.when(u == 1)
        def _():
            arrive(2)
            coarse_map()

        for n in range(3, len(chunks) - 1):

            @pl.when(2 * u + 2 == sum(chunks[n]) - 1)
            def _(n=n):
                arrive(n)

        def write(i, h, value):
            at = pl.multiple_of(u * PAIR + h * P_SIZE, P_SIZE)
            maps[i * P_SIZE : (i + 1) * P_SIZE, pl.ds(at, P_SIZE)] = value

        match_unit(
            bands,
            (row_gain, col_gain),
            unit_windows(u, bands, offsets, peaks, ext),
            unit_keep(u, bands, keep),
            spec[u],
            row_tab,
            col_tab,
            inv_tab,
            write,
        )

        return carry

    lax.fori_loop(0, units - 1, unit_step, 0)
    @pl.when(receives & has_up)
    def _():
        side_copy(0).wait_send()

    @pl.when(receives & has_down)
    def _():
        side_copy(1).wait_send()

    @pl.when(sends)
    def _():
        edge_copy(0).wait_send()
        edge_copy(1).wait_send()
        small_copy().wait_send()
        for n in range(len(chunks)):
            chunk_copy(n).wait_send()

    @pl.when(relays)
    def _():
        relay_out().wait_send()

    arrive(len(chunks) - 1)
    for i, window in enumerate(unit_windows(units - 1, bands, offsets, peaks, ext)):
        windows[i] = window


def finish_kernel(
    bands,
    gains,
    maps,
    coarse,
    windows,
    last_spec,
    flags,
    row_tab,
    col_tab,
    inv_tab,
    coarse_out,
    flow_out,
    last_maps,
    sems,
):
    done = maps.shape[1]
    copies = [pltpu.make_async_copy(coarse, coarse_out.at[0], sems.at[2 * bands])]
    for i in range(bands):
        band = pl.ds(i * P_SIZE, P_SIZE)
        copies.append(pltpu.make_async_copy(maps.at[band], flow_out.at[0, band, pl.ds(0, done)], sems.at[i]))
    for copy in copies:
        copy.start()

    def write(i, h, value):
        last_maps[i * P_SIZE : (i + 1) * P_SIZE, h * P_SIZE : (h + 1) * P_SIZE] = value

    match_unit(
        bands,
        gains[:2],
        [windows[i] for i in range(bands)],
        flags[...],
        last_spec[...],
        row_tab,
        col_tab,
        inv_tab,
        write,
    )
    for i in range(bands):
        band = pl.ds(i * P_SIZE, P_SIZE)
        copies.append(
            pltpu.make_async_copy(last_maps.at[band], flow_out.at[0, band, pl.ds(done, PAIR)], sems.at[bands + i])
        )
        copies[-1].start()
    for copy in copies:
        copy.wait()


def shards(section_image, offsets, peak_shift, accepted):
    own = section_image[0]
    rows, width = own.shape
    bands = rows // P_SIZE
    units = width // PAIR
    columns = width // LANES
    reach = rows + 2 * HALO
    small_width = width // DS
    forward_row, inverse_row, row_gain = row_tables()
    col, col_gain = col_table(P_SIZE)
    wide, wide_gain = col_table(small_width)
    gains = (float(row_gain), float(col_gain), float(wide_gain))
    span = DS * LANES
    pool = quantized(np.arange(span)[:, None] // DS == np.arange(LANES)[None, :])
    tables = [jnp.asarray(x) for x in (forward_row, col, inverse_row, wide, pool)]
    scalars = (offsets, jnp.swapaxes(peak_shift, 2, 3), accepted)
    high = 2 * bands * HALF + 2 * SUB
    small_high = HALF + 2 * SUB
    small_rows = rows // DS + 2 * COARSE
    hbm = pl.BlockSpec(memory_space=pltpu.HBM)
    vmem = pl.BlockSpec(memory_space=pltpu.VMEM)
    limit = 30 * 2**20
    operands = [pltpu.with_memory_space_constraint(x, pltpu.HBM) for x in (*scalars, own, *tables)]
    between = pl.pallas_call(
        functools.partial(exchange_kernel, bands, units, gains),
        name="exchange",
        out_shape=(
            jax.ShapeDtypeStruct((rows, width - PAIR), jnp.float32),
            jax.ShapeDtypeStruct((rows // DS, small_width), jnp.float32),
            jax.ShapeDtypeStruct((bands, P_SIZE, PAIR), jnp.bfloat16),
            jax.ShapeDtypeStruct((high, PAIR), jnp.float32),
            jax.ShapeDtypeStruct((SUB, LANES), jnp.float32),
        )
        + tuple(jax.ShapeDtypeStruct(x.shape, x.dtype) for x in tables[:3]),
        in_specs=[hbm] * 9,
        out_specs=(vmem,) * 8,
        scratch_shapes=[
            pltpu.VMEM((rows, width), jnp.bfloat16),
            pltpu.VMEM((reach, width), jnp.bfloat16),
            pltpu.VMEM((columns + 2, reach, LANES), jnp.float32),
            pltpu.VMEM((units, high, PAIR), jnp.float32),
            pltpu.VMEM((rows // DS, small_width), jnp.bfloat16),
            pltpu.VMEM((rows // DS - 2 * COARSE, LANES), jnp.bfloat16),
            pltpu.VMEM((small_width // LANES + 2, small_rows, LANES), jnp.float32),
            pltpu.VMEM((small_high, 2 * small_width), jnp.float32),
            pltpu.VMEM((rows // DS, width), jnp.bfloat16),
            pltpu.VMEM((rows // DS, width), jnp.bfloat16),
            pltpu.VMEM((small_rows, span), jnp.bfloat16),
            pltpu.VMEM((small_rows, span), jnp.bfloat16),
            pltpu.VMEM(wide.shape, jnp.bfloat16),
            pltpu.VMEM(pool.shape, jnp.bfloat16),
        ]
        + [pltpu.SMEM(x.shape, jnp.int32) for x in scalars]
        + [
            pltpu.VMEM((rows - 2 * HALO, chunk_list(columns)[1][1] * LANES), jnp.bfloat16),
            pltpu.SemaphoreType.DMA((len(chunk_list(columns)) + 3,)),
            pltpu.SemaphoreType.DMA((len(chunk_list(columns)) + 3,)),
            pltpu.SemaphoreType.DMA((2,)),
            pltpu.SemaphoreType.DMA((2,)),
            pltpu.SemaphoreType.DMA((2,)),
            pltpu.SemaphoreType.DMA((len(operands),)),
        ],
        compiler_params=pltpu.CompilerParams(
            collective_id=0, has_side_effects=True, vmem_limit_bytes=limit
        ),
    )(*operands)
    return pl.pallas_call(
        functools.partial(finish_kernel, bands, gains),
        name="finish",
        out_shape=(
            jax.ShapeDtypeStruct((1, rows // DS, small_width), jnp.float32),
            jax.ShapeDtypeStruct((1, rows, width), jnp.float32),
        ),
        in_specs=[vmem] * 8,
        out_specs=(hbm, hbm),
        scratch_shapes=[
            pltpu.VMEM((rows, PAIR), jnp.float32),
            pltpu.SemaphoreType.DMA((2 * bands + 1,)),
        ],
        compiler_params=pltpu.CompilerParams(vmem_limit_bytes=limit),
    )(*between)


def solution(mesh):
    return jax.shard_map(
        shards,
        mesh=mesh,
        in_specs=(
            P("sec", "tile", None),
            P("sec", "tile", None),
            P("sec", "tile", None, None),
            P("sec", "tile", None),
        ),
        out_specs=(P("sec", "tile", None), P("sec", "tile", None)),
        check_vma=False,
    )
```

```python
import functools
import math

import jax
import jax.numpy as jnp
import ml_dtypes
import numpy as np
from jax import lax
from jax.experimental import pallas as pl
from jax.experimental.pallas import tpu as pltpu
from jax.sharding import PartitionSpec as P

P_SIZE = 128
HALF = P_SIZE // 2
DS = 4
COARSE = 16
HALO = 80
LANES = 128
PAIR = 2 * P_SIZE
SUB = 8
POOLED = P_SIZE // DS
EPSILON = 1e-05
MESH = pl.DeviceIdType.MESH


def quantized(table):
    return table.astype(np.float32).astype(ml_dtypes.bfloat16)


def table_scale(n):
    cosines = np.cos(2.0 * np.pi * np.arange(n) / n)
    best = None
    for factor in np.linspace(1.0, 2.0, 4001):
        table = quantized(cosines * factor).astype(np.float64)
        gain = (table @ cosines) / (cosines @ cosines)
        error = np.mean((table / gain - cosines) ** 2)
        if best is None or error < best[0]:
            best = (error, factor, gain)
    return best[1], best[2]


def waves(n):
    k = np.arange(n)
    angles = (k[:, None] * k[None, :] % n) * (2.0 * np.pi / n)
    return np.cos(angles), np.sin(angles)


def row_tables():
    n = P_SIZE
    factor, gain = table_scale(n)
    cosines, sines = waves(n)
    alternating = np.where(np.arange(n) % 2 == 0, 1.0, -1.0)
    forward = np.concatenate([cosines[:HALF], sines[:HALF]])
    forward[HALF] = alternating
    weight = np.where(np.arange(HALF) == 0, 1.0, 2.0)[:, None]
    inverse = np.concatenate([cosines[:HALF] * weight, -sines[:HALF] * weight])
    inverse[HALF] = alternating
    pool = (np.arange(POOLED)[:, None] == np.arange(n)[None, :] // DS).astype(np.float64)
    forward = np.concatenate([forward * (factor / n), pool])
    return quantized(forward), quantized(inverse.T * (factor / n)), gain


def col_table(n):
    factor, gain = table_scale(n)
    cosines, sines = waves(n)
    table = np.block([[cosines, sines], [-sines, cosines]]) * (factor / n)
    return quantized(table), gain


def mm(a, b):
    return jnp.dot(a, b, preferred_element_type=jnp.float32)


def sublanes():
    return lax.broadcasted_iota(jnp.int32, (SUB, LANES), 0)


def to_lhs(rows):
    return jnp.concatenate([rows[:HALF], rows[HALF:]], axis=1).astype(jnp.bfloat16)


def energy(block):
    width = block.shape[1] // 2
    total = block[:, :width] * block[:, :width] + block[:, width:] * block[:, width:]
    head = jnp.where(lax.broadcasted_iota(jnp.int32, (SUB, width), 0) == 0, 0.0, total[:SUB])
    for at in range(SUB, HALF, SUB):
        head = head + total[at : at + SUB]
    return jnp.sum(head, axis=0, keepdims=True)


def spectrum(blocks, table):
    count = len(blocks)
    width = blocks[0].shape[1]
    sub = lax.broadcasted_iota(jnp.int32, (SUB, width), 0)
    first = jnp.zeros((SUB, width), jnp.float32)
    middle = jnp.zeros((SUB, width), jnp.float32)
    for p, rows in enumerate(blocks):
        first = jnp.where(sub == p, rows[0:1], first)
        middle = jnp.where(sub == p, rows[HALF : HALF + 1], middle)
    first = first - jnp.sum(first, axis=1, keepdims=True) * (1.0 / width)
    ends = jnp.concatenate([first, middle], axis=0)
    ends = jnp.concatenate([ends, jnp.zeros_like(ends)], axis=1).astype(jnp.bfloat16)
    freq = mm(jnp.concatenate([to_lhs(rows) for rows in blocks] + [ends], axis=0), table)
    power = jnp.zeros((SUB, width), jnp.float32)
    for p in range(count):
        power = jnp.where(sub == p, energy(freq[p * HALF : (p + 1) * HALF]), power)
    tail = freq[count * HALF :] * freq[count * HALF :]
    tail = tail[:SUB] + tail[SUB:]
    power = 2.0 * power + tail[:, :width] + tail[:, width:]
    return freq, jnp.sum(power, axis=1, keepdims=True)


def scaled(freq, count, factors):
    parts = [freq[p * HALF : (p + 1) * HALF] * factors[p : p + 1] for p in range(count)]
    for at in (0, SUB):
        parts.append(freq[count * HALF + at : count * HALF + at + SUB] * factors)
    return parts


def correlate(own, other, count, table):
    width = own.shape[1] // 2
    a_re, a_im = own[:, :width], own[:, width:]
    b_re, b_im = other[:, :width], other[:, width:]
    product = jnp.concatenate([a_re * b_re + a_im * b_im, a_im * b_re - a_re * b_im], axis=1)
    rows = mm(product.astype(jnp.bfloat16), table)
    sub = lax.broadcasted_iota(jnp.int32, (SUB, width), 0)
    at = count * HALF
    blocks = []
    for p in range(count):
        block = rows[p * HALF : (p + 1) * HALF]
        first = rows[at + p : at + p + 1, :width]
        middle = rows[at + SUB + p : at + SUB + p + 1, :width]
        parts = [
            jnp.where(sub == 0, first, block[:SUB, :width]),
            block[SUB:, :width],
            jnp.where(sub == 0, middle, block[:SUB, width:]),
            block[SUB:, width:],
        ]
        blocks.append(jnp.concatenate(parts, axis=0).astype(jnp.bfloat16))
    return blocks


def window_at(ref, row_at, col_at, height):
    block = lax.div(col_at, LANES)
    shift = lax.rem(col_at, LANES)
    left = ref[block, pl.ds(row_at, height), :]
    right = ref[block + 1, pl.ds(row_at, height), :]
    lane = lax.broadcasted_iota(jnp.int32, (height, LANES), 1)
    return pltpu.roll(jnp.where(lane >= shift, left, right), lax.rem(LANES - shift, LANES), 1)


def unit_windows(unit, bands, offsets, peaks, ext):
    off_row = HALO + DS * offsets[0, 0, 0]
    off_col = LANES + DS * offsets[0, 0, 1]
    windows = []
    for i in range(bands):
        pair = []
        for h in range(2):
            column = 2 * unit + h
            row_at = off_row + i * P_SIZE + peaks[0, i, 0, column]
            col_at = off_col + column * P_SIZE + peaks[0, i, 1, column]
            pair.append(window_at(ext, row_at, col_at, P_SIZE).astype(jnp.bfloat16))
        windows.append(jnp.concatenate(pair, axis=1))
    return windows


def unit_keep(unit, bands, keep):
    sub = sublanes()
    flags = jnp.zeros((SUB, LANES), jnp.float32)
    for i in range(bands):
        for h in range(2):
            flag = keep[0, i, 2 * unit + h].astype(jnp.float32)
            flags = jnp.where(sub == 2 * i + h, flag, flags)
    return flags


def match_unit(bands, gains, windows, flags, own, row_tab, col_tab, inv_tab, write):
    blocks = []
    for window in windows:
        rows = mm(row_tab[:P_SIZE, :], window)
        blocks += [rows[:, :P_SIZE], rows[:, P_SIZE:]]
    yield
    freq, power = spectrum(blocks, col_tab[...])
    yield
    gain = gains[0] * gains[1]
    scale = (P_SIZE * P_SIZE / gain) ** 2 / P_SIZE
    factors = flags * (scale / jnp.sqrt(power * (1.0 / gain**2) + EPSILON))
    rows = correlate(own, freq, 2 * bands, col_tab[...])
    yield
    for i in range(bands):
        maps = mm(inv_tab[...], jnp.concatenate(rows[2 * i : 2 * i + 2], axis=1))
        for h in range(2):
            p = 2 * i + h
            write(i, h, maps[:, h * P_SIZE : (h + 1) * P_SIZE] * factors[p : p + 1])


def run(*stages):
    parts = list(stages)
    while parts:
        parts = [part for part in parts if next(part, True) is None]


def split(x):
    hi = x.astype(jnp.bfloat16)
    return hi, (x - hi.astype(jnp.float32)).astype(jnp.bfloat16)


def pooled(hi, lo, pool):
    span = pool.shape[0]
    parts = []
    for at in range(0, hi.shape[1], span):
        sums = mm(hi[:, at : at + span], pool) + mm(lo[:, at : at + span], pool)
        parts.append((sums * (1.0 / (DS * DS))).astype(jnp.bfloat16))
    return parts


def exchange_kernel(
    bands,
    units,
    gains,
    offsets_hbm,
    peaks_hbm,
    keep_hbm,
    img,
    row_hbm,
    col_hbm,
    inv_hbm,
    wide_hbm,
    pool_hbm,
    maps,
    coarse,
    windows,
    last_spec,
    flags,
    row_tab,
    col_tab,
    inv_tab,
    own,
    land,
    ext,
    spec,
    small_own,
    small_land,
    small,
    small_spec,
    own_hi,
    own_lo,
    sum_hi,
    sum_lo,
    wide_tab,
    pool,
    offsets,
    peaks,
    keep,
    relayed,
    send_sems,
    recv_sems,
    side_send,
    side_recv,
    relay_sems,
    local_sems,
):
    s = lax.axis_index("sec")
    t = lax.axis_index("tile")
    ns = lax.axis_size("sec")
    nt = lax.axis_size("tile")
    rows, width = own.shape
    columns = width // LANES
    centre = rows - 2 * HALO
    reach = rows + 2 * HALO
    row_gain, col_gain, wide_gain = gains
    early = 2
    detours = (columns // 2, columns // 2 + 1)

    sends = s < ns - 1
    receives = s > 0
    has_up = t > 0
    has_down = t < nt - 1
    s_next = jnp.minimum(s + 1, ns - 1)
    s_prev = jnp.maximum(s - 1, 0)
    t_next = jnp.minimum(t + 1, nt - 1)
    t_prev = jnp.maximum(t - 1, 0)

    eighth = lax.rem(s, 8)
    starts_relay = (eighth == 3) & (s + 4 < ns)
    relays = eighth == 7
    ends_relay = (eighth == 4) & (s + 3 < ns)
    relay_from = jnp.maximum(s - 4, 0)
    relay_by = jnp.minimum(s + 4, ns - 1)
    relay_to = jnp.maximum(s - 3, 0)
    relayed_by = jnp.minimum(s + 3, ns - 1)

    barrier = pltpu.get_barrier_semaphore()
    for cond, peer in (
        (receives, (s_prev, t)),
        (ends_relay, (relayed_by, t)),
        (relays, (relay_from, t)),
        (has_up, (s, t_prev)),
        (has_down, (s, t_next)),
    ):

        @pl.when(cond)
        def _(peer=peer):
            pl.semaphore_signal(barrier, inc=1, device_id=peer, device_id_type=MESH)

    loads = [
        pltpu.make_async_copy(source, target, local_sems.at[n])
        for n, (source, target) in enumerate(
            (
                (img, own),
                (row_hbm, row_tab),
                (col_hbm, col_tab),
                (inv_hbm, inv_tab),
                (wide_hbm, wide_tab),
                (pool_hbm, pool),
                (offsets_hbm, offsets),
                (peaks_hbm, peaks),
                (keep_hbm, keep),
            )
        )
    ]
    for load in loads:
        load.start()
    peers = sum(jnp.where(cond, 1, 0) for cond in (sends, starts_relay, relays, has_up, has_down))
    pl.semaphore_wait(barrier, peers)

    def edge_copy(n):
        start = n * (rows - HALO)
        return pltpu.make_async_remote_copy(
            src_ref=img.at[pl.ds(start, HALO)],
            dst_ref=land.at[pl.ds(HALO + start, HALO)],
            send_sem=send_sems.at[n],
            recv_sem=recv_sems.at[n],
            device_id=(s_next, t),
            device_id_type=MESH,
        )

    def column_copy(c):
        at = pl.multiple_of(c * LANES, LANES)
        return pltpu.make_async_remote_copy(
            src_ref=img.at[pl.ds(HALO, centre), pl.ds(at, LANES)],
            dst_ref=land.at[pl.ds(2 * HALO, centre), pl.ds(at, LANES)],
            send_sem=send_sems.at[3 + c],
            recv_sem=recv_sems.at[3 + c],
            device_id=(s_next, t),
            device_id_type=MESH,
        )

    def relay_in(n):
        return pltpu.make_async_remote_copy(
            src_ref=img.at[pl.ds(HALO, centre), pl.ds(detours[n] * LANES, LANES)],
            dst_ref=relayed.at[n],
            send_sem=send_sems.at[3 + detours[n]],
            recv_sem=relay_sems.at[n],
            device_id=(relay_by, t),
            device_id_type=MESH,
        )

    def relay_out(n):
        return pltpu.make_async_remote_copy(
            src_ref=relayed.at[n],
            dst_ref=land.at[pl.ds(2 * HALO, centre), pl.ds(detours[n] * LANES, LANES)],
            send_sem=relay_sems.at[2 + n],
            recv_sem=recv_sems.at[3 + detours[n]],
            device_id=(relay_to, t),
            device_id_type=MESH,
        )

    def small_copy():
        return pltpu.make_async_remote_copy(
            src_ref=small_own.at[pl.ds(COARSE, small_land.shape[0]), pl.ds(LANES, LANES)],
            dst_ref=small_land,
            send_sem=send_sems.at[2],
            recv_sem=recv_sems.at[2],
            device_id=(s_next, t),
            device_id_type=MESH,
        )

    def side_copy(n):
        source, target, peer = ((HALO, HALO + rows, t_prev), (rows, 0, t_next))[n]
        return pltpu.make_async_remote_copy(
            src_ref=land.at[pl.ds(source, HALO)],
            dst_ref=land.at[pl.ds(target, HALO)],
            send_sem=side_send.at[n],
            recv_sem=side_recv.at[n],
            device_id=(s, peer),
            device_id_type=MESH,
        )

    @pl.when(sends)
    def _():
        edge_copy(0).start()
        edge_copy(1).start()
        for c in range(early):
            if c not in detours:
                column_copy(c).start()

    @pl.when(starts_relay)
    def _():
        for n in range(len(detours)):
            relay_in(n).start()

    @pl.when(sends & jnp.logical_not(starts_relay))
    def _():
        for c in range(early):
            if c in detours:
                column_copy(c).start()

    @pl.when(jnp.logical_not(receives))
    def _():
        land[...] = jnp.zeros_like(land)
        small_land[...] = jnp.zeros_like(small_land)

    @pl.when(receives & jnp.logical_not(has_up))
    def _():
        land[:HALO, :] = jnp.zeros((HALO, width), jnp.bfloat16)

    @pl.when(receives & jnp.logical_not(has_down))
    def _():
        land[HALO + rows :, :] = jnp.zeros((HALO, width), jnp.bfloat16)

    ext[0] = jnp.zeros((reach, LANES), jnp.float32)
    ext[columns + 1] = jnp.zeros((reach, LANES), jnp.float32)
    small[0] = jnp.zeros(small.shape[1:], jnp.float32)
    small[3] = jnp.zeros(small.shape[1:], jnp.float32)
    for load in loads:
        load.wait()

    def own_unit(u, carry):
        at = pl.multiple_of(u * PAIR, PAIR)
        blocks = []
        for i in range(bands):
            both = mm(row_tab[...], own[i * P_SIZE : (i + 1) * P_SIZE, pl.ds(at, PAIR)])
            blocks += [both[:P_SIZE, :P_SIZE], both[:P_SIZE, P_SIZE:]]
            hi, lo = split(both[P_SIZE:])
            own_hi[i * POOLED : (i + 1) * POOLED, pl.ds(at, PAIR)] = hi
            own_lo[i * POOLED : (i + 1) * POOLED, pl.ds(at, PAIR)] = lo
        freq, power = spectrum(blocks, col_tab[...])
        gain = row_gain * col_gain
        factors = (1.0 / gain) / jnp.sqrt(power * (1.0 / gain**2) + EPSILON)
        base = 0
        for part in scaled(freq, 2 * bands, factors):
            spec[u, base : base + part.shape[0], :] = part
            base += part.shape[0]
        return carry

    lax.fori_loop(0, units, own_unit, 0)
    for n, part in enumerate(pooled(own_hi[...], own_lo[...], pool[...])):
        small_own[:, n * LANES : (n + 1) * LANES] = part

    @pl.when(sends)
    def _():
        small_copy().start()

    @pl.when(sends & jnp.logical_not(starts_relay))
    def _():
        for c in range(early, columns):
            if c in detours:
                column_copy(c).start()

    @pl.when(sends)
    def _():
        for c in range(early, columns):
            if c not in detours:
                column_copy(c).start()

    @pl.when(receives)
    def _():
        edge_copy(0).wait_recv()

        @pl.when(has_up)
        def _():
            side_copy(0).start()

        edge_copy(1).wait_recv()

        @pl.when(has_down)
        def _():
            side_copy(1).start()

    last_spec[...] = spec[units - 1]
    flags[...] = unit_keep(units - 1, bands, keep)
    freq, power = spectrum([mm(row_tab[:P_SIZE, :], small_own[...])], wide_tab[...])
    gain = row_gain * wide_gain
    factors = (1.0 / gain) / jnp.sqrt(power * (1.0 / gain**2) + EPSILON)
    base = 0
    for part in scaled(freq, 1, factors):
        small_spec[base : base + part.shape[0], :] = part
        base += part.shape[0]

    @pl.when(receives)
    def _():
        @pl.when(has_up)
        def _():
            side_copy(1).wait_recv()

        @pl.when(has_down)
        def _():
            side_copy(0).wait_recv()

    for at in (0, HALO + rows - HALO):
        for c in range(columns):
            ext[c + 1, at : at + 2 * HALO, :] = land[
                at : at + 2 * HALO, c * LANES : (c + 1) * LANES
            ].astype(jnp.float32)

    def row_sums(c, at, count):
        sums = ext[c + 1, pl.ds(at, count, stride=DS), :]
        for k in range(1, DS):
            sums = sums + ext[c + 1, pl.ds(at + k, count, stride=DS), :]
        return split(sums)

    def arrive(c):
        @pl.when(receives)
        def _():
            column_copy(c).wait_recv()

        at = pl.multiple_of(c * LANES, LANES)
        ext[c + 1, 2 * HALO : 2 * HALO + centre, :] = land[
            2 * HALO : 2 * HALO + centre, pl.ds(at, LANES)
        ].astype(jnp.float32)

    def coarse_map():
        half = columns // 2
        first = HALO - DS * COARSE
        count = small.shape[1]
        for c in range(half):
            hi, lo = row_sums(c, first, count)
            sum_hi[:, c * LANES : (c + 1) * LANES] = hi
            sum_lo[:, c * LANES : (c + 1) * LANES] = lo
        small[1] = pooled(sum_hi[...], sum_lo[...], pool[...])[0].astype(jnp.float32)
        side = 2 * COARSE
        for c in range(half):
            for n, at in enumerate((first, first + DS * (count - side))):
                hi, lo = row_sums(half + c, at, side)
                sum_hi[n * side : (n + 1) * side, c * LANES : (c + 1) * LANES] = hi
                sum_lo[n * side : (n + 1) * side, c * LANES : (c + 1) * LANES] = lo

        ends = pooled(sum_hi[: 2 * side], sum_lo[: 2 * side], pool[...])[0].astype(jnp.float32)
        small[2, :side] = ends[:side]
        small[2, side : count - side] = small_land[...].astype(jnp.float32)
        small[2, count - side :] = ends[side:]
        yield
        height = count - 2 * COARSE
        window = [
            window_at(
                small, COARSE + offsets[0, 0, 0], LANES * (n + 1) + offsets[0, 0, 1], height
            ).astype(jnp.bfloat16)
            for n in range(2)
        ]
        block = mm(row_tab[:P_SIZE, :], jnp.concatenate(window, axis=1))
        yield
        freq, power = spectrum([block], wide_tab[...])
        yield
        gain = row_gain * wide_gain
        size = height * 2 * LANES
        scale = (size / gain) ** 2 / math.sqrt(size)
        factors = scale / jnp.sqrt(power * (1.0 / gain**2) + EPSILON)
        found = correlate(small_spec[...], freq, 1, wide_tab[...])[0]
        yield
        coarse[...] = mm(inv_tab[...], found) * factors[0:1]

    def unit_step(u):
        def write(i, h, value):
            at = u * PAIR + h * P_SIZE
            maps[i * P_SIZE : (i + 1) * P_SIZE, at : at + P_SIZE] = value

        return match_unit(
            bands,
            (row_gain, col_gain),
            unit_windows(u, bands, offsets, peaks, ext),
            unit_keep(u, bands, keep),
            spec[u],
            row_tab,
            col_tab,
            inv_tab,
            write,
        )

    arrive(0)
    for u in range(units - 1):
        arrive(2 * u + 1)
        arrive(2 * u + 2)
        if u == columns // 4 - 1:

            @pl.when(receives)
            def _():
                small_copy().wait_recv()

            run(coarse_map(), unit_step(u))
        else:
            run(unit_step(u))
        if u == 0:

            @pl.when(relays)
            def _():
                for n in range(len(detours)):
                    relay_in(n).wait_recv()
                    relay_out(n).start()

    @pl.when(receives & has_up)
    def _():
        side_copy(0).wait_send()

    @pl.when(receives & has_down)
    def _():
        side_copy(1).wait_send()

    @pl.when(sends)
    def _():
        edge_copy(0).wait_send()
        edge_copy(1).wait_send()
        small_copy().wait_send()
        for c in range(columns):
            column_copy(c).wait_send()

    @pl.when(relays)
    def _():
        for n in range(len(detours)):
            relay_out(n).wait_send()

    arrive(columns - 1)
    for i, window in enumerate(unit_windows(units - 1, bands, offsets, peaks, ext)):
        windows[i] = window


def finish_kernel(
    bands,
    gains,
    maps,
    coarse,
    windows,
    last_spec,
    flags,
    row_tab,
    col_tab,
    inv_tab,
    coarse_out,
    flow_out,
    last_maps,
    sems,
):
    done = maps.shape[1]
    copies = [pltpu.make_async_copy(coarse, coarse_out.at[0], sems.at[2 * bands])]
    for i in range(bands):
        band = pl.ds(i * P_SIZE, P_SIZE)
        copies.append(pltpu.make_async_copy(maps.at[band], flow_out.at[0, band, pl.ds(0, done)], sems.at[i]))
    for copy in copies:
        copy.start()

    def write(i, h, value):
        last_maps[i * P_SIZE : (i + 1) * P_SIZE, h * P_SIZE : (h + 1) * P_SIZE] = value

    run(
        match_unit(
            bands,
            gains[:2],
            [windows[i] for i in range(bands)],
            flags[...],
            last_spec[...],
            row_tab,
            col_tab,
            inv_tab,
            write,
        )
    )
    for i in range(bands):
        band = pl.ds(i * P_SIZE, P_SIZE)
        copies.append(
            pltpu.make_async_copy(last_maps.at[band], flow_out.at[0, band, pl.ds(done, PAIR)], sems.at[bands + i])
        )
        copies[-1].start()
    for copy in copies:
        copy.wait()


def shards(section_image, offsets, peak_shift, accepted):
    own = section_image[0]
    rows, width = own.shape
    bands = rows // P_SIZE
    units = width // PAIR
    columns = width // LANES
    reach = rows + 2 * HALO
    small_width = width // DS
    forward_row, inverse_row, row_gain = row_tables()
    col, col_gain = col_table(P_SIZE)
    wide, wide_gain = col_table(small_width)
    gains = (float(row_gain), float(col_gain), float(wide_gain))
    span = DS * LANES
    pool = quantized(np.arange(span)[:, None] // DS == np.arange(LANES)[None, :])
    tables = [jnp.asarray(x) for x in (forward_row, col, inverse_row, wide, pool)]
    scalars = (offsets, jnp.swapaxes(peak_shift, 2, 3), accepted)
    high = 2 * bands * HALF + 2 * SUB
    small_high = HALF + 2 * SUB
    small_rows = rows // DS + 2 * COARSE
    hbm = pl.BlockSpec(memory_space=pltpu.HBM)
    vmem = pl.BlockSpec(memory_space=pltpu.VMEM)
    limit = 30 * 2**20
    operands = [pltpu.with_memory_space_constraint(x, pltpu.HBM) for x in (*scalars, own, *tables)]
    between = pl.pallas_call(
        functools.partial(exchange_kernel, bands, units, gains),
        name="exchange",
        out_shape=(
            jax.ShapeDtypeStruct((rows, width - PAIR), jnp.float32),
            jax.ShapeDtypeStruct((rows // DS, small_width), jnp.float32),
            jax.ShapeDtypeStruct((bands, P_SIZE, PAIR), jnp.bfloat16),
            jax.ShapeDtypeStruct((high, PAIR), jnp.float32),
            jax.ShapeDtypeStruct((SUB, LANES), jnp.float32),
        )
        + tuple(jax.ShapeDtypeStruct(x.shape, x.dtype) for x in tables[:3]),
        in_specs=[hbm] * 9,
        out_specs=(vmem,) * 8,
        scratch_shapes=[
            pltpu.VMEM((rows, width), jnp.bfloat16),
            pltpu.VMEM((reach, width), jnp.bfloat16),
            pltpu.VMEM((columns + 2, reach, LANES), jnp.float32),
            pltpu.VMEM((units, high, PAIR), jnp.float32),
            pltpu.VMEM((rows // DS, small_width), jnp.bfloat16),
            pltpu.VMEM((rows // DS - 2 * COARSE, LANES), jnp.bfloat16),
            pltpu.VMEM((small_width // LANES + 2, small_rows, LANES), jnp.float32),
            pltpu.VMEM((small_high, 2 * small_width), jnp.float32),
            pltpu.VMEM((rows // DS, width), jnp.bfloat16),
            pltpu.VMEM((rows // DS, width), jnp.bfloat16),
            pltpu.VMEM((small_rows, span), jnp.bfloat16),
            pltpu.VMEM((small_rows, span), jnp.bfloat16),
            pltpu.VMEM(wide.shape, jnp.bfloat16),
            pltpu.VMEM(pool.shape, jnp.bfloat16),
        ]
        + [pltpu.SMEM(x.shape, jnp.int32) for x in scalars]
        + [
            pltpu.VMEM((2, rows - 2 * HALO, LANES), jnp.bfloat16),
            pltpu.SemaphoreType.DMA((columns + 3,)),
            pltpu.SemaphoreType.DMA((columns + 3,)),
            pltpu.SemaphoreType.DMA((2,)),
            pltpu.SemaphoreType.DMA((2,)),
            pltpu.SemaphoreType.DMA((4,)),
            pltpu.SemaphoreType.DMA((len(operands),)),
        ],
        compiler_params=pltpu.CompilerParams(
            collective_id=0, has_side_effects=True, vmem_limit_bytes=limit
        ),
    )(*operands)
    return pl.pallas_call(
        functools.partial(finish_kernel, bands, gains),
        name="finish",
        out_shape=(
            jax.ShapeDtypeStruct((1, rows // DS, small_width), jnp.float32),
            jax.ShapeDtypeStruct((1, rows, width), jnp.float32),
        ),
        in_specs=[vmem] * 8,
        out_specs=(hbm, hbm),
        scratch_shapes=[
            pltpu.VMEM((rows, PAIR), jnp.float32),
            pltpu.SemaphoreType.DMA((2 * bands + 1,)),
        ],
        compiler_params=pltpu.CompilerParams(vmem_limit_bytes=limit),
    )(*between)


def solution(mesh):
    return jax.shard_map(
        shards,
        mesh=mesh,
        in_specs=(
            P("sec", "tile", None),
            P("sec", "tile", None),
            P("sec", "tile", None, None),
            P("sec", "tile", None),
        ),
        out_specs=(P("sec", "tile", None), P("sec", "tile", None)),
        check_vma=False,
    )
```

```python
import functools
import math

import jax
import jax.numpy as jnp
import ml_dtypes
import numpy as np
from jax import lax
from jax.experimental import pallas as pl
from jax.experimental.pallas import tpu as pltpu
from jax.sharding import PartitionSpec as P

P_SIZE = 128
HALF = P_SIZE // 2
DS = 4
COARSE = 16
HALO = 80
LANES = 128
PAIR = 2 * P_SIZE
SUB = 8
POOLED = P_SIZE // DS
EPSILON = 1e-05
MESH = pl.DeviceIdType.MESH


def quantized(table):
    return table.astype(np.float32).astype(ml_dtypes.bfloat16)


def table_scale(n):
    cosines = np.cos(2.0 * np.pi * np.arange(n) / n)
    best = None
    for factor in np.linspace(1.0, 2.0, 4001):
        table = quantized(cosines * factor).astype(np.float64)
        gain = (table @ cosines) / (cosines @ cosines)
        error = np.mean((table / gain - cosines) ** 2)
        if best is None or error < best[0]:
            best = (error, factor, gain)
    return best[1], best[2]


def waves(n):
    k = np.arange(n)
    angles = (k[:, None] * k[None, :] % n) * (2.0 * np.pi / n)
    return np.cos(angles), np.sin(angles)


def row_tables():
    n = P_SIZE
    factor, gain = table_scale(n)
    cosines, sines = waves(n)
    alternating = np.where(np.arange(n) % 2 == 0, 1.0, -1.0)
    forward = np.concatenate([cosines[:HALF], sines[:HALF]])
    forward[HALF] = alternating
    weight = np.where(np.arange(HALF) == 0, 1.0, 2.0)[:, None]
    inverse = np.concatenate([cosines[:HALF] * weight, -sines[:HALF] * weight])
    inverse[HALF] = alternating
    pool = (np.arange(POOLED)[:, None] == np.arange(n)[None, :] // DS).astype(np.float64)
    forward = np.concatenate([forward * (factor / n), pool])
    return quantized(forward), quantized(inverse.T * (factor / n)), gain


def col_table(n):
    factor, gain = table_scale(n)
    cosines, sines = waves(n)
    table = np.block([[cosines, sines], [-sines, cosines]]) * (factor / n)
    return quantized(table), gain


def mm(a, b):
    return jnp.dot(a, b, preferred_element_type=jnp.float32)


def sublanes():
    return lax.broadcasted_iota(jnp.int32, (SUB, LANES), 0)


def to_lhs(rows):
    return jnp.concatenate([rows[:HALF], rows[HALF:]], axis=1).astype(jnp.bfloat16)


def energy(block):
    width = block.shape[1] // 2
    total = block[:, :width] * block[:, :width] + block[:, width:] * block[:, width:]
    head = jnp.where(lax.broadcasted_iota(jnp.int32, (SUB, width), 0) == 0, 0.0, total[:SUB])
    for at in range(SUB, HALF, SUB):
        head = head + total[at : at + SUB]
    return jnp.sum(head, axis=0, keepdims=True)


def spectrum(blocks, table):
    count = len(blocks)
    width = blocks[0].shape[1]
    sub = lax.broadcasted_iota(jnp.int32, (SUB, width), 0)
    first = jnp.zeros((SUB, width), jnp.float32)
    middle = jnp.zeros((SUB, width), jnp.float32)
    for p, rows in enumerate(blocks):
        first = jnp.where(sub == p, rows[0:1], first)
        middle = jnp.where(sub == p, rows[HALF : HALF + 1], middle)
    first = first - jnp.sum(first, axis=1, keepdims=True) * (1.0 / width)
    ends = jnp.concatenate([first, middle], axis=0)
    ends = jnp.concatenate([ends, jnp.zeros_like(ends)], axis=1).astype(jnp.bfloat16)
    freq = mm(jnp.concatenate([to_lhs(rows) for rows in blocks] + [ends], axis=0), table)
    power = jnp.zeros((SUB, width), jnp.float32)
    for p in range(count):
        power = jnp.where(sub == p, energy(freq[p * HALF : (p + 1) * HALF]), power)
    tail = freq[count * HALF :] * freq[count * HALF :]
    tail = tail[:SUB] + tail[SUB:]
    power = 2.0 * power + tail[:, :width] + tail[:, width:]
    return freq, jnp.sum(power, axis=1, keepdims=True)


def scaled(freq, count, factors):
    parts = [freq[p * HALF : (p + 1) * HALF] * factors[p : p + 1] for p in range(count)]
    for at in (0, SUB):
        parts.append(freq[count * HALF + at : count * HALF + at + SUB] * factors)
    return parts


def correlate(own, other, count, table):
    width = own.shape[1] // 2
    a_re, a_im = own[:, :width], own[:, width:]
    b_re, b_im = other[:, :width], other[:, width:]
    product = jnp.concatenate([a_re * b_re + a_im * b_im, a_im * b_re - a_re * b_im], axis=1)
    rows = mm(product.astype(jnp.bfloat16), table)
    sub = lax.broadcasted_iota(jnp.int32, (SUB, width), 0)
    at = count * HALF
    blocks = []
    for p in range(count):
        block = rows[p * HALF : (p + 1) * HALF]
        first = rows[at + p : at + p + 1, :width]
        middle = rows[at + SUB + p : at + SUB + p + 1, :width]
        parts = [
            jnp.where(sub == 0, first, block[:SUB, :width]),
            block[SUB:, :width],
            jnp.where(sub == 0, middle, block[:SUB, width:]),
            block[SUB:, width:],
        ]
        blocks.append(jnp.concatenate(parts, axis=0).astype(jnp.bfloat16))
    return blocks


def window_at(ref, row_at, col_at, height):
    block = lax.div(col_at, LANES)
    shift = lax.rem(col_at, LANES)
    left = ref[block, pl.ds(row_at, height), :]
    right = ref[block + 1, pl.ds(row_at, height), :]
    lane = lax.broadcasted_iota(jnp.int32, (height, LANES), 1)
    return pltpu.roll(jnp.where(lane >= shift, left, right), lax.rem(LANES - shift, LANES), 1)


def unit_windows(unit, bands, offsets, peaks, ext):
    off_row = HALO + DS * offsets[0, 0, 0]
    off_col = LANES + DS * offsets[0, 0, 1]
    windows = []
    for i in range(bands):
        pair = []
        for h in range(2):
            column = 2 * unit + h
            row_at = off_row + i * P_SIZE + peaks[0, i, 0, column]
            col_at = off_col + column * P_SIZE + peaks[0, i, 1, column]
            pair.append(window_at(ext, row_at, col_at, P_SIZE).astype(jnp.bfloat16))
        windows.append(jnp.concatenate(pair, axis=1))
    return windows


def unit_keep(unit, bands, keep):
    sub = sublanes()
    flags = jnp.zeros((SUB, LANES), jnp.float32)
    for i in range(bands):
        for h in range(2):
            flag = keep[0, i, 2 * unit + h].astype(jnp.float32)
            flags = jnp.where(sub == 2 * i + h, flag, flags)
    return flags


def match_unit(bands, gains, windows, flags, own, row_tab, col_tab, inv_tab, write):
    blocks = []
    for window in windows:
        rows = mm(row_tab[:P_SIZE, :], window)
        blocks += [rows[:, :P_SIZE], rows[:, P_SIZE:]]
    yield
    freq, power = spectrum(blocks, col_tab[...])
    yield
    gain = gains[0] * gains[1]
    scale = (P_SIZE * P_SIZE / gain) ** 2 / P_SIZE
    factors = flags * (scale / jnp.sqrt(power * (1.0 / gain**2) + EPSILON))
    rows = correlate(own, freq, 2 * bands, col_tab[...])
    yield
    for i in range(bands):
        maps = mm(inv_tab[...], jnp.concatenate(rows[2 * i : 2 * i + 2], axis=1))
        for h in range(2):
            p = 2 * i + h
            write(i, h, maps[:, h * P_SIZE : (h + 1) * P_SIZE] * factors[p : p + 1])


def run(*stages):
    parts = list(stages)
    while parts:
        parts = [part for part in parts if next(part, True) is None]


def split(x):
    hi = x.astype(jnp.bfloat16)
    return hi, (x - hi.astype(jnp.float32)).astype(jnp.bfloat16)


def pooled(hi, lo, pool):
    span = pool.shape[0]
    parts = []
    for at in range(0, hi.shape[1], span):
        sums = mm(hi[:, at : at + span], pool) + mm(lo[:, at : at + span], pool)
        parts.append((sums * (1.0 / (DS * DS))).astype(jnp.bfloat16))
    return parts


def exchange_kernel(
    bands,
    units,
    gains,
    offsets_hbm,
    peaks_hbm,
    keep_hbm,
    img,
    row_hbm,
    col_hbm,
    inv_hbm,
    wide_hbm,
    pool_hbm,
    maps,
    coarse,
    windows,
    last_spec,
    flags,
    row_tab,
    col_tab,
    inv_tab,
    own,
    land,
    ext,
    spec,
    small_own,
    small_land,
    small,
    small_spec,
    own_hi,
    own_lo,
    sum_hi,
    sum_lo,
    wide_tab,
    pool,
    offsets,
    peaks,
    keep,
    relayed,
    send_sems,
    recv_sems,
    side_send,
    side_recv,
    relay_sems,
    local_sems,
):
    s = lax.axis_index("sec")
    t = lax.axis_index("tile")
    ns = lax.axis_size("sec")
    nt = lax.axis_size("tile")
    rows, width = own.shape
    columns = width // LANES
    centre = rows - 2 * HALO
    reach = rows + 2 * HALO
    row_gain, col_gain, wide_gain = gains
    early = 3
    detours = (columns // 2, columns // 2 + 1)

    sends = s < ns - 1
    receives = s > 0
    has_up = t > 0
    has_down = t < nt - 1
    s_next = jnp.minimum(s + 1, ns - 1)
    s_prev = jnp.maximum(s - 1, 0)
    t_next = jnp.minimum(t + 1, nt - 1)
    t_prev = jnp.maximum(t - 1, 0)

    eighth = lax.rem(s, 8)
    starts_relay = (eighth == 3) & (s + 4 < ns)
    relays = eighth == 7
    ends_relay = (eighth == 4) & (s + 3 < ns)
    relay_from = jnp.maximum(s - 4, 0)
    relay_by = jnp.minimum(s + 4, ns - 1)
    relay_to = jnp.maximum(s - 3, 0)
    relayed_by = jnp.minimum(s + 3, ns - 1)

    barrier = pltpu.get_barrier_semaphore()
    for cond, peer in (
        (receives, (s_prev, t)),
        (ends_relay, (relayed_by, t)),
        (relays, (relay_from, t)),
        (has_up, (s, t_prev)),
        (has_down, (s, t_next)),
    ):

        @pl.when(cond)
        def _(peer=peer):
            pl.semaphore_signal(barrier, inc=1, device_id=peer, device_id_type=MESH)

    loads = [
        pltpu.make_async_copy(source, target, local_sems.at[n])
        for n, (source, target) in enumerate(
            (
                (img, own),
                (row_hbm, row_tab),
                (col_hbm, col_tab),
                (inv_hbm, inv_tab),
                (wide_hbm, wide_tab),
                (pool_hbm, pool),
                (offsets_hbm, offsets),
                (peaks_hbm, peaks),
                (keep_hbm, keep),
            )
        )
    ]
    for load in loads:
        load.start()
    peers = sum(jnp.where(cond, 1, 0) for cond in (sends, starts_relay, relays, has_up, has_down))
    pl.semaphore_wait(barrier, peers)

    def edge_copy(n):
        start = n * (rows - HALO)
        return pltpu.make_async_remote_copy(
            src_ref=img.at[pl.ds(start, HALO)],
            dst_ref=land.at[pl.ds(HALO + start, HALO)],
            send_sem=send_sems.at[n],
            recv_sem=recv_sems.at[n],
            device_id=(s_next, t),
            device_id_type=MESH,
        )

    def column_copy(c):
        at = pl.multiple_of(c * LANES, LANES)
        return pltpu.make_async_remote_copy(
            src_ref=img.at[pl.ds(HALO, centre), pl.ds(at, LANES)],
            dst_ref=land.at[pl.ds(2 * HALO, centre), pl.ds(at, LANES)],
            send_sem=send_sems.at[3 + c],
            recv_sem=recv_sems.at[3 + c],
            device_id=(s_next, t),
            device_id_type=MESH,
        )

    def relay_in(n):
        return pltpu.make_async_remote_copy(
            src_ref=img.at[pl.ds(HALO, centre), pl.ds(detours[n] * LANES, LANES)],
            dst_ref=relayed.at[n],
            send_sem=send_sems.at[3 + detours[n]],
            recv_sem=relay_sems.at[n],
            device_id=(relay_by, t),
            device_id_type=MESH,
        )

    def relay_out(n):
        return pltpu.make_async_remote_copy(
            src_ref=relayed.at[n],
            dst_ref=land.at[pl.ds(2 * HALO, centre), pl.ds(detours[n] * LANES, LANES)],
            send_sem=relay_sems.at[2 + n],
            recv_sem=recv_sems.at[3 + detours[n]],
            device_id=(relay_to, t),
            device_id_type=MESH,
        )

    def small_copy():
        return pltpu.make_async_remote_copy(
            src_ref=small_own.at[pl.ds(COARSE, small_land.shape[0]), pl.ds(LANES, LANES)],
            dst_ref=small_land,
            send_sem=send_sems.at[2],
            recv_sem=recv_sems.at[2],
            device_id=(s_next, t),
            device_id_type=MESH,
        )

    def side_copy(n):
        source, target, peer = ((HALO, HALO + rows, t_prev), (rows, 0, t_next))[n]
        return pltpu.make_async_remote_copy(
            src_ref=land.at[pl.ds(source, HALO)],
            dst_ref=land.at[pl.ds(target, HALO)],
            send_sem=side_send.at[n],
            recv_sem=side_recv.at[n],
            device_id=(s, peer),
            device_id_type=MESH,
        )

    @pl.when(sends)
    def _():
        edge_copy(0).start()
        edge_copy(1).start()
        for c in range(early):
            if c not in detours:
                column_copy(c).start()

    @pl.when(starts_relay)
    def _():
        for n in range(len(detours)):
            relay_in(n).start()

    @pl.when(sends & jnp.logical_not(starts_relay))
    def _():
        for c in range(early):
            if c in detours:
                column_copy(c).start()

    @pl.when(jnp.logical_not(receives))
    def _():
        land[...] = jnp.zeros_like(land)
        small_land[...] = jnp.zeros_like(small_land)

    @pl.when(receives & jnp.logical_not(has_up))
    def _():
        land[:HALO, :] = jnp.zeros((HALO, width), jnp.bfloat16)

    @pl.when(receives & jnp.logical_not(has_down))
    def _():
        land[HALO + rows :, :] = jnp.zeros((HALO, width), jnp.bfloat16)

    ext[0] = jnp.zeros((reach, LANES), jnp.float32)
    ext[columns + 1] = jnp.zeros((reach, LANES), jnp.float32)
    small[0] = jnp.zeros(small.shape[1:], jnp.float32)
    small[3] = jnp.zeros(small.shape[1:], jnp.float32)
    for load in loads:
        load.wait()

    def own_unit(u, carry):
        at = pl.multiple_of(u * PAIR, PAIR)
        blocks = []
        for i in range(bands):
            both = mm(row_tab[...], own[i * P_SIZE : (i + 1) * P_SIZE, pl.ds(at, PAIR)])
            blocks += [both[:P_SIZE, :P_SIZE], both[:P_SIZE, P_SIZE:]]
            hi, lo = split(both[P_SIZE:])
            own_hi[i * POOLED : (i + 1) * POOLED, pl.ds(at, PAIR)] = hi
            own_lo[i * POOLED : (i + 1) * POOLED, pl.ds(at, PAIR)] = lo
        freq, power = spectrum(blocks, col_tab[...])
        gain = row_gain * col_gain
        factors = (1.0 / gain) / jnp.sqrt(power * (1.0 / gain**2) + EPSILON)
        base = 0
        for part in scaled(freq, 2 * bands, factors):
            spec[u, base : base + part.shape[0], :] = part
            base += part.shape[0]
        return carry

    lax.fori_loop(0, units, own_unit, 0)
    for n, part in enumerate(pooled(own_hi[...], own_lo[...], pool[...])):
        small_own[:, n * LANES : (n + 1) * LANES] = part

    @pl.when(sends)
    def _():
        small_copy().start()

    @pl.when(sends & jnp.logical_not(starts_relay))
    def _():
        for c in range(early, columns):
            if c in detours:
                column_copy(c).start()

    @pl.when(sends)
    def _():
        for c in range(early, columns):
            if c not in detours:
                column_copy(c).start()

    @pl.when(receives)
    def _():
        edge_copy(0).wait_recv()

        @pl.when(has_up)
        def _():
            side_copy(0).start()

        edge_copy(1).wait_recv()

        @pl.when(has_down)
        def _():
            side_copy(1).start()

    last_spec[...] = spec[units - 1]
    flags[...] = unit_keep(units - 1, bands, keep)
    freq, power = spectrum([mm(row_tab[:P_SIZE, :], small_own[...])], wide_tab[...])
    gain = row_gain * wide_gain
    factors = (1.0 / gain) / jnp.sqrt(power * (1.0 / gain**2) + EPSILON)
    base = 0
    for part in scaled(freq, 1, factors):
        small_spec[base : base + part.shape[0], :] = part
        base += part.shape[0]

    @pl.when(receives)
    def _():
        @pl.when(has_up)
        def _():
            side_copy(1).wait_recv()

        @pl.when(has_down)
        def _():
            side_copy(0).wait_recv()

    for at in (0, HALO + rows - HALO):
        for c in range(columns):
            ext[c + 1, at : at + 2 * HALO, :] = land[
                at : at + 2 * HALO, c * LANES : (c + 1) * LANES
            ].astype(jnp.float32)

    def row_sums(c, at, count):
        sums = ext[c + 1, pl.ds(at, count, stride=DS), :]
        for k in range(1, DS):
            sums = sums + ext[c + 1, pl.ds(at + k, count, stride=DS), :]
        return split(sums)

    def arrive(c):
        @pl.when(receives)
        def _():
            column_copy(c).wait_recv()

        at = pl.multiple_of(c * LANES, LANES)
        ext[c + 1, 2 * HALO : 2 * HALO + centre, :] = land[
            2 * HALO : 2 * HALO + centre, pl.ds(at, LANES)
        ].astype(jnp.float32)

    def coarse_map():
        half = columns // 2
        first = HALO - DS * COARSE
        count = small.shape[1]
        for c in range(half):
            hi, lo = row_sums(c, first, count)
            sum_hi[:, c * LANES : (c + 1) * LANES] = hi
            sum_lo[:, c * LANES : (c + 1) * LANES] = lo
        small[1] = pooled(sum_hi[...], sum_lo[...], pool[...])[0].astype(jnp.float32)
        side = 2 * COARSE
        for c in range(half):
            for n, at in enumerate((first, first + DS * (count - side))):
                hi, lo = row_sums(half + c, at, side)
                sum_hi[n * side : (n + 1) * side, c * LANES : (c + 1) * LANES] = hi
                sum_lo[n * side : (n + 1) * side, c * LANES : (c + 1) * LANES] = lo

        ends = pooled(sum_hi[: 2 * side], sum_lo[: 2 * side], pool[...])[0].astype(jnp.float32)
        small[2, :side] = ends[:side]
        small[2, side : count - side] = small_land[...].astype(jnp.float32)
        small[2, count - side :] = ends[side:]
        yield
        height = count - 2 * COARSE
        window = [
            window_at(
                small, COARSE + offsets[0, 0, 0], LANES * (n + 1) + offsets[0, 0, 1], height
            ).astype(jnp.bfloat16)
            for n in range(2)
        ]
        block = mm(row_tab[:P_SIZE, :], jnp.concatenate(window, axis=1))
        yield
        freq, power = spectrum([block], wide_tab[...])
        yield
        gain = row_gain * wide_gain
        size = height * 2 * LANES
        scale = (size / gain) ** 2 / math.sqrt(size)
        factors = scale / jnp.sqrt(power * (1.0 / gain**2) + EPSILON)
        found = correlate(small_spec[...], freq, 1, wide_tab[...])[0]
        yield
        coarse[...] = mm(inv_tab[...], found) * factors[0:1]

    def unit_step(u):
        def write(i, h, value):
            at = u * PAIR + h * P_SIZE
            maps[i * P_SIZE : (i + 1) * P_SIZE, at : at + P_SIZE] = value

        return match_unit(
            bands,
            (row_gain, col_gain),
            unit_windows(u, bands, offsets, peaks, ext),
            unit_keep(u, bands, keep),
            spec[u],
            row_tab,
            col_tab,
            inv_tab,
            write,
        )

    arrive(0)
    for u in range(units - 1):
        arrive(2 * u + 1)
        arrive(2 * u + 2)
        if u == columns // 4 - 1:

            @pl.when(receives)
            def _():
                small_copy().wait_recv()

            run(coarse_map(), unit_step(u))
        else:
            run(unit_step(u))
        if u == 0:

            @pl.when(relays)
            def _():
                for n in range(len(detours)):
                    relay_in(n).wait_recv()
                    relay_out(n).start()

    @pl.when(receives & has_up)
    def _():
        side_copy(0).wait_send()

    @pl.when(receives & has_down)
    def _():
        side_copy(1).wait_send()

    @pl.when(sends)
    def _():
        edge_copy(0).wait_send()
        edge_copy(1).wait_send()
        small_copy().wait_send()
        for c in range(columns):
            column_copy(c).wait_send()

    @pl.when(relays)
    def _():
        for n in range(len(detours)):
            relay_out(n).wait_send()

    arrive(columns - 1)
    for i, window in enumerate(unit_windows(units - 1, bands, offsets, peaks, ext)):
        windows[i] = window


def finish_kernel(
    bands,
    gains,
    maps,
    coarse,
    windows,
    last_spec,
    flags,
    row_tab,
    col_tab,
    inv_tab,
    coarse_out,
    flow_out,
    last_maps,
    sems,
):
    done = maps.shape[1]
    copies = [pltpu.make_async_copy(coarse, coarse_out.at[0], sems.at[2 * bands])]
    for i in range(bands):
        band = pl.ds(i * P_SIZE, P_SIZE)
        copies.append(pltpu.make_async_copy(maps.at[band], flow_out.at[0, band, pl.ds(0, done)], sems.at[i]))
    for copy in copies:
        copy.start()

    def write(i, h, value):
        last_maps[i * P_SIZE : (i + 1) * P_SIZE, h * P_SIZE : (h + 1) * P_SIZE] = value

    run(
        match_unit(
            bands,
            gains[:2],
            [windows[i] for i in range(bands)],
            flags[...],
            last_spec[...],
            row_tab,
            col_tab,
            inv_tab,
            write,
        )
    )
    for i in range(bands):
        band = pl.ds(i * P_SIZE, P_SIZE)
        copies.append(
            pltpu.make_async_copy(last_maps.at[band], flow_out.at[0, band, pl.ds(done, PAIR)], sems.at[bands + i])
        )
        copies[-1].start()
    for copy in copies:
        copy.wait()


def shards(section_image, offsets, peak_shift, accepted):
    own = section_image[0]
    rows, width = own.shape
    bands = rows // P_SIZE
    units = width // PAIR
    columns = width // LANES
    reach = rows + 2 * HALO
    small_width = width // DS
    forward_row, inverse_row, row_gain = row_tables()
    col, col_gain = col_table(P_SIZE)
    wide, wide_gain = col_table(small_width)
    gains = (float(row_gain), float(col_gain), float(wide_gain))
    span = DS * LANES
    pool = quantized(np.arange(span)[:, None] // DS == np.arange(LANES)[None, :])
    tables = [jnp.asarray(x) for x in (forward_row, col, inverse_row, wide, pool)]
    scalars = (offsets, jnp.swapaxes(peak_shift, 2, 3), accepted)
    high = 2 * bands * HALF + 2 * SUB
    small_high = HALF + 2 * SUB
    small_rows = rows // DS + 2 * COARSE
    hbm = pl.BlockSpec(memory_space=pltpu.HBM)
    vmem = pl.BlockSpec(memory_space=pltpu.VMEM)
    limit = 30 * 2**20
    operands = [pltpu.with_memory_space_constraint(x, pltpu.HBM) for x in (*scalars, own, *tables)]
    between = pl.pallas_call(
        functools.partial(exchange_kernel, bands, units, gains),
        name="exchange",
        out_shape=(
            jax.ShapeDtypeStruct((rows, width - PAIR), jnp.float32),
            jax.ShapeDtypeStruct((rows // DS, small_width), jnp.float32),
            jax.ShapeDtypeStruct((bands, P_SIZE, PAIR), jnp.bfloat16),
            jax.ShapeDtypeStruct((high, PAIR), jnp.float32),
            jax.ShapeDtypeStruct((SUB, LANES), jnp.float32),
        )
        + tuple(jax.ShapeDtypeStruct(x.shape, x.dtype) for x in tables[:3]),
        in_specs=[hbm] * 9,
        out_specs=(vmem,) * 8,
        scratch_shapes=[
            pltpu.VMEM((rows, width), jnp.bfloat16),
            pltpu.VMEM((reach, width), jnp.bfloat16),
            pltpu.VMEM((columns + 2, reach, LANES), jnp.float32),
            pltpu.VMEM((units, high, PAIR), jnp.float32),
            pltpu.VMEM((rows // DS, small_width), jnp.bfloat16),
            pltpu.VMEM((rows // DS - 2 * COARSE, LANES), jnp.bfloat16),
            pltpu.VMEM((small_width // LANES + 2, small_rows, LANES), jnp.float32),
            pltpu.VMEM((small_high, 2 * small_width), jnp.float32),
            pltpu.VMEM((rows // DS, width), jnp.bfloat16),
            pltpu.VMEM((rows // DS, width), jnp.bfloat16),
            pltpu.VMEM((small_rows, span), jnp.bfloat16),
            pltpu.VMEM((small_rows, span), jnp.bfloat16),
            pltpu.VMEM(wide.shape, jnp.bfloat16),
            pltpu.VMEM(pool.shape, jnp.bfloat16),
        ]
        + [pltpu.SMEM(x.shape, jnp.int32) for x in scalars]
        + [
            pltpu.VMEM((2, rows - 2 * HALO, LANES), jnp.bfloat16),
            pltpu.SemaphoreType.DMA((columns + 3,)),
            pltpu.SemaphoreType.DMA((columns + 3,)),
            pltpu.SemaphoreType.DMA((2,)),
            pltpu.SemaphoreType.DMA((2,)),
            pltpu.SemaphoreType.DMA((4,)),
            pltpu.SemaphoreType.DMA((len(operands),)),
        ],
        compiler_params=pltpu.CompilerParams(
            collective_id=0, has_side_effects=True, vmem_limit_bytes=limit
        ),
    )(*operands)
    return pl.pallas_call(
        functools.partial(finish_kernel, bands, gains),
        name="finish",
        out_shape=(
            jax.ShapeDtypeStruct((1, rows // DS, small_width), jnp.float32),
            jax.ShapeDtypeStruct((1, rows, width), jnp.float32),
        ),
        in_specs=[vmem] * 8,
        out_specs=(hbm, hbm),
        scratch_shapes=[
            pltpu.VMEM((rows, PAIR), jnp.float32),
            pltpu.SemaphoreType.DMA((2 * bands + 1,)),
        ],
        compiler_params=pltpu.CompilerParams(vmem_limit_bytes=limit),
    )(*between)


def solution(mesh):
    return jax.shard_map(
        shards,
        mesh=mesh,
        in_specs=(
            P("sec", "tile", None),
            P("sec", "tile", None),
            P("sec", "tile", None, None),
            P("sec", "tile", None),
        ),
        out_specs=(P("sec", "tile", None), P("sec", "tile", None)),
        check_vma=False,
    )
```

```python
import functools
import math

import jax
import jax.numpy as jnp
import ml_dtypes
import numpy as np
from jax import lax
from jax.experimental import pallas as pl
from jax.experimental.pallas import tpu as pltpu
from jax.sharding import PartitionSpec as P

P_SIZE = 128
HALF = P_SIZE // 2
DS = 4
COARSE = 16
HALO = 80
LANES = 128
PAIR = 2 * P_SIZE
SUB = 8
POOLED = P_SIZE // DS
EPSILON = 1e-05
MESH = pl.DeviceIdType.MESH


def quantized(table):
    return table.astype(np.float32).astype(ml_dtypes.bfloat16)


def table_scale(n):
    cosines = np.cos(2.0 * np.pi * np.arange(n) / n)
    best = None
    for factor in np.linspace(1.0, 2.0, 4001):
        table = quantized(cosines * factor).astype(np.float64)
        gain = (table @ cosines) / (cosines @ cosines)
        error = np.mean((table / gain - cosines) ** 2)
        if best is None or error < best[0]:
            best = (error, factor, gain)
    return best[1], best[2]


def waves(n):
    k = np.arange(n)
    angles = (k[:, None] * k[None, :] % n) * (2.0 * np.pi / n)
    return np.cos(angles), np.sin(angles)


def row_tables():
    n = P_SIZE
    factor, gain = table_scale(n)
    cosines, sines = waves(n)
    alternating = np.where(np.arange(n) % 2 == 0, 1.0, -1.0)
    forward = np.concatenate([cosines[:HALF], sines[:HALF]])
    forward[HALF] = alternating
    weight = np.where(np.arange(HALF) == 0, 1.0, 2.0)[:, None]
    inverse = np.concatenate([cosines[:HALF] * weight, -sines[:HALF] * weight])
    inverse[HALF] = alternating
    pool = (np.arange(POOLED)[:, None] == np.arange(n)[None, :] // DS).astype(np.float64)
    forward = np.concatenate([forward * (factor / n), pool])
    return quantized(forward), quantized(inverse.T * (factor / n)), gain


def col_table(n):
    factor, gain = table_scale(n)
    cosines, sines = waves(n)
    table = np.block([[cosines, sines], [-sines, cosines]]) * (factor / n)
    return quantized(table), gain


def mm(a, b):
    return jnp.dot(a, b, preferred_element_type=jnp.float32)


def sublanes():
    return lax.broadcasted_iota(jnp.int32, (SUB, LANES), 0)


def to_lhs(rows):
    return jnp.concatenate([rows[:HALF], rows[HALF:]], axis=1).astype(jnp.bfloat16)


def energy(block):
    width = block.shape[1] // 2
    total = block[:, :width] * block[:, :width] + block[:, width:] * block[:, width:]
    head = jnp.where(lax.broadcasted_iota(jnp.int32, (SUB, width), 0) == 0, 0.0, total[:SUB])
    for at in range(SUB, HALF, SUB):
        head = head + total[at : at + SUB]
    return jnp.sum(head, axis=0, keepdims=True)


def spectrum(blocks, table):
    count = len(blocks)
    width = blocks[0].shape[1]
    sub = lax.broadcasted_iota(jnp.int32, (SUB, width), 0)
    first = jnp.zeros((SUB, width), jnp.float32)
    middle = jnp.zeros((SUB, width), jnp.float32)
    for p, rows in enumerate(blocks):
        first = jnp.where(sub == p, rows[0:1], first)
        middle = jnp.where(sub == p, rows[HALF : HALF + 1], middle)
    first = first - jnp.sum(first, axis=1, keepdims=True) * (1.0 / width)
    ends = jnp.concatenate([first, middle], axis=0)
    ends = jnp.concatenate([ends, jnp.zeros_like(ends)], axis=1).astype(jnp.bfloat16)
    freq = mm(jnp.concatenate([to_lhs(rows) for rows in blocks] + [ends], axis=0), table)
    power = jnp.zeros((SUB, width), jnp.float32)
    for p in range(count):
        power = jnp.where(sub == p, energy(freq[p * HALF : (p + 1) * HALF]), power)
    tail = freq[count * HALF :] * freq[count * HALF :]
    tail = tail[:SUB] + tail[SUB:]
    power = 2.0 * power + tail[:, :width] + tail[:, width:]
    return freq, jnp.sum(power, axis=1, keepdims=True)


def scaled(freq, count, factors):
    parts = [freq[p * HALF : (p + 1) * HALF] * factors[p : p + 1] for p in range(count)]
    for at in (0, SUB):
        parts.append(freq[count * HALF + at : count * HALF + at + SUB] * factors)
    return parts


def correlate(own, other, count, table):
    width = own.shape[1] // 2
    a_re, a_im = own[:, :width], own[:, width:]
    b_re, b_im = other[:, :width], other[:, width:]
    product = jnp.concatenate([a_re * b_re + a_im * b_im, a_im * b_re - a_re * b_im], axis=1)
    rows = mm(product.astype(jnp.bfloat16), table)
    sub = lax.broadcasted_iota(jnp.int32, (SUB, width), 0)
    at = count * HALF
    blocks = []
    for p in range(count):
        block = rows[p * HALF : (p + 1) * HALF]
        first = rows[at + p : at + p + 1, :width]
        middle = rows[at + SUB + p : at + SUB + p + 1, :width]
        parts = [
            jnp.where(sub == 0, first, block[:SUB, :width]),
            block[SUB:, :width],
            jnp.where(sub == 0, middle, block[:SUB, width:]),
            block[SUB:, width:],
        ]
        blocks.append(jnp.concatenate(parts, axis=0).astype(jnp.bfloat16))
    return blocks


def window_at(ref, row_at, col_at, height):
    block = lax.div(col_at, LANES)
    shift = lax.rem(col_at, LANES)
    left = ref[block, pl.ds(row_at, height), :]
    right = ref[block + 1, pl.ds(row_at, height), :]
    lane = lax.broadcasted_iota(jnp.int32, (height, LANES), 1)
    return pltpu.roll(jnp.where(lane >= shift, left, right), lax.rem(LANES - shift, LANES), 1)


def unit_windows(unit, bands, offsets, peaks, ext):
    off_row = HALO + DS * offsets[0, 0, 0]
    off_col = LANES + DS * offsets[0, 0, 1]
    windows = []
    for i in range(bands):
        pair = []
        for h in range(2):
            column = 2 * unit + h
            row_at = off_row + i * P_SIZE + peaks[0, i, 0, column]
            col_at = off_col + column * P_SIZE + peaks[0, i, 1, column]
            pair.append(window_at(ext, row_at, col_at, P_SIZE).astype(jnp.bfloat16))
        windows.append(jnp.concatenate(pair, axis=1))
    return windows


def unit_keep(unit, bands, keep):
    sub = sublanes()
    flags = jnp.zeros((SUB, LANES), jnp.float32)
    for i in range(bands):
        for h in range(2):
            flag = keep[0, i, 2 * unit + h].astype(jnp.float32)
            flags = jnp.where(sub == 2 * i + h, flag, flags)
    return flags


def match_unit(bands, gains, windows, flags, own, row_tab, col_tab, inv_tab, write):
    blocks = []
    for window in windows:
        rows = mm(row_tab[:P_SIZE, :], window)
        blocks += [rows[:, :P_SIZE], rows[:, P_SIZE:]]
    yield
    freq, power = spectrum(blocks, col_tab[...])
    yield
    gain = gains[0] * gains[1]
    scale = (P_SIZE * P_SIZE / gain) ** 2 / P_SIZE
    factors = flags * (scale / jnp.sqrt(power * (1.0 / gain**2) + EPSILON))
    rows = correlate(own, freq, 2 * bands, col_tab[...])
    yield
    for i in range(bands):
        maps = mm(inv_tab[...], jnp.concatenate(rows[2 * i : 2 * i + 2], axis=1))
        for h in range(2):
            p = 2 * i + h
            write(i, h, maps[:, h * P_SIZE : (h + 1) * P_SIZE] * factors[p : p + 1])


def run(*stages):
    parts = list(stages)
    while parts:
        parts = [part for part in parts if next(part, True) is None]


def split(x):
    hi = x.astype(jnp.bfloat16)
    return hi, (x - hi.astype(jnp.float32)).astype(jnp.bfloat16)


def pooled(hi, lo, pool):
    span = pool.shape[0]
    parts = []
    for at in range(0, hi.shape[1], span):
        sums = mm(hi[:, at : at + span], pool) + mm(lo[:, at : at + span], pool)
        parts.append((sums * (1.0 / (DS * DS))).astype(jnp.bfloat16))
    return parts


def exchange_kernel(
    bands,
    units,
    gains,
    offsets_hbm,
    peaks_hbm,
    keep_hbm,
    img,
    row_hbm,
    col_hbm,
    inv_hbm,
    wide_hbm,
    pool_hbm,
    maps,
    coarse,
    windows,
    last_spec,
    flags,
    row_tab,
    col_tab,
    inv_tab,
    own,
    land,
    ext,
    spec,
    small_own,
    small_land,
    small,
    small_spec,
    own_hi,
    own_lo,
    sum_hi,
    sum_lo,
    wide_tab,
    pool,
    offsets,
    peaks,
    keep,
    relayed,
    send_sems,
    recv_sems,
    side_send,
    side_recv,
    relay_sems,
    local_sems,
):
    s = lax.axis_index("sec")
    t = lax.axis_index("tile")
    ns = lax.axis_size("sec")
    nt = lax.axis_size("tile")
    rows, width = own.shape
    columns = width // LANES
    centre = rows - 2 * HALO
    reach = rows + 2 * HALO
    row_gain, col_gain, wide_gain = gains
    early = 3
    detours = (columns // 2, columns // 2 + 1)

    sends = s < ns - 1
    receives = s > 0
    has_up = t > 0
    has_down = t < nt - 1
    s_next = jnp.minimum(s + 1, ns - 1)
    s_prev = jnp.maximum(s - 1, 0)
    t_next = jnp.minimum(t + 1, nt - 1)
    t_prev = jnp.maximum(t - 1, 0)

    eighth = lax.rem(s, 8)
    starts_relay = (eighth == 3) & (s + 4 < ns)
    relays = eighth == 7
    ends_relay = (eighth == 4) & (s + 3 < ns)
    relay_from = jnp.maximum(s - 4, 0)
    relay_by = jnp.minimum(s + 4, ns - 1)
    relay_to = jnp.maximum(s - 3, 0)
    relayed_by = jnp.minimum(s + 3, ns - 1)

    barrier = pltpu.get_barrier_semaphore()
    for cond, peer in (
        (receives, (s_prev, t)),
        (ends_relay, (relayed_by, t)),
        (relays, (relay_from, t)),
        (has_up, (s, t_prev)),
        (has_down, (s, t_next)),
    ):

        @pl.when(cond)
        def _(peer=peer):
            pl.semaphore_signal(barrier, inc=1, device_id=peer, device_id_type=MESH)

    loads = [
        pltpu.make_async_copy(source, target, local_sems.at[n])
        for n, (source, target) in enumerate(
            (
                (img, own),
                (row_hbm, row_tab),
                (col_hbm, col_tab),
                (inv_hbm, inv_tab),
                (wide_hbm, wide_tab),
                (pool_hbm, pool),
                (offsets_hbm, offsets),
                (peaks_hbm, peaks),
                (keep_hbm, keep),
            )
        )
    ]
    for load in loads:
        load.start()
    peers = sum(jnp.where(cond, 1, 0) for cond in (sends, starts_relay, relays, has_up, has_down))
    pl.semaphore_wait(barrier, peers)

    def edge_copy(n):
        start = n * (rows - HALO)
        return pltpu.make_async_remote_copy(
            src_ref=img.at[pl.ds(start, HALO)],
            dst_ref=land.at[pl.ds(HALO + start, HALO)],
            send_sem=send_sems.at[n],
            recv_sem=recv_sems.at[n],
            device_id=(s_next, t),
            device_id_type=MESH,
        )

    def column_copy(c):
        at = pl.multiple_of(c * LANES, LANES)
        return pltpu.make_async_remote_copy(
            src_ref=img.at[pl.ds(HALO, centre), pl.ds(at, LANES)],
            dst_ref=land.at[pl.ds(2 * HALO, centre), pl.ds(at, LANES)],
            send_sem=send_sems.at[3 + c],
            recv_sem=recv_sems.at[3 + c],
            device_id=(s_next, t),
            device_id_type=MESH,
        )

    def relay_in(n):
        return pltpu.make_async_remote_copy(
            src_ref=img.at[pl.ds(HALO, centre), pl.ds(detours[n] * LANES, LANES)],
            dst_ref=relayed.at[n],
            send_sem=send_sems.at[3 + detours[n]],
            recv_sem=relay_sems.at[n],
            device_id=(relay_by, t),
            device_id_type=MESH,
        )

    def relay_out(n):
        return pltpu.make_async_remote_copy(
            src_ref=relayed.at[n],
            dst_ref=land.at[pl.ds(2 * HALO, centre), pl.ds(detours[n] * LANES, LANES)],
            send_sem=relay_sems.at[2 + n],
            recv_sem=recv_sems.at[3 + detours[n]],
            device_id=(relay_to, t),
            device_id_type=MESH,
        )

    def small_copy():
        return pltpu.make_async_remote_copy(
            src_ref=small_own.at[pl.ds(COARSE, small_land.shape[0]), pl.ds(LANES, LANES)],
            dst_ref=small_land,
            send_sem=send_sems.at[2],
            recv_sem=recv_sems.at[2],
            device_id=(s_next, t),
            device_id_type=MESH,
        )

    def side_copy(n):
        source, target, peer = ((HALO, HALO + rows, t_prev), (rows, 0, t_next))[n]
        return pltpu.make_async_remote_copy(
            src_ref=land.at[pl.ds(source, HALO)],
            dst_ref=land.at[pl.ds(target, HALO)],
            send_sem=side_send.at[n],
            recv_sem=side_recv.at[n],
            device_id=(s, peer),
            device_id_type=MESH,
        )

    @pl.when(sends)
    def _():
        edge_copy(0).start()
        edge_copy(1).start()
        for c in range(early):
            if c not in detours:
                column_copy(c).start()

    @pl.when(starts_relay)
    def _():
        for n in range(len(detours)):
            relay_in(n).start()

    @pl.when(sends & jnp.logical_not(starts_relay))
    def _():
        for c in range(early):
            if c in detours:
                column_copy(c).start()

    @pl.when(jnp.logical_not(receives))
    def _():
        land[...] = jnp.zeros_like(land)
        small_land[...] = jnp.zeros_like(small_land)

    @pl.when(receives & jnp.logical_not(has_up))
    def _():
        land[:HALO, :] = jnp.zeros((HALO, width), jnp.bfloat16)

    @pl.when(receives & jnp.logical_not(has_down))
    def _():
        land[HALO + rows :, :] = jnp.zeros((HALO, width), jnp.bfloat16)

    ext[0] = jnp.zeros((reach, LANES), jnp.float32)
    ext[columns + 1] = jnp.zeros((reach, LANES), jnp.float32)
    small[0] = jnp.zeros(small.shape[1:], jnp.float32)
    small[3] = jnp.zeros(small.shape[1:], jnp.float32)
    for load in loads:
        load.wait()

    def own_unit(u, carry):
        at = pl.multiple_of(u * PAIR, PAIR)
        blocks = []
        for i in range(bands):
            both = mm(row_tab[...], own[i * P_SIZE : (i + 1) * P_SIZE, pl.ds(at, PAIR)])
            blocks += [both[:P_SIZE, :P_SIZE], both[:P_SIZE, P_SIZE:]]
            hi, lo = split(both[P_SIZE:])
            own_hi[i * POOLED : (i + 1) * POOLED, pl.ds(at, PAIR)] = hi
            own_lo[i * POOLED : (i + 1) * POOLED, pl.ds(at, PAIR)] = lo
        freq, power = spectrum(blocks, col_tab[...])
        gain = row_gain * col_gain
        factors = (1.0 / gain) / jnp.sqrt(power * (1.0 / gain**2) + EPSILON)
        base = 0
        for part in scaled(freq, 2 * bands, factors):
            spec[u, base : base + part.shape[0], :] = part
            base += part.shape[0]
        return carry

    lax.fori_loop(0, units, own_unit, 0)
    for n, part in enumerate(pooled(own_hi[...], own_lo[...], pool[...])):
        small_own[:, n * LANES : (n + 1) * LANES] = part

    @pl.when(sends)
    def _():
        small_copy().start()

    @pl.when(sends & jnp.logical_not(starts_relay))
    def _():
        for c in range(early, columns):
            if c in detours:
                column_copy(c).start()

    @pl.when(sends)
    def _():
        for c in range(early, columns):
            if c not in detours:
                column_copy(c).start()

    @pl.when(receives)
    def _():
        edge_copy(0).wait_recv()

        @pl.when(has_up)
        def _():
            side_copy(0).start()

        edge_copy(1).wait_recv()

        @pl.when(has_down)
        def _():
            side_copy(1).start()

    last_spec[...] = spec[units - 1]
    flags[...] = unit_keep(units - 1, bands, keep)
    freq, power = spectrum([mm(row_tab[:P_SIZE, :], small_own[...])], wide_tab[...])
    gain = row_gain * wide_gain
    factors = (1.0 / gain) / jnp.sqrt(power * (1.0 / gain**2) + EPSILON)
    base = 0
    for part in scaled(freq, 1, factors):
        small_spec[base : base + part.shape[0], :] = part
        base += part.shape[0]

    @pl.when(receives)
    def _():
        @pl.when(has_up)
        def _():
            side_copy(1).wait_recv()

        @pl.when(has_down)
        def _():
            side_copy(0).wait_recv()

    for at in (0, HALO + rows - HALO):
        for c in range(columns):
            ext[c + 1, at : at + 2 * HALO, :] = land[
                at : at + 2 * HALO, c * LANES : (c + 1) * LANES
            ].astype(jnp.float32)

    def row_sums(c, at, count):
        sums = ext[c + 1, pl.ds(at, count, stride=DS), :]
        for k in range(1, DS):
            sums = sums + ext[c + 1, pl.ds(at + k, count, stride=DS), :]
        return split(sums)

    def arrive(c):
        @pl.when(receives)
        def _():
            column_copy(c).wait_recv()

        at = pl.multiple_of(c * LANES, LANES)
        ext[c + 1, 2 * HALO : 2 * HALO + centre, :] = land[
            2 * HALO : 2 * HALO + centre, pl.ds(at, LANES)
        ].astype(jnp.float32)

    def coarse_map():
        half = columns // 2
        first = HALO - DS * COARSE
        count = small.shape[1]
        for c in range(half):
            hi, lo = row_sums(c, first, count)
            sum_hi[:, c * LANES : (c + 1) * LANES] = hi
            sum_lo[:, c * LANES : (c + 1) * LANES] = lo
        small[1] = pooled(sum_hi[...], sum_lo[...], pool[...])[0].astype(jnp.float32)
        side = 2 * COARSE
        for c in range(half):
            for n, at in enumerate((first, first + DS * (count - side))):
                hi, lo = row_sums(half + c, at, side)
                sum_hi[n * side : (n + 1) * side, c * LANES : (c + 1) * LANES] = hi
                sum_lo[n * side : (n + 1) * side, c * LANES : (c + 1) * LANES] = lo

        ends = pooled(sum_hi[: 2 * side], sum_lo[: 2 * side], pool[...])[0].astype(jnp.float32)
        small[2, :side] = ends[:side]
        small[2, side : count - side] = small_land[...].astype(jnp.float32)
        small[2, count - side :] = ends[side:]
        yield
        height = count - 2 * COARSE
        window = [
            window_at(
                small, COARSE + offsets[0, 0, 0], LANES * (n + 1) + offsets[0, 0, 1], height
            ).astype(jnp.bfloat16)
            for n in range(2)
        ]
        block = mm(row_tab[:P_SIZE, :], jnp.concatenate(window, axis=1))
        yield
        freq, power = spectrum([block], wide_tab[...])
        yield
        gain = row_gain * wide_gain
        size = height * 2 * LANES
        scale = (size / gain) ** 2 / math.sqrt(size)
        factors = scale / jnp.sqrt(power * (1.0 / gain**2) + EPSILON)
        found = correlate(small_spec[...], freq, 1, wide_tab[...])[0]
        yield
        coarse[...] = mm(inv_tab[...], found) * factors[0:1]

    def unit_step(u):
        def write(i, h, value):
            at = u * PAIR + h * P_SIZE
            at = at if isinstance(u, int) else pl.multiple_of(at, P_SIZE)
            maps[i * P_SIZE : (i + 1) * P_SIZE, pl.ds(at, P_SIZE)] = value

        return match_unit(
            bands,
            (row_gain, col_gain),
            unit_windows(u, bands, offsets, peaks, ext),
            unit_keep(u, bands, keep),
            spec[u],
            row_tab,
            col_tab,
            inv_tab,
            write,
        )

    arrive(0)

    def step(k, carry):
        @pl.when(k == 0)
        def _():
            arrive(1)
            arrive(2)

        @pl.when(k == 1)
        def _():
            arrive(3)
            arrive(4)

            @pl.when(receives)
            def _():
                small_copy().wait_recv()

            run(coarse_map(), unit_step(1))
            arrive(5)
            arrive(6)

        run(unit_step(2 * k))

        @pl.when(relays & (k == 0))
        def _():
            for n in range(len(detours)):
                relay_in(n).wait_recv()
                relay_out(n).start()

        return carry

    lax.fori_loop(0, 2, step, 0)

    @pl.when(receives & has_up)
    def _():
        side_copy(0).wait_send()

    @pl.when(receives & has_down)
    def _():
        side_copy(1).wait_send()

    @pl.when(sends)
    def _():
        edge_copy(0).wait_send()
        edge_copy(1).wait_send()
        small_copy().wait_send()
        for c in range(columns):
            column_copy(c).wait_send()

    @pl.when(relays)
    def _():
        for n in range(len(detours)):
            relay_out(n).wait_send()

    arrive(columns - 1)
    for i, window in enumerate(unit_windows(units - 1, bands, offsets, peaks, ext)):
        windows[i] = window


def finish_kernel(
    bands,
    gains,
    maps,
    coarse,
    windows,
    last_spec,
    flags,
    row_tab,
    col_tab,
    inv_tab,
    coarse_out,
    flow_out,
    last_maps,
    sems,
):
    done = maps.shape[1]
    copies = [pltpu.make_async_copy(coarse, coarse_out.at[0], sems.at[2 * bands])]
    for i in range(bands):
        band = pl.ds(i * P_SIZE, P_SIZE)
        copies.append(pltpu.make_async_copy(maps.at[band], flow_out.at[0, band, pl.ds(0, done)], sems.at[i]))
    for copy in copies:
        copy.start()

    def write(i, h, value):
        last_maps[i * P_SIZE : (i + 1) * P_SIZE, h * P_SIZE : (h + 1) * P_SIZE] = value

    run(
        match_unit(
            bands,
            gains[:2],
            [windows[i] for i in range(bands)],
            flags[...],
            last_spec[...],
            row_tab,
            col_tab,
            inv_tab,
            write,
        )
    )
    for i in range(bands):
        band = pl.ds(i * P_SIZE, P_SIZE)
        copies.append(
            pltpu.make_async_copy(last_maps.at[band], flow_out.at[0, band, pl.ds(done, PAIR)], sems.at[bands + i])
        )
        copies[-1].start()
    for copy in copies:
        copy.wait()


def shards(section_image, offsets, peak_shift, accepted):
    own = section_image[0]
    rows, width = own.shape
    bands = rows // P_SIZE
    units = width // PAIR
    columns = width // LANES
    reach = rows + 2 * HALO
    small_width = width // DS
    forward_row, inverse_row, row_gain = row_tables()
    col, col_gain = col_table(P_SIZE)
    wide, wide_gain = col_table(small_width)
    gains = (float(row_gain), float(col_gain), float(wide_gain))
    span = DS * LANES
    pool = quantized(np.arange(span)[:, None] // DS == np.arange(LANES)[None, :])
    tables = [jnp.asarray(x) for x in (forward_row, col, inverse_row, wide, pool)]
    scalars = (offsets, jnp.swapaxes(peak_shift, 2, 3), accepted)
    high = 2 * bands * HALF + 2 * SUB
    small_high = HALF + 2 * SUB
    small_rows = rows // DS + 2 * COARSE
    hbm = pl.BlockSpec(memory_space=pltpu.HBM)
    vmem = pl.BlockSpec(memory_space=pltpu.VMEM)
    limit = 30 * 2**20
    operands = [pltpu.with_memory_space_constraint(x, pltpu.HBM) for x in (*scalars, own, *tables)]
    between = pl.pallas_call(
        functools.partial(exchange_kernel, bands, units, gains),
        name="exchange",
        out_shape=(
            jax.ShapeDtypeStruct((rows, width - PAIR), jnp.float32),
            jax.ShapeDtypeStruct((rows // DS, small_width), jnp.float32),
            jax.ShapeDtypeStruct((bands, P_SIZE, PAIR), jnp.bfloat16),
            jax.ShapeDtypeStruct((high, PAIR), jnp.float32),
            jax.ShapeDtypeStruct((SUB, LANES), jnp.float32),
        )
        + tuple(jax.ShapeDtypeStruct(x.shape, x.dtype) for x in tables[:3]),
        in_specs=[hbm] * 9,
        out_specs=(vmem,) * 8,
        scratch_shapes=[
            pltpu.VMEM((rows, width), jnp.bfloat16),
            pltpu.VMEM((reach, width), jnp.bfloat16),
            pltpu.VMEM((columns + 2, reach, LANES), jnp.float32),
            pltpu.VMEM((units, high, PAIR), jnp.float32),
            pltpu.VMEM((rows // DS, small_width), jnp.bfloat16),
            pltpu.VMEM((rows // DS - 2 * COARSE, LANES), jnp.bfloat16),
            pltpu.VMEM((small_width // LANES + 2, small_rows, LANES), jnp.float32),
            pltpu.VMEM((small_high, 2 * small_width), jnp.float32),
            pltpu.VMEM((rows // DS, width), jnp.bfloat16),
            pltpu.VMEM((rows // DS, width), jnp.bfloat16),
            pltpu.VMEM((small_rows, span), jnp.bfloat16),
            pltpu.VMEM((small_rows, span), jnp.bfloat16),
            pltpu.VMEM(wide.shape, jnp.bfloat16),
            pltpu.VMEM(pool.shape, jnp.bfloat16),
        ]
        + [pltpu.SMEM(x.shape, jnp.int32) for x in scalars]
        + [
            pltpu.VMEM((2, rows - 2 * HALO, LANES), jnp.bfloat16),
            pltpu.SemaphoreType.DMA((columns + 3,)),
            pltpu.SemaphoreType.DMA((columns + 3,)),
            pltpu.SemaphoreType.DMA((2,)),
            pltpu.SemaphoreType.DMA((2,)),
            pltpu.SemaphoreType.DMA((4,)),
            pltpu.SemaphoreType.DMA((len(operands),)),
        ],
        compiler_params=pltpu.CompilerParams(
            collective_id=0, has_side_effects=True, vmem_limit_bytes=limit
        ),
    )(*operands)
    return pl.pallas_call(
        functools.partial(finish_kernel, bands, gains),
        name="finish",
        out_shape=(
            jax.ShapeDtypeStruct((1, rows // DS, small_width), jnp.float32),
            jax.ShapeDtypeStruct((1, rows, width), jnp.float32),
        ),
        in_specs=[vmem] * 8,
        out_specs=(hbm, hbm),
        scratch_shapes=[
            pltpu.VMEM((rows, PAIR), jnp.float32),
            pltpu.SemaphoreType.DMA((2 * bands + 1,)),
        ],
        compiler_params=pltpu.CompilerParams(vmem_limit_bytes=limit),
    )(*between)


def solution(mesh):
    return jax.shard_map(
        shards,
        mesh=mesh,
        in_specs=(
            P("sec", "tile", None),
            P("sec", "tile", None),
            P("sec", "tile", None, None),
            P("sec", "tile", None),
        ),
        out_specs=(P("sec", "tile", None), P("sec", "tile", None)),
        check_vma=False,
    )
```

```python
import functools
import math

import jax
import jax.numpy as jnp
import ml_dtypes
import numpy as np
from jax import lax
from jax.experimental import pallas as pl
from jax.experimental.pallas import tpu as pltpu
from jax.sharding import PartitionSpec as P

P_SIZE = 128
HALF = P_SIZE // 2
DS = 4
COARSE = 16
HALO = 80
LANES = 128
PAIR = 2 * P_SIZE
SUB = 8
POOLED = P_SIZE // DS
EPSILON = 1e-05
MESH = pl.DeviceIdType.MESH


def quantized(table):
    return table.astype(np.float32).astype(ml_dtypes.bfloat16)


def table_scale(n):
    cosines = np.cos(2.0 * np.pi * np.arange(n) / n)
    best = None
    for factor in np.linspace(1.0, 2.0, 4001):
        table = quantized(cosines * factor).astype(np.float64)
        gain = (table @ cosines) / (cosines @ cosines)
        error = np.mean((table / gain - cosines) ** 2)
        if best is None or error < best[0]:
            best = (error, factor, gain)
    return best[1], best[2]


def waves(n):
    k = np.arange(n)
    angles = (k[:, None] * k[None, :] % n) * (2.0 * np.pi / n)
    return np.cos(angles), np.sin(angles)


def row_tables():
    n = P_SIZE
    factor, gain = table_scale(n)
    cosines, sines = waves(n)
    alternating = np.where(np.arange(n) % 2 == 0, 1.0, -1.0)
    forward = np.concatenate([cosines[:HALF], sines[:HALF]])
    forward[HALF] = alternating
    weight = np.where(np.arange(HALF) == 0, 1.0, 2.0)[:, None]
    inverse = np.concatenate([cosines[:HALF] * weight, -sines[:HALF] * weight])
    inverse[HALF] = alternating
    pool = (np.arange(POOLED)[:, None] == np.arange(n)[None, :] // DS).astype(np.float64)
    forward = np.concatenate([forward * (factor / n), pool])
    return quantized(forward), quantized(inverse.T * (factor / n)), gain


def col_table(n):
    factor, gain = table_scale(n)
    cosines, sines = waves(n)
    table = np.block([[cosines, sines], [-sines, cosines]]) * (factor / n)
    return quantized(table), gain


def mm(a, b):
    return jnp.dot(a, b, preferred_element_type=jnp.float32)


def sublanes():
    return lax.broadcasted_iota(jnp.int32, (SUB, LANES), 0)


def to_lhs(rows):
    return jnp.concatenate([rows[:HALF], rows[HALF:]], axis=1).astype(jnp.bfloat16)


def energy(block):
    width = block.shape[1] // 2
    total = block[:, :width] * block[:, :width] + block[:, width:] * block[:, width:]
    head = jnp.where(lax.broadcasted_iota(jnp.int32, (SUB, width), 0) == 0, 0.0, total[:SUB])
    for at in range(SUB, HALF, SUB):
        head = head + total[at : at + SUB]
    return jnp.sum(head, axis=0, keepdims=True)


def spectrum(blocks, table):
    count = len(blocks)
    width = blocks[0].shape[1]
    sub = lax.broadcasted_iota(jnp.int32, (SUB, width), 0)
    first = jnp.zeros((SUB, width), jnp.float32)
    middle = jnp.zeros((SUB, width), jnp.float32)
    for p, rows in enumerate(blocks):
        first = jnp.where(sub == p, rows[0:1], first)
        middle = jnp.where(sub == p, rows[HALF : HALF + 1], middle)
    first = first - jnp.sum(first, axis=1, keepdims=True) * (1.0 / width)
    ends = jnp.concatenate([first, middle], axis=0)
    ends = jnp.concatenate([ends, jnp.zeros_like(ends)], axis=1).astype(jnp.bfloat16)
    freq = mm(jnp.concatenate([to_lhs(rows) for rows in blocks] + [ends], axis=0), table)
    power = jnp.zeros((SUB, width), jnp.float32)
    for p in range(count):
        power = jnp.where(sub == p, energy(freq[p * HALF : (p + 1) * HALF]), power)
    tail = freq[count * HALF :] * freq[count * HALF :]
    tail = tail[:SUB] + tail[SUB:]
    power = 2.0 * power + tail[:, :width] + tail[:, width:]
    return freq, jnp.sum(power, axis=1, keepdims=True)


def scaled(freq, count, factors):
    parts = [freq[p * HALF : (p + 1) * HALF] * factors[p : p + 1] for p in range(count)]
    for at in (0, SUB):
        parts.append(freq[count * HALF + at : count * HALF + at + SUB] * factors)
    return parts


def correlate(own, other, count, table):
    width = own.shape[1] // 2
    a_re, a_im = own[:, :width], own[:, width:]
    b_re, b_im = other[:, :width], other[:, width:]
    product = jnp.concatenate([a_re * b_re + a_im * b_im, a_im * b_re - a_re * b_im], axis=1)
    rows = mm(product.astype(jnp.bfloat16), table)
    sub = lax.broadcasted_iota(jnp.int32, (SUB, width), 0)
    at = count * HALF
    blocks = []
    for p in range(count):
        block = rows[p * HALF : (p + 1) * HALF]
        first = rows[at + p : at + p + 1, :width]
        middle = rows[at + SUB + p : at + SUB + p + 1, :width]
        parts = [
            jnp.where(sub == 0, first, block[:SUB, :width]),
            block[SUB:, :width],
            jnp.where(sub == 0, middle, block[:SUB, width:]),
            block[SUB:, width:],
        ]
        blocks.append(jnp.concatenate(parts, axis=0).astype(jnp.bfloat16))
    return blocks


def window_at(ref, row_at, col_at, height):
    block = lax.div(col_at, LANES)
    shift = lax.rem(col_at, LANES)
    left = ref[block, pl.ds(row_at, height), :]
    right = ref[block + 1, pl.ds(row_at, height), :]
    lane = lax.broadcasted_iota(jnp.int32, (height, LANES), 1)
    return pltpu.roll(jnp.where(lane >= shift, left, right), lax.rem(LANES - shift, LANES), 1)


def unit_windows(unit, bands, offsets, peaks, ext):
    off_row = HALO + DS * offsets[0, 0, 0]
    off_col = LANES + DS * offsets[0, 0, 1]
    windows = []
    for i in range(bands):
        pair = []
        for h in range(2):
            column = 2 * unit + h
            row_at = off_row + i * P_SIZE + peaks[0, i, 0, column]
            col_at = off_col + column * P_SIZE + peaks[0, i, 1, column]
            pair.append(window_at(ext, row_at, col_at, P_SIZE).astype(jnp.bfloat16))
        windows.append(jnp.concatenate(pair, axis=1))
    return windows


def unit_keep(unit, bands, keep):
    sub = sublanes()
    flags = jnp.zeros((SUB, LANES), jnp.float32)
    for i in range(bands):
        for h in range(2):
            flag = keep[0, i, 2 * unit + h].astype(jnp.float32)
            flags = jnp.where(sub == 2 * i + h, flag, flags)
    return flags


def match_unit(bands, gains, windows, flags, own, row_tab, col_tab, inv_tab, write):
    blocks = []
    for window in windows:
        rows = mm(row_tab[:P_SIZE, :], window)
        blocks += [rows[:, :P_SIZE], rows[:, P_SIZE:]]
    freq, power = spectrum(blocks, col_tab[...])
    gain = gains[0] * gains[1]
    scale = (P_SIZE * P_SIZE / gain) ** 2 / P_SIZE
    factors = flags * (scale / jnp.sqrt(power * (1.0 / gain**2) + EPSILON))
    rows = correlate(own, freq, 2 * bands, col_tab[...])
    for i in range(bands):
        maps = mm(inv_tab[...], jnp.concatenate(rows[2 * i : 2 * i + 2], axis=1))
        for h in range(2):
            p = 2 * i + h
            write(i, h, maps[:, h * P_SIZE : (h + 1) * P_SIZE] * factors[p : p + 1])


def split(x):
    hi = x.astype(jnp.bfloat16)
    return hi, (x - hi.astype(jnp.float32)).astype(jnp.bfloat16)


def pooled(hi, lo, pool):
    span = pool.shape[0]
    parts = []
    for at in range(0, hi.shape[1], span):
        sums = mm(hi[:, at : at + span], pool) + mm(lo[:, at : at + span], pool)
        parts.append((sums * (1.0 / (DS * DS))).astype(jnp.bfloat16))
    return parts


def exchange_kernel(
    bands,
    units,
    gains,
    offsets_hbm,
    peaks_hbm,
    keep_hbm,
    img,
    row_hbm,
    col_hbm,
    inv_hbm,
    wide_hbm,
    pool_hbm,
    maps,
    coarse,
    windows,
    last_spec,
    flags,
    row_tab,
    col_tab,
    inv_tab,
    own,
    land,
    ext,
    spec,
    small_own,
    small_land,
    small,
    small_spec,
    own_hi,
    own_lo,
    sum_hi,
    sum_lo,
    wide_tab,
    pool,
    offsets,
    peaks,
    keep,
    relayed,
    send_sems,
    recv_sems,
    side_send,
    side_recv,
    relay_sems,
    local_sems,
):
    s = lax.axis_index("sec")
    t = lax.axis_index("tile")
    ns = lax.axis_size("sec")
    nt = lax.axis_size("tile")
    rows, width = own.shape
    columns = width // LANES
    centre = rows - 2 * HALO
    reach = rows + 2 * HALO
    row_gain, col_gain, wide_gain = gains
    early = 3
    detours = (columns // 2, columns // 2 + 1)

    sends = s < ns - 1
    receives = s > 0
    has_up = t > 0
    has_down = t < nt - 1
    s_next = jnp.minimum(s + 1, ns - 1)
    s_prev = jnp.maximum(s - 1, 0)
    t_next = jnp.minimum(t + 1, nt - 1)
    t_prev = jnp.maximum(t - 1, 0)

    eighth = lax.rem(s, 8)
    starts_relay = (eighth == 3) & (s + 4 < ns)
    relays = eighth == 7
    ends_relay = (eighth == 4) & (s + 3 < ns)
    relay_from = jnp.maximum(s - 4, 0)
    relay_by = jnp.minimum(s + 4, ns - 1)
    relay_to = jnp.maximum(s - 3, 0)
    relayed_by = jnp.minimum(s + 3, ns - 1)

    barrier = pltpu.get_barrier_semaphore()
    for cond, peer in (
        (receives, (s_prev, t)),
        (ends_relay, (relayed_by, t)),
        (relays, (relay_from, t)),
        (has_up, (s, t_prev)),
        (has_down, (s, t_next)),
    ):

        @pl.when(cond)
        def _(peer=peer):
            pl.semaphore_signal(barrier, inc=1, device_id=peer, device_id_type=MESH)

    loads = [
        pltpu.make_async_copy(source, target, local_sems.at[n])
        for n, (source, target) in enumerate(
            (
                (img, own),
                (row_hbm, row_tab),
                (col_hbm, col_tab),
                (inv_hbm, inv_tab),
                (wide_hbm, wide_tab),
                (pool_hbm, pool),
                (offsets_hbm, offsets),
                (peaks_hbm, peaks),
                (keep_hbm, keep),
            )
        )
    ]
    for load in loads:
        load.start()
    peers = sum(jnp.where(cond, 1, 0) for cond in (sends, starts_relay, relays, has_up, has_down))
    pl.semaphore_wait(barrier, peers)

    def edge_copy(n):
        start = n * (rows - HALO)
        return pltpu.make_async_remote_copy(
            src_ref=img.at[pl.ds(start, HALO)],
            dst_ref=land.at[pl.ds(HALO + start, HALO)],
            send_sem=send_sems.at[n],
            recv_sem=recv_sems.at[n],
            device_id=(s_next, t),
            device_id_type=MESH,
        )

    def column_copy(c):
        at = pl.multiple_of(c * LANES, LANES)
        return pltpu.make_async_remote_copy(
            src_ref=img.at[pl.ds(HALO, centre), pl.ds(at, LANES)],
            dst_ref=land.at[pl.ds(2 * HALO, centre), pl.ds(at, LANES)],
            send_sem=send_sems.at[3 + c],
            recv_sem=recv_sems.at[3 + c],
            device_id=(s_next, t),
            device_id_type=MESH,
        )

    def relay_in(n):
        return pltpu.make_async_remote_copy(
            src_ref=img.at[pl.ds(HALO, centre), pl.ds(detours[n] * LANES, LANES)],
            dst_ref=relayed.at[n],
            send_sem=send_sems.at[3 + detours[n]],
            recv_sem=relay_sems.at[n],
            device_id=(relay_by, t),
            device_id_type=MESH,
        )

    def relay_out(n):
        return pltpu.make_async_remote_copy(
            src_ref=relayed.at[n],
            dst_ref=land.at[pl.ds(2 * HALO, centre), pl.ds(detours[n] * LANES, LANES)],
            send_sem=relay_sems.at[2 + n],
            recv_sem=recv_sems.at[3 + detours[n]],
            device_id=(relay_to, t),
            device_id_type=MESH,
        )

    def small_copy():
        return pltpu.make_async_remote_copy(
            src_ref=small_own.at[pl.ds(COARSE, small_land.shape[0]), pl.ds(LANES, LANES)],
            dst_ref=small_land,
            send_sem=send_sems.at[2],
            recv_sem=recv_sems.at[2],
            device_id=(s_next, t),
            device_id_type=MESH,
        )

    def side_copy(n):
        source, target, peer = ((HALO, HALO + rows, t_prev), (rows, 0, t_next))[n]
        return pltpu.make_async_remote_copy(
            src_ref=land.at[pl.ds(source, HALO)],
            dst_ref=land.at[pl.ds(target, HALO)],
            send_sem=side_send.at[n],
            recv_sem=side_recv.at[n],
            device_id=(s, peer),
            device_id_type=MESH,
        )

    @pl.when(sends)
    def _():
        edge_copy(0).start()
        edge_copy(1).start()
        for c in range(early):
            if c not in detours:
                column_copy(c).start()

    @pl.when(starts_relay)
    def _():
        for n in range(len(detours)):
            relay_in(n).start()

    @pl.when(sends & jnp.logical_not(starts_relay))
    def _():
        for c in range(early):
            if c in detours:
                column_copy(c).start()

    @pl.when(jnp.logical_not(receives))
    def _():
        land[...] = jnp.zeros_like(land)
        small_land[...] = jnp.zeros_like(small_land)

    @pl.when(receives & jnp.logical_not(has_up))
    def _():
        land[:HALO, :] = jnp.zeros((HALO, width), jnp.bfloat16)

    @pl.when(receives & jnp.logical_not(has_down))
    def _():
        land[HALO + rows :, :] = jnp.zeros((HALO, width), jnp.bfloat16)

    ext[0] = jnp.zeros((reach, LANES), jnp.float32)
    ext[columns + 1] = jnp.zeros((reach, LANES), jnp.float32)
    small[0] = jnp.zeros(small.shape[1:], jnp.float32)
    small[3] = jnp.zeros(small.shape[1:], jnp.float32)
    for load in loads:
        load.wait()

    def own_unit(u, carry):
        at = pl.multiple_of(u * PAIR, PAIR)
        blocks = []
        for i in range(bands):
            both = mm(row_tab[...], own[i * P_SIZE : (i + 1) * P_SIZE, pl.ds(at, PAIR)])
            blocks += [both[:P_SIZE, :P_SIZE], both[:P_SIZE, P_SIZE:]]
            hi, lo = split(both[P_SIZE:])
            own_hi[i * POOLED : (i + 1) * POOLED, pl.ds(at, PAIR)] = hi
            own_lo[i * POOLED : (i + 1) * POOLED, pl.ds(at, PAIR)] = lo
        freq, power = spectrum(blocks, col_tab[...])
        gain = row_gain * col_gain
        factors = (1.0 / gain) / jnp.sqrt(power * (1.0 / gain**2) + EPSILON)
        base = 0
        for part in scaled(freq, 2 * bands, factors):
            spec[u, base : base + part.shape[0], :] = part
            base += part.shape[0]
        return carry

    lax.fori_loop(0, units, own_unit, 0)
    for n, part in enumerate(pooled(own_hi[...], own_lo[...], pool[...])):
        small_own[:, n * LANES : (n + 1) * LANES] = part

    @pl.when(sends)
    def _():
        small_copy().start()

    @pl.when(sends & jnp.logical_not(starts_relay))
    def _():
        for c in range(early, columns):
            if c in detours:
                column_copy(c).start()

    @pl.when(sends)
    def _():
        for c in range(early, columns):
            if c not in detours:
                column_copy(c).start()

    @pl.when(receives)
    def _():
        edge_copy(0).wait_recv()

        @pl.when(has_up)
        def _():
            side_copy(0).start()

        edge_copy(1).wait_recv()

        @pl.when(has_down)
        def _():
            side_copy(1).start()

    last_spec[...] = spec[units - 1]
    flags[...] = unit_keep(units - 1, bands, keep)
    freq, power = spectrum([mm(row_tab[:P_SIZE, :], small_own[...])], wide_tab[...])
    gain = row_gain * wide_gain
    factors = (1.0 / gain) / jnp.sqrt(power * (1.0 / gain**2) + EPSILON)
    base = 0
    for part in scaled(freq, 1, factors):
        small_spec[base : base + part.shape[0], :] = part
        base += part.shape[0]

    @pl.when(receives)
    def _():
        @pl.when(has_up)
        def _():
            side_copy(1).wait_recv()

        @pl.when(has_down)
        def _():
            side_copy(0).wait_recv()

    for at in (0, HALO + rows - HALO):
        for c in range(columns):
            ext[c + 1, at : at + 2 * HALO, :] = land[
                at : at + 2 * HALO, c * LANES : (c + 1) * LANES
            ].astype(jnp.float32)

    def row_sums(c, at, count):
        sums = ext[c + 1, pl.ds(at, count, stride=DS), :]
        for k in range(1, DS):
            sums = sums + ext[c + 1, pl.ds(at + k, count, stride=DS), :]
        return split(sums)

    def arrive(c):
        @pl.when(receives)
        def _():
            column_copy(c).wait_recv()

        at = pl.multiple_of(c * LANES, LANES)
        ext[c + 1, 2 * HALO : 2 * HALO + centre, :] = land[
            2 * HALO : 2 * HALO + centre, pl.ds(at, LANES)
        ].astype(jnp.float32)

    half = columns // 2
    first = HALO - DS * COARSE
    count = small.shape[1]
    side = 2 * COARSE

    def keep_sums(c):
        hi, lo = row_sums(c, first, count)
        sum_hi[:, c * LANES : (c + 1) * LANES] = hi
        sum_lo[:, c * LANES : (c + 1) * LANES] = lo

    for c in range(half):
        for n, at in enumerate((first, first + DS * (count - side))):
            hi, lo = row_sums(half + c, at, side)
            sum_hi[n * side : (n + 1) * side, c * LANES : (c + 1) * LANES] = hi
            sum_lo[n * side : (n + 1) * side, c * LANES : (c + 1) * LANES] = lo
    ends = pooled(sum_hi[: 2 * side], sum_lo[: 2 * side], pool[...])[0].astype(jnp.float32)
    small[2, :side] = ends[:side]
    small[2, count - side :] = ends[side:]

    def coarse_map():
        keep_sums(half - 1)
        small[1] = pooled(sum_hi[...], sum_lo[...], pool[...])[0].astype(jnp.float32)

        @pl.when(receives)
        def _():
            small_copy().wait_recv()

        small[2, side : count - side] = small_land[...].astype(jnp.float32)
        height = count - 2 * COARSE
        window = [
            window_at(
                small, COARSE + offsets[0, 0, 0], LANES * (n + 1) + offsets[0, 0, 1], height
            ).astype(jnp.bfloat16)
            for n in range(2)
        ]
        freq, power = spectrum(
            [mm(row_tab[:P_SIZE, :], jnp.concatenate(window, axis=1))], wide_tab[...]
        )
        gain = row_gain * wide_gain
        size = height * 2 * LANES
        scale = (size / gain) ** 2 / math.sqrt(size)
        factors = scale / jnp.sqrt(power * (1.0 / gain**2) + EPSILON)
        found = correlate(small_spec[...], freq, 1, wide_tab[...])[0]
        coarse[...] = mm(inv_tab[...], found) * factors[0:1]

    arrive(0)
    keep_sums(0)
    arrive(1)
    keep_sums(1)

    def unit_step(u, carry):
        @pl.when(u > 0)
        def _():
            arrive(2 * u + 1)

        @pl.when(u == columns // 4 - 1)
        def _():
            coarse_map()

        @pl.when(sends & (u == units - 2))
        def _():
            edge_copy(0).wait_send()
            edge_copy(1).wait_send()
            small_copy().wait_send()
            for c in range(half):
                column_copy(c).wait_send()

        arrive(2 * u + 2)

        @pl.when(u == 0)
        def _():
            keep_sums(2)

        def write(i, h, value):
            at = pl.multiple_of(u * PAIR + h * P_SIZE, P_SIZE)
            maps[i * P_SIZE : (i + 1) * P_SIZE, pl.ds(at, P_SIZE)] = value

        match_unit(
            bands,
            (row_gain, col_gain),
            unit_windows(u, bands, offsets, peaks, ext),
            unit_keep(u, bands, keep),
            spec[u],
            row_tab,
            col_tab,
            inv_tab,
            write,
        )

        @pl.when(relays & (u == 0))
        def _():
            for n in range(len(detours)):
                relay_in(n).wait_recv()
                relay_out(n).start()

        return carry

    lax.fori_loop(0, units - 1, unit_step, 0)
    @pl.when(receives & has_up)
    def _():
        side_copy(0).wait_send()

    @pl.when(receives & has_down)
    def _():
        side_copy(1).wait_send()

    @pl.when(sends)
    def _():
        for c in range(half, columns):
            column_copy(c).wait_send()

    @pl.when(relays)
    def _():
        for n in range(len(detours)):
            relay_out(n).wait_send()

    arrive(columns - 1)
    for i, window in enumerate(unit_windows(units - 1, bands, offsets, peaks, ext)):
        windows[i] = window


def finish_kernel(
    bands,
    gains,
    maps,
    coarse,
    windows,
    last_spec,
    flags,
    row_tab,
    col_tab,
    inv_tab,
    coarse_out,
    flow_out,
    last_maps,
    sems,
):
    done = maps.shape[1]
    copies = [pltpu.make_async_copy(coarse, coarse_out.at[0], sems.at[2 * bands])]
    for i in range(bands):
        band = pl.ds(i * P_SIZE, P_SIZE)
        copies.append(pltpu.make_async_copy(maps.at[band], flow_out.at[0, band, pl.ds(0, done)], sems.at[i]))
    for copy in copies:
        copy.start()

    def write(i, h, value):
        last_maps[i * P_SIZE : (i + 1) * P_SIZE, h * P_SIZE : (h + 1) * P_SIZE] = value

    match_unit(
        bands,
        gains[:2],
        [windows[i] for i in range(bands)],
        flags[...],
        last_spec[...],
        row_tab,
        col_tab,
        inv_tab,
        write,
    )
    for i in range(bands):
        band = pl.ds(i * P_SIZE, P_SIZE)
        copies.append(
            pltpu.make_async_copy(last_maps.at[band], flow_out.at[0, band, pl.ds(done, PAIR)], sems.at[bands + i])
        )
        copies[-1].start()
    for copy in copies:
        copy.wait()


def shards(section_image, offsets, peak_shift, accepted):
    own = section_image[0]
    rows, width = own.shape
    bands = rows // P_SIZE
    units = width // PAIR
    columns = width // LANES
    reach = rows + 2 * HALO
    small_width = width // DS
    forward_row, inverse_row, row_gain = row_tables()
    col, col_gain = col_table(P_SIZE)
    wide, wide_gain = col_table(small_width)
    gains = (float(row_gain), float(col_gain), float(wide_gain))
    span = DS * LANES
    pool = quantized(np.arange(span)[:, None] // DS == np.arange(LANES)[None, :])
    tables = [jnp.asarray(x) for x in (forward_row, col, inverse_row, wide, pool)]
    scalars = (offsets, jnp.swapaxes(peak_shift, 2, 3), accepted)
    high = 2 * bands * HALF + 2 * SUB
    small_high = HALF + 2 * SUB
    small_rows = rows // DS + 2 * COARSE
    hbm = pl.BlockSpec(memory_space=pltpu.HBM)
    vmem = pl.BlockSpec(memory_space=pltpu.VMEM)
    limit = 30 * 2**20
    operands = [pltpu.with_memory_space_constraint(x, pltpu.HBM) for x in (*scalars, own, *tables)]
    between = pl.pallas_call(
        functools.partial(exchange_kernel, bands, units, gains),
        name="exchange",
        out_shape=(
            jax.ShapeDtypeStruct((rows, width - PAIR), jnp.float32),
            jax.ShapeDtypeStruct((rows // DS, small_width), jnp.float32),
            jax.ShapeDtypeStruct((bands, P_SIZE, PAIR), jnp.bfloat16),
            jax.ShapeDtypeStruct((high, PAIR), jnp.float32),
            jax.ShapeDtypeStruct((SUB, LANES), jnp.float32),
        )
        + tuple(jax.ShapeDtypeStruct(x.shape, x.dtype) for x in tables[:3]),
        in_specs=[hbm] * 9,
        out_specs=(vmem,) * 8,
        scratch_shapes=[
            pltpu.VMEM((rows, width), jnp.bfloat16),
            pltpu.VMEM((reach, width), jnp.bfloat16),
            pltpu.VMEM((columns + 2, reach, LANES), jnp.float32),
            pltpu.VMEM((units, high, PAIR), jnp.float32),
            pltpu.VMEM((rows // DS, small_width), jnp.bfloat16),
            pltpu.VMEM((rows // DS - 2 * COARSE, LANES), jnp.bfloat16),
            pltpu.VMEM((small_width // LANES + 2, small_rows, LANES), jnp.float32),
            pltpu.VMEM((small_high, 2 * small_width), jnp.float32),
            pltpu.VMEM((rows // DS, width), jnp.bfloat16),
            pltpu.VMEM((rows // DS, width), jnp.bfloat16),
            pltpu.VMEM((small_rows, span), jnp.bfloat16),
            pltpu.VMEM((small_rows, span), jnp.bfloat16),
            pltpu.VMEM(wide.shape, jnp.bfloat16),
            pltpu.VMEM(pool.shape, jnp.bfloat16),
        ]
        + [pltpu.SMEM(x.shape, jnp.int32) for x in scalars]
        + [
            pltpu.VMEM((2, rows - 2 * HALO, LANES), jnp.bfloat16),
            pltpu.SemaphoreType.DMA((columns + 3,)),
            pltpu.SemaphoreType.DMA((columns + 3,)),
            pltpu.SemaphoreType.DMA((2,)),
            pltpu.SemaphoreType.DMA((2,)),
            pltpu.SemaphoreType.DMA((4,)),
            pltpu.SemaphoreType.DMA((len(operands),)),
        ],
        compiler_params=pltpu.CompilerParams(
            collective_id=0, has_side_effects=True, vmem_limit_bytes=limit
        ),
    )(*operands)
    return pl.pallas_call(
        functools.partial(finish_kernel, bands, gains),
        name="finish",
        out_shape=(
            jax.ShapeDtypeStruct((1, rows // DS, small_width), jnp.float32),
            jax.ShapeDtypeStruct((1, rows, width), jnp.float32),
        ),
        in_specs=[vmem] * 8,
        out_specs=(hbm, hbm),
        scratch_shapes=[
            pltpu.VMEM((rows, PAIR), jnp.float32),
            pltpu.SemaphoreType.DMA((2 * bands + 1,)),
        ],
        compiler_params=pltpu.CompilerParams(vmem_limit_bytes=limit),
    )(*between)


def solution(mesh):
    return jax.shard_map(
        shards,
        mesh=mesh,
        in_specs=(
            P("sec", "tile", None),
            P("sec", "tile", None),
            P("sec", "tile", None, None),
            P("sec", "tile", None),
        ),
        out_specs=(P("sec", "tile", None), P("sec", "tile", None)),
        check_vma=False,
    )
```

```python
import functools
import math

import jax
import jax.numpy as jnp
import ml_dtypes
import numpy as np
from jax import lax
from jax.experimental import pallas as pl
from jax.experimental.pallas import tpu as pltpu
from jax.sharding import PartitionSpec as P

P_SIZE = 128
HALF = P_SIZE // 2
DS = 4
COARSE = 16
HALO = 80
LANES = 128
PAIR = 2 * P_SIZE
SUB = 8
POOLED = P_SIZE // DS
EPSILON = 1e-05
MESH = pl.DeviceIdType.MESH


def quantized(table):
    return table.astype(np.float32).astype(ml_dtypes.bfloat16)


def table_scale(n):
    cosines = np.cos(2.0 * np.pi * np.arange(n) / n)
    best = None
    for factor in np.linspace(1.0, 2.0, 4001):
        table = quantized(cosines * factor).astype(np.float64)
        gain = (table @ cosines) / (cosines @ cosines)
        error = np.mean((table / gain - cosines) ** 2)
        if best is None or error < best[0]:
            best = (error, factor, gain)
    return best[1], best[2]


def waves(n):
    k = np.arange(n)
    angles = (k[:, None] * k[None, :] % n) * (2.0 * np.pi / n)
    return np.cos(angles), np.sin(angles)


def row_tables():
    n = P_SIZE
    factor, gain = table_scale(n)
    cosines, sines = waves(n)
    alternating = np.where(np.arange(n) % 2 == 0, 1.0, -1.0)
    forward = np.concatenate([cosines[:HALF], sines[:HALF]])
    forward[HALF] = alternating
    weight = np.where(np.arange(HALF) == 0, 1.0, 2.0)[:, None]
    inverse = np.concatenate([cosines[:HALF] * weight, -sines[:HALF] * weight])
    inverse[HALF] = alternating
    pool = (np.arange(POOLED)[:, None] == np.arange(n)[None, :] // DS).astype(np.float64)
    forward = np.concatenate([forward * (factor / n), pool])
    return quantized(forward), quantized(inverse.T * (factor / n)), gain


def col_table(n):
    factor, gain = table_scale(n)
    cosines, sines = waves(n)
    table = np.block([[cosines, sines], [-sines, cosines]]) * (factor / n)
    return quantized(table), gain


def mm(a, b):
    return jnp.dot(a, b, preferred_element_type=jnp.float32)


def sublanes():
    return lax.broadcasted_iota(jnp.int32, (SUB, LANES), 0)


def to_lhs(rows):
    return jnp.concatenate([rows[:HALF], rows[HALF:]], axis=1).astype(jnp.bfloat16)


def energy(block):
    width = block.shape[1] // 2
    total = block[:, :width] * block[:, :width] + block[:, width:] * block[:, width:]
    head = jnp.where(lax.broadcasted_iota(jnp.int32, (SUB, width), 0) == 0, 0.0, total[:SUB])
    for at in range(SUB, HALF, SUB):
        head = head + total[at : at + SUB]
    return jnp.sum(head, axis=0, keepdims=True)


def spectrum(blocks, table):
    count = len(blocks)
    width = blocks[0].shape[1]
    sub = lax.broadcasted_iota(jnp.int32, (SUB, width), 0)
    first = jnp.zeros((SUB, width), jnp.float32)
    middle = jnp.zeros((SUB, width), jnp.float32)
    for p, rows in enumerate(blocks):
        first = jnp.where(sub == p, rows[0:1], first)
        middle = jnp.where(sub == p, rows[HALF : HALF + 1], middle)
    first = first - jnp.sum(first, axis=1, keepdims=True) * (1.0 / width)
    ends = jnp.concatenate([first, middle], axis=0)
    ends = jnp.concatenate([ends, jnp.zeros_like(ends)], axis=1).astype(jnp.bfloat16)
    freq = mm(jnp.concatenate([to_lhs(rows) for rows in blocks] + [ends], axis=0), table)
    power = jnp.zeros((SUB, width), jnp.float32)
    for p in range(count):
        power = jnp.where(sub == p, energy(freq[p * HALF : (p + 1) * HALF]), power)
    tail = freq[count * HALF :] * freq[count * HALF :]
    tail = tail[:SUB] + tail[SUB:]
    power = 2.0 * power + tail[:, :width] + tail[:, width:]
    return freq, jnp.sum(power, axis=1, keepdims=True)


def scaled(freq, count, factors):
    parts = [freq[p * HALF : (p + 1) * HALF] * factors[p : p + 1] for p in range(count)]
    for at in (0, SUB):
        parts.append(freq[count * HALF + at : count * HALF + at + SUB] * factors)
    return parts


def correlate(own, other, count, table):
    width = own.shape[1] // 2
    a_re, a_im = own[:, :width], own[:, width:]
    b_re, b_im = other[:, :width], other[:, width:]
    product = jnp.concatenate([a_re * b_re + a_im * b_im, a_im * b_re - a_re * b_im], axis=1)
    rows = mm(product.astype(jnp.bfloat16), table)
    sub = lax.broadcasted_iota(jnp.int32, (SUB, width), 0)
    at = count * HALF
    blocks = []
    for p in range(count):
        block = rows[p * HALF : (p + 1) * HALF]
        first = rows[at + p : at + p + 1, :width]
        middle = rows[at + SUB + p : at + SUB + p + 1, :width]
        parts = [
            jnp.where(sub == 0, first, block[:SUB, :width]),
            block[SUB:, :width],
            jnp.where(sub == 0, middle, block[:SUB, width:]),
            block[SUB:, width:],
        ]
        blocks.append(jnp.concatenate(parts, axis=0).astype(jnp.bfloat16))
    return blocks


def window_at(ref, row_at, col_at, height):
    block = lax.div(col_at, LANES)
    shift = lax.rem(col_at, LANES)
    left = ref[block, pl.ds(row_at, height), :]
    right = ref[block + 1, pl.ds(row_at, height), :]
    lane = lax.broadcasted_iota(jnp.int32, (height, LANES), 1)
    return pltpu.roll(jnp.where(lane >= shift, left, right), lax.rem(LANES - shift, LANES), 1)


def unit_windows(unit, bands, offsets, peaks, ext):
    off_row = HALO + DS * offsets[0, 0, 0]
    off_col = LANES + DS * offsets[0, 0, 1]
    windows = []
    for i in range(bands):
        pair = []
        for h in range(2):
            column = 2 * unit + h
            row_at = off_row + i * P_SIZE + peaks[0, i, 0, column]
            col_at = off_col + column * P_SIZE + peaks[0, i, 1, column]
            pair.append(window_at(ext, row_at, col_at, P_SIZE).astype(jnp.bfloat16))
        windows.append(jnp.concatenate(pair, axis=1))
    return windows


def unit_keep(unit, bands, keep):
    sub = sublanes()
    flags = jnp.zeros((SUB, LANES), jnp.float32)
    for i in range(bands):
        for h in range(2):
            flag = keep[0, i, 2 * unit + h].astype(jnp.float32)
            flags = jnp.where(sub == 2 * i + h, flag, flags)
    return flags


def match_unit(bands, gains, windows, flags, own, row_tab, col_tab, inv_tab, write):
    blocks = []
    for window in windows:
        rows = mm(row_tab[:P_SIZE, :], window)
        blocks += [rows[:, :P_SIZE], rows[:, P_SIZE:]]
    yield
    freq, power = spectrum(blocks, col_tab[...])
    yield
    gain = gains[0] * gains[1]
    scale = (P_SIZE * P_SIZE / gain) ** 2 / P_SIZE
    factors = flags * (scale / jnp.sqrt(power * (1.0 / gain**2) + EPSILON))
    rows = correlate(own, freq, 2 * bands, col_tab[...])
    yield
    for i in range(bands):
        maps = mm(inv_tab[...], jnp.concatenate(rows[2 * i : 2 * i + 2], axis=1))
        for h in range(2):
            p = 2 * i + h
            write(i, h, maps[:, h * P_SIZE : (h + 1) * P_SIZE] * factors[p : p + 1])


def run(*stages):
    parts = list(stages)
    while parts:
        parts = [part for part in parts if next(part, True) is None]


def split(x):
    hi = x.astype(jnp.bfloat16)
    return hi, (x - hi.astype(jnp.float32)).astype(jnp.bfloat16)


def pooled(hi, lo, pool):
    span = pool.shape[0]
    parts = []
    for at in range(0, hi.shape[1], span):
        sums = mm(hi[:, at : at + span], pool) + mm(lo[:, at : at + span], pool)
        parts.append((sums * (1.0 / (DS * DS))).astype(jnp.bfloat16))
    return parts


def exchange_kernel(
    bands,
    units,
    gains,
    offsets_hbm,
    peaks_hbm,
    keep_hbm,
    img,
    row_hbm,
    col_hbm,
    inv_hbm,
    wide_hbm,
    pool_hbm,
    maps,
    coarse,
    windows,
    last_spec,
    flags,
    row_tab,
    col_tab,
    inv_tab,
    own,
    land,
    ext,
    spec,
    small_own,
    small_land,
    small,
    small_spec,
    own_hi,
    own_lo,
    sum_hi,
    sum_lo,
    wide_tab,
    pool,
    offsets,
    peaks,
    keep,
    relayed,
    send_sems,
    recv_sems,
    side_send,
    side_recv,
    relay_sems,
    local_sems,
):
    s = lax.axis_index("sec")
    t = lax.axis_index("tile")
    ns = lax.axis_size("sec")
    nt = lax.axis_size("tile")
    rows, width = own.shape
    columns = width // LANES
    centre = rows - 2 * HALO
    reach = rows + 2 * HALO
    row_gain, col_gain, wide_gain = gains
    early = columns // 2 + 1
    detours = (columns // 2, columns // 2 + 1)

    sends = s < ns - 1
    receives = s > 0
    has_up = t > 0
    has_down = t < nt - 1
    s_next = jnp.minimum(s + 1, ns - 1)
    s_prev = jnp.maximum(s - 1, 0)
    t_next = jnp.minimum(t + 1, nt - 1)
    t_prev = jnp.maximum(t - 1, 0)

    eighth = lax.rem(s, 8)
    starts_relay = (eighth == 3) & (s + 4 < ns)
    relays = eighth == 7
    ends_relay = (eighth == 4) & (s + 3 < ns)
    relay_from = jnp.maximum(s - 4, 0)
    relay_by = jnp.minimum(s + 4, ns - 1)
    relay_to = jnp.maximum(s - 3, 0)
    relayed_by = jnp.minimum(s + 3, ns - 1)

    barrier = pltpu.get_barrier_semaphore()
    for cond, peer in (
        (receives, (s_prev, t)),
        (ends_relay, (relayed_by, t)),
        (relays, (relay_from, t)),
        (has_up, (s, t_prev)),
        (has_down, (s, t_next)),
    ):

        @pl.when(cond)
        def _(peer=peer):
            pl.semaphore_signal(barrier, inc=1, device_id=peer, device_id_type=MESH)

    loads = [
        pltpu.make_async_copy(source, target, local_sems.at[n])
        for n, (source, target) in enumerate(
            (
                (img, own),
                (row_hbm, row_tab),
                (col_hbm, col_tab),
                (inv_hbm, inv_tab),
                (wide_hbm, wide_tab),
                (pool_hbm, pool),
                (offsets_hbm, offsets),
                (peaks_hbm, peaks),
                (keep_hbm, keep),
            )
        )
    ]
    for load in loads:
        load.start()
    peers = sum(jnp.where(cond, 1, 0) for cond in (sends, starts_relay, relays, has_up, has_down))
    pl.semaphore_wait(barrier, peers)

    def edge_copy(n):
        start = n * (rows - HALO)
        return pltpu.make_async_remote_copy(
            src_ref=img.at[pl.ds(start, HALO)],
            dst_ref=land.at[pl.ds(HALO + start, HALO)],
            send_sem=send_sems.at[n],
            recv_sem=recv_sems.at[n],
            device_id=(s_next, t),
            device_id_type=MESH,
        )

    def column_copy(c):
        at = pl.multiple_of(c * LANES, LANES)
        return pltpu.make_async_remote_copy(
            src_ref=img.at[pl.ds(HALO, centre), pl.ds(at, LANES)],
            dst_ref=land.at[pl.ds(2 * HALO, centre), pl.ds(at, LANES)],
            send_sem=send_sems.at[3 + c],
            recv_sem=recv_sems.at[3 + c],
            device_id=(s_next, t),
            device_id_type=MESH,
        )

    def relay_in(n):
        return pltpu.make_async_remote_copy(
            src_ref=img.at[pl.ds(HALO, centre), pl.ds(detours[n] * LANES, LANES)],
            dst_ref=relayed.at[n],
            send_sem=send_sems.at[3 + detours[n]],
            recv_sem=relay_sems.at[n],
            device_id=(relay_by, t),
            device_id_type=MESH,
        )

    def relay_out(n):
        return pltpu.make_async_remote_copy(
            src_ref=relayed.at[n],
            dst_ref=land.at[pl.ds(2 * HALO, centre), pl.ds(detours[n] * LANES, LANES)],
            send_sem=relay_sems.at[2 + n],
            recv_sem=recv_sems.at[3 + detours[n]],
            device_id=(relay_to, t),
            device_id_type=MESH,
        )

    def small_copy():
        return pltpu.make_async_remote_copy(
            src_ref=small_own.at[pl.ds(COARSE, small_land.shape[0]), pl.ds(LANES, LANES)],
            dst_ref=small_land,
            send_sem=send_sems.at[2],
            recv_sem=recv_sems.at[2],
            device_id=(s_next, t),
            device_id_type=MESH,
        )

    def side_copy(n):
        source, target, peer = ((HALO, HALO + rows, t_prev), (rows, 0, t_next))[n]
        return pltpu.make_async_remote_copy(
            src_ref=land.at[pl.ds(source, HALO)],
            dst_ref=land.at[pl.ds(target, HALO)],
            send_sem=side_send.at[n],
            recv_sem=side_recv.at[n],
            device_id=(s, peer),
            device_id_type=MESH,
        )

    @pl.when(sends)
    def _():
        edge_copy(0).start()
        edge_copy(1).start()
        for c in range(early):
            if c not in detours:
                column_copy(c).start()

    @pl.when(starts_relay)
    def _():
        for n in range(len(detours)):
            relay_in(n).start()

    @pl.when(sends & jnp.logical_not(starts_relay))
    def _():
        for c in range(early):
            if c in detours:
                column_copy(c).start()

    @pl.when(jnp.logical_not(receives))
    def _():
        land[...] = jnp.zeros_like(land)
        small_land[...] = jnp.zeros_like(small_land)

    @pl.when(receives & jnp.logical_not(has_up))
    def _():
        land[:HALO, :] = jnp.zeros((HALO, width), jnp.bfloat16)

    @pl.when(receives & jnp.logical_not(has_down))
    def _():
        land[HALO + rows :, :] = jnp.zeros((HALO, width), jnp.bfloat16)

    ext[0] = jnp.zeros((reach, LANES), jnp.float32)
    ext[columns + 1] = jnp.zeros((reach, LANES), jnp.float32)
    small[0] = jnp.zeros(small.shape[1:], jnp.float32)
    small[3] = jnp.zeros(small.shape[1:], jnp.float32)
    for load in loads:
        load.wait()

    def own_unit(u, carry):
        at = pl.multiple_of(u * PAIR, PAIR)
        blocks = []
        for i in range(bands):
            both = mm(row_tab[...], own[i * P_SIZE : (i + 1) * P_SIZE, pl.ds(at, PAIR)])
            blocks += [both[:P_SIZE, :P_SIZE], both[:P_SIZE, P_SIZE:]]
            hi, lo = split(both[P_SIZE:])
            own_hi[i * POOLED : (i + 1) * POOLED, pl.ds(at, PAIR)] = hi
            own_lo[i * POOLED : (i + 1) * POOLED, pl.ds(at, PAIR)] = lo
        freq, power = spectrum(blocks, col_tab[...])
        gain = row_gain * col_gain
        factors = (1.0 / gain) / jnp.sqrt(power * (1.0 / gain**2) + EPSILON)
        base = 0
        for part in scaled(freq, 2 * bands, factors):
            spec[u, base : base + part.shape[0], :] = part
            base += part.shape[0]
        return carry

    lax.fori_loop(0, units, own_unit, 0)
    for n, part in enumerate(pooled(own_hi[...], own_lo[...], pool[...])):
        small_own[:, n * LANES : (n + 1) * LANES] = part

    @pl.when(sends)
    def _():
        small_copy().start()

    @pl.when(sends & jnp.logical_not(starts_relay))
    def _():
        for c in range(early, columns):
            if c in detours:
                column_copy(c).start()

    @pl.when(sends)
    def _():
        for c in range(early, columns):
            if c not in detours:
                column_copy(c).start()

    @pl.when(receives)
    def _():
        edge_copy(0).wait_recv()

        @pl.when(has_up)
        def _():
            side_copy(0).start()

        edge_copy(1).wait_recv()

        @pl.when(has_down)
        def _():
            side_copy(1).start()

    last_spec[...] = spec[units - 1]
    flags[...] = unit_keep(units - 1, bands, keep)
    freq, power = spectrum([mm(row_tab[:P_SIZE, :], small_own[...])], wide_tab[...])
    gain = row_gain * wide_gain
    factors = (1.0 / gain) / jnp.sqrt(power * (1.0 / gain**2) + EPSILON)
    base = 0
    for part in scaled(freq, 1, factors):
        small_spec[base : base + part.shape[0], :] = part
        base += part.shape[0]

    @pl.when(receives)
    def _():
        @pl.when(has_up)
        def _():
            side_copy(1).wait_recv()

        @pl.when(has_down)
        def _():
            side_copy(0).wait_recv()

    for at in (0, HALO + rows - HALO):
        for c in range(columns):
            ext[c + 1, at : at + 2 * HALO, :] = land[
                at : at + 2 * HALO, c * LANES : (c + 1) * LANES
            ].astype(jnp.float32)

    def row_sums(c, at, count):
        sums = ext[c + 1, pl.ds(at, count, stride=DS), :]
        for k in range(1, DS):
            sums = sums + ext[c + 1, pl.ds(at + k, count, stride=DS), :]
        return split(sums)

    def arrive(c):
        @pl.when(receives)
        def _():
            column_copy(c).wait_recv()

        at = pl.multiple_of(c * LANES, LANES)
        ext[c + 1, 2 * HALO : 2 * HALO + centre, :] = land[
            2 * HALO : 2 * HALO + centre, pl.ds(at, LANES)
        ].astype(jnp.float32)

    def coarse_map():
        half = columns // 2
        first = HALO - DS * COARSE
        count = small.shape[1]
        for c in range(half):
            hi, lo = row_sums(c, first, count)
            sum_hi[:, c * LANES : (c + 1) * LANES] = hi
            sum_lo[:, c * LANES : (c + 1) * LANES] = lo
        small[1] = pooled(sum_hi[...], sum_lo[...], pool[...])[0].astype(jnp.float32)
        side = 2 * COARSE
        for c in range(half):
            for n, at in enumerate((first, first + DS * (count - side))):
                hi, lo = row_sums(half + c, at, side)
                sum_hi[n * side : (n + 1) * side, c * LANES : (c + 1) * LANES] = hi
                sum_lo[n * side : (n + 1) * side, c * LANES : (c + 1) * LANES] = lo

        ends = pooled(sum_hi[: 2 * side], sum_lo[: 2 * side], pool[...])[0].astype(jnp.float32)
        small[2, :side] = ends[:side]
        small[2, side : count - side] = small_land[...].astype(jnp.float32)
        small[2, count - side :] = ends[side:]
        yield
        height = count - 2 * COARSE
        window = [
            window_at(
                small, COARSE + offsets[0, 0, 0], LANES * (n + 1) + offsets[0, 0, 1], height
            ).astype(jnp.bfloat16)
            for n in range(2)
        ]
        block = mm(row_tab[:P_SIZE, :], jnp.concatenate(window, axis=1))
        yield
        freq, power = spectrum([block], wide_tab[...])
        yield
        gain = row_gain * wide_gain
        size = height * 2 * LANES
        scale = (size / gain) ** 2 / math.sqrt(size)
        factors = scale / jnp.sqrt(power * (1.0 / gain**2) + EPSILON)
        found = correlate(small_spec[...], freq, 1, wide_tab[...])[0]
        yield
        coarse[...] = mm(inv_tab[...], found) * factors[0:1]

    def unit_step(u):
        def write(i, h, value):
            at = u * PAIR + h * P_SIZE
            at = at if isinstance(u, int) else pl.multiple_of(at, P_SIZE)
            maps[i * P_SIZE : (i + 1) * P_SIZE, pl.ds(at, P_SIZE)] = value

        return match_unit(
            bands,
            (row_gain, col_gain),
            unit_windows(u, bands, offsets, peaks, ext),
            unit_keep(u, bands, keep),
            spec[u],
            row_tab,
            col_tab,
            inv_tab,
            write,
        )

    arrive(0)

    def step(k, carry):
        @pl.when(k == 0)
        def _():
            arrive(1)
            arrive(2)

        @pl.when(k == 1)
        def _():
            arrive(3)
            arrive(4)

            @pl.when(receives)
            def _():
                small_copy().wait_recv()

            run(coarse_map(), unit_step(1))
            arrive(5)
            arrive(6)

        run(unit_step(2 * k))

        @pl.when(relays & (k == 0))
        def _():
            for n in range(len(detours)):
                relay_in(n).wait_recv()
                relay_out(n).start()

        return carry

    lax.fori_loop(0, 2, step, 0)

    @pl.when(receives & has_up)
    def _():
        side_copy(0).wait_send()

    @pl.when(receives & has_down)
    def _():
        side_copy(1).wait_send()

    @pl.when(sends)
    def _():
        edge_copy(0).wait_send()
        edge_copy(1).wait_send()
        small_copy().wait_send()
        for c in range(columns):
            column_copy(c).wait_send()

    @pl.when(relays)
    def _():
        for n in range(len(detours)):
            relay_out(n).wait_send()

    arrive(columns - 1)
    for i, window in enumerate(unit_windows(units - 1, bands, offsets, peaks, ext)):
        windows[i] = window


def finish_kernel(
    bands,
    gains,
    maps,
    coarse,
    windows,
    last_spec,
    flags,
    row_tab,
    col_tab,
    inv_tab,
    coarse_out,
    flow_out,
    last_maps,
    sems,
):
    done = maps.shape[1]
    copies = [pltpu.make_async_copy(coarse, coarse_out.at[0], sems.at[2 * bands])]
    for i in range(bands):
        band = pl.ds(i * P_SIZE, P_SIZE)
        copies.append(pltpu.make_async_copy(maps.at[band], flow_out.at[0, band, pl.ds(0, done)], sems.at[i]))
    for copy in copies:
        copy.start()

    def write(i, h, value):
        last_maps[i * P_SIZE : (i + 1) * P_SIZE, h * P_SIZE : (h + 1) * P_SIZE] = value

    run(
        match_unit(
            bands,
            gains[:2],
            [windows[i] for i in range(bands)],
            flags[...],
            last_spec[...],
            row_tab,
            col_tab,
            inv_tab,
            write,
        )
    )
    for i in range(bands):
        band = pl.ds(i * P_SIZE, P_SIZE)
        copies.append(
            pltpu.make_async_copy(last_maps.at[band], flow_out.at[0, band, pl.ds(done, PAIR)], sems.at[bands + i])
        )
        copies[-1].start()
    for copy in copies:
        copy.wait()


def shards(section_image, offsets, peak_shift, accepted):
    own = section_image[0]
    rows, width = own.shape
    bands = rows // P_SIZE
    units = width // PAIR
    columns = width // LANES
    reach = rows + 2 * HALO
    small_width = width // DS
    forward_row, inverse_row, row_gain = row_tables()
    col, col_gain = col_table(P_SIZE)
    wide, wide_gain = col_table(small_width)
    gains = (float(row_gain), float(col_gain), float(wide_gain))
    span = DS * LANES
    pool = quantized(np.arange(span)[:, None] // DS == np.arange(LANES)[None, :])
    tables = [jnp.asarray(x) for x in (forward_row, col, inverse_row, wide, pool)]
    scalars = (offsets, jnp.swapaxes(peak_shift, 2, 3), accepted)
    high = 2 * bands * HALF + 2 * SUB
    small_high = HALF + 2 * SUB
    small_rows = rows // DS + 2 * COARSE
    hbm = pl.BlockSpec(memory_space=pltpu.HBM)
    vmem = pl.BlockSpec(memory_space=pltpu.VMEM)
    limit = 30 * 2**20
    operands = [pltpu.with_memory_space_constraint(x, pltpu.HBM) for x in (*scalars, own, *tables)]
    between = pl.pallas_call(
        functools.partial(exchange_kernel, bands, units, gains),
        name="exchange",
        out_shape=(
            jax.ShapeDtypeStruct((rows, width - PAIR), jnp.float32),
            jax.ShapeDtypeStruct((rows // DS, small_width), jnp.float32),
            jax.ShapeDtypeStruct((bands, P_SIZE, PAIR), jnp.bfloat16),
            jax.ShapeDtypeStruct((high, PAIR), jnp.float32),
            jax.ShapeDtypeStruct((SUB, LANES), jnp.float32),
        )
        + tuple(jax.ShapeDtypeStruct(x.shape, x.dtype) for x in tables[:3]),
        in_specs=[hbm] * 9,
        out_specs=(vmem,) * 8,
        scratch_shapes=[
            pltpu.VMEM((rows, width), jnp.bfloat16),
            pltpu.VMEM((reach, width), jnp.bfloat16),
            pltpu.VMEM((columns + 2, reach, LANES), jnp.float32),
            pltpu.VMEM((units, high, PAIR), jnp.float32),
            pltpu.VMEM((rows // DS, small_width), jnp.bfloat16),
            pltpu.VMEM((rows // DS - 2 * COARSE, LANES), jnp.bfloat16),
            pltpu.VMEM((small_width // LANES + 2, small_rows, LANES), jnp.float32),
            pltpu.VMEM((small_high, 2 * small_width), jnp.float32),
            pltpu.VMEM((rows // DS, width), jnp.bfloat16),
            pltpu.VMEM((rows // DS, width), jnp.bfloat16),
            pltpu.VMEM((small_rows, span), jnp.bfloat16),
            pltpu.VMEM((small_rows, span), jnp.bfloat16),
            pltpu.VMEM(wide.shape, jnp.bfloat16),
            pltpu.VMEM(pool.shape, jnp.bfloat16),
        ]
        + [pltpu.SMEM(x.shape, jnp.int32) for x in scalars]
        + [
            pltpu.VMEM((2, rows - 2 * HALO, LANES), jnp.bfloat16),
            pltpu.SemaphoreType.DMA((columns + 3,)),
            pltpu.SemaphoreType.DMA((columns + 3,)),
            pltpu.SemaphoreType.DMA((2,)),
            pltpu.SemaphoreType.DMA((2,)),
            pltpu.SemaphoreType.DMA((4,)),
            pltpu.SemaphoreType.DMA((len(operands),)),
        ],
        compiler_params=pltpu.CompilerParams(
            collective_id=0, has_side_effects=True, vmem_limit_bytes=limit
        ),
    )(*operands)
    return pl.pallas_call(
        functools.partial(finish_kernel, bands, gains),
        name="finish",
        out_shape=(
            jax.ShapeDtypeStruct((1, rows // DS, small_width), jnp.float32),
            jax.ShapeDtypeStruct((1, rows, width), jnp.float32),
        ),
        in_specs=[vmem] * 8,
        out_specs=(hbm, hbm),
        scratch_shapes=[
            pltpu.VMEM((rows, PAIR), jnp.float32),
            pltpu.SemaphoreType.DMA((2 * bands + 1,)),
        ],
        compiler_params=pltpu.CompilerParams(vmem_limit_bytes=limit),
    )(*between)


def solution(mesh):
    return jax.shard_map(
        shards,
        mesh=mesh,
        in_specs=(
            P("sec", "tile", None),
            P("sec", "tile", None),
            P("sec", "tile", None, None),
            P("sec", "tile", None),
        ),
        out_specs=(P("sec", "tile", None), P("sec", "tile", None)),
        check_vma=False,
    )
```

```python
import functools
import math

import jax
import jax.numpy as jnp
import ml_dtypes
import numpy as np
from jax import lax
from jax.experimental import pallas as pl
from jax.experimental.pallas import tpu as pltpu
from jax.sharding import PartitionSpec as P

P_SIZE = 128
HALF = P_SIZE // 2
DS = 4
COARSE = 16
HALO = 80
LANES = 128
PAIR = 2 * P_SIZE
SUB = 8
POOLED = P_SIZE // DS
EPSILON = 1e-05
MESH = pl.DeviceIdType.MESH


def quantized(table):
    return table.astype(np.float32).astype(ml_dtypes.bfloat16)


def table_scale(n):
    cosines = np.cos(2.0 * np.pi * np.arange(n) / n)
    best = None
    for factor in np.linspace(1.0, 2.0, 4001):
        table = quantized(cosines * factor).astype(np.float64)
        gain = (table @ cosines) / (cosines @ cosines)
        error = np.mean((table / gain - cosines) ** 2)
        if best is None or error < best[0]:
            best = (error, factor, gain)
    return best[1], best[2]


def waves(n):
    k = np.arange(n)
    angles = (k[:, None] * k[None, :] % n) * (2.0 * np.pi / n)
    return np.cos(angles), np.sin(angles)


def row_tables():
    n = P_SIZE
    factor, gain = table_scale(n)
    cosines, sines = waves(n)
    alternating = np.where(np.arange(n) % 2 == 0, 1.0, -1.0)
    forward = np.concatenate([cosines[:HALF], sines[:HALF]])
    forward[HALF] = alternating
    weight = np.where(np.arange(HALF) == 0, 1.0, 2.0)[:, None]
    inverse = np.concatenate([cosines[:HALF] * weight, -sines[:HALF] * weight])
    inverse[HALF] = alternating
    pool = (np.arange(POOLED)[:, None] == np.arange(n)[None, :] // DS).astype(np.float64)
    forward = np.concatenate([forward * (factor / n), pool])
    return quantized(forward), quantized(inverse.T * (factor / n)), gain


def col_table(n):
    factor, gain = table_scale(n)
    cosines, sines = waves(n)
    table = np.block([[cosines, sines], [-sines, cosines]]) * (factor / n)
    return quantized(table), gain


def mm(a, b):
    return jnp.dot(a, b, preferred_element_type=jnp.float32)


def sublanes():
    return lax.broadcasted_iota(jnp.int32, (SUB, LANES), 0)


def to_lhs(rows):
    return jnp.concatenate([rows[:HALF], rows[HALF:]], axis=1).astype(jnp.bfloat16)


def energy(block):
    width = block.shape[1] // 2
    total = block[:, :width] * block[:, :width] + block[:, width:] * block[:, width:]
    head = jnp.where(lax.broadcasted_iota(jnp.int32, (SUB, width), 0) == 0, 0.0, total[:SUB])
    for at in range(SUB, HALF, SUB):
        head = head + total[at : at + SUB]
    return jnp.sum(head, axis=0, keepdims=True)


def spectrum(blocks, table):
    count = len(blocks)
    width = blocks[0].shape[1]
    sub = lax.broadcasted_iota(jnp.int32, (SUB, width), 0)
    first = jnp.zeros((SUB, width), jnp.float32)
    middle = jnp.zeros((SUB, width), jnp.float32)
    for p, rows in enumerate(blocks):
        first = jnp.where(sub == p, rows[0:1], first)
        middle = jnp.where(sub == p, rows[HALF : HALF + 1], middle)
    first = first - jnp.sum(first, axis=1, keepdims=True) * (1.0 / width)
    ends = jnp.concatenate([first, middle], axis=0)
    ends = jnp.concatenate([ends, jnp.zeros_like(ends)], axis=1).astype(jnp.bfloat16)
    freq = mm(jnp.concatenate([to_lhs(rows) for rows in blocks] + [ends], axis=0), table)
    power = jnp.zeros((SUB, width), jnp.float32)
    for p in range(count):
        power = jnp.where(sub == p, energy(freq[p * HALF : (p + 1) * HALF]), power)
    tail = freq[count * HALF :] * freq[count * HALF :]
    tail = tail[:SUB] + tail[SUB:]
    power = 2.0 * power + tail[:, :width] + tail[:, width:]
    return freq, jnp.sum(power, axis=1, keepdims=True)


def scaled(freq, count, factors):
    parts = [freq[p * HALF : (p + 1) * HALF] * factors[p : p + 1] for p in range(count)]
    for at in (0, SUB):
        parts.append(freq[count * HALF + at : count * HALF + at + SUB] * factors)
    return parts


def correlate(own, other, count, table):
    width = own.shape[1] // 2
    a_re, a_im = own[:, :width], own[:, width:]
    b_re, b_im = other[:, :width], other[:, width:]
    product = jnp.concatenate([a_re * b_re + a_im * b_im, a_im * b_re - a_re * b_im], axis=1)
    rows = mm(product.astype(jnp.bfloat16), table)
    sub = lax.broadcasted_iota(jnp.int32, (SUB, width), 0)
    at = count * HALF
    blocks = []
    for p in range(count):
        block = rows[p * HALF : (p + 1) * HALF]
        first = rows[at + p : at + p + 1, :width]
        middle = rows[at + SUB + p : at + SUB + p + 1, :width]
        parts = [
            jnp.where(sub == 0, first, block[:SUB, :width]),
            block[SUB:, :width],
            jnp.where(sub == 0, middle, block[:SUB, width:]),
            block[SUB:, width:],
        ]
        blocks.append(jnp.concatenate(parts, axis=0).astype(jnp.bfloat16))
    return blocks


def window_at(ref, row_at, col_at, height):
    block = lax.shift_right_logical(col_at, 7)
    shift = col_at & (LANES - 1)
    left = ref[block, pl.ds(row_at, height), :]
    right = ref[block + 1, pl.ds(row_at, height), :]
    lane = lax.broadcasted_iota(jnp.int32, (height, LANES), 1)
    return pltpu.roll(jnp.where(lane >= shift, left, right), (LANES - shift) & (LANES - 1), 1)


def unit_places(unit, bands, offsets, peaks):
    off_row = HALO + DS * offsets[0, 0, 0]
    off_col = LANES + DS * offsets[0, 0, 1]
    places = []
    for i in range(bands):
        for h in range(2):
            column = 2 * unit + h
            row_at = off_row + i * P_SIZE + peaks[0, i, 0, column]
            col_at = off_col + column * P_SIZE + peaks[0, i, 1, column]
            places.append((row_at, col_at))
    return places


def unit_windows(places, ext):
    cut = [window_at(ext, *place, P_SIZE).astype(jnp.bfloat16) for place in places]
    return [jnp.concatenate(cut[n : n + 2], axis=1) for n in range(0, len(cut), 2)]


def unit_keep(unit, bands, keep):
    sub = sublanes()
    flags = jnp.zeros((SUB, LANES), jnp.float32)
    for i in range(bands):
        for h in range(2):
            flag = keep[0, i, 2 * unit + h].astype(jnp.float32)
            flags = jnp.where(sub == 2 * i + h, flag, flags)
    return flags


def match_unit(bands, gains, windows, flags, own, row_tab, col_tab, inv_tab, write):
    blocks = []
    for window in windows:
        rows = mm(row_tab[:P_SIZE, :], window)
        blocks += [rows[:, :P_SIZE], rows[:, P_SIZE:]]
    yield
    freq, power = spectrum(blocks, col_tab[...])
    yield
    gain = gains[0] * gains[1]
    scale = (P_SIZE * P_SIZE / gain) ** 2 / P_SIZE
    factors = flags * (scale / jnp.sqrt(power * (1.0 / gain**2) + EPSILON))
    rows = correlate(own, freq, 2 * bands, col_tab[...])
    yield
    for i in range(bands):
        maps = mm(inv_tab[...], jnp.concatenate(rows[2 * i : 2 * i + 2], axis=1))
        for h in range(2):
            p = 2 * i + h
            write(i, h, maps[:, h * P_SIZE : (h + 1) * P_SIZE] * factors[p : p + 1])


def run(*stages):
    parts = list(stages)
    while parts:
        parts = [part for part in parts if next(part, True) is None]


def split(x):
    hi = x.astype(jnp.bfloat16)
    return hi, (x - hi.astype(jnp.float32)).astype(jnp.bfloat16)


def pooled(hi, lo, pool):
    span = pool.shape[0]
    parts = []
    for at in range(0, hi.shape[1], span):
        sums = mm(hi[:, at : at + span], pool) + mm(lo[:, at : at + span], pool)
        parts.append((sums * (1.0 / (DS * DS))).astype(jnp.bfloat16))
    return parts


def exchange_kernel(
    bands,
    units,
    gains,
    offsets_hbm,
    peaks_hbm,
    keep_hbm,
    img,
    row_hbm,
    col_hbm,
    inv_hbm,
    wide_hbm,
    pool_hbm,
    maps,
    coarse,
    windows,
    last_spec,
    flags,
    row_tab,
    col_tab,
    inv_tab,
    own,
    land,
    ext,
    spec,
    small_own,
    small_land,
    small,
    small_spec,
    own_hi,
    own_lo,
    sum_hi,
    sum_lo,
    wide_tab,
    pool,
    offsets,
    peaks,
    keep,
    relayed,
    send_sems,
    recv_sems,
    side_send,
    side_recv,
    relay_sems,
    local_sems,
):
    s = lax.axis_index("sec")
    t = lax.axis_index("tile")
    ns = lax.axis_size("sec")
    nt = lax.axis_size("tile")
    rows, width = own.shape
    columns = width // LANES
    centre = rows - 2 * HALO
    reach = rows + 2 * HALO
    row_gain, col_gain, wide_gain = gains
    early = columns // 2 + 1
    detours = (columns // 2, columns // 2 + 1)

    sends = s < ns - 1
    receives = s > 0
    has_up = t > 0
    has_down = t < nt - 1
    s_next = jnp.minimum(s + 1, ns - 1)
    s_prev = jnp.maximum(s - 1, 0)
    t_next = jnp.minimum(t + 1, nt - 1)
    t_prev = jnp.maximum(t - 1, 0)

    eighth = lax.rem(s, 8)
    starts_relay = (eighth == 3) & (s + 4 < ns)
    relays = eighth == 7
    ends_relay = (eighth == 4) & (s + 3 < ns)
    relay_from = jnp.maximum(s - 4, 0)
    relay_by = jnp.minimum(s + 4, ns - 1)
    relay_to = jnp.maximum(s - 3, 0)
    relayed_by = jnp.minimum(s + 3, ns - 1)

    barrier = pltpu.get_barrier_semaphore()
    for cond, peer in (
        (receives, (s_prev, t)),
        (ends_relay, (relayed_by, t)),
        (relays, (relay_from, t)),
        (has_up, (s, t_prev)),
        (has_down, (s, t_next)),
    ):

        @pl.when(cond)
        def _(peer=peer):
            pl.semaphore_signal(barrier, inc=1, device_id=peer, device_id_type=MESH)

    loads = [
        pltpu.make_async_copy(source, target, local_sems.at[n])
        for n, (source, target) in enumerate(
            (
                (img, own),
                (row_hbm, row_tab),
                (col_hbm, col_tab),
                (inv_hbm, inv_tab),
                (wide_hbm, wide_tab),
                (pool_hbm, pool),
                (offsets_hbm, offsets),
                (peaks_hbm, peaks),
                (keep_hbm, keep),
            )
        )
    ]
    for load in loads:
        load.start()
    peers = sum(jnp.where(cond, 1, 0) for cond in (sends, starts_relay, relays, has_up, has_down))
    pl.semaphore_wait(barrier, peers)

    def edge_copy(n):
        start = n * (rows - HALO)
        return pltpu.make_async_remote_copy(
            src_ref=img.at[pl.ds(start, HALO)],
            dst_ref=land.at[pl.ds(HALO + start, HALO)],
            send_sem=send_sems.at[n],
            recv_sem=recv_sems.at[n],
            device_id=(s_next, t),
            device_id_type=MESH,
        )

    def column_copy(c):
        at = pl.multiple_of(c * LANES, LANES)
        return pltpu.make_async_remote_copy(
            src_ref=img.at[pl.ds(HALO, centre), pl.ds(at, LANES)],
            dst_ref=land.at[pl.ds(2 * HALO, centre), pl.ds(at, LANES)],
            send_sem=send_sems.at[3 + c],
            recv_sem=recv_sems.at[3 + c],
            device_id=(s_next, t),
            device_id_type=MESH,
        )

    def relay_in(n):
        return pltpu.make_async_remote_copy(
            src_ref=img.at[pl.ds(HALO, centre), pl.ds(detours[n] * LANES, LANES)],
            dst_ref=relayed.at[n],
            send_sem=send_sems.at[3 + detours[n]],
            recv_sem=relay_sems.at[n],
            device_id=(relay_by, t),
            device_id_type=MESH,
        )

    def relay_out(n):
        return pltpu.make_async_remote_copy(
            src_ref=relayed.at[n],
            dst_ref=land.at[pl.ds(2 * HALO, centre), pl.ds(detours[n] * LANES, LANES)],
            send_sem=relay_sems.at[2 + n],
            recv_sem=recv_sems.at[3 + detours[n]],
            device_id=(relay_to, t),
            device_id_type=MESH,
        )

    def small_copy():
        return pltpu.make_async_remote_copy(
            src_ref=small_own.at[pl.ds(COARSE, small_land.shape[0]), pl.ds(LANES, LANES)],
            dst_ref=small_land,
            send_sem=send_sems.at[2],
            recv_sem=recv_sems.at[2],
            device_id=(s_next, t),
            device_id_type=MESH,
        )

    def side_copy(n):
        source, target, peer = ((HALO, HALO + rows, t_prev), (rows, 0, t_next))[n]
        return pltpu.make_async_remote_copy(
            src_ref=land.at[pl.ds(source, HALO)],
            dst_ref=land.at[pl.ds(target, HALO)],
            send_sem=side_send.at[n],
            recv_sem=side_recv.at[n],
            device_id=(s, peer),
            device_id_type=MESH,
        )

    @pl.when(sends)
    def _():
        edge_copy(0).start()
        edge_copy(1).start()
        for c in range(early):
            if c not in detours:
                column_copy(c).start()

    @pl.when(starts_relay)
    def _():
        for n in range(len(detours)):
            relay_in(n).start()

    @pl.when(sends & jnp.logical_not(starts_relay))
    def _():
        for c in range(early):
            if c in detours:
                column_copy(c).start()

    @pl.when(jnp.logical_not(receives))
    def _():
        land[...] = jnp.zeros_like(land)
        small_land[...] = jnp.zeros_like(small_land)

    @pl.when(receives & jnp.logical_not(has_up))
    def _():
        land[:HALO, :] = jnp.zeros((HALO, width), jnp.bfloat16)

    @pl.when(receives & jnp.logical_not(has_down))
    def _():
        land[HALO + rows :, :] = jnp.zeros((HALO, width), jnp.bfloat16)

    ext[0] = jnp.zeros((reach, LANES), jnp.float32)
    ext[columns + 1] = jnp.zeros((reach, LANES), jnp.float32)
    small[0] = jnp.zeros(small.shape[1:], jnp.float32)
    small[3] = jnp.zeros(small.shape[1:], jnp.float32)
    for load in loads:
        load.wait()

    def own_unit(u, carry):
        at = pl.multiple_of(u * PAIR, PAIR)
        blocks = []
        for i in range(bands):
            both = mm(row_tab[...], own[i * P_SIZE : (i + 1) * P_SIZE, pl.ds(at, PAIR)])
            blocks += [both[:P_SIZE, :P_SIZE], both[:P_SIZE, P_SIZE:]]
            hi, lo = split(both[P_SIZE:])
            own_hi[i * POOLED : (i + 1) * POOLED, pl.ds(at, PAIR)] = hi
            own_lo[i * POOLED : (i + 1) * POOLED, pl.ds(at, PAIR)] = lo
        freq, power = spectrum(blocks, col_tab[...])
        gain = row_gain * col_gain
        factors = (1.0 / gain) / jnp.sqrt(power * (1.0 / gain**2) + EPSILON)
        base = 0
        for part in scaled(freq, 2 * bands, factors):
            spec[u, base : base + part.shape[0], :] = part
            base += part.shape[0]
        return carry

    lax.fori_loop(0, units, own_unit, 0)
    for n, part in enumerate(pooled(own_hi[...], own_lo[...], pool[...])):
        small_own[:, n * LANES : (n + 1) * LANES] = part

    @pl.when(sends)
    def _():
        small_copy().start()

    @pl.when(sends & jnp.logical_not(starts_relay))
    def _():
        for c in range(early, columns):
            if c in detours:
                column_copy(c).start()

    @pl.when(sends)
    def _():
        for c in range(early, columns):
            if c not in detours:
                column_copy(c).start()

    @pl.when(receives)
    def _():
        edge_copy(0).wait_recv()

        @pl.when(has_up)
        def _():
            side_copy(0).start()

        edge_copy(1).wait_recv()

        @pl.when(has_down)
        def _():
            side_copy(1).start()

    last_spec[...] = spec[units - 1]
    flags[...] = unit_keep(units - 1, bands, keep)
    freq, power = spectrum([mm(row_tab[:P_SIZE, :], small_own[...])], wide_tab[...])
    gain = row_gain * wide_gain
    factors = (1.0 / gain) / jnp.sqrt(power * (1.0 / gain**2) + EPSILON)
    base = 0
    for part in scaled(freq, 1, factors):
        small_spec[base : base + part.shape[0], :] = part
        base += part.shape[0]

    @pl.when(receives)
    def _():
        @pl.when(has_up)
        def _():
            side_copy(1).wait_recv()

        @pl.when(has_down)
        def _():
            side_copy(0).wait_recv()

    for at in (0, HALO + rows - HALO):
        for c in range(columns):
            ext[c + 1, at : at + 2 * HALO, :] = land[
                at : at + 2 * HALO, c * LANES : (c + 1) * LANES
            ].astype(jnp.float32)

    def row_sums(c, at, count):
        sums = ext[c + 1, pl.ds(at, count, stride=DS), :]
        for k in range(1, DS):
            sums = sums + ext[c + 1, pl.ds(at + k, count, stride=DS), :]
        return split(sums)

    def arrive(c):
        @pl.when(receives)
        def _():
            column_copy(c).wait_recv()

        at = pl.multiple_of(c * LANES, LANES)
        ext[c + 1, 2 * HALO : 2 * HALO + centre, :] = land[
            2 * HALO : 2 * HALO + centre, pl.ds(at, LANES)
        ].astype(jnp.float32)

    def coarse_map():
        half = columns // 2
        first = HALO - DS * COARSE
        count = small.shape[1]
        for c in range(half):
            hi, lo = row_sums(c, first, count)
            sum_hi[:, c * LANES : (c + 1) * LANES] = hi
            sum_lo[:, c * LANES : (c + 1) * LANES] = lo
        small[1] = pooled(sum_hi[...], sum_lo[...], pool[...])[0].astype(jnp.float32)
        side = 2 * COARSE
        for c in range(half):
            for n, at in enumerate((first, first + DS * (count - side))):
                hi, lo = row_sums(half + c, at, side)
                sum_hi[n * side : (n + 1) * side, c * LANES : (c + 1) * LANES] = hi
                sum_lo[n * side : (n + 1) * side, c * LANES : (c + 1) * LANES] = lo

        ends = pooled(sum_hi[: 2 * side], sum_lo[: 2 * side], pool[...])[0].astype(jnp.float32)
        small[2, :side] = ends[:side]
        small[2, side : count - side] = small_land[...].astype(jnp.float32)
        small[2, count - side :] = ends[side:]
        yield
        height = count - 2 * COARSE
        window = [
            window_at(
                small, COARSE + offsets[0, 0, 0], LANES * (n + 1) + offsets[0, 0, 1], height
            ).astype(jnp.bfloat16)
            for n in range(2)
        ]
        block = mm(row_tab[:P_SIZE, :], jnp.concatenate(window, axis=1))
        yield
        freq, power = spectrum([block], wide_tab[...])
        yield
        gain = row_gain * wide_gain
        size = height * 2 * LANES
        scale = (size / gain) ** 2 / math.sqrt(size)
        factors = scale / jnp.sqrt(power * (1.0 / gain**2) + EPSILON)
        found = correlate(small_spec[...], freq, 1, wide_tab[...])[0]
        yield
        coarse[...] = mm(inv_tab[...], found) * factors[0:1]

    def unit_step(u):
        def write(i, h, value):
            at = u * PAIR + h * P_SIZE
            at = at if isinstance(u, int) else pl.multiple_of(at, P_SIZE)
            maps[i * P_SIZE : (i + 1) * P_SIZE, pl.ds(at, P_SIZE)] = value

        return match_unit(
            bands,
            (row_gain, col_gain),
            unit_windows(unit_places(u, bands, offsets, peaks), ext),
            unit_keep(u, bands, keep),
            spec[u],
            row_tab,
            col_tab,
            inv_tab,
            write,
        )

    def early_waits():
        @pl.when(receives & has_up)
        def _():
            side_copy(0).wait_send()

        @pl.when(receives & has_down)
        def _():
            side_copy(1).wait_send()

        @pl.when(sends)
        def _():
            edge_copy(0).wait_send()
            edge_copy(1).wait_send()
            small_copy().wait_send()
            for c in range(columns // 2):
                column_copy(c).wait_send()

    arrive(0)

    def step(k, carry):
        @pl.when(k == 0)
        def _():
            arrive(1)
            arrive(2)

        @pl.when(k == 1)
        def _():
            arrive(3)
            arrive(4)

            @pl.when(receives)
            def _():
                small_copy().wait_recv()

            run(coarse_map(), unit_step(1))
            early_waits()
            arrive(5)
            arrive(6)

        run(unit_step(2 * k))

        @pl.when(relays & (k == 0))
        def _():
            for n in range(len(detours)):
                relay_in(n).wait_recv()
                relay_out(n).start()

        return carry

    lax.fori_loop(0, 2, step, 0)
    places = unit_places(units - 1, bands, offsets, peaks)

    @pl.when(sends)
    def _():
        for c in range(columns // 2, columns):
            column_copy(c).wait_send()

    @pl.when(relays)
    def _():
        for n in range(len(detours)):
            relay_out(n).wait_send()

    arrive(columns - 1)
    for i, window in enumerate(unit_windows(places, ext)):
        windows[i] = window


def finish_kernel(
    bands,
    gains,
    maps,
    coarse,
    windows,
    last_spec,
    flags,
    row_tab,
    col_tab,
    inv_tab,
    coarse_out,
    flow_out,
    last_maps,
    sems,
):
    done = maps.shape[1]
    copies = [pltpu.make_async_copy(coarse, coarse_out.at[0], sems.at[2 * bands])]
    for i in range(bands):
        band = pl.ds(i * P_SIZE, P_SIZE)
        copies.append(pltpu.make_async_copy(maps.at[band], flow_out.at[0, band, pl.ds(0, done)], sems.at[i]))
    for copy in copies:
        copy.start()

    def write(i, h, value):
        last_maps[i * P_SIZE : (i + 1) * P_SIZE, h * P_SIZE : (h + 1) * P_SIZE] = value

    run(
        match_unit(
            bands,
            gains[:2],
            [windows[i] for i in range(bands)],
            flags[...],
            last_spec[...],
            row_tab,
            col_tab,
            inv_tab,
            write,
        )
    )
    for i in range(bands):
        band = pl.ds(i * P_SIZE, P_SIZE)
        copies.append(
            pltpu.make_async_copy(last_maps.at[band], flow_out.at[0, band, pl.ds(done, PAIR)], sems.at[bands + i])
        )
        copies[-1].start()
    for copy in copies:
        copy.wait()


def shards(section_image, offsets, peak_shift, accepted):
    own = section_image[0]
    rows, width = own.shape
    bands = rows // P_SIZE
    units = width // PAIR
    columns = width // LANES
    reach = rows + 2 * HALO
    small_width = width // DS
    forward_row, inverse_row, row_gain = row_tables()
    col, col_gain = col_table(P_SIZE)
    wide, wide_gain = col_table(small_width)
    gains = (float(row_gain), float(col_gain), float(wide_gain))
    span = DS * LANES
    pool = quantized(np.arange(span)[:, None] // DS == np.arange(LANES)[None, :])
    tables = [jnp.asarray(x) for x in (forward_row, col, inverse_row, wide, pool)]
    scalars = (offsets, jnp.swapaxes(peak_shift, 2, 3), accepted)
    high = 2 * bands * HALF + 2 * SUB
    small_high = HALF + 2 * SUB
    small_rows = rows // DS + 2 * COARSE
    hbm = pl.BlockSpec(memory_space=pltpu.HBM)
    vmem = pl.BlockSpec(memory_space=pltpu.VMEM)
    limit = 30 * 2**20
    operands = [pltpu.with_memory_space_constraint(x, pltpu.HBM) for x in (*scalars, own, *tables)]
    between = pl.pallas_call(
        functools.partial(exchange_kernel, bands, units, gains),
        name="exchange",
        out_shape=(
            jax.ShapeDtypeStruct((rows, width - PAIR), jnp.float32),
            jax.ShapeDtypeStruct((rows // DS, small_width), jnp.float32),
            jax.ShapeDtypeStruct((bands, P_SIZE, PAIR), jnp.bfloat16),
            jax.ShapeDtypeStruct((high, PAIR), jnp.float32),
            jax.ShapeDtypeStruct((SUB, LANES), jnp.float32),
        )
        + tuple(jax.ShapeDtypeStruct(x.shape, x.dtype) for x in tables[:3]),
        in_specs=[hbm] * 9,
        out_specs=(vmem,) * 8,
        scratch_shapes=[
            pltpu.VMEM((rows, width), jnp.bfloat16),
            pltpu.VMEM((reach, width), jnp.bfloat16),
            pltpu.VMEM((columns + 2, reach, LANES), jnp.float32),
            pltpu.VMEM((units, high, PAIR), jnp.float32),
            pltpu.VMEM((rows // DS, small_width), jnp.bfloat16),
            pltpu.VMEM((rows // DS - 2 * COARSE, LANES), jnp.bfloat16),
            pltpu.VMEM((small_width // LANES + 2, small_rows, LANES), jnp.float32),
            pltpu.VMEM((small_high, 2 * small_width), jnp.float32),
            pltpu.VMEM((rows // DS, width), jnp.bfloat16),
            pltpu.VMEM((rows // DS, width), jnp.bfloat16),
            pltpu.VMEM((small_rows, span), jnp.bfloat16),
            pltpu.VMEM((small_rows, span), jnp.bfloat16),
            pltpu.VMEM(wide.shape, jnp.bfloat16),
            pltpu.VMEM(pool.shape, jnp.bfloat16),
        ]
        + [pltpu.SMEM(x.shape, jnp.int32) for x in scalars]
        + [
            pltpu.VMEM((2, rows - 2 * HALO, LANES), jnp.bfloat16),
            pltpu.SemaphoreType.DMA((columns + 3,)),
            pltpu.SemaphoreType.DMA((columns + 3,)),
            pltpu.SemaphoreType.DMA((2,)),
            pltpu.SemaphoreType.DMA((2,)),
            pltpu.SemaphoreType.DMA((4,)),
            pltpu.SemaphoreType.DMA((len(operands),)),
        ],
        compiler_params=pltpu.CompilerParams(
            collective_id=0, has_side_effects=True, vmem_limit_bytes=limit
        ),
    )(*operands)
    return pl.pallas_call(
        functools.partial(finish_kernel, bands, gains),
        name="finish",
        out_shape=(
            jax.ShapeDtypeStruct((1, rows // DS, small_width), jnp.float32),
            jax.ShapeDtypeStruct((1, rows, width), jnp.float32),
        ),
        in_specs=[vmem] * 8,
        out_specs=(hbm, hbm),
        scratch_shapes=[
            pltpu.VMEM((rows, PAIR), jnp.float32),
            pltpu.SemaphoreType.DMA((2 * bands + 1,)),
        ],
        compiler_params=pltpu.CompilerParams(vmem_limit_bytes=limit),
    )(*between)


def solution(mesh):
    return jax.shard_map(
        shards,
        mesh=mesh,
        in_specs=(
            P("sec", "tile", None),
            P("sec", "tile", None),
            P("sec", "tile", None, None),
            P("sec", "tile", None),
        ),
        out_specs=(P("sec", "tile", None), P("sec", "tile", None)),
        check_vma=False,
    )
```

```python
import functools
import math

import jax
import jax.numpy as jnp
import ml_dtypes
import numpy as np
from jax import lax
from jax.experimental import pallas as pl
from jax.experimental.pallas import tpu as pltpu
from jax.sharding import PartitionSpec as P

P_SIZE = 128
HALF = P_SIZE // 2
DS = 4
COARSE = 16
HALO = 80
LANES = 128
PAIR = 2 * P_SIZE
SUB = 8
POOLED = P_SIZE // DS
EPSILON = 1e-05
MESH = pl.DeviceIdType.MESH


def quantized(table):
    return table.astype(np.float32).astype(ml_dtypes.bfloat16)


def table_scale(n):
    cosines = np.cos(2.0 * np.pi * np.arange(n) / n)
    best = None
    for factor in np.linspace(1.0, 2.0, 4001):
        table = quantized(cosines * factor).astype(np.float64)
        gain = (table @ cosines) / (cosines @ cosines)
        error = np.mean((table / gain - cosines) ** 2)
        if best is None or error < best[0]:
            best = (error, factor, gain)
    return best[1], best[2]


def waves(n):
    k = np.arange(n)
    angles = (k[:, None] * k[None, :] % n) * (2.0 * np.pi / n)
    return np.cos(angles), np.sin(angles)


def row_tables():
    n = P_SIZE
    factor, gain = table_scale(n)
    cosines, sines = waves(n)
    alternating = np.where(np.arange(n) % 2 == 0, 1.0, -1.0)
    forward = np.concatenate([cosines[:HALF], sines[:HALF]])
    forward[HALF] = alternating
    weight = np.where(np.arange(HALF) == 0, 1.0, 2.0)[:, None]
    inverse = np.concatenate([cosines[:HALF] * weight, -sines[:HALF] * weight])
    inverse[HALF] = alternating
    pool = (np.arange(POOLED)[:, None] == np.arange(n)[None, :] // DS).astype(np.float64)
    forward = np.concatenate([forward * (factor / n), pool])
    return quantized(forward), quantized(inverse.T * (factor / n)), gain


def col_table(n):
    factor, gain = table_scale(n)
    cosines, sines = waves(n)
    table = np.block([[cosines, sines], [-sines, cosines]]) * (factor / n)
    return quantized(table), gain


def mm(a, b):
    return jnp.dot(a, b, preferred_element_type=jnp.float32)


def sublanes():
    return lax.broadcasted_iota(jnp.int32, (SUB, LANES), 0)


def to_lhs(rows):
    return jnp.concatenate([rows[:HALF], rows[HALF:]], axis=1).astype(jnp.bfloat16)


def energy(block):
    width = block.shape[1] // 2
    total = block[:, :width] * block[:, :width] + block[:, width:] * block[:, width:]
    head = jnp.where(lax.broadcasted_iota(jnp.int32, (SUB, width), 0) == 0, 0.0, total[:SUB])
    for at in range(SUB, HALF, SUB):
        head = head + total[at : at + SUB]
    return jnp.sum(head, axis=0, keepdims=True)


def spectrum(blocks, table):
    count = len(blocks)
    width = blocks[0].shape[1]
    sub = lax.broadcasted_iota(jnp.int32, (SUB, width), 0)
    first = jnp.zeros((SUB, width), jnp.float32)
    middle = jnp.zeros((SUB, width), jnp.float32)
    for p, rows in enumerate(blocks):
        first = jnp.where(sub == p, rows[0:1], first)
        middle = jnp.where(sub == p, rows[HALF : HALF + 1], middle)
    first = first - jnp.sum(first, axis=1, keepdims=True) * (1.0 / width)
    ends = jnp.concatenate([first, middle], axis=0)
    ends = jnp.concatenate([ends, jnp.zeros_like(ends)], axis=1).astype(jnp.bfloat16)
    freq = mm(jnp.concatenate([to_lhs(rows) for rows in blocks] + [ends], axis=0), table)
    power = jnp.zeros((SUB, width), jnp.float32)
    for p in range(count):
        power = jnp.where(sub == p, energy(freq[p * HALF : (p + 1) * HALF]), power)
    tail = freq[count * HALF :] * freq[count * HALF :]
    tail = tail[:SUB] + tail[SUB:]
    power = 2.0 * power + tail[:, :width] + tail[:, width:]
    return freq, jnp.sum(power, axis=1, keepdims=True)


def scaled(freq, count, factors):
    parts = [freq[p * HALF : (p + 1) * HALF] * factors[p : p + 1] for p in range(count)]
    for at in (0, SUB):
        parts.append(freq[count * HALF + at : count * HALF + at + SUB] * factors)
    return parts


def correlate(own, other, count, table):
    width = own.shape[1] // 2
    a_re, a_im = own[:, :width], own[:, width:]
    b_re, b_im = other[:, :width], other[:, width:]
    product = jnp.concatenate([a_re * b_re + a_im * b_im, a_im * b_re - a_re * b_im], axis=1)
    rows = mm(product.astype(jnp.bfloat16), table)
    sub = lax.broadcasted_iota(jnp.int32, (SUB, width), 0)
    at = count * HALF
    blocks = []
    for p in range(count):
        block = rows[p * HALF : (p + 1) * HALF]
        first = rows[at + p : at + p + 1, :width]
        middle = rows[at + SUB + p : at + SUB + p + 1, :width]
        parts = [
            jnp.where(sub == 0, first, block[:SUB, :width]),
            block[SUB:, :width],
            jnp.where(sub == 0, middle, block[:SUB, width:]),
            block[SUB:, width:],
        ]
        blocks.append(jnp.concatenate(parts, axis=0).astype(jnp.bfloat16))
    return blocks


def window_at(ref, row_at, col_at, height):
    block = lax.shift_right_logical(col_at, 7)
    shift = col_at & (LANES - 1)
    left = ref[block, pl.ds(row_at, height), :]
    right = ref[block + 1, pl.ds(row_at, height), :]
    lane = lax.broadcasted_iota(jnp.int32, (height, LANES), 1)
    return pltpu.roll(jnp.where(lane >= shift, left, right), (LANES - shift) & (LANES - 1), 1)


def unit_places(unit, bands, offsets, peaks):
    off_row = HALO + DS * offsets[0, 0, 0]
    off_col = LANES + DS * offsets[0, 0, 1]
    places = []
    for i in range(bands):
        for h in range(2):
            column = 2 * unit + h
            row_at = off_row + i * P_SIZE + peaks[0, i, 0, column]
            col_at = off_col + column * P_SIZE + peaks[0, i, 1, column]
            places.append((row_at, col_at))
    return places


def unit_windows(places, ext):
    cut = [window_at(ext, *place, P_SIZE).astype(jnp.bfloat16) for place in places]
    return [jnp.concatenate(cut[n : n + 2], axis=1) for n in range(0, len(cut), 2)]


def unit_keep(unit, bands, keep):
    sub = sublanes()
    flags = jnp.zeros((SUB, LANES), jnp.float32)
    for i in range(bands):
        for h in range(2):
            flag = keep[0, i, 2 * unit + h].astype(jnp.float32)
            flags = jnp.where(sub == 2 * i + h, flag, flags)
    return flags


def match_unit(bands, gains, windows, flags, own, row_tab, col_tab, inv_tab, write):
    blocks = []
    for window in windows:
        rows = mm(row_tab[:P_SIZE, :], window)
        blocks += [rows[:, :P_SIZE], rows[:, P_SIZE:]]
    yield
    freq, power = spectrum(blocks, col_tab[...])
    yield
    gain = gains[0] * gains[1]
    scale = (P_SIZE * P_SIZE / gain) ** 2 / P_SIZE
    factors = flags * (scale / jnp.sqrt(power * (1.0 / gain**2) + EPSILON))
    rows = correlate(own, freq, 2 * bands, col_tab[...])
    yield
    for i in range(bands):
        maps = mm(inv_tab[...], jnp.concatenate(rows[2 * i : 2 * i + 2], axis=1))
        for h in range(2):
            p = 2 * i + h
            write(i, h, maps[:, h * P_SIZE : (h + 1) * P_SIZE] * factors[p : p + 1])


def run(*stages):
    parts = list(stages)
    while parts:
        parts = [part for part in parts if next(part, True) is None]


def split(x):
    hi = x.astype(jnp.bfloat16)
    return hi, (x - hi.astype(jnp.float32)).astype(jnp.bfloat16)


def pooled(hi, lo, pool):
    span = pool.shape[0]
    parts = []
    for at in range(0, hi.shape[1], span):
        sums = mm(hi[:, at : at + span], pool) + mm(lo[:, at : at + span], pool)
        parts.append((sums * (1.0 / (DS * DS))).astype(jnp.bfloat16))
    return parts


def exchange_kernel(
    bands,
    units,
    gains,
    offsets_hbm,
    peaks_hbm,
    keep_hbm,
    img,
    row_hbm,
    col_hbm,
    inv_hbm,
    wide_hbm,
    pool_hbm,
    maps,
    coarse,
    windows,
    last_spec,
    flags,
    row_tab,
    col_tab,
    inv_tab,
    own,
    land,
    ext,
    spec,
    small_own,
    small_land,
    small,
    small_spec,
    own_hi,
    own_lo,
    sum_hi,
    sum_lo,
    wide_tab,
    pool,
    offsets,
    peaks,
    keep,
    relayed,
    send_sems,
    recv_sems,
    side_send,
    side_recv,
    relay_sems,
    local_sems,
):
    s = lax.axis_index("sec")
    t = lax.axis_index("tile")
    ns = lax.axis_size("sec")
    nt = lax.axis_size("tile")
    rows, width = own.shape
    columns = width // LANES
    centre = rows - 2 * HALO
    reach = rows + 2 * HALO
    row_gain, col_gain, wide_gain = gains
    early = columns // 2 + 1
    detours = (columns // 2, columns // 2 + 1)

    sends = s < ns - 1
    receives = s > 0
    has_up = t > 0
    has_down = t < nt - 1
    s_next = jnp.minimum(s + 1, ns - 1)
    s_prev = jnp.maximum(s - 1, 0)
    t_next = jnp.minimum(t + 1, nt - 1)
    t_prev = jnp.maximum(t - 1, 0)

    eighth = lax.rem(s, 8)
    starts_relay = (eighth == 3) & (s + 4 < ns)
    relays = eighth == 7
    ends_relay = (eighth == 4) & (s + 3 < ns)
    relay_from = jnp.maximum(s - 4, 0)
    relay_by = jnp.minimum(s + 4, ns - 1)
    relay_to = jnp.maximum(s - 3, 0)
    relayed_by = jnp.minimum(s + 3, ns - 1)

    barrier = pltpu.get_barrier_semaphore()
    for cond, peer in (
        (receives, (s_prev, t)),
        (ends_relay, (relayed_by, t)),
        (relays, (relay_from, t)),
        (has_up, (s, t_prev)),
        (has_down, (s, t_next)),
    ):

        @pl.when(cond)
        def _(peer=peer):
            pl.semaphore_signal(barrier, inc=1, device_id=peer, device_id_type=MESH)

    loads = [
        pltpu.make_async_copy(source, target, local_sems.at[n])
        for n, (source, target) in enumerate(
            (
                (img, own),
                (row_hbm, row_tab),
                (col_hbm, col_tab),
                (inv_hbm, inv_tab),
                (wide_hbm, wide_tab),
                (pool_hbm, pool),
                (offsets_hbm, offsets),
                (peaks_hbm, peaks),
                (keep_hbm, keep),
            )
        )
    ]
    for load in loads:
        load.start()
    peers = sum(jnp.where(cond, 1, 0) for cond in (sends, starts_relay, relays, has_up, has_down))
    pl.semaphore_wait(barrier, peers)

    def edge_copy(n):
        start = n * (rows - HALO)
        return pltpu.make_async_remote_copy(
            src_ref=img.at[pl.ds(start, HALO)],
            dst_ref=land.at[pl.ds(HALO + start, HALO)],
            send_sem=send_sems.at[n],
            recv_sem=recv_sems.at[n],
            device_id=(s_next, t),
            device_id_type=MESH,
        )

    def column_copy(c):
        at = pl.multiple_of(c * LANES, LANES)
        return pltpu.make_async_remote_copy(
            src_ref=img.at[pl.ds(HALO, centre), pl.ds(at, LANES)],
            dst_ref=land.at[pl.ds(2 * HALO, centre), pl.ds(at, LANES)],
            send_sem=send_sems.at[3 + c],
            recv_sem=recv_sems.at[3 + c],
            device_id=(s_next, t),
            device_id_type=MESH,
        )

    def relay_in(n):
        return pltpu.make_async_remote_copy(
            src_ref=img.at[pl.ds(HALO, centre), pl.ds(detours[n] * LANES, LANES)],
            dst_ref=relayed.at[n],
            send_sem=send_sems.at[3 + detours[n]],
            recv_sem=relay_sems.at[n],
            device_id=(relay_by, t),
            device_id_type=MESH,
        )

    def relay_out(n):
        return pltpu.make_async_remote_copy(
            src_ref=relayed.at[n],
            dst_ref=land.at[pl.ds(2 * HALO, centre), pl.ds(detours[n] * LANES, LANES)],
            send_sem=relay_sems.at[2 + n],
            recv_sem=recv_sems.at[3 + detours[n]],
            device_id=(relay_to, t),
            device_id_type=MESH,
        )

    def small_copy():
        return pltpu.make_async_remote_copy(
            src_ref=small_own.at[pl.ds(COARSE, small_land.shape[0]), pl.ds(LANES, LANES)],
            dst_ref=small_land,
            send_sem=send_sems.at[2],
            recv_sem=recv_sems.at[2],
            device_id=(s_next, t),
            device_id_type=MESH,
        )

    def side_copy(n):
        source, target, peer = ((HALO, HALO + rows, t_prev), (rows, 0, t_next))[n]
        return pltpu.make_async_remote_copy(
            src_ref=land.at[pl.ds(source, HALO)],
            dst_ref=land.at[pl.ds(target, HALO)],
            send_sem=side_send.at[n],
            recv_sem=side_recv.at[n],
            device_id=(s, peer),
            device_id_type=MESH,
        )

    @pl.when(sends)
    def _():
        edge_copy(0).start()
        edge_copy(1).start()
        for c in range(early):
            if c not in detours:
                column_copy(c).start()

    @pl.when(starts_relay)
    def _():
        for n in range(len(detours)):
            relay_in(n).start()

    @pl.when(sends & jnp.logical_not(starts_relay))
    def _():
        for c in range(early):
            if c in detours:
                column_copy(c).start()

    @pl.when(jnp.logical_not(receives))
    def _():
        land[...] = jnp.zeros_like(land)
        small_land[...] = jnp.zeros_like(small_land)

    @pl.when(receives & jnp.logical_not(has_up))
    def _():
        land[:HALO, :] = jnp.zeros((HALO, width), jnp.bfloat16)

    @pl.when(receives & jnp.logical_not(has_down))
    def _():
        land[HALO + rows :, :] = jnp.zeros((HALO, width), jnp.bfloat16)

    ext[0] = jnp.zeros((reach, LANES), jnp.float32)
    ext[columns + 1] = jnp.zeros((reach, LANES), jnp.float32)
    small[0] = jnp.zeros(small.shape[1:], jnp.float32)
    small[3] = jnp.zeros(small.shape[1:], jnp.float32)
    for load in loads:
        load.wait()

    def own_unit(u, carry):
        at = pl.multiple_of(u * PAIR, PAIR)
        blocks = []
        for i in range(bands):
            both = mm(row_tab[...], own[i * P_SIZE : (i + 1) * P_SIZE, pl.ds(at, PAIR)])
            blocks += [both[:P_SIZE, :P_SIZE], both[:P_SIZE, P_SIZE:]]
            hi, lo = split(both[P_SIZE:])
            own_hi[i * POOLED : (i + 1) * POOLED, pl.ds(at, PAIR)] = hi
            own_lo[i * POOLED : (i + 1) * POOLED, pl.ds(at, PAIR)] = lo
        freq, power = spectrum(blocks, col_tab[...])
        gain = row_gain * col_gain
        factors = (1.0 / gain) / jnp.sqrt(power * (1.0 / gain**2) + EPSILON)
        base = 0
        for part in scaled(freq, 2 * bands, factors):
            spec[u, base : base + part.shape[0], :] = part
            base += part.shape[0]
        return carry

    lax.fori_loop(0, units, own_unit, 0)
    for n, part in enumerate(pooled(own_hi[...], own_lo[...], pool[...])):
        small_own[:, n * LANES : (n + 1) * LANES] = part

    @pl.when(sends)
    def _():
        small_copy().start()

    @pl.when(sends & jnp.logical_not(starts_relay))
    def _():
        for c in range(early, columns):
            if c in detours:
                column_copy(c).start()

    @pl.when(sends)
    def _():
        for c in range(early, columns):
            if c not in detours:
                column_copy(c).start()

    @pl.when(receives)
    def _():
        edge_copy(0).wait_recv()

        @pl.when(has_up)
        def _():
            side_copy(0).start()

        edge_copy(1).wait_recv()

        @pl.when(has_down)
        def _():
            side_copy(1).start()

    last_spec[...] = spec[units - 1]
    flags[...] = unit_keep(units - 1, bands, keep)
    freq, power = spectrum([mm(row_tab[:P_SIZE, :], small_own[...])], wide_tab[...])
    gain = row_gain * wide_gain
    factors = (1.0 / gain) / jnp.sqrt(power * (1.0 / gain**2) + EPSILON)
    base = 0
    for part in scaled(freq, 1, factors):
        small_spec[base : base + part.shape[0], :] = part
        base += part.shape[0]

    @pl.when(receives)
    def _():
        @pl.when(has_up)
        def _():
            side_copy(1).wait_recv()

        @pl.when(has_down)
        def _():
            side_copy(0).wait_recv()

    for at in (0, HALO + rows - HALO):
        for c in range(columns):
            ext[c + 1, at : at + 2 * HALO, :] = land[
                at : at + 2 * HALO, c * LANES : (c + 1) * LANES
            ].astype(jnp.float32)

    def row_sums(c, at, count):
        sums = ext[c + 1, pl.ds(at, count, stride=DS), :]
        for k in range(1, DS):
            sums = sums + ext[c + 1, pl.ds(at + k, count, stride=DS), :]
        return split(sums)

    def arrive(c):
        @pl.when(receives)
        def _():
            column_copy(c).wait_recv()

        at = pl.multiple_of(c * LANES, LANES)
        ext[c + 1, 2 * HALO : 2 * HALO + centre, :] = land[
            2 * HALO : 2 * HALO + centre, pl.ds(at, LANES)
        ].astype(jnp.float32)

    def coarse_map():
        half = columns // 2
        first = HALO - DS * COARSE
        count = small.shape[1]
        for c in range(half):
            hi, lo = row_sums(c, first, count)
            sum_hi[:, c * LANES : (c + 1) * LANES] = hi
            sum_lo[:, c * LANES : (c + 1) * LANES] = lo
        small[1] = pooled(sum_hi[...], sum_lo[...], pool[...])[0].astype(jnp.float32)
        side = 2 * COARSE
        for c in range(half):
            for n, at in enumerate((first, first + DS * (count - side))):
                hi, lo = row_sums(half + c, at, side)
                sum_hi[n * side : (n + 1) * side, c * LANES : (c + 1) * LANES] = hi
                sum_lo[n * side : (n + 1) * side, c * LANES : (c + 1) * LANES] = lo

        ends = pooled(sum_hi[: 2 * side], sum_lo[: 2 * side], pool[...])[0].astype(jnp.float32)
        small[2, :side] = ends[:side]
        small[2, side : count - side] = small_land[...].astype(jnp.float32)
        small[2, count - side :] = ends[side:]
        yield
        height = count - 2 * COARSE
        window = [
            window_at(
                small, COARSE + offsets[0, 0, 0], LANES * (n + 1) + offsets[0, 0, 1], height
            ).astype(jnp.bfloat16)
            for n in range(2)
        ]
        block = mm(row_tab[:P_SIZE, :], jnp.concatenate(window, axis=1))
        yield
        freq, power = spectrum([block], wide_tab[...])
        yield
        gain = row_gain * wide_gain
        size = height * 2 * LANES
        scale = (size / gain) ** 2 / math.sqrt(size)
        factors = scale / jnp.sqrt(power * (1.0 / gain**2) + EPSILON)
        found = correlate(small_spec[...], freq, 1, wide_tab[...])[0]
        yield
        coarse[...] = mm(inv_tab[...], found) * factors[0:1]

    def unit_step(u):
        def write(i, h, value):
            at = u * PAIR + h * P_SIZE
            at = at if isinstance(u, int) else pl.multiple_of(at, P_SIZE)
            maps[i * P_SIZE : (i + 1) * P_SIZE, pl.ds(at, P_SIZE)] = value

        return match_unit(
            bands,
            (row_gain, col_gain),
            unit_windows(unit_places(u, bands, offsets, peaks), ext),
            unit_keep(u, bands, keep),
            spec[u],
            row_tab,
            col_tab,
            inv_tab,
            write,
        )

    def early_waits():
        @pl.when(receives & has_up)
        def _():
            side_copy(0).wait_send()

        @pl.when(receives & has_down)
        def _():
            side_copy(1).wait_send()

        @pl.when(sends)
        def _():
            edge_copy(0).wait_send()
            edge_copy(1).wait_send()
            small_copy().wait_send()
            for c in range(columns // 2):
                column_copy(c).wait_send()

    arrive(0)

    def step(k, carry):
        @pl.when(k == 0)
        def _():
            arrive(1)
            arrive(2)

        @pl.when(k == 1)
        def _():
            arrive(3)
            arrive(4)

            @pl.when(receives)
            def _():
                small_copy().wait_recv()

            run(coarse_map(), unit_step(1))
            early_waits()
            arrive(5)
            arrive(6)

        run(unit_step(2 * k))

        @pl.when(relays & (k == 0))
        def _():
            for n in range(len(detours)):
                relay_in(n).wait_recv()
                relay_out(n).start()

        return carry

    lax.fori_loop(0, 2, step, 0)
    places = unit_places(units - 1, bands, offsets, peaks)

    @pl.when(sends)
    def _():
        for c in range(columns // 2, columns):
            column_copy(c).wait_send()

    @pl.when(relays)
    def _():
        for n in range(len(detours)):
            relay_out(n).wait_send()

    arrive(columns - 1)
    for i, window in enumerate(unit_windows(places, ext)):
        windows[i] = window


def finish_kernel(
    bands,
    gains,
    maps,
    coarse,
    windows,
    last_spec,
    flags,
    row_tab,
    col_tab,
    inv_tab,
    coarse_out,
    flow_out,
    last_maps,
    sems,
):
    done = maps.shape[1]
    copies = [pltpu.make_async_copy(coarse, coarse_out.at[0], sems.at[2 * bands])]
    for i in range(bands):
        band = pl.ds(i * P_SIZE, P_SIZE)
        copies.append(pltpu.make_async_copy(maps.at[band], flow_out.at[0, band, pl.ds(0, done)], sems.at[i]))
    for copy in copies:
        copy.start()

    def write(i, h, value):
        last_maps[i * P_SIZE : (i + 1) * P_SIZE, h * P_SIZE : (h + 1) * P_SIZE] = value
        if h == 1:
            band = pl.ds(i * P_SIZE, P_SIZE)
            target = flow_out.at[0, band, pl.ds(done, PAIR)]
            copies.append(pltpu.make_async_copy(last_maps.at[band], target, sems.at[bands + i]))
            copies[-1].start()

    run(
        match_unit(
            bands,
            gains[:2],
            [windows[i] for i in range(bands)],
            flags[...],
            last_spec[...],
            row_tab,
            col_tab,
            inv_tab,
            write,
        )
    )
    for copy in copies:
        copy.wait()


def shards(section_image, offsets, peak_shift, accepted):
    own = section_image[0]
    rows, width = own.shape
    bands = rows // P_SIZE
    units = width // PAIR
    columns = width // LANES
    reach = rows + 2 * HALO
    small_width = width // DS
    forward_row, inverse_row, row_gain = row_tables()
    col, col_gain = col_table(P_SIZE)
    wide, wide_gain = col_table(small_width)
    gains = (float(row_gain), float(col_gain), float(wide_gain))
    span = DS * LANES
    pool = quantized(np.arange(span)[:, None] // DS == np.arange(LANES)[None, :])
    tables = [jnp.asarray(x) for x in (forward_row, col, inverse_row, wide, pool)]
    scalars = (offsets, jnp.swapaxes(peak_shift, 2, 3), accepted)
    high = 2 * bands * HALF + 2 * SUB
    small_high = HALF + 2 * SUB
    small_rows = rows // DS + 2 * COARSE
    hbm = pl.BlockSpec(memory_space=pltpu.HBM)
    vmem = pl.BlockSpec(memory_space=pltpu.VMEM)
    limit = 30 * 2**20
    operands = [pltpu.with_memory_space_constraint(x, pltpu.HBM) for x in (*scalars, own, *tables)]
    between = pl.pallas_call(
        functools.partial(exchange_kernel, bands, units, gains),
        name="exchange",
        out_shape=(
            jax.ShapeDtypeStruct((rows, width - PAIR), jnp.float32),
            jax.ShapeDtypeStruct((rows // DS, small_width), jnp.float32),
            jax.ShapeDtypeStruct((bands, P_SIZE, PAIR), jnp.bfloat16),
            jax.ShapeDtypeStruct((high, PAIR), jnp.float32),
            jax.ShapeDtypeStruct((SUB, LANES), jnp.float32),
        )
        + tuple(jax.ShapeDtypeStruct(x.shape, x.dtype) for x in tables[:3]),
        in_specs=[hbm] * 9,
        out_specs=(vmem,) * 8,
        scratch_shapes=[
            pltpu.VMEM((rows, width), jnp.bfloat16),
            pltpu.VMEM((reach, width), jnp.bfloat16),
            pltpu.VMEM((columns + 2, reach, LANES), jnp.float32),
            pltpu.VMEM((units, high, PAIR), jnp.float32),
            pltpu.VMEM((rows // DS, small_width), jnp.bfloat16),
            pltpu.VMEM((rows // DS - 2 * COARSE, LANES), jnp.bfloat16),
            pltpu.VMEM((small_width // LANES + 2, small_rows, LANES), jnp.float32),
            pltpu.VMEM((small_high, 2 * small_width), jnp.float32),
            pltpu.VMEM((rows // DS, width), jnp.bfloat16),
            pltpu.VMEM((rows // DS, width), jnp.bfloat16),
            pltpu.VMEM((small_rows, span), jnp.bfloat16),
            pltpu.VMEM((small_rows, span), jnp.bfloat16),
            pltpu.VMEM(wide.shape, jnp.bfloat16),
            pltpu.VMEM(pool.shape, jnp.bfloat16),
        ]
        + [pltpu.SMEM(x.shape, jnp.int32) for x in scalars]
        + [
            pltpu.VMEM((2, rows - 2 * HALO, LANES), jnp.bfloat16),
            pltpu.SemaphoreType.DMA((columns + 3,)),
            pltpu.SemaphoreType.DMA((columns + 3,)),
            pltpu.SemaphoreType.DMA((2,)),
            pltpu.SemaphoreType.DMA((2,)),
            pltpu.SemaphoreType.DMA((4,)),
            pltpu.SemaphoreType.DMA((len(operands),)),
        ],
        compiler_params=pltpu.CompilerParams(
            collective_id=0, has_side_effects=True, vmem_limit_bytes=limit
        ),
    )(*operands)
    return pl.pallas_call(
        functools.partial(finish_kernel, bands, gains),
        name="finish",
        out_shape=(
            jax.ShapeDtypeStruct((1, rows // DS, small_width), jnp.float32),
            jax.ShapeDtypeStruct((1, rows, width), jnp.float32),
        ),
        in_specs=[vmem] * 8,
        out_specs=(hbm, hbm),
        scratch_shapes=[
            pltpu.VMEM((rows, PAIR), jnp.float32),
            pltpu.SemaphoreType.DMA((2 * bands + 1,)),
        ],
        compiler_params=pltpu.CompilerParams(vmem_limit_bytes=limit),
    )(*between)


def solution(mesh):
    return jax.shard_map(
        shards,
        mesh=mesh,
        in_specs=(
            P("sec", "tile", None),
            P("sec", "tile", None),
            P("sec", "tile", None, None),
            P("sec", "tile", None),
        ),
        out_specs=(P("sec", "tile", None), P("sec", "tile", None)),
        check_vma=False,
    )
```
